32 devices in a mesh: fsdp: 8 (over y, x, core), seq: 4 (over z).
Axes of the slice: x: 2, y: 2, z: 4, core: 2. Of those that a mesh axis runs over, the one named last changes fastest.
Arguments:
- layer_input: bfloat16 [16, 1024, 512], P('fsdp', 'seq'), may hold values from -6 to 6
- lengths: int32 [16], P('fsdp'), may hold values from 512 to 1024, as said below
- ln1_gain: bfloat16 [512], P('fsdp'), may hold values from 0.099609375 to 1.8984375
- ln1_bias: bfloat16 [512], P('fsdp'), may hold values from -1.5 to 1.5
- w_qkv: bfloat16 [512, 1536], P('fsdp'), may hold values from -0.25 to 0.25
- w_rel: bfloat16 [512, 512], P('fsdp'), may hold values from -0.25 to 0.25
- bias_u: bfloat16 [512], P('fsdp'), may hold values from -2.5 to 2.5
- bias_v: bfloat16 [512], P('fsdp'), may hold values from -2.5 to 2.5
- w_out: bfloat16 [512, 512], P('fsdp'), may hold values from -3 to 3
- ln2_gain: bfloat16 [512], P('fsdp'), may hold values from 0.099609375 to 1.8984375
- ln2_bias: bfloat16 [512], P('fsdp'), may hold values from -1.5 to 1.5
- w_up: bfloat16 [512, 2048], P('fsdp'), may hold values from -0.25 to 0.25
- up_bias: bfloat16 [2048], P('fsdp'), may hold values from -2.5 to 2.5
- w_down: bfloat16 [2048, 512], P('fsdp'), may hold values from -0.125 to 0.125
- down_bias: bfloat16 [512], P('fsdp'), may hold values from -1.5 to 1.5
- grad_out: bfloat16 [16, 1024, 512], P('fsdp', 'seq'), may hold values from -6 to 6
Outputs:
- layer_output: bfloat16 [16, 1024, 512], P('fsdp', 'seq')
- grad_x: float32 [16, 1024, 512], P('fsdp', 'seq')
- grad_ln1_gain: float32 [512], P('fsdp')
- grad_ln1_bias: float32 [512], P('fsdp')
- grad_w_qkv: float32 [512, 1536], P('fsdp')
- grad_w_rel: float32 [512, 512], P('fsdp')
- grad_bias_u: float32 [512], P('fsdp')
- grad_bias_v: float32 [512], P('fsdp')
- grad_w_out: float32 [512, 512], P('fsdp')
- grad_ln2_gain: float32 [512], P('fsdp')
- grad_ln2_bias: float32 [512], P('fsdp')
- grad_w_up: float32 [512, 2048], P('fsdp')
- grad_up_bias: float32 [2048], P('fsdp')
- grad_w_down: float32 [2048, 512], P('fsdp')
- grad_down_bias: float32 [512], P('fsdp')
The draws below stay inside these ranges and needn't reach their ends.
Inputs may be any that keep to these rules, and one draw needn't show every extreme that they name: `lengths`: in every draw some slot has exactly 1024 live positions and some exactly 512.
All inputs are finite; a program needn't handle non-finite values.
Results may differ from the reference program's by a relative error of at most 0.017.
Values may be sent and summed in bfloat16 or wider, within the bound.
No kernel may reach another device: no remote copies, remote signals or barrier semaphores. Data moves between devices by JAX's collectives and lax.ppermute only.
A program may use at most 192 MiB of HBM per device.

```python
import math
import jax
import jax.numpy as jnp
from jax import lax

D = 512
H = 8
FF = 2048
HEAD_DIM = 64
SEQ_LEN = 1024
BATCH = 16


def draw_lengths(key, part):
    base = jax.random.randint(jax.random.fold_in(key, 11), (BATCH,), SEQ_LEN // 2, SEQ_LEN + 1)
    first = jax.random.randint(jax.random.fold_in(key, 12), (), 0, BATCH)
    other = (first + 1 + jax.random.randint(jax.random.fold_in(key, 13), (), 0, BATCH - 1)) % BATCH
    return base.at[first].set(SEQ_LEN).at[other].set(SEQ_LEN // 2).astype(jnp.int32)


def block_scale(stream_key, extent, cuts, low, largest):
    def one(axis_at, shards_of):
        draws = jax.random.uniform(jax.random.fold_in(jax.random.fold_in(stream_key, 6), axis_at), (shards_of,), jnp.float32, low / len(cuts), largest / len(cuts))
        return jnp.repeat(jnp.exp(draws), extent[axis_at] // shards_of).reshape((-1,) + (1,) * (len(extent) - axis_at - 1))

    level = one(*cuts[0])
    for cut in cuts[1:]:
        level = level * one(*cut)
    return level


def scatter_about(stream_key, extent, scale, limit, split=(), dtype=jnp.bfloat16):
    factor_of = block_scale(stream_key, extent, split, -0.22, 0.18) if split else 1.0
    array = jax.random.normal(stream_key, extent, jnp.float32) * scale * factor_of
    return jnp.minimum(jnp.maximum(array, -limit), limit).astype(dtype)


def setup_inputs(seed: int = 0) -> dict:
    arg_keys = jax.random.split(jax.random.key(seed), 17)
    return {
        "layer_input": scatter_about(arg_keys[0], (BATCH, SEQ_LEN, D), 1.0, 6.0, ((0, 8), (1, 4))),
        "lengths": draw_lengths(jax.random.fold_in(arg_keys[16], 71), 0),
        "ln1_gain": jnp.clip(1.0 + 0.18 * jax.random.normal(arg_keys[2], (D,), jnp.float32), 0.099609375, 1.8984375).astype(jnp.bfloat16),
        "ln1_bias": scatter_about(arg_keys[3], (D,), 0.3, 1.5, ((0, 8),)),
        "w_qkv": scatter_about(arg_keys[4], (D, 3 * D), D ** -0.5, 0.25, ((0, 8),)),
        "w_rel": scatter_about(arg_keys[5], (D, D), D ** -0.5, 0.25, ((0, 8),)),
        "bias_u": scatter_about(arg_keys[6], (D,), 0.5, 2.5, ((0, 8),)),
        "bias_v": scatter_about(arg_keys[7], (D,), 0.5, 2.5, ((0, 8),)),
        "w_out": scatter_about(arg_keys[8], (D, D), (max(D // 128, 1)) ** -0.5, 3.0, ((0, 8),)),
        "ln2_gain": jnp.clip(1.0 + 0.18 * jax.random.normal(arg_keys[9], (D,), jnp.float32), 0.099609375, 1.8984375).astype(jnp.bfloat16),
        "ln2_bias": scatter_about(arg_keys[10], (D,), 0.3, 1.5, ((0, 8),)),
        "w_up": scatter_about(arg_keys[11], (D, FF), D ** -0.5, 0.25, ((0, 8),)),
        "up_bias": scatter_about(arg_keys[12], (FF,), 0.5, 2.5, ((0, 8),)),
        "w_down": scatter_about(arg_keys[13], (FF, D), FF ** -0.5, 0.125, ((0, 8),)),
        "down_bias": scatter_about(arg_keys[14], (D,), 0.3, 1.5, ((0, 8),)),
        "grad_out": scatter_about(arg_keys[15], (BATCH, SEQ_LEN, D), 1.0, 6.0, ((0, 8), (1, 4))),
    }


@jax.custom_vjp
def low(v):
    return lax.optimization_barrier(v.astype(jnp.bfloat16)).astype(jnp.float32)

@jax.custom_vjp
def low_back(v):
    return v

def low_keep(v):
    return (low(v), None)

def low_pass(kept, grad):
    return (grad,)

def back_keep(v):
    return (v, None)

def back_low(kept, grad):
    return (low(grad),)
low.defvjp(low_keep, low_pass)
low_back.defvjp(back_keep, back_low)

def layer_norm(values, gain, shift):
    mean_val = lax.optimization_barrier(jnp.mean(values, axis=-1, keepdims=True))
    centered = values - mean_val
    variance = lax.optimization_barrier(jnp.mean(centered * centered, axis=-1, keepdims=True))
    return centered * lax.rsqrt(variance + 1e-05) * gain + shift

def position_table(count_rows, feature_count):
    steps = jnp.arange(count_rows).astype(jnp.float32)
    half_count = feature_count // 2
    inv_freq = jnp.exp(jnp.arange(half_count).astype(jnp.float32) * (-2.0 * math.log(10000.0) / feature_count))
    angles = steps[:, None] * inv_freq[None, :]
    return jnp.concatenate([jnp.sin(angles), jnp.cos(angles)], axis=1)

def mat_dot(left, right):
    return jnp.dot(left, right, precision=lax.Precision.HIGHEST, preferred_element_type=jnp.float32)

def attend(query_u, query_v, keys, values, rel_table, length):
    content = jnp.einsum('ihe,jhe->hij', query_u, keys, precision=lax.Precision.HIGHEST)
    rel_all = jnp.einsum('ihe,the->hit', query_v, rel_table, precision=lax.Precision.HIGHEST)
    rows = jnp.arange(SEQ_LEN).astype(jnp.int32)
    dist = jnp.clip(rows[:, None] - rows[None, :], 0, SEQ_LEN - 1).astype(jnp.int32)
    rel = jnp.take_along_axis(rel_all, jnp.broadcast_to(dist[None], (H, SEQ_LEN, SEQ_LEN)), axis=2)
    scores = (content + rel) * (1.0 / math.sqrt(HEAD_DIM))
    allowed = (rows[None, :] <= rows[:, None]) & (rows[None, :] < length)
    scores = jnp.where(allowed[None], scores, -1e+30)
    scores = low_back(scores)
    top = lax.optimization_barrier(jnp.max(scores, axis=-1, keepdims=True))
    expo = jnp.exp(scores - top)
    probs = low(expo / lax.optimization_barrier(jnp.sum(expo, axis=-1, keepdims=True)))
    return jnp.einsum('hij,jhe->ihe', probs, values, precision=lax.Precision.HIGHEST)

def forward_seq(params, inputs, length):
    gain_one, shift_one, query_key_value_matrix, rel_weight, bias_first, bias_second, output_matrix, gain_two, shift_two, up_matrix, up_shift, down_matrix, down_shift = params
    first_normalized = low(layer_norm(inputs, gain_one, shift_one))
    qkv = low(low_back(mat_dot(first_normalized, query_key_value_matrix))).reshape(SEQ_LEN, H, 3, HEAD_DIM)
    queries = qkv[:, :, 0]
    keys = qkv[:, :, 1]
    values = qkv[:, :, 2]
    query_u = low(queries + bias_first.reshape(H, HEAD_DIM))
    query_v = low(queries + bias_second.reshape(H, HEAD_DIM))
    table = low(position_table(SEQ_LEN, D))
    rel_table = low(low_back(mat_dot(table, rel_weight))).reshape(SEQ_LEN, H, HEAD_DIM)
    attended = jax.checkpoint(attend)(query_u, query_v, keys, values, rel_table, length)
    attended = low(low_back(attended)).reshape(SEQ_LEN, D)
    projected = low_back(mat_dot(attended, output_matrix))
    resid = inputs + projected
    second_normalized = low(layer_norm(resid, gain_two, shift_two))
    pre_act = low_back(mat_dot(second_normalized, up_matrix) + up_shift)
    hidden_state = low(0.5 * pre_act * (1.0 + lax.erf(pre_act * (1.0 / math.sqrt(2.0)))))
    return resid + mat_dot(hidden_state, down_matrix) + down_shift

def reference(layer_input, lengths, ln1_gain, ln1_bias, w_qkv, w_rel, bias_u, bias_v, w_out, ln2_gain, ln2_bias, w_up, up_bias, w_down, down_bias, grad_out):
    params = tuple((p.astype(jnp.float32) for p in (ln1_gain, ln1_bias, w_qkv, w_rel, bias_u, bias_v, w_out, ln2_gain, ln2_bias, w_up, up_bias, w_down, down_bias)))
    rows = jnp.arange(SEQ_LEN).astype(jnp.int32)

    def one_seq(totals, item):
        inputs, length, cotangent = item
        live = (rows < length).astype(jnp.float32)
        result, pull = jax.vjp(lambda p, v: forward_seq(p, v, length), params, inputs.astype(jnp.float32))
        grads, grad_in = pull(cotangent.astype(jnp.float32) * live[:, None])
        totals = jax.tree.map(lambda a, b: a + b, totals, grads)
        return (totals, (result.astype(jnp.bfloat16), grad_in))
    zeros = tuple((jnp.zeros(p.shape, jnp.float32) for p in params))
    totals, (outputs, grad_inputs) = lax.scan(one_seq, zeros, (layer_input, lengths, grad_out))
    return (outputs, grad_inputs, totals[0], totals[1], totals[2], totals[3], totals[4], totals[5], totals[6], totals[7], totals[8], totals[9], totals[10], totals[11], totals[12])
```

```python
import functools
import math

import jax
import jax.numpy as jnp
from jax import lax
from jax.experimental import pallas as pl
from jax.experimental.pallas import tpu as pltpu
from jax.sharding import PartitionSpec as P

H = 8
HEAD_DIM = 64


NEG_FILL = -1e30
NORM_EPS = 1e-05


bf,f32=jnp.bfloat16,jnp.float32
NEG = NEG_FILL
HD = HEAD_DIM
NT=(((1,),(1,)),((),()))
NN=(((1,),(0,)),((),()))
def dot(a,b,dims): return lax.dot_general(a,b,dims,preferred_element_type=f32)

def fwd_kernel(len_ref,q_ref,k_ref,v_ref,r_ref,bu_ref,bv_ref,o_ref,lse_ref,*,L,B):
    odd=pl.program_id(0)%2
    lane=lax.broadcasted_iota(jnp.int32,(B,2*HD),1)
    mine=(lane//HD)==odd
    length=len_ref[0]
    col=lax.broadcasted_iota(jnp.int32,(1,L),1)
    bias=jnp.where(col<length,0.0,NEG)
    tri=lax.broadcasted_iota(jnp.int32,(B,B),1)<=lax.broadcasted_iota(jnp.int32,(B,B),0)
    for i in range(L//B):
        W=(i+1)*B
        q=q_ref[i*B:W,:].astype(f32)
        qu=jnp.where(mine,(q+bu_ref[...]).astype(bf).astype(f32)*0.125,0.0).astype(bf)
        qv=jnp.where(mine,(q+bv_ref[...]).astype(bf).astype(f32)*0.125,0.0).astype(bf)
        s=dot(qu,k_ref[:W,:],NT)
        rel=dot(qv,r_ref[L-W:,:],NT)
        s=s+pltpu.roll(rel,(W-B+1)%W,1,stride=1,stride_axis=0)+bias[:,:W]
        diag=jnp.where(tri,s[:,W-B:],NEG)
        s=jnp.concatenate([s[:,:W-B],diag],axis=1) if i else diag
        m=jnp.max(s,axis=1,keepdims=True)
        e=jnp.exp(s-m)
        l=jnp.sum(e,axis=1,keepdims=True)
        o=dot(e.astype(bf),v_ref[:W,:],NN)/l
        o=jnp.where(mine,o,0.0).astype(bf)
        @pl.when(odd==0)
        def _(): o_ref[i*B:W,:]=o
        @pl.when(odd==1)
        def _(): o_ref[i*B:W,:]=o_ref[i*B:W,:]+o
        lse_ref[0,i*B:W,:]=m+jnp.log(l)

def attn_fwd(length,qkv,rrev,bu,bv,*,L,heads,B=256):
    hp=heads//2
    return pl.pallas_call(functools.partial(fwd_kernel,L=L,B=B),
        out_shape=(jax.ShapeDtypeStruct((L,heads*HD),bf),jax.ShapeDtypeStruct((heads,L,1),f32)),
        grid_spec=pltpu.PrefetchScalarGridSpec(num_scalar_prefetch=1,grid=(heads,),
          in_specs=[pl.BlockSpec((L,128),lambda h,_:(0,h//2)),
                    pl.BlockSpec((L,128),lambda h,_:(0,hp+h//2)),
                    pl.BlockSpec((L,128),lambda h,_:(0,2*hp+h//2)),
                    pl.BlockSpec((L,128),lambda h,_:(0,h//2)),
                    pl.BlockSpec((1,128),lambda h,_:(0,h//2)),
                    pl.BlockSpec((1,128),lambda h,_:(0,h//2))],
          out_specs=(pl.BlockSpec((L,128),lambda h,_:(0,h//2)),pl.BlockSpec((1,L,1),lambda h,_:(h,0,0)))),
        compiler_params=pltpu.CompilerParams(vmem_limit_bytes=48<<20),name="attn_fwd")(length,qkv,qkv,qkv,rrev,bu,bv)

def bwd_kernel(len_ref,q_ref,k_ref,v_ref,r_ref,bu_ref,bv_ref,lse_ref,do_ref,
               dq_ref,dk_ref,dv_ref,dr_ref,gu_ref,gv_ref,dkT,dvT,drT,*,L,B):
    odd=pl.program_id(0)%2
    lane=lax.broadcasted_iota(jnp.int32,(B,2*HD),1)
    mine=(lane//HD)==odd
    length=len_ref[0]
    rows=lax.broadcasted_iota(jnp.int32,(B,B),0)
    cols=lax.broadcasted_iota(jnp.int32,(B,B),1)
    tri=cols<=rows
    flip=jnp.where(rows+cols==B-1,1.0,0.0).astype(bf)
    rowc=lax.broadcasted_iota(jnp.int32,(B,1),0)
    half=pl.multiple_of(odd*HD,HD)
    dkT[pl.ds(half,HD),:]=jnp.zeros((HD,L),f32)
    dvT[pl.ds(half,HD),:]=jnp.zeros((HD,L),f32)
    drT[pl.ds(half,HD),:]=jnp.zeros((HD,L),f32)
    @pl.when(odd==0)
    def _():
        dq_ref[...]=jnp.zeros_like(dq_ref)
        gu_ref[...]=jnp.zeros_like(gu_ref)
        gv_ref[...]=jnp.zeros_like(gv_ref)
    for i in range(L//B):
        W=(i+1)*B
        @pl.when(i*B<length)
        def _():
            q=q_ref[i*B:W,:].astype(f32)
            qu=jnp.where(mine,(q+bu_ref[...]).astype(bf).astype(f32)*0.125,0.0)
            qv=jnp.where(mine,(q+bv_ref[...]).astype(bf).astype(f32)*0.125,0.0)
            do=jnp.where(mine,do_ref[i*B:W,:].astype(f32),0.0)
            qub,qvb,dob=qu.astype(bf),qv.astype(bf),do.astype(bf)
            quT=jnp.transpose(qu); doT=jnp.transpose(do)
            quT=(quT[:HD]+quT[HD:]).astype(bf); doT=(doT[:HD]+doT[HD:]).astype(bf)
            qvr=dot(flip,qvb,NN)
            qvrT=jnp.transpose(qvr); qvrT=(qvrT[:HD]+qvrT[HD:]).astype(bf)
            lse=jnp.where(i*B+rowc<length,lse_ref[0,i*B:W,:],-NEG)
            s=dot(qub,k_ref[:W,:],NT)
            rel=dot(qvb,r_ref[L-W:,:],NT)
            s=s+pltpu.roll(rel,(W-B+1)%W,1,stride=1,stride_axis=0)
            diag=jnp.where(tri,s[:,W-B:],NEG)
            s=jnp.concatenate([s[:,:W-B],diag],axis=1) if i else diag
            p=jnp.exp(s-lse)
            dp=dot(dob,v_ref[:W,:],NT)
            t=p*dp
            inner=jnp.sum(t,axis=1,keepdims=True)
            ds=(t-p*inner).astype(bf)
            dvT[pl.ds(half,HD),:W]+=dot(doT,p.astype(bf),NN)
            both=dot(jnp.concatenate([quT,flip],axis=0),ds,NN)
            dkT[pl.ds(half,HD),:W]+=both[:HD]
            dqu=jnp.where(mine,dot(ds,k_ref[:W,:],NN)*0.125,0.0)
            dsr=pltpu.roll(both[HD:],0,1,stride=1,stride_axis=0).astype(bf)
            drT[pl.ds(half,HD),L-W:]+=dot(qvrT,dsr,NN)
            dqvr=jnp.where(mine,dot(dsr,r_ref[L-W:,:],NN)*0.125,0.0)
            dqv=dot(flip,dqvr.astype(bf),NN)
            dq_ref[i*B:W,:]+=(dqu+dqv).astype(bf)
            gu_ref[...]+=jnp.sum(dqu,axis=0,keepdims=True)
            gv_ref[...]+=jnp.sum(dqvr,axis=0,keepdims=True)
    @pl.when(odd==1)
    def _():
        dk_ref[...]=jnp.transpose(dkT[...]).astype(bf)
        dv_ref[...]=jnp.transpose(dvT[...]).astype(bf)
        dr_ref[...]=jnp.transpose(drT[...]).astype(bf)

def attn_bwd(length,qkv,rrev,bu,bv,lse,do,*,L,heads,B=256):
    hp=heads//2
    pair=lambda off: pl.BlockSpec((L,128),lambda h,_:(0,off+h//2))
    row=pl.BlockSpec((1,128),lambda h,_:(0,h//2))
    return pl.pallas_call(functools.partial(bwd_kernel,L=L,B=B),
        out_shape=(jax.ShapeDtypeStruct((L,heads*HD),bf),)*4+(jax.ShapeDtypeStruct((1,heads*HD),f32),)*2,
        grid_spec=pltpu.PrefetchScalarGridSpec(num_scalar_prefetch=1,grid=(heads,),
          in_specs=[pair(0),pair(hp),pair(2*hp),pair(0),row,row,pl.BlockSpec((1,L,1),lambda h,_:(h,0,0)),pair(0)],
          out_specs=(pair(0),)*4+(row,row),
          scratch_shapes=[pltpu.VMEM((128,L),f32)]*3),
        compiler_params=pltpu.CompilerParams(vmem_limit_bytes=48<<20),name="attn_bwd")(length,qkv,qkv,qkv,rrev,bu,bv,lse,do)


def norm_parts(values):
    mean_val = jnp.mean(values, axis=-1, keepdims=True)
    centered = values - mean_val
    inv_std = lax.rsqrt(jnp.mean(centered * centered, axis=-1, keepdims=True) + NORM_EPS)
    return (centered * inv_std, inv_std)


def norm_back(grad_norm, x_hat, inv_std):
    first_mean = jnp.mean(grad_norm, axis=-1, keepdims=True)
    second_mean = jnp.mean(grad_norm * x_hat, axis=-1, keepdims=True)
    return inv_std * (grad_norm - first_mean - x_hat * second_mean)


def position_table(count_rows, feature_count):
    steps = lax.iota(jnp.float32, count_rows)
    half_count = feature_count // 2
    inv_freq = jnp.exp(
        lax.iota(jnp.float32, half_count) * (-2.0 * math.log(10000.0) / feature_count)
    )
    angles = steps[:, None] * inv_freq[None, :]
    return jnp.concatenate([jnp.sin(angles), jnp.cos(angles)], axis=1)


def skew_rows(matrix):
    leading = matrix.shape[:-2]
    row_count, col_count = matrix.shape[-2:]
    flattened = matrix.reshape(leading + (row_count * col_count,))
    picked = flattened[..., row_count - 1 : row_count - 1 + row_count * (col_count - 1)]
    return picked.reshape(leading + (row_count, col_count - 1))[..., : col_count - row_count]


def unskew_rows(matrix):
    leading = matrix.shape[:-2]
    row_count, key_count = matrix.shape[-2:]
    axis_pos = len(leading)
    widened = jnp.pad(matrix, [(0, 0)] * axis_pos + [(0, 0), (0, row_count - 1)])
    flattened = widened.reshape(leading + (row_count * (key_count + row_count - 1),))
    flattened = jnp.pad(flattened, [(0, 0)] * axis_pos + [(row_count - 1, 1)])
    return flattened.reshape(leading + (row_count, key_count + row_count))


def head_split_device(
    layer_input,
    lengths,
    ln1_gain,
    ln1_bias,
    w_qkv,
    w_rel,
    bias_u,
    bias_v,
    w_out,
    ln2_gain,
    ln2_bias,
    w_up,
    up_bias,
    w_down,
    down_bias,
    grad_out,
):
    weights = (
        lax.all_gather(ln1_gain, "fsdp", axis=0, tiled=True),
        lax.all_gather(ln1_bias, "fsdp", axis=0, tiled=True),
        lax.all_gather(w_qkv, "fsdp", axis=0, tiled=True),
        lax.all_gather(w_rel, "fsdp", axis=0, tiled=True),
        lax.all_gather(bias_u, "fsdp", axis=0, tiled=True),
        lax.all_gather(bias_v, "fsdp", axis=0, tiled=True),
        lax.all_gather(w_out, "fsdp", axis=0, tiled=True),
        lax.all_gather(ln2_gain, "fsdp", axis=0, tiled=True),
        lax.all_gather(ln2_bias, "fsdp", axis=0, tiled=True),
        lax.all_gather(w_up, "fsdp", axis=0, tiled=True),
        lax.all_gather(up_bias, "fsdp", axis=0, tiled=True),
        lax.all_gather(w_down, "fsdp", axis=0, tiled=True),
        lax.all_gather(down_bias, "fsdp", axis=0, tiled=True),
    )
    (
        gain_one,
        shift_one,
        query_key_value_matrix,
        rel_weight,
        first_bias,
        second_bias,
        output_matrix,
        gain_two,
        shift_two,
        up_matrix,
        up_shift,
        down_matrix,
        down_shift,
    ) = weights
    gain_one = gain_one.astype(jnp.float32)
    shift_one = shift_one.astype(jnp.float32)
    gain_two = gain_two.astype(jnp.float32)
    shift_two = shift_two.astype(jnp.float32)
    up_shift = up_shift.astype(jnp.float32)
    down_shift = down_shift.astype(jnp.float32)
    slots, block_len, width = layer_input.shape
    seq_count = lax.axis_size("seq")
    seq_rank = lax.axis_index("seq")
    head_dim = HEAD_DIM
    group = H // seq_count
    full_len = block_len * seq_count
    score_scale = 1.0 / math.sqrt(head_dim)
    q_block = 512
    num_blocks = full_len // q_block
    win_len = full_len + q_block
    x_float = layer_input.astype(jnp.float32)
    x_hat_one, inv_std_one = norm_parts(x_float)
    first_normalized = (x_hat_one * gain_one + shift_one).astype(jnp.bfloat16)
    qkv_local = jnp.einsum(
        "mcr,rk->mck", first_normalized, query_key_value_matrix, preferred_element_type=jnp.float32
    ).astype(jnp.bfloat16)
    qkv_heads = lax.all_to_all(qkv_local, "seq", split_axis=2, concat_axis=1, tiled=True)
    qkv_heads = qkv_heads.reshape(slots, full_len, group, 3, head_dim)
    queries = qkv_heads[:, :, :, 0]
    keys = qkv_heads[:, :, :, 1]
    values = qkv_heads[:, :, :, 2]
    head_start = seq_rank * group
    head_bias_u = lax.dynamic_slice_in_dim(
        first_bias.astype(jnp.float32).reshape(H, head_dim), head_start, group, 0
    )
    head_bias_v = lax.dynamic_slice_in_dim(
        second_bias.astype(jnp.float32).reshape(H, head_dim), head_start, group, 0
    )
    query_u = (queries.astype(jnp.float32) + head_bias_u).astype(jnp.bfloat16)
    query_v = (queries.astype(jnp.float32) + head_bias_v).astype(jnp.bfloat16)
    table_rev = position_table(full_len, width).astype(jnp.bfloat16)[::-1]
    rel_cols = lax.dynamic_slice_in_dim(rel_weight, head_start * head_dim, group * head_dim, 1)
    rel_rev = jnp.dot(table_rev, rel_cols, preferred_element_type=jnp.float32).astype(jnp.bfloat16)
    rel_ext = jnp.concatenate([rel_rev, jnp.zeros_like(rel_rev)], axis=0).reshape(
        2 * full_len, group, head_dim
    )
    col_ids = lax.iota(jnp.int32, full_len)

    def scores_block(first_row):
        qu_part = lax.dynamic_slice_in_dim(query_u, first_row, q_block, 1)
        qv_part = lax.dynamic_slice_in_dim(query_v, first_row, q_block, 1)
        window_start = full_len - q_block - first_row
        rel_win = lax.dynamic_slice_in_dim(rel_ext, window_start, win_len, 0)
        content = jnp.einsum("sqhe,skhe->shqk", qu_part, keys, preferred_element_type=jnp.float32)
        rel_raw = jnp.einsum("sqhe,the->shqt", qv_part, rel_win, preferred_element_type=jnp.float32)
        rel_part = skew_rows(rel_raw)
        row_ids = first_row + lax.iota(jnp.int32, q_block)
        causal = col_ids[None, :] <= row_ids[:, None]
        inside = col_ids[None, :] < lengths[:, None]
        allowed = causal[None, None, :, :] & inside[:, None, None, :]
        scores = jnp.where(allowed, (content + rel_part) * score_scale, NEG_FILL)
        return (scores, qu_part, qv_part, rel_win, window_start)

    def forward_block(block_index):
        first_row = block_index * q_block
        scores, qu_part, qv_part, rel_win, window_start = scores_block(first_row)
        top = jnp.max(scores, axis=-1, keepdims=True)
        expo = jnp.exp(scores - top)
        total = jnp.sum(expo, axis=-1, keepdims=True)
        probs = (expo / total).astype(jnp.bfloat16)
        out_part = jnp.einsum(
            "shqk,skhe->sqhe", probs, values, preferred_element_type=jnp.float32
        ).astype(jnp.bfloat16)
        return (out_part, top[..., 0] + jnp.log(total[..., 0]))

    block_outs, block_lse = lax.map(forward_block, jnp.arange(num_blocks, dtype=jnp.int32))
    attn_heads = jnp.moveaxis(block_outs, 0, 1).reshape(slots, full_len, group * head_dim)
    attention_sequence = lax.all_to_all(attn_heads, "seq", split_axis=1, concat_axis=2, tiled=True)
    attention_projected = jnp.einsum(
        "mcr,rk->mck", attention_sequence, output_matrix, preferred_element_type=jnp.float32
    )
    resid = x_float + attention_projected
    x_hat_two, inv_std_two = norm_parts(resid)
    second_normalized = (x_hat_two * gain_two + shift_two).astype(jnp.bfloat16)
    pre_act = (
        jnp.einsum("oka,ac->okc", second_normalized, up_matrix, preferred_element_type=jnp.float32)
        + up_shift
    )
    normal_cdf = 0.5 * (1.0 + lax.erf(pre_act * (1.0 / math.sqrt(2.0))))
    hidden_state = (pre_act * normal_cdf).astype(jnp.bfloat16)
    down_proj = (
        jnp.einsum("zcp,pr->zcr", hidden_state, down_matrix, preferred_element_type=jnp.float32)
        + down_shift
    )
    output = (resid + down_proj).astype(jnp.bfloat16)
    positions = seq_rank * block_len + lax.iota(jnp.int32, block_len)
    live = (positions[None, :] < lengths[:, None]).astype(jnp.bfloat16)
    result_gradient = grad_out * live[:, :, None]
    grad_y_float = result_gradient.astype(jnp.float32)
    g_down_shift = jnp.sum(grad_y_float, axis=(0, 1))
    down_gradient = jnp.einsum(
        "hki,hku->iu", hidden_state, result_gradient, preferred_element_type=jnp.float32
    )
    hidden_gradient = jnp.einsum(
        "gvu,ju->gvj", result_gradient, down_matrix, preferred_element_type=jnp.float32
    )
    deriv = normal_cdf + pre_act * jnp.exp(-0.5 * pre_act * pre_act) * (
        1.0 / math.sqrt(2.0 * math.pi)
    )
    preactivation_gradient = (hidden_gradient * deriv).astype(jnp.bfloat16)
    g_up_shift = jnp.sum(preactivation_gradient.astype(jnp.float32), axis=(0, 1))
    up_gradient = jnp.einsum(
        "oiz,oix->zx", second_normalized, preactivation_gradient, preferred_element_type=jnp.float32
    )
    second_norm_gradient = jnp.einsum(
        "rau,ku->rak", preactivation_gradient, up_matrix, preferred_element_type=jnp.float32
    )
    g_gain_two = jnp.sum(second_norm_gradient * x_hat_two, axis=(0, 1))
    g_shift_two = jnp.sum(second_norm_gradient, axis=(0, 1))
    g_resid = grad_y_float + norm_back(second_norm_gradient * gain_two, x_hat_two, inv_std_two)
    attention_gradient = g_resid.astype(jnp.bfloat16)
    output_gradient = jnp.einsum(
        "zau,zam->um", attention_sequence, attention_gradient, preferred_element_type=jnp.float32
    )
    g_attn_seq = jnp.einsum(
        "urz,jz->urj", attention_gradient, output_matrix, preferred_element_type=jnp.float32
    ).astype(jnp.bfloat16)
    g_attn_heads = lax.all_to_all(
        g_attn_seq, "seq", split_axis=2, concat_axis=1, tiled=True
    ).reshape(slots, full_len, group, head_dim)

    def backward_block(carry, block_index):
        g_keys, g_vals, g_ext = carry
        first_row = block_index * q_block
        scores, qu_part, qv_part, rel_win, window_start = scores_block(first_row)
        probs = jnp.exp(scores - block_lse[block_index][..., None])
        d_out = lax.dynamic_slice_in_dim(g_attn_heads, first_row, q_block, 1)
        g_vals = g_vals + jnp.einsum(
            "shqk,sqhe->skhe", probs.astype(jnp.bfloat16), d_out, preferred_element_type=jnp.float32
        )
        g_probs = jnp.einsum("sqhe,skhe->shqk", d_out, values, preferred_element_type=jnp.float32)
        inner = jnp.sum(probs * g_probs, axis=-1, keepdims=True)
        g_scores = (probs * (g_probs - inner)).astype(jnp.bfloat16)
        g_qu = (
            jnp.einsum("shqk,skhe->sqhe", g_scores, keys, preferred_element_type=jnp.float32)
            * score_scale
        )
        g_keys = (
            g_keys
            + jnp.einsum("shqk,sqhe->skhe", g_scores, qu_part, preferred_element_type=jnp.float32)
            * score_scale
        )
        g_wide = unskew_rows(g_scores)
        g_qv = (
            jnp.einsum("shqt,the->sqhe", g_wide, rel_win, preferred_element_type=jnp.float32)
            * score_scale
        )
        g_win = (
            jnp.einsum("shqt,sqhe->sthe", g_wide, qv_part, preferred_element_type=jnp.float32)
            * score_scale
        )
        g_old = lax.dynamic_slice_in_dim(g_ext, window_start, win_len, 1)
        g_ext = lax.dynamic_update_slice_in_dim(g_ext, g_old + g_win, window_start, 1)
        return ((g_keys, g_vals, g_ext), (g_qu, g_qv))

    zero_heads = jnp.zeros((slots, full_len, group, head_dim), jnp.float32)
    zero_ext = jnp.zeros((slots, 2 * full_len, group, head_dim), jnp.float32)
    (g_keys, g_vals, g_ext), (g_qu_blocks, g_qv_blocks) = lax.scan(
        backward_block, (zero_heads, zero_heads, zero_ext), jnp.arange(num_blocks, dtype=jnp.int32)
    )
    g_qu = jnp.moveaxis(g_qu_blocks, 0, 1).reshape(slots, full_len, group, head_dim)
    g_qv = jnp.moveaxis(g_qv_blocks, 0, 1).reshape(slots, full_len, group, head_dim)
    g_queries = g_qu + g_qv
    g_bias_u_heads = jnp.sum(g_qu, axis=(0, 1))
    g_bias_v_heads = jnp.sum(g_qv, axis=(0, 1))
    g_qkv_heads = (
        jnp.stack([g_queries, g_keys, g_vals], axis=3)
        .astype(jnp.bfloat16)
        .reshape(slots, full_len, group * 3 * head_dim)
    )
    query_key_value_gradient = lax.all_to_all(
        g_qkv_heads, "seq", split_axis=1, concat_axis=2, tiled=True
    )
    g_rel_low = g_ext[:, :full_len].astype(jnp.bfloat16)
    g_rel_heads = jnp.einsum(
        "td,sthe->dhe", table_rev, g_rel_low, preferred_element_type=jnp.float32
    ).reshape(width, group * head_dim)
    g_rel_weight = lax.dynamic_update_slice_in_dim(
        jnp.zeros((width, width), jnp.float32), g_rel_heads, head_start * head_dim, 1
    )
    g_bias_u = lax.dynamic_update_slice_in_dim(
        jnp.zeros((H, head_dim), jnp.float32), g_bias_u_heads, head_start, 0
    ).reshape(width)
    g_bias_v = lax.dynamic_update_slice_in_dim(
        jnp.zeros((H, head_dim), jnp.float32), g_bias_v_heads, head_start, 0
    ).reshape(width)
    query_key_value_weight_gradient = jnp.einsum(
        "zau,zam->um",
        first_normalized,
        query_key_value_gradient,
        preferred_element_type=jnp.float32,
    )
    first_norm_gradient = jnp.einsum(
        "urz,jz->urj",
        query_key_value_gradient,
        query_key_value_matrix,
        preferred_element_type=jnp.float32,
    )
    g_gain_one = jnp.sum(first_norm_gradient * x_hat_one, axis=(0, 1))
    g_shift_one = jnp.sum(first_norm_gradient, axis=(0, 1))
    g_input = g_resid + norm_back(first_norm_gradient * gain_one, x_hat_one, inv_std_one)
    partial_shards = (
        lax.psum_scatter(g_gain_one, "fsdp", scatter_dimension=0, tiled=True),
        lax.psum_scatter(g_shift_one, "fsdp", scatter_dimension=0, tiled=True),
        lax.psum_scatter(query_key_value_weight_gradient, "fsdp", scatter_dimension=0, tiled=True),
        lax.psum_scatter(g_rel_weight, "fsdp", scatter_dimension=0, tiled=True),
        lax.psum_scatter(g_bias_u, "fsdp", scatter_dimension=0, tiled=True),
        lax.psum_scatter(g_bias_v, "fsdp", scatter_dimension=0, tiled=True),
        lax.psum_scatter(output_gradient, "fsdp", scatter_dimension=0, tiled=True),
        lax.psum_scatter(g_gain_two, "fsdp", scatter_dimension=0, tiled=True),
        lax.psum_scatter(g_shift_two, "fsdp", scatter_dimension=0, tiled=True),
        lax.psum_scatter(up_gradient, "fsdp", scatter_dimension=0, tiled=True),
        lax.psum_scatter(g_up_shift, "fsdp", scatter_dimension=0, tiled=True),
        lax.psum_scatter(down_gradient, "fsdp", scatter_dimension=0, tiled=True),
        lax.psum_scatter(g_down_shift, "fsdp", scatter_dimension=0, tiled=True),
    )
    shards = lax.psum(
        (
            partial_shards[0],
            partial_shards[1],
            partial_shards[2],
            partial_shards[3],
            partial_shards[4],
            partial_shards[5],
            partial_shards[6],
            partial_shards[7],
            partial_shards[8],
            partial_shards[9],
            partial_shards[10],
            partial_shards[11],
            partial_shards[12],
        ),
        "seq",
    )
    return (
        output,
        g_input,
        shards[0],
        shards[1],
        shards[2],
        shards[3],
        shards[4],
        shards[5],
        shards[6],
        shards[7],
        shards[8],
        shards[9],
        shards[10],
        shards[11],
        shards[12],
    )


def flat(values):
    return values.reshape((-1,) + values.shape[2:])


def pick(values, index):
    return lax.dynamic_index_in_dim(values, index, 0, keepdims=False)


def relative_to_natural(blocks, me):
    rows = blocks[0].shape[0]
    out = jnp.zeros((rows * len(blocks),) + blocks[0].shape[1:], blocks[0].dtype)
    for k, block in enumerate(blocks):
        out = lax.dynamic_update_slice_in_dim(out, block, (me ^ k) * rows, 0)
    return out


def swap_fsdp(values, mask):
    size = lax.axis_size("fsdp")
    return lax.ppermute(values, "fsdp", [(i, i ^ mask) for i in range(size)])


def swap_seq(values, mask):
    size = lax.axis_size("seq")
    return lax.ppermute(values, "seq", [(i, i ^ mask) for i in range(size)])


def slot_pairs(turn):
    seq, pairs = lax.axis_size("seq"), []
    for f in range(lax.axis_size("fsdp")):
        for z in range(seq):
            to_f, to_z = (f & ~1) | (z & 1), 2 * (f & 1) + (turn ^ (z >> 1))
            pairs.append((f * seq + z, to_f * seq + to_z))
    return pairs


def to_slots(values, seq_rank):
    high, low = seq_rank >> 1, seq_rank & 1
    got = [
        lax.ppermute(pick(values, turn ^ high), ("fsdp", "seq"), slot_pairs(turn))
        for turn in (0, 1)
    ]
    swap = low == 1
    return jnp.stack([jnp.where(swap, got[1], got[0]), jnp.where(swap, got[0], got[1])])


def from_slots(values, seq_rank):
    high, low = seq_rank >> 1, seq_rank & 1
    got = [
        lax.ppermute(
            pick(values, turn ^ low), ("fsdp", "seq"), [(b, a) for a, b in slot_pairs(turn)]
        )
        for turn in (0, 1)
    ]
    swap = high == 1
    return jnp.stack([jnp.where(swap, got[1], got[0]), jnp.where(swap, got[0], got[1])])


def interleave(mine, other, core):
    first = jnp.where(core == 0, mine, other)
    second = jnp.where(core == 0, other, mine)
    return jnp.stack([first, second], axis=1).reshape((-1,) + mine.shape[2:])


def gather_weight(shard, chip, core):
    blocks = jnp.stack([shard] + [swap_fsdp(shard, 2 * k) for k in (1, 2, 3)])
    other = swap_fsdp(blocks, 1)
    first = jnp.where(core == 0, blocks, other)
    second = jnp.where(core == 0, other, blocks)
    pairs = jnp.stack([first, second], axis=1)
    return relative_to_natural([flat(pairs[k]) for k in range(4)], chip)


def reduce_chips(parts, chip):
    total = pick(parts, chip)
    for k in (1, 2, 3):
        sent = pick(parts, chip ^ k).astype(jnp.bfloat16)
        total = total + swap_fsdp(sent, 2 * k).astype(jnp.float32)
    return total


def reduce_seq(part, seq_rank):
    rows, cols = part.shape
    quarters = part.reshape(4, rows // 4, cols)
    total = pick(quarters, seq_rank)
    for k in (1, 2, 3):
        sent = pick(quarters, seq_rank ^ k).astype(jnp.bfloat16)
        total = total + swap_seq(sent, k).astype(jnp.float32)
    mine = total.astype(jnp.bfloat16)
    return relative_to_natural([mine] + [swap_seq(mine, k) for k in (1, 2, 3)], seq_rank).astype(
        jnp.float32
    )


def slot_split_device(
    layer_input,
    lengths,
    ln1_gain,
    ln1_bias,
    w_qkv,
    w_rel,
    bias_u,
    bias_v,
    w_out,
    ln2_gain,
    ln2_bias,
    w_up,
    up_bias,
    w_down,
    down_bias,
    grad_out,
):
    bf, f32 = jnp.bfloat16, jnp.float32
    slots, block, width = layer_input.shape
    seq_rank = lax.axis_index("seq")
    device = lax.axis_index("fsdp")
    core, chip = device & 1, device >> 1
    full = block * 4
    heads = H // 2
    cols = heads * HEAD_DIM
    shard = width // 8
    ff = up_bias.shape[0] * 8

    qkv_own = w_qkv.reshape(shard, 2, heads, 3, HEAD_DIM).transpose(1, 0, 3, 2, 4)
    qkv_own = qkv_own.reshape(2, shard, 3 * cols)
    rel_own = w_rel.reshape(shard, 2, cols).transpose(1, 0, 2)
    packed = jnp.concatenate([qkv_own, rel_own], axis=2)
    small = jnp.concatenate(
        [ln1_gain, ln1_bias, bias_u, bias_v, ln2_gain, ln2_bias, down_bias, up_bias]
    )
    small = jnp.zeros((8, 4 * cols), bf).at[0, : small.shape[0]].set(small)
    packed = jnp.concatenate([packed, jnp.stack([small, small])], axis=1)
    mine = pick(packed, core)
    other = swap_fsdp(pick(packed, 1 - core), 1)
    chip_pack = jnp.stack(
        [jnp.where(core == 0, mine, other), jnp.where(core == 0, other, mine)]
    )
    packs = [chip_pack] + [swap_fsdp(chip_pack, 2 * k) for k in (1, 2, 3)]
    attn_pack = relative_to_natural(packs, chip)
    attn_weight = attn_pack[:, :shard].reshape(width, 4 * cols)
    own_qkv, own_rel = attn_weight[:, : 3 * cols], attn_weight[:, 3 * cols :]
    vectors = attn_pack[:, shard].astype(f32)
    vector = lambda i: vectors[:, i * shard : (i + 1) * shard].reshape(width)
    gain_one, shift_one, first_bias, second_bias, gain_two, shift_two, down_shift = map(
        vector, range(7)
    )
    up_shift = vectors[:, 7 * shard : 7 * shard + ff // 8].reshape(ff)

    x_own = to_slots(layer_input, seq_rank)
    x_slot = interleave(x_own, swap_fsdp(x_own, 1), core).astype(f32)
    both_lengths = swap_fsdp(lengths, 1)
    length = pick(jnp.where(core == seq_rank >> 1, lengths, both_lengths), seq_rank & 1)
    length_arr = length.reshape(1)

    x_hat_slot, _ = norm_parts(x_slot)
    first_normalized = (x_hat_slot * gain_one + shift_one).astype(bf)
    qkv = jnp.dot(first_normalized, own_qkv, preferred_element_type=f32).astype(bf)
    steps = (full - 1 - lax.iota(jnp.int32, full)).astype(f32)
    half_count = width // 2
    inv_freq = jnp.exp(lax.iota(f32, half_count) * (-2.0 * math.log(10000.0) / width))
    angles = steps[:, None] * inv_freq[None, :]
    table_rev = jnp.concatenate([jnp.sin(angles), jnp.cos(angles)], axis=1).astype(bf)
    rel_rev = jnp.dot(table_rev, own_rel, preferred_element_type=f32).astype(bf)
    own_u = lax.dynamic_slice_in_dim(first_bias, core * cols, cols, 0).reshape(1, cols)
    own_v = lax.dynamic_slice_in_dim(second_bias, core * cols, cols, 0).reshape(1, cols)

    attn, lse = attn_fwd(length_arr, qkv, rel_rev, own_u, own_v, L=full, heads=heads)

    output_matrix = gather_weight(w_out, chip, core)
    up_matrix = gather_weight(w_up, chip, core)
    down_matrix = gather_weight(w_down, chip, core)

    attn = attn.reshape(2, 2, block, cols).transpose(1, 0, 2, 3)
    kept = pick(attn, core).reshape(2 * block, cols)
    came = swap_fsdp(pick(attn, 1 - core), 1).reshape(2 * block, cols)
    attention_sequence = jnp.concatenate(
        [jnp.where(core == 0, kept, came), jnp.where(core == 0, came, kept)], axis=1
    )
    x_float = flat(x_own).astype(f32)
    resid = x_float + jnp.dot(attention_sequence, output_matrix, preferred_element_type=f32)
    x_hat_two, inv_std_two = norm_parts(resid)
    second_normalized = (x_hat_two * gain_two + shift_two).astype(bf)
    pre_act = jnp.dot(second_normalized, up_matrix, preferred_element_type=f32) + up_shift
    normal_cdf = 0.5 * (1.0 + lax.erf(pre_act * (1.0 / math.sqrt(2.0))))
    hidden_state = (pre_act * normal_cdf).astype(bf)
    down_proj = jnp.dot(hidden_state, down_matrix, preferred_element_type=f32) + down_shift
    output_tokens = (resid + down_proj).astype(bf)
    output = from_slots(output_tokens.reshape(2, block, width), seq_rank)

    grad_own = to_slots(grad_out, seq_rank)
    starts = (2 * lax.iota(jnp.int32, 2) + core) * block
    positions = starts[:, None] + lax.iota(jnp.int32, block)[None, :]
    live = (positions < length).astype(bf)
    result_gradient = flat(grad_own * live[:, :, None])
    grad_y_float = result_gradient.astype(f32)
    g_down_shift = jnp.sum(grad_y_float, axis=0)
    tn = lambda a, b: lax.dot_general(a, b, (((0,), (0,)), ((), ())), preferred_element_type=f32)
    nt = lambda a, b: lax.dot_general(a, b, (((1,), (1,)), ((), ())), preferred_element_type=f32)
    down_gradient = tn(hidden_state, result_gradient)
    hidden_gradient = nt(result_gradient, down_matrix)
    deriv = normal_cdf + pre_act * jnp.exp(-0.5 * pre_act * pre_act) * (
        1.0 / math.sqrt(2.0 * math.pi)
    )
    preactivation_gradient = (hidden_gradient * deriv).astype(bf)
    g_up_shift = jnp.sum(preactivation_gradient.astype(f32), axis=0)
    up_gradient = tn(second_normalized, preactivation_gradient)
    second_norm_gradient = nt(preactivation_gradient, up_matrix)
    g_gain_two = jnp.sum(second_norm_gradient * x_hat_two, axis=0)
    g_shift_two = jnp.sum(second_norm_gradient, axis=0)
    g_resid = grad_y_float + norm_back(second_norm_gradient * gain_two, x_hat_two, inv_std_two)
    attention_gradient = g_resid.astype(bf)
    output_gradient = tn(attention_sequence, attention_gradient)
    g_attn = nt(attention_gradient, output_matrix).astype(bf)
    g_attn = g_attn.reshape(2, block, 2, cols).transpose(2, 0, 1, 3)
    g_own = pick(g_attn, core)
    g_other = swap_fsdp(pick(g_attn, 1 - core), 1)
    g_heads = interleave(g_own, g_other, core)

    columns = [g_gain_two[:, None], g_shift_two[:, None], g_down_shift[:, None]]
    columns.append(g_up_shift.reshape(width, ff // width))
    extra = jnp.concatenate(columns, axis=1)
    extra = jnp.pad(extra, ((0, 0), (0, 128 - extra.shape[1])))

    def reduce_cores(full_gradient):
        rows, columns = full_gradient.shape
        parts = full_gradient.reshape(4, 2, rows // 8, columns).transpose(1, 0, 2, 3)
        sent = pick(parts, 1 - core).astype(bf)
        return pick(parts, core) + swap_fsdp(sent, 1).astype(f32)

    def reduce_all(full_gradient):
        return reduce_seq(reduce_chips(reduce_cores(full_gradient), chip), seq_rank)

    g_up_matrix = reduce_all(up_gradient)
    g_down_matrix = reduce_all(down_gradient)
    g_out_extra = reduce_all(jnp.concatenate([output_gradient, extra], axis=1))
    g_output_matrix = g_out_extra[:, :width]
    early = g_out_extra[:, width:]

    g_q, g_k, g_v, g_rel, g_bias_u, g_bias_v = attn_bwd(
        length_arr, qkv, rel_rev, own_u, own_v, lse, g_heads, L=full, heads=heads
    )
    g_qkv = jnp.concatenate([g_q, g_k, g_v], axis=1)
    g_parts = g_qkv.reshape(2, 2, block, 3 * cols).transpose(1, 0, 2, 3)
    dh_other = nt(pick(g_parts, 1 - core).reshape(2 * block, 3 * cols), own_qkv).astype(bf)
    dh_came = swap_fsdp(dh_other, 1).astype(f32)
    first_norm_gradient = dh_came + nt(pick(g_parts, core).reshape(2 * block, 3 * cols), own_qkv)
    own_gradient = tn(first_normalized, g_qkv)
    rel_gradient = tn(table_rev, g_rel)
    x_hat_one, inv_std_one = norm_parts(x_float)
    g_gain_one = jnp.sum(first_norm_gradient * x_hat_one, axis=0)
    g_shift_one = jnp.sum(first_norm_gradient, axis=0)
    g_input = g_resid + norm_back(first_norm_gradient * gain_one, x_hat_one, inv_std_one)
    grad_x = from_slots(g_input.astype(bf).reshape(2, block, width), seq_rank).astype(f32)

    place = lambda v: lax.dynamic_update_slice_in_dim(
        jnp.zeros((width,), f32), v.reshape(cols), core * cols, 0
    )
    late = jnp.stack([g_gain_one, g_shift_one, place(g_bias_u), place(g_bias_v)], axis=1)
    late = jnp.pad(late, ((0, 0), (0, 128 - late.shape[1])))
    bundle = jnp.concatenate([own_gradient, rel_gradient, late], axis=1)
    bundle = reduce_seq(reduce_chips(bundle.reshape(4, 2 * shard, -1), chip), seq_rank)
    bundle = bundle.reshape(2, shard, -1)
    bundle_own = pick(bundle, core)
    bundle_other = swap_fsdp(pick(bundle, 1 - core).astype(bf), 1).astype(f32)
    halves = jnp.stack(
        [
            jnp.where(core == 0, bundle_own, bundle_other),
            jnp.where(core == 0, bundle_other, bundle_own),
        ],
        axis=1,
    )
    g_qkv_matrix = halves[:, :, : 3 * cols].reshape(shard, 2, 3, heads, HEAD_DIM)
    g_qkv_matrix = g_qkv_matrix.transpose(0, 1, 3, 2, 4).reshape(shard, 6 * cols)
    g_rel_matrix = halves[:, :, 3 * cols : 4 * cols].reshape(shard, 2 * cols)
    late = halves[:, 0, 4 * cols :] + halves[:, 1, 4 * cols :]
    return (
        output,
        grad_x,
        late[:, 0],
        late[:, 1],
        g_qkv_matrix,
        g_rel_matrix,
        late[:, 2],
        late[:, 3],
        g_output_matrix,
        early[:, 0],
        early[:, 1],
        g_up_matrix,
        early[:, 3 : 3 + ff // width].reshape(ff // 8),
        g_down_matrix,
        early[:, 2],
    )


def per_device(*args):
    one_slot_a_chip = lax.axis_size("fsdp") == 8 and lax.axis_size("seq") == 4
    if one_slot_a_chip and args[0].shape[0] == 2:
        return slot_split_device(*args)
    return head_split_device(*args)


def solution(mesh):
    placed = (
        P("fsdp", "seq", None),
        P("fsdp"),
        P("fsdp"),
        P("fsdp"),
        P("fsdp", None),
        P("fsdp", None),
        P("fsdp"),
        P("fsdp"),
        P("fsdp", None),
        P("fsdp"),
        P("fsdp"),
        P("fsdp", None),
        P("fsdp"),
        P("fsdp", None),
        P("fsdp"),
        P("fsdp", "seq", None),
    )
    return jax.shard_map(
        per_device,
        mesh=mesh,
        in_specs=placed,
        out_specs=(
            P("fsdp", "seq", None),
            P("fsdp", "seq", None),
            P("fsdp"),
            P("fsdp"),
            P("fsdp", None),
            P("fsdp", None),
            P("fsdp"),
            P("fsdp"),
            P("fsdp", None),
            P("fsdp"),
            P("fsdp"),
            P("fsdp", None),
            P("fsdp"),
            P("fsdp", None),
            P("fsdp"),
        ),
        check_vma=False,
    )
```

```python
import functools
import math

import jax
import jax.numpy as jnp
from jax import lax
from jax.experimental import pallas as pl
from jax.experimental.pallas import tpu as pltpu
from jax.sharding import PartitionSpec as P

H = 8
HEAD_DIM = 64


NEG_FILL = -1e30
NORM_EPS = 1e-05


bf, f32 = jnp.bfloat16, jnp.float32
NEG = NEG_FILL
HD = HEAD_DIM
NT = (((1,), (1,)), ((), ()))
NN = (((1,), (0,)), ((), ()))


def dot(a, b, dims):
    return lax.dot_general(a, b, dims, preferred_element_type=f32)


def masked_tail(s, keep, block):
    tail = jnp.where(keep, s[:, s.shape[1] - block :], NEG)
    if s.shape[1] == block:
        return tail
    return jnp.concatenate([s[:, : s.shape[1] - block], tail], axis=1)


def scores(qu, qv, keys, rel_rev, keep, block):
    span = keys.shape[0]
    rel = dot(qv, rel_rev, NT)
    rel = pltpu.roll(rel, (span - block + 1) % span, 1, stride=1, stride_axis=0)
    return masked_tail(dot(qu, keys, NT) + rel, keep, block)


def attn_fwd_body(len_ref, q_ref, k_ref, v_ref, r_ref, bu_ref, bv_ref, o_ref, lse_ref, *, block):
    full = q_ref.shape[0]
    lane = lax.broadcasted_iota(jnp.int32, (block, 2 * HD), 1)
    sides = (lane < HD, lane >= HD)
    length = len_ref[0]
    col = lax.broadcasted_iota(jnp.int32, (1, full), 1)
    bias = jnp.where(col < length, 0.0, NEG)
    tri = lax.broadcasted_iota(jnp.int32, (block, block), 1) <= lax.broadcasted_iota(
        jnp.int32, (block, block), 0
    )
    for first in range(0, full, block):
        span = first + block
        q = q_ref[first:span, :].astype(f32)
        qu = (q + bu_ref[...]).astype(bf).astype(f32) * 0.125
        qv = (q + bv_ref[...]).astype(bf).astype(f32) * 0.125
        outs = []
        for head, side in enumerate(sides):
            s = scores(
                jnp.where(side, qu, 0.0).astype(bf),
                jnp.where(side, qv, 0.0).astype(bf),
                k_ref[:span, :],
                r_ref[full - span :, :],
                tri,
                block,
            )
            s = s + bias[:, :span]
            top = jnp.max(s, axis=1, keepdims=True)
            e = jnp.exp(s - top)
            total = jnp.sum(e, axis=1, keepdims=True)
            outs.append(dot(e.astype(bf), v_ref[:span, :], NN) / total)
            lse_ref[head, first:span, :] = top + jnp.log(total)
        o_ref[first:span, :] = jnp.where(sides[0], outs[0], outs[1]).astype(bf)


def attn_fwd(length, qkv, rel_rev, bias_u, bias_v, *, block=256):
    full, cols = rel_rev.shape
    pairs = cols // (2 * HD)
    at = lambda part: pl.BlockSpec((full, 2 * HD), lambda pair, _: (0, part * pairs + pair))
    row = pl.BlockSpec((1, 2 * HD), lambda pair, _: (0, pair))
    return pl.pallas_call(
        functools.partial(attn_fwd_body, block=block),
        out_shape=(
            jax.ShapeDtypeStruct((full, cols), bf),
            jax.ShapeDtypeStruct((2 * pairs, full, 1), f32),
        ),
        grid_spec=pltpu.PrefetchScalarGridSpec(
            num_scalar_prefetch=1,
            grid=(pairs,),
            in_specs=[at(0), at(1), at(2), at(0), row, row],
            out_specs=(at(0), pl.BlockSpec((2, full, 1), lambda pair, _: (pair, 0, 0))),
        ),
        cost_estimate=pl.CostEstimate(
            flops=12 * full * full * cols, bytes_accessed=10 * full * cols, transcendentals=0
        ),
        compiler_params=pltpu.CompilerParams(vmem_limit_bytes=60 << 20),
        name="attn_fwd",
    )(length, qkv, qkv, qkv, rel_rev, bias_u, bias_v)


def attn_bwd_body(len_ref, q_ref, k_ref, v_ref, r_ref, bu_ref, bv_ref, lse_ref, do_ref, *refs, block):
    dq_ref, dk_ref, dv_ref, dr_ref, gu_ref, gv_ref, dk_t, dv_t, dr_t = refs
    full = q_ref.shape[0]
    length = len_ref[0]
    lane = lax.broadcasted_iota(jnp.int32, (block, 2 * HD), 1)
    sides = (lane < HD, lane >= HD)
    rows = lax.broadcasted_iota(jnp.int32, (block, block), 0)
    cols = lax.broadcasted_iota(jnp.int32, (block, block), 1)
    tri = cols <= rows
    flip = jnp.where(rows + cols == block - 1, 1.0, 0.0).astype(bf)
    row = lax.broadcasted_iota(jnp.int32, (block, 1), 0)
    for ref in (dk_t, dv_t, dr_t, dq_ref, gu_ref, gv_ref):
        ref[...] = jnp.zeros_like(ref)
    for first in range(0, full, block):
        span = first + block

        @pl.when(first < length)
        def _():
            q = q_ref[first:span, :].astype(f32)
            qu = (q + bu_ref[...]).astype(bf).astype(f32) * 0.125
            qv = (q + bv_ref[...]).astype(bf).astype(f32) * 0.125
            do = do_ref[first:span, :].astype(f32)
            qu_t = jnp.transpose(qu).astype(bf)
            do_t = jnp.transpose(do).astype(bf)
            qv_t = jnp.transpose(dot(flip, qv.astype(bf), NN)).astype(bf)
            dqu, dqv = [], []
            for head, side in enumerate(sides):
                at = slice(head * HD, (head + 1) * HD)
                s = scores(
                    jnp.where(side, qu, 0.0).astype(bf),
                    jnp.where(side, qv, 0.0).astype(bf),
                    k_ref[:span, :],
                    r_ref[full - span :, :],
                    tri,
                    block,
                )
                lse = jnp.where(first + row < length, lse_ref[head, first:span, :], -NEG)
                p = jnp.exp(s - lse)
                dp = dot(jnp.where(side, do, 0.0).astype(bf), v_ref[:span, :], NT)
                t = p * dp
                ds = (t - p * jnp.sum(t, axis=1, keepdims=True)).astype(bf)
                dv_t[at, :span] += dot(do_t[at], p.astype(bf), NN)
                both = dot(jnp.concatenate([qu_t[at], flip], axis=0), ds, NN)
                dk_t[at, :span] += both[:HD]
                dqu.append(dot(ds, k_ref[:span, :], NN))
                ds_rev = pltpu.roll(both[HD:], 0, 1, stride=1, stride_axis=0).astype(bf)
                dr_t[at, full - span :] += dot(qv_t[at], ds_rev, NN)
                dqv.append(dot(ds_rev, r_ref[full - span :, :], NN))
            dqu = jnp.where(sides[0], dqu[0], dqu[1]) * 0.125
            dqv = jnp.where(sides[0], dqv[0], dqv[1]) * 0.125
            gu_ref[...] += jnp.sum(dqu, axis=0, keepdims=True)
            gv_ref[...] += jnp.sum(dqv, axis=0, keepdims=True)
            dq_ref[first:span, :] = (dqu + dot(flip, dqv.astype(bf), NN)).astype(bf)

    dk_ref[...] = jnp.transpose(dk_t[...]).astype(bf)
    dv_ref[...] = jnp.transpose(dv_t[...]).astype(bf)
    dr_ref[...] = jnp.transpose(dr_t[...]).astype(bf)


def attn_bwd(length, qkv, rel_rev, bias_u, bias_v, lse, d_out, *, pair, block=256):
    full, cols = rel_rev.shape
    pairs = cols // (2 * HD)
    at = lambda part: pl.BlockSpec((full, 2 * HD), lambda i, _: (0, part * pairs + pair))
    row = pl.BlockSpec((1, 2 * HD), lambda i, _: (0, pair))
    out = pl.BlockSpec((full, 2 * HD), lambda i, _: (0, 0))
    out_row = pl.BlockSpec((1, 2 * HD), lambda i, _: (0, 0))
    return pl.pallas_call(
        functools.partial(attn_bwd_body, block=block),
        out_shape=(jax.ShapeDtypeStruct((full, 2 * HD), bf),) * 4
        + (jax.ShapeDtypeStruct((1, 2 * HD), f32),) * 2,
        grid_spec=pltpu.PrefetchScalarGridSpec(
            num_scalar_prefetch=1,
            grid=(1,),
            in_specs=[at(0), at(1), at(2), at(0), row, row]
            + [pl.BlockSpec((2, full, 1), lambda i, _: (pair, 0, 0)), at(0)],
            out_specs=(out,) * 4 + (out_row, out_row),
            scratch_shapes=[pltpu.VMEM((2 * HD, full), f32)] * 3,
        ),
        cost_estimate=pl.CostEstimate(
            flops=36 * full * full * HD * 4, bytes_accessed=20 * full * HD * 2, transcendentals=0
        ),
        compiler_params=pltpu.CompilerParams(vmem_limit_bytes=60 << 20),
        name="attn_bwd",
    )(length, qkv, qkv, qkv, rel_rev, bias_u, bias_v, lse, d_out)


def norm_parts(values):
    mean_val = jnp.mean(values, axis=-1, keepdims=True)
    centered = values - mean_val
    inv_std = lax.rsqrt(jnp.mean(centered * centered, axis=-1, keepdims=True) + NORM_EPS)
    return (centered * inv_std, inv_std)


def norm_back(grad_norm, x_hat, inv_std):
    first_mean = jnp.mean(grad_norm, axis=-1, keepdims=True)
    second_mean = jnp.mean(grad_norm * x_hat, axis=-1, keepdims=True)
    return inv_std * (grad_norm - first_mean - x_hat * second_mean)


def position_table(count_rows, feature_count):
    steps = lax.iota(jnp.float32, count_rows)
    half_count = feature_count // 2
    inv_freq = jnp.exp(
        lax.iota(jnp.float32, half_count) * (-2.0 * math.log(10000.0) / feature_count)
    )
    angles = steps[:, None] * inv_freq[None, :]
    return jnp.concatenate([jnp.sin(angles), jnp.cos(angles)], axis=1)


def skew_rows(matrix):
    leading = matrix.shape[:-2]
    row_count, col_count = matrix.shape[-2:]
    flattened = matrix.reshape(leading + (row_count * col_count,))
    picked = flattened[..., row_count - 1 : row_count - 1 + row_count * (col_count - 1)]
    return picked.reshape(leading + (row_count, col_count - 1))[..., : col_count - row_count]


def unskew_rows(matrix):
    leading = matrix.shape[:-2]
    row_count, key_count = matrix.shape[-2:]
    axis_pos = len(leading)
    widened = jnp.pad(matrix, [(0, 0)] * axis_pos + [(0, 0), (0, row_count - 1)])
    flattened = widened.reshape(leading + (row_count * (key_count + row_count - 1),))
    flattened = jnp.pad(flattened, [(0, 0)] * axis_pos + [(row_count - 1, 1)])
    return flattened.reshape(leading + (row_count, key_count + row_count))


def head_split_device(
    layer_input,
    lengths,
    ln1_gain,
    ln1_bias,
    w_qkv,
    w_rel,
    bias_u,
    bias_v,
    w_out,
    ln2_gain,
    ln2_bias,
    w_up,
    up_bias,
    w_down,
    down_bias,
    grad_out,
):
    weights = (
        lax.all_gather(ln1_gain, "fsdp", axis=0, tiled=True),
        lax.all_gather(ln1_bias, "fsdp", axis=0, tiled=True),
        lax.all_gather(w_qkv, "fsdp", axis=0, tiled=True),
        lax.all_gather(w_rel, "fsdp", axis=0, tiled=True),
        lax.all_gather(bias_u, "fsdp", axis=0, tiled=True),
        lax.all_gather(bias_v, "fsdp", axis=0, tiled=True),
        lax.all_gather(w_out, "fsdp", axis=0, tiled=True),
        lax.all_gather(ln2_gain, "fsdp", axis=0, tiled=True),
        lax.all_gather(ln2_bias, "fsdp", axis=0, tiled=True),
        lax.all_gather(w_up, "fsdp", axis=0, tiled=True),
        lax.all_gather(up_bias, "fsdp", axis=0, tiled=True),
        lax.all_gather(w_down, "fsdp", axis=0, tiled=True),
        lax.all_gather(down_bias, "fsdp", axis=0, tiled=True),
    )
    (
        gain_one,
        shift_one,
        query_key_value_matrix,
        rel_weight,
        first_bias,
        second_bias,
        output_matrix,
        gain_two,
        shift_two,
        up_matrix,
        up_shift,
        down_matrix,
        down_shift,
    ) = weights
    gain_one = gain_one.astype(jnp.float32)
    shift_one = shift_one.astype(jnp.float32)
    gain_two = gain_two.astype(jnp.float32)
    shift_two = shift_two.astype(jnp.float32)
    up_shift = up_shift.astype(jnp.float32)
    down_shift = down_shift.astype(jnp.float32)
    slots, block_len, width = layer_input.shape
    seq_count = lax.axis_size("seq")
    seq_rank = lax.axis_index("seq")
    head_dim = HEAD_DIM
    group = H // seq_count
    full_len = block_len * seq_count
    score_scale = 1.0 / math.sqrt(head_dim)
    q_block = 512
    num_blocks = full_len // q_block
    win_len = full_len + q_block
    x_float = layer_input.astype(jnp.float32)
    x_hat_one, inv_std_one = norm_parts(x_float)
    first_normalized = (x_hat_one * gain_one + shift_one).astype(jnp.bfloat16)
    qkv_local = jnp.einsum(
        "mcr,rk->mck", first_normalized, query_key_value_matrix, preferred_element_type=jnp.float32
    ).astype(jnp.bfloat16)
    qkv_heads = lax.all_to_all(qkv_local, "seq", split_axis=2, concat_axis=1, tiled=True)
    qkv_heads = qkv_heads.reshape(slots, full_len, group, 3, head_dim)
    queries = qkv_heads[:, :, :, 0]
    keys = qkv_heads[:, :, :, 1]
    values = qkv_heads[:, :, :, 2]
    head_start = seq_rank * group
    head_bias_u = lax.dynamic_slice_in_dim(
        first_bias.astype(jnp.float32).reshape(H, head_dim), head_start, group, 0
    )
    head_bias_v = lax.dynamic_slice_in_dim(
        second_bias.astype(jnp.float32).reshape(H, head_dim), head_start, group, 0
    )
    query_u = (queries.astype(jnp.float32) + head_bias_u).astype(jnp.bfloat16)
    query_v = (queries.astype(jnp.float32) + head_bias_v).astype(jnp.bfloat16)
    table_rev = position_table(full_len, width).astype(jnp.bfloat16)[::-1]
    rel_cols = lax.dynamic_slice_in_dim(rel_weight, head_start * head_dim, group * head_dim, 1)
    rel_rev = jnp.dot(table_rev, rel_cols, preferred_element_type=jnp.float32).astype(jnp.bfloat16)
    rel_ext = jnp.concatenate([rel_rev, jnp.zeros_like(rel_rev)], axis=0).reshape(
        2 * full_len, group, head_dim
    )
    col_ids = lax.iota(jnp.int32, full_len)

    def scores_block(first_row):
        qu_part = lax.dynamic_slice_in_dim(query_u, first_row, q_block, 1)
        qv_part = lax.dynamic_slice_in_dim(query_v, first_row, q_block, 1)
        window_start = full_len - q_block - first_row
        rel_win = lax.dynamic_slice_in_dim(rel_ext, window_start, win_len, 0)
        content = jnp.einsum("sqhe,skhe->shqk", qu_part, keys, preferred_element_type=jnp.float32)
        rel_raw = jnp.einsum("sqhe,the->shqt", qv_part, rel_win, preferred_element_type=jnp.float32)
        rel_part = skew_rows(rel_raw)
        row_ids = first_row + lax.iota(jnp.int32, q_block)
        causal = col_ids[None, :] <= row_ids[:, None]
        inside = col_ids[None, :] < lengths[:, None]
        allowed = causal[None, None, :, :] & inside[:, None, None, :]
        scores = jnp.where(allowed, (content + rel_part) * score_scale, NEG_FILL)
        return (scores, qu_part, qv_part, rel_win, window_start)

    def forward_block(block_index):
        first_row = block_index * q_block
        scores, qu_part, qv_part, rel_win, window_start = scores_block(first_row)
        top = jnp.max(scores, axis=-1, keepdims=True)
        expo = jnp.exp(scores - top)
        total = jnp.sum(expo, axis=-1, keepdims=True)
        probs = (expo / total).astype(jnp.bfloat16)
        out_part = jnp.einsum(
            "shqk,skhe->sqhe", probs, values, preferred_element_type=jnp.float32
        ).astype(jnp.bfloat16)
        return (out_part, top[..., 0] + jnp.log(total[..., 0]))

    block_outs, block_lse = lax.map(forward_block, jnp.arange(num_blocks, dtype=jnp.int32))
    attn_heads = jnp.moveaxis(block_outs, 0, 1).reshape(slots, full_len, group * head_dim)
    attention_sequence = lax.all_to_all(attn_heads, "seq", split_axis=1, concat_axis=2, tiled=True)
    attention_projected = jnp.einsum(
        "mcr,rk->mck", attention_sequence, output_matrix, preferred_element_type=jnp.float32
    )
    resid = x_float + attention_projected
    x_hat_two, inv_std_two = norm_parts(resid)
    second_normalized = (x_hat_two * gain_two + shift_two).astype(jnp.bfloat16)
    pre_act = (
        jnp.einsum("oka,ac->okc", second_normalized, up_matrix, preferred_element_type=jnp.float32)
        + up_shift
    )
    normal_cdf = 0.5 * (1.0 + lax.erf(pre_act * (1.0 / math.sqrt(2.0))))
    hidden_state = (pre_act * normal_cdf).astype(jnp.bfloat16)
    down_proj = (
        jnp.einsum("zcp,pr->zcr", hidden_state, down_matrix, preferred_element_type=jnp.float32)
        + down_shift
    )
    output = (resid + down_proj).astype(jnp.bfloat16)
    positions = seq_rank * block_len + lax.iota(jnp.int32, block_len)
    live = (positions[None, :] < lengths[:, None]).astype(jnp.bfloat16)
    result_gradient = grad_out * live[:, :, None]
    grad_y_float = result_gradient.astype(jnp.float32)
    g_down_shift = jnp.sum(grad_y_float, axis=(0, 1))
    down_gradient = jnp.einsum(
        "hki,hku->iu", hidden_state, result_gradient, preferred_element_type=jnp.float32
    )
    hidden_gradient = jnp.einsum(
        "gvu,ju->gvj", result_gradient, down_matrix, preferred_element_type=jnp.float32
    )
    deriv = normal_cdf + pre_act * jnp.exp(-0.5 * pre_act * pre_act) * (
        1.0 / math.sqrt(2.0 * math.pi)
    )
    preactivation_gradient = (hidden_gradient * deriv).astype(jnp.bfloat16)
    g_up_shift = jnp.sum(preactivation_gradient.astype(jnp.float32), axis=(0, 1))
    up_gradient = jnp.einsum(
        "oiz,oix->zx", second_normalized, preactivation_gradient, preferred_element_type=jnp.float32
    )
    second_norm_gradient = jnp.einsum(
        "rau,ku->rak", preactivation_gradient, up_matrix, preferred_element_type=jnp.float32
    )
    g_gain_two = jnp.sum(second_norm_gradient * x_hat_two, axis=(0, 1))
    g_shift_two = jnp.sum(second_norm_gradient, axis=(0, 1))
    g_resid = grad_y_float + norm_back(second_norm_gradient * gain_two, x_hat_two, inv_std_two)
    attention_gradient = g_resid.astype(jnp.bfloat16)
    output_gradient = jnp.einsum(
        "zau,zam->um", attention_sequence, attention_gradient, preferred_element_type=jnp.float32
    )
    g_attn_seq = jnp.einsum(
        "urz,jz->urj", attention_gradient, output_matrix, preferred_element_type=jnp.float32
    ).astype(jnp.bfloat16)
    g_attn_heads = lax.all_to_all(
        g_attn_seq, "seq", split_axis=2, concat_axis=1, tiled=True
    ).reshape(slots, full_len, group, head_dim)

    def backward_block(carry, block_index):
        g_keys, g_vals, g_ext = carry
        first_row = block_index * q_block
        scores, qu_part, qv_part, rel_win, window_start = scores_block(first_row)
        probs = jnp.exp(scores - block_lse[block_index][..., None])
        d_out = lax.dynamic_slice_in_dim(g_attn_heads, first_row, q_block, 1)
        g_vals = g_vals + jnp.einsum(
            "shqk,sqhe->skhe", probs.astype(jnp.bfloat16), d_out, preferred_element_type=jnp.float32
        )
        g_probs = jnp.einsum("sqhe,skhe->shqk", d_out, values, preferred_element_type=jnp.float32)
        inner = jnp.sum(probs * g_probs, axis=-1, keepdims=True)
        g_scores = (probs * (g_probs - inner)).astype(jnp.bfloat16)
        g_qu = (
            jnp.einsum("shqk,skhe->sqhe", g_scores, keys, preferred_element_type=jnp.float32)
            * score_scale
        )
        g_keys = (
            g_keys
            + jnp.einsum("shqk,sqhe->skhe", g_scores, qu_part, preferred_element_type=jnp.float32)
            * score_scale
        )
        g_wide = unskew_rows(g_scores)
        g_qv = (
            jnp.einsum("shqt,the->sqhe", g_wide, rel_win, preferred_element_type=jnp.float32)
            * score_scale
        )
        g_win = (
            jnp.einsum("shqt,sqhe->sthe", g_wide, qv_part, preferred_element_type=jnp.float32)
            * score_scale
        )
        g_old = lax.dynamic_slice_in_dim(g_ext, window_start, win_len, 1)
        g_ext = lax.dynamic_update_slice_in_dim(g_ext, g_old + g_win, window_start, 1)
        return ((g_keys, g_vals, g_ext), (g_qu, g_qv))

    zero_heads = jnp.zeros((slots, full_len, group, head_dim), jnp.float32)
    zero_ext = jnp.zeros((slots, 2 * full_len, group, head_dim), jnp.float32)
    (g_keys, g_vals, g_ext), (g_qu_blocks, g_qv_blocks) = lax.scan(
        backward_block, (zero_heads, zero_heads, zero_ext), jnp.arange(num_blocks, dtype=jnp.int32)
    )
    g_qu = jnp.moveaxis(g_qu_blocks, 0, 1).reshape(slots, full_len, group, head_dim)
    g_qv = jnp.moveaxis(g_qv_blocks, 0, 1).reshape(slots, full_len, group, head_dim)
    g_queries = g_qu + g_qv
    g_bias_u_heads = jnp.sum(g_qu, axis=(0, 1))
    g_bias_v_heads = jnp.sum(g_qv, axis=(0, 1))
    g_qkv_heads = (
        jnp.stack([g_queries, g_keys, g_vals], axis=3)
        .astype(jnp.bfloat16)
        .reshape(slots, full_len, group * 3 * head_dim)
    )
    query_key_value_gradient = lax.all_to_all(
        g_qkv_heads, "seq", split_axis=1, concat_axis=2, tiled=True
    )
    g_rel_low = g_ext[:, :full_len].astype(jnp.bfloat16)
    g_rel_heads = jnp.einsum(
        "td,sthe->dhe", table_rev, g_rel_low, preferred_element_type=jnp.float32
    ).reshape(width, group * head_dim)
    g_rel_weight = lax.dynamic_update_slice_in_dim(
        jnp.zeros((width, width), jnp.float32), g_rel_heads, head_start * head_dim, 1
    )
    g_bias_u = lax.dynamic_update_slice_in_dim(
        jnp.zeros((H, head_dim), jnp.float32), g_bias_u_heads, head_start, 0
    ).reshape(width)
    g_bias_v = lax.dynamic_update_slice_in_dim(
        jnp.zeros((H, head_dim), jnp.float32), g_bias_v_heads, head_start, 0
    ).reshape(width)
    query_key_value_weight_gradient = jnp.einsum(
        "zau,zam->um",
        first_normalized,
        query_key_value_gradient,
        preferred_element_type=jnp.float32,
    )
    first_norm_gradient = jnp.einsum(
        "urz,jz->urj",
        query_key_value_gradient,
        query_key_value_matrix,
        preferred_element_type=jnp.float32,
    )
    g_gain_one = jnp.sum(first_norm_gradient * x_hat_one, axis=(0, 1))
    g_shift_one = jnp.sum(first_norm_gradient, axis=(0, 1))
    g_input = g_resid + norm_back(first_norm_gradient * gain_one, x_hat_one, inv_std_one)
    partial_shards = (
        lax.psum_scatter(g_gain_one, "fsdp", scatter_dimension=0, tiled=True),
        lax.psum_scatter(g_shift_one, "fsdp", scatter_dimension=0, tiled=True),
        lax.psum_scatter(query_key_value_weight_gradient, "fsdp", scatter_dimension=0, tiled=True),
        lax.psum_scatter(g_rel_weight, "fsdp", scatter_dimension=0, tiled=True),
        lax.psum_scatter(g_bias_u, "fsdp", scatter_dimension=0, tiled=True),
        lax.psum_scatter(g_bias_v, "fsdp", scatter_dimension=0, tiled=True),
        lax.psum_scatter(output_gradient, "fsdp", scatter_dimension=0, tiled=True),
        lax.psum_scatter(g_gain_two, "fsdp", scatter_dimension=0, tiled=True),
        lax.psum_scatter(g_shift_two, "fsdp", scatter_dimension=0, tiled=True),
        lax.psum_scatter(up_gradient, "fsdp", scatter_dimension=0, tiled=True),
        lax.psum_scatter(g_up_shift, "fsdp", scatter_dimension=0, tiled=True),
        lax.psum_scatter(down_gradient, "fsdp", scatter_dimension=0, tiled=True),
        lax.psum_scatter(g_down_shift, "fsdp", scatter_dimension=0, tiled=True),
    )
    shards = lax.psum(
        (
            partial_shards[0],
            partial_shards[1],
            partial_shards[2],
            partial_shards[3],
            partial_shards[4],
            partial_shards[5],
            partial_shards[6],
            partial_shards[7],
            partial_shards[8],
            partial_shards[9],
            partial_shards[10],
            partial_shards[11],
            partial_shards[12],
        ),
        "seq",
    )
    return (
        output,
        g_input,
        shards[0],
        shards[1],
        shards[2],
        shards[3],
        shards[4],
        shards[5],
        shards[6],
        shards[7],
        shards[8],
        shards[9],
        shards[10],
        shards[11],
        shards[12],
    )


def swap_core(values):
    size = lax.axis_size("fsdp")
    return lax.ppermute(values, "fsdp", [(i, i ^ 1) for i in range(size)])


def swap_chip(values, mask):
    size = lax.axis_size("fsdp")
    return lax.ppermute(values, "fsdp", [(i, i ^ (2 * mask)) for i in range(size)])


def swap_seq(values, mask):
    size = lax.axis_size("seq")
    return lax.ppermute(values, "seq", [(i, i ^ mask) for i in range(size)])


def slot_pairs(turn):
    seq, pairs = lax.axis_size("seq"), []
    for f in range(lax.axis_size("fsdp")):
        for z in range(seq):
            to_f, to_z = (f & ~1) | (z & 1), 2 * (f & 1) + (turn ^ (z >> 1))
            pairs.append((f * seq + z, to_f * seq + to_z))
    return pairs


def to_slots(values, seq_rank):
    return [
        lax.ppermute(
            lax.dynamic_index_in_dim(values, turn ^ (seq_rank >> 1), 0, keepdims=False),
            ("fsdp", "seq"),
            slot_pairs(turn),
        )
        for turn in (0, 1)
    ]


def together(*values):
    return lax.optimization_barrier(values)


def whole(*shape):
    return pl.BlockSpec(shape, lambda *_: (0,) * len(shape))


def kernel_call(body, name, meta, args, outs, *, grid=(1,), in_specs=None, out_specs=None, scratch=(), flops=0):
    in_specs = in_specs or [whole(*a.shape) for a in args]
    out_specs = out_specs or [whole(*shape) for shape, _ in outs]
    moved = sum(a.size * a.dtype.itemsize for a in args)
    moved += sum(math.prod(shape) * jnp.dtype(kind).itemsize for shape, kind in outs)
    return pl.pallas_call(
        body,
        out_shape=[jax.ShapeDtypeStruct(shape, kind) for shape, kind in outs],
        grid_spec=pltpu.PrefetchScalarGridSpec(
            num_scalar_prefetch=1,
            grid=grid,
            in_specs=in_specs,
            out_specs=out_specs,
            scratch_shapes=scratch,
        ),
        compiler_params=pltpu.CompilerParams(vmem_limit_bytes=60 << 20),
        cost_estimate=pl.CostEstimate(flops=flops, bytes_accessed=moved, transcendentals=0),
        name=name,
    )(meta, *args)


TN = (((0,), (0,)), ((), ()))
CORE, CHIP, RANK, LIVE = range(4)


def aligned(index, size):
    return pl.multiple_of(index * size, size)


def pack_body(meta, qkv_ref, rel_ref, up_ref, out_ref, down_ref, *refs):
    small, (attn_ref, feed_ref, send_ref) = refs[:8], refs[8:]
    core = meta[CORE]
    shard = qkv_ref.shape[0]
    qkv, rel, up, out, down = qkv_ref[...], rel_ref[...], up_ref[...], out_ref[...], down_ref[...]
    heads, hd = rel.shape[1] // HEAD_DIM // 2, HEAD_DIM
    unit = up.shape[1] // 8
    packs, ups = [], []
    row = jnp.concatenate([ref[i : i + 1] for ref in small for i in range(ref.shape[0])], axis=1)
    row = jnp.concatenate([row, jnp.zeros((1, 4 * heads * hd - row.shape[1]), row.dtype)], axis=1)
    rows = jnp.broadcast_to(row, (8, row.shape[1]))
    for side in (0, 1):
        parts = [
            qkv[:, ((2 * j + side) * 3 + t) * hd : ((2 * j + side) * 3 + t + 1) * hd]
            for t in range(3)
            for j in range(heads)
        ]
        parts += [rel[:, (2 * j + side) * hd : (2 * j + side + 1) * hd] for j in range(heads)]
        packs.append(jnp.concatenate(parts, axis=1))
        ups.append(
            jnp.concatenate([up[:, (2 * j + side) * unit : (2 * j + side + 1) * unit] for j in range(4)], axis=1)
        )
    first = core == 0
    folded = jnp.concatenate([out[: shard // 2], out[shard // 2 :]], axis=1)
    attn_ref[:shard] = jnp.where(first, packs[0], packs[1])
    attn_ref[shard:] = rows
    send_ref[:shard] = jnp.where(first, packs[1], packs[0])
    send_ref[shard : shard + 8] = rows
    send_ref[shard + 8 : 2 * shard + 8] = jnp.where(first, ups[1], ups[0])
    send_ref[2 * shard + 8 :] = folded
    feed_ref[:shard] = jnp.where(first, ups[0], ups[1])
    feed_ref[shard : shard + shard // 2] = folded
    feed_ref[shard + shard // 2 :] = jnp.concatenate([down[: 2 * shard], down[2 * shard :]], axis=1)


def ordered(meta, own, other):
    first = meta[CORE] == 0
    return jnp.concatenate([jnp.where(first, own, other), jnp.where(first, other, own)], axis=0)


def slot_block(meta, step, own, other, store):
    turn = (step >> 1) ^ (meta[RANK] & 1)
    local = (step & 1) == meta[CORE]
    for t in (0, 1):
        pl.when(local & (turn == t))(functools.partial(store, own[t]))
        pl.when(jnp.logical_not(local) & (turn == t))(functools.partial(store, other[t]))


def norm_rows(values):
    mean_val = jnp.mean(values, axis=1, keepdims=True)
    centered = values - mean_val
    inv_std = lax.rsqrt(jnp.mean(centered * centered, axis=1, keepdims=True) + NORM_EPS)
    return centered * inv_std, inv_std


def project_body(meta, *refs):
    packs, own_x, other_x = refs[0:4], refs[4:6], refs[6:8]
    table_ref, qkv_ref, h_ref, x_ref, rel_ref, w_ref, vec_ref, up_ref, bias_ref = refs[8:17]
    step, chip = pl.program_id(0), meta[CHIP]
    width = w_ref.shape[0]
    shard = width // 8
    span = qkv_ref.shape[1]
    cols = span // 3

    @pl.when(step == 0)
    def _():
        first = meta[CORE] == 0
        vec_ref[...] = jnp.zeros_like(vec_ref)
        own_rows = []
        for k in range(4):
            at = pl.ds(aligned(chip ^ k, 2 * shard), 2 * shard)
            own, other = packs[k][: shard + 8], packs[k][shard + 8 :]
            w_ref[at, :] = ordered(meta, own[:shard], other[:shard])
            own_row, other_row = own[shard : shard + 1].astype(f32), other[shard : shard + 1].astype(f32)
            own_rows.append(own_row)
            low, high = jnp.where(first, own_row, other_row), jnp.where(first, other_row, own_row)
            for row, source in enumerate((0, 1, 4, 5, 6)):
                piece = slice(source * shard, (source + 1) * shard)
                vec_ref[row : row + 1, at] = jnp.concatenate([low[:, piece], high[:, piece]], axis=1)
            unit = up_ref.shape[1] // 4
            up_ref[:, pl.ds(aligned(chip ^ k, unit), unit)] = own_row[:, 7 * shard : 7 * shard + unit]
        even = chip & 1 == 0
        for k in (0, 2):
            at = pl.ds(aligned((chip ^ k) >> 1, 2 * shard), 2 * shard)
            low = jnp.where(even, own_rows[k], own_rows[k + 1])
            high = jnp.where(even, own_rows[k + 1], own_rows[k])
            for row, source in enumerate((2, 3)):
                piece = slice(source * shard, (source + 1) * shard)
                bias_ref[row : row + 1, at] = jnp.concatenate([low[:, piece], high[:, piece]], axis=1)

    def copy(ref):
        x_ref[...] = ref[...]

    slot_block(meta, step, own_x, other_x, copy)
    x_hat, _ = norm_rows(x_ref[...].astype(f32))
    h = (x_hat * vec_ref[0:1, :] + vec_ref[1:2, :]).astype(bf)
    h_ref[...] = h
    qkv_ref[...] = dot(h, w_ref[:, :span], NN).astype(bf)
    rel_ref[...] = dot(table_ref[...], w_ref[:, span:], NN).astype(bf)


def feed_body(meta, *refs):
    packs, own_g, other_g = refs[0:4], refs[4:6], refs[6:8]
    x_ref, o_own, o_other, vec_ref, bias_ref = refs[8:13]
    (g_ref, df_ref, h_ref, dy_ref, y1_ref, y_keep, dh_keep, dh_send, y_send, sum_ref, wo_mine) = refs[13:24]
    up_w, down_w, wo_theirs = refs[24:27]
    step, chip, core = pl.program_id(0), meta[CHIP], meta[CORE]
    width = up_w.shape[0]
    shard, unit, block = width // 8, down_w.shape[0] // 4, x_ref.shape[0]
    fold = shard // 2

    @pl.when(step == 0)
    def _():
        sum_ref[...] = jnp.zeros_like(sum_ref)
        for k in range(4):
            pack = packs[k]
            own, other = pack[:shard], pack[shard + fold + 2 * shard : 2 * shard + fold + 2 * shard]
            up_w[pl.ds(aligned(chip ^ k, 2 * shard), 2 * shard), :] = ordered(meta, own, other)
            at = pl.ds(aligned(chip ^ k, shard), shard)
            rows = pack[shard : shard + fold]
            wo_mine[at, :] = jnp.concatenate([rows[:, :width], rows[:, width:]], axis=0)
            rows = pack[4 * shard + fold :]
            wo_theirs[at, :] = jnp.concatenate([rows[:, :width], rows[:, width:]], axis=0)
            rows = pack[shard + fold : 3 * shard + fold]
            down_w[pl.ds(aligned(chip ^ k, unit), unit), :] = jnp.concatenate(
                [rows[:, :width], rows[:, width:]], axis=0
            )

    at = step * block + lax.broadcasted_iota(jnp.int32, (block, 1), 0)

    def load(ref):
        dy_ref[...] = jnp.where(at < meta[LIVE], ref[...].astype(f32), 0.0).astype(bf)

    slot_block(meta, step, own_g, other_g, load)
    y1 = x_ref[...].astype(f32) + (dot(o_own[...], wo_mine[...], NN) + dot(o_other[...], wo_theirs[...], NN))
    y1_ref[...] = y1
    x_hat, _ = norm_rows(y1)
    h = (x_hat * vec_ref[2:3, :] + vec_ref[3:4, :]).astype(bf)
    h_ref[...] = h
    f = dot(h, up_w[...], NN) + bias_ref[...]
    cdf = 0.5 * (1.0 + lax.erf(f * (1.0 / math.sqrt(2.0))))
    g = (f * cdf).astype(bf)
    g_ref[...] = g
    z = dot(g, down_w[...], NN)
    dy = dy_ref[...]
    dg = dot(dy, down_w[...], NT)
    df = (dg * (cdf + f * jnp.exp(-0.5 * f * f) * (1.0 / math.sqrt(2.0 * math.pi)))).astype(bf)
    df_ref[...] = df
    dh = dot(df, up_w[...], NT)
    dh_keep[...] = dh
    dh_send[...] = dh.astype(bf)
    sum_ref[0:1, :width] += jnp.sum(dh * x_hat, axis=0, keepdims=True)
    sum_ref[1:2, :width] += jnp.sum(dh, axis=0, keepdims=True)
    sum_ref[3:4, :] += jnp.sum(df.astype(f32), axis=0, keepdims=True)
    local = (step & 1) == core

    @pl.when(local)
    def _():
        y_keep[...] = y1 + z + vec_ref[4:5, :]
        sum_ref[2:3, :width] += jnp.sum(dy.astype(f32), axis=0, keepdims=True)

    @pl.when(jnp.logical_not(local))
    def _():
        y_send[...] = z.astype(bf)


def norm_two_body(meta, y1_ref, dh_keep, dh_came, dy_ref, vec_ref, y_keep, y_came, wo_ref, o_ref, *refs):
    out0, out1, resid_ref, do_ref, go_ref = refs
    step = pl.program_id(0)

    @pl.when(step == 0)
    def _():
        go_ref[...] = jnp.zeros_like(go_ref)

    x_hat, inv_std = norm_rows(y1_ref[...])
    e = (dh_keep[...] + dh_came[...].astype(f32)) * vec_ref[2:3, :]
    first = jnp.mean(e, axis=1, keepdims=True)
    second = jnp.mean(e * x_hat, axis=1, keepdims=True)
    grad = dy_ref[...].astype(f32) + inv_std * (e - first - x_hat * second)
    da = grad.astype(bf)
    do_ref[...] = dot(da, wo_ref[...], NT).astype(bf)
    go_ref[...] += dot(o_ref[...], da, TN)
    turn = (step >> 1) ^ (meta[RANK] & 1)
    local = (step & 1) == meta[CORE]

    @pl.when(local)
    def _():
        resid_ref[...] = grad
        y = (y_keep[...] + y_came[...].astype(f32)).astype(bf)

        @pl.when(turn == 0)
        def _():
            out0[...] = y

        @pl.when(turn == 1)
        def _():
            out1[...] = y


def feed_grad_body(meta, h_ref, df_ref, sum_ref, g_ref, dy_ref, *outs):
    k = pl.program_id(0)
    rows = h_ref.shape[1]
    grad = dot(h_ref[...], df_ref[...], TN)
    at = pl.ds(aligned(meta[CHIP] ^ k, rows), rows)
    unit = df_ref.shape[1] // 4
    tail = jnp.concatenate(
        [sum_ref[0:1, at], sum_ref[1:2, at], sum_ref[2:3, at]]
        + [sum_ref[3:4, pl.ds(aligned(meta[CHIP] ^ k, unit), unit)]],
        axis=1,
    )
    tail = jnp.concatenate([tail, jnp.zeros((1, df_ref.shape[1] - tail.shape[1]), f32)], axis=1)
    tail = jnp.broadcast_to(tail, (16, tail.shape[1]))
    down = dot(g_ref[...], dy_ref[...], TN)
    half = unit // 2
    for index, out in enumerate(outs):

        @pl.when(k == index)
        def _():
            out[:rows] = grad.astype(out.dtype)
            out[rows : rows + 16] = tail.astype(out.dtype)
            out[rows + 16 :] = jnp.concatenate([down[:half], down[half:]], axis=1).astype(out.dtype)


def qkv_back_body(meta, *refs):
    grads, rels = refs[:6], refs[6:8]
    w_ref, x_ref, h_ref, table_ref, gu_ref, gv_ref, go_ref = refs[8:15]
    keep_ref, send_ref = refs[15:17]
    outs, acc, sums = refs[17:21], refs[21], refs[22]
    step, chip = pl.program_id(0), meta[CHIP]
    width = x_ref.shape[1]
    rows = width // 4

    @pl.when(step == 0)
    def _():
        sums[...] = jnp.zeros_like(sums)
        acc[...] = jnp.zeros_like(acc)

    dqkv = jnp.concatenate([ref[...] for ref in grads], axis=1)
    drel = jnp.concatenate([ref[...] for ref in rels], axis=1)
    span = dqkv.shape[1]
    acc[:, :span] += dot(h_ref[...], dqkv, TN)
    acc[:, span:] += dot(table_ref[...], drel, TN)
    dh = dot(dqkv, w_ref[:, :span], NT)
    x_hat, _ = norm_rows(x_ref[...].astype(f32))
    sums[0:1, :] += jnp.sum(dh * x_hat, axis=0, keepdims=True)
    sums[1:2, :] += jnp.sum(dh, axis=0, keepdims=True)
    local = (step & 1) == meta[CORE]

    @pl.when(local)
    def _():
        keep_ref[...] = dh

    @pl.when(jnp.logical_not(local))
    def _():
        send_ref[...] = dh.astype(bf)

    @pl.when(step == pl.num_programs(0) - 1)
    def _():
        for k, out in enumerate(outs):
            at = pl.ds(aligned(chip ^ k, rows), rows)
            pair = pl.ds(aligned((chip ^ k) >> 1, rows), rows)
            tail = [sums[0:1, at], sums[1:2, at], gu_ref[0:1, pair], gv_ref[0:1, pair]]
            tail = jnp.concatenate(tail + [jnp.zeros((1, acc.shape[1] - 4 * rows), f32)], axis=1)
            out[:rows] = acc[at, :].astype(out.dtype)
            out[rows : rows + 16] = jnp.broadcast_to(tail, (16, tail.shape[1])).astype(out.dtype)
            shard = rows // 2
            lines = go_ref[pl.ds(aligned(chip ^ k, shard), shard), :]
            lines = jnp.concatenate([lines[: shard // 2], lines[shard // 2 :]], axis=1)
            out[rows + 16 :] = lines.astype(out.dtype)


def norm_one_body(meta, x_ref, dh_keep, dh_came, resid_ref, vec_ref, out0, out1):
    turn = pl.program_id(0) ^ (meta[RANK] & 1)
    x_hat, inv_std = norm_rows(x_ref[...].astype(f32))
    e = (dh_keep[...] + dh_came[...].astype(f32)) * vec_ref[0:1, :]
    first = jnp.mean(e, axis=1, keepdims=True)
    second = jnp.mean(e * x_hat, axis=1, keepdims=True)
    grad = (resid_ref[...] + inv_std * (e - first - x_hat * second)).astype(bf)

    @pl.when(turn == 0)
    def _():
        out0[...] = grad

    @pl.when(turn == 1)
    def _():
        out1[...] = grad


def chip_sum_body(meta, own, *refs):
    *came, keep, send = refs
    half = keep.shape[1]
    for out, side in ((keep, meta[RANK] & 1), (send, 1 - (meta[RANK] & 1))):
        at = pl.ds(aligned(side, half), half)
        total = own[:, at]
        for ref in came:
            total = total + ref[:, at].astype(f32)
        out[...] = total.astype(out.dtype)


def chip_sum(meta, parts, name):
    rows, size = parts[0].shape
    return kernel_call(chip_sum_body, name, meta, parts, [((rows, size // 2), f32), ((rows, size // 2), bf)])


def halves(meta, mine, other):
    low = meta[RANK] & 1 == 0
    return jnp.concatenate([jnp.where(low, mine, other), jnp.where(low, other, mine)], axis=1)


def early_out_body(meta, mine, other, up_ref, down_ref):
    both = halves(meta, mine[...], other[...])
    rows, width = up_ref.shape[0], down_ref.shape[1]
    up_ref[...] = both[:rows]
    down = both[rows:].astype(f32)
    down_ref[...] = jnp.concatenate([down[:, :width], down[:, width:]], axis=0)


def late_pack_body(meta, up_ref, mine, other, late_ref, out_ref, send_ref):
    both = halves(meta, mine[...], other[...])
    rows, width = up_ref.shape[0] - 16, out_ref.shape[1]
    shard = rows // 2
    late_ref[...] = both[: rows + 16]
    out = both[rows + 16 :].astype(f32)
    out_ref[...] = jnp.concatenate([out[:, :width], out[:, width:]], axis=0)
    up = up_ref[...]
    for at, part in ((0, up), (up.shape[1], both)):
        theirs = jnp.where(meta[CORE] == 0, part[shard:rows], part[:shard])
        send_ref[:shard, at : at + up.shape[1]] = theirs
        send_ref[shard:, at : at + up.shape[1]] = part[rows : rows + 8]


def late_out_body(meta, up_ref, late_ref, came_ref, g_up, g_qkv, g_rel, vec_ref):
    shard = g_up.shape[0]
    rows, size = 2 * shard, up_ref.shape[1]
    unit, hd, heads = size // 4, HEAD_DIM, H // 2
    first = meta[CORE] == 0
    came = came_ref[...]
    pair = []
    for at, ref in ((0, up_ref), (size, late_ref)):
        mine = jnp.where(first, ref[:shard], ref[shard:rows])
        theirs = came[:shard, at : at + size]
        pair.append([jnp.where(first, mine, theirs), jnp.where(first, theirs, mine)])
    for j in range(4):
        for side in (0, 1):
            at = (2 * j + side) * unit
            g_up[:, at : at + unit] = pair[0][side][:, j * unit : (j + 1) * unit].astype(f32)
    cols = heads * hd
    g_qkv[...] = jnp.concatenate(
        [
            pair[1][h & 1][:, t * cols + (h >> 1) * hd : t * cols + ((h >> 1) + 1) * hd]
            for h in range(2 * heads)
            for t in range(3)
        ],
        axis=1,
    ).astype(f32)
    g_rel[...] = jnp.concatenate(
        [
            pair[1][h & 1][:, 3 * cols + (h >> 1) * hd : 3 * cols + ((h >> 1) + 1) * hd]
            for h in range(2 * heads)
        ],
        axis=1,
    ).astype(f32)
    own = [ref[rows : rows + 1].astype(f32) for ref in (up_ref, late_ref)]
    both = [own[0] + came[shard : shard + 1, :size].astype(f32), own[1] + came[shard : shard + 1, size:].astype(f32)]
    odd_chip = meta[CHIP] & 1 == 0
    vec_ref[...] = jnp.zeros_like(vec_ref)
    picks = [(both[1], 0, first), (both[1], 1, first), (own[1], 2, odd_chip), (own[1], 3, odd_chip)]
    picks += [(both[0], 0, first), (both[0], 1, first), (both[0], 2, first)]
    for row, (source, at, low) in enumerate(picks):
        piece = source[:, at * rows : (at + 1) * rows]
        vec_ref[row : row + 1, :shard] = jnp.where(low, piece[:, :shard], piece[:, shard:])
    vec_ref[7:8, :] = own[0][:, 3 * rows : 3 * rows + unit]


def place_body(meta, y0, y1, x0, x1, y_ref, x_ref):
    high = meta[RANK] >> 1 == 1
    y_ref[0] = jnp.where(high, y1[...], y0[...])
    y_ref[1] = jnp.where(high, y0[...], y1[...])
    x_ref[0] = jnp.where(high, x1[...], x0[...]).astype(f32)
    x_ref[1] = jnp.where(high, x0[...], x1[...]).astype(f32)


def slot_split_device(
    layer_input,
    lengths,
    ln1_gain,
    ln1_bias,
    w_qkv,
    w_rel,
    bias_u,
    bias_v,
    w_out,
    ln2_gain,
    ln2_bias,
    w_up,
    up_bias,
    w_down,
    down_bias,
    grad_out,
):
    slots, block, width = layer_input.shape
    rank, device = lax.axis_index("seq"), lax.axis_index("fsdp")
    core, chip = device & 1, device >> 1
    full, heads = 4 * block, H // 2
    cols, shard, unit = heads * HEAD_DIM, width // 8, up_bias.shape[0]
    mine_ff = 4 * unit

    x_own = to_slots(layer_input, rank)
    where = jnp.stack([core, chip, rank, rank]).astype(jnp.int32)
    vectors = (ln1_gain, ln1_bias, bias_u, bias_v, ln2_gain, ln2_bias, down_bias, up_bias)
    attn_rows, fold = shard + 8, shard // 2
    attn_pack, feed_pack, pack_send = kernel_call(
        pack_body,
        "pack",
        where,
        [w_qkv, w_rel, w_up, w_out, w_down] + [v.reshape(-1, min(128, v.size)) for v in vectors],
        [((attn_rows, 4 * cols), bf), ((3 * shard + fold, 4 * cols), bf), ((attn_rows + shard + fold, 4 * cols), bf)],
    )
    pack_came = swap_core(pack_send)
    attn_pack = jnp.concatenate([attn_pack, pack_came[:attn_rows]], axis=0)
    both = swap_core(lengths)
    length = jnp.where(core == rank >> 1, lengths, both)
    length = jnp.where(rank & 1 == 0, length[0], length[1])
    meta = jnp.stack([core, chip, rank, length]).astype(jnp.int32)
    length_arr = length.reshape(1)

    steps = (full - 1 - lax.iota(jnp.int32, full)).astype(f32)
    attn_pack, steps = together(attn_pack, steps)
    attn_packs = [attn_pack] + [swap_chip(attn_pack, k) for k in (1, 2, 3)]
    grad_out, *x_own = together(grad_out, *x_own)
    grad_own = to_slots(grad_out, rank)
    inv_freq = jnp.exp(lax.iota(f32, width // 2) * (-2.0 * math.log(10000.0) / width))
    angles = steps[:, None] * inv_freq[None, :]
    table = jnp.concatenate([jnp.sin(angles), jnp.cos(angles)], axis=1).astype(bf)

    x_other = [swap_core(x) for x in x_own]
    by_step = lambda width: pl.BlockSpec((block, width), lambda i, _: (i, 0))
    qkv, h1, x_slot, rel, w_own, vecs, up_b, biases = kernel_call(
        project_body,
        "project",
        where,
        attn_packs + x_own + x_other + [table],
        [((full, 3 * cols), bf), ((full, width), bf), ((full, width), bf), ((full, cols), bf)]
        + [((width, 4 * cols), bf), ((8, width), f32), ((1, mine_ff), f32), ((2, cols), f32)],
        grid=(4,),
        in_specs=[whole(2 * attn_rows, 4 * cols)] * 4 + [whole(block, width)] * 4 + [by_step(width)],
        out_specs=[by_step(3 * cols), by_step(width), by_step(width), by_step(cols)]
        + [whole(width, 4 * cols), whole(8, width), whole(1, mine_ff), whole(2, cols)],
        flops=2 * full * width * 4 * cols,
    )
    own_u, own_v = biases[0:1], biases[1:2]
    qkv, *grad_own = together(qkv, *grad_own)
    attn, lse = attn_fwd(length_arr, qkv, rel, own_u, own_v)

    feed_pack = jnp.concatenate([feed_pack, pack_came[attn_rows:]], axis=0)
    feed_pack, *_ = together(feed_pack, *attn_packs)
    feed_packs = [swap_chip(feed_pack, k) for k in (1, 2, 3)]
    grad_other = [swap_core(g) for g in grad_own]
    attn, *rest = together(attn, *feed_packs, *grad_other)
    feed_packs, grad_other = [feed_pack] + rest[:3], rest[3:]

    attn_other = swap_core(attn)
    kept = lambda width: pl.BlockSpec((block, width), lambda i, _: (i >> 1, 0))
    half = full // 2
    g, df, h2, dy, y1, y_keep, dh_keep, dh_send, y_send, early, wo_mine = kernel_call(
        feed_body,
        "feed",
        meta,
        feed_packs + grad_own + grad_other + [x_slot, attn, attn_other, vecs, up_b],
        [((full, mine_ff), bf)] * 2 + [((full, width), bf)] * 2
        + [((full, width), f32), ((half, width), f32), ((full, width), f32), ((full, width), bf)]
        + [((half, width), bf), ((8, mine_ff), f32), ((cols, width), bf)],
        grid=(4,),
        in_specs=[whole(*feed_pack.shape)] * 4 + [whole(block, width)] * 4
        + [by_step(width), by_step(cols), by_step(cols), whole(8, width), whole(1, mine_ff)],
        out_specs=[by_step(mine_ff)] * 2 + [by_step(width)] * 3 + [kept(width)] + [by_step(width)] * 2
        + [kept(width), whole(8, mine_ff), whole(cols, width)],
        scratch=[
            pltpu.VMEM((width, mine_ff), bf),
            pltpu.VMEM((mine_ff, width), bf),
            pltpu.VMEM((cols, width), bf),
        ],
        flops=8 * full * width * mine_ff,
    )
    dh_came = swap_core(dh_send)
    y_came = swap_core(y_send)
    by_chip = lambda rows, size: pl.BlockSpec((rows, size), lambda k, m: (0, m[CHIP] ^ k))
    blocks = lambda rows: [((rows, 2 * width), f32)] + [((rows, 2 * width), bf)] * 3
    early_parts = kernel_call(
        feed_grad_body,
        "feed_grad",
        meta,
        [h2, df, early, g, dy],
        blocks(2 * shard + 16 + unit // 2),
        grid=(4,),
        in_specs=[by_chip(full, 2 * shard), whole(full, mine_ff), whole(8, mine_ff)]
        + [by_chip(full, unit), whole(full, width)],
        flops=4 * full * width * mine_ff,
    )
    out0, out1, g_resid, d_attn, g_out = kernel_call(
        norm_two_body,
        "norm_two",
        meta,
        [y1, dh_keep, dh_came, dy, vecs, y_keep, y_came, wo_mine, attn],
        [((block, width), bf)] * 2 + [((half, width), f32), ((full, cols), bf), ((cols, width), f32)],
        grid=(4,),
        in_specs=[by_step(width)] * 4 + [whole(8, width)] + [kept(width)] * 2 + [whole(cols, width), by_step(cols)],
        out_specs=[whole(block, width)] * 2 + [kept(width), by_step(cols), whole(cols, width)],
        flops=4 * full * width * cols,
    )
    y_turns = [
        lax.ppermute(out, ("fsdp", "seq"), [(b, a) for a, b in slot_pairs(turn)])
        for turn, out in enumerate((out0, out1))
    ]
    back = lambda pair: attn_bwd(length_arr, qkv, rel, own_u, own_v, lse, d_attn, pair=pair)
    early_came = [swap_chip(early_parts[k], k) for k in (1, 2, 3)]
    *first_pair, y0, y1, e1, e2, e3 = together(*back(0), *y_turns, *early_came)
    y_turns = [y0, y1]
    early_keep, early_send = chip_sum(meta, [early_parts[0], e1, e2, e3], "early_chips")
    d_attn, early_send, lse = together(d_attn, early_send, lse)
    *second_pair, early_came = together(*back(1), swap_seq(early_send, 1))
    q0, k0, v0, r0, u0, b0 = first_pair
    q1, k1, v1, r1, u1, b1 = second_pair
    early_pair = (early_keep + early_came.astype(f32)).astype(bf)
    early_pair, q1 = together(early_pair, q1)
    early_came = swap_seq(early_pair, 2)
    rows = 2 * shard + 16
    pair_step = pl.BlockSpec((block, 2 * HEAD_DIM), lambda i, _: (i, 0))
    dh1_keep, dh1_send, *late_parts = kernel_call(
        qkv_back_body,
        "qkv_back",
        meta,
        [q0, q1, k0, k1, v0, v1, r0, r1, w_own, x_slot, h1, table]
        + [jnp.concatenate([u0, u1], axis=1), jnp.concatenate([b0, b1], axis=1), g_out],
        [((half, width), f32), ((half, width), bf)] + blocks(rows + fold),
        grid=(4,),
        in_specs=[pair_step] * 8 + [whole(width, 4 * cols)] + [by_step(width)] * 3
        + [whole(1, cols), whole(1, cols), whole(cols, width)],
        out_specs=[kept(width)] * 2 + [whole(rows + fold, 2 * width)] * 4,
        scratch=[pltpu.VMEM((width, 4 * cols), f32), pltpu.VMEM((8, width), f32)],
        flops=14 * full * width * cols,
    )
    late_came = [swap_chip(late_parts[k], k) for k in (1, 2, 3)]
    dh1_came = swap_core(dh1_send)
    dh1_came, early_came = together(dh1_came, early_came)
    early_mine = (early_pair.astype(f32) + early_came.astype(f32)).astype(bf)
    early_other = swap_seq(early_mine, 1)
    by_half = pl.BlockSpec((block, width), lambda i, _: (i, 0))
    own_rows = pl.BlockSpec((block, width), lambda i, m: (2 * i + m[CORE], 0))
    x0, x1 = kernel_call(
        norm_one_body,
        "norm_one",
        meta,
        [x_slot, dh1_keep, dh1_came, g_resid, vecs],
        [((block, width), bf)] * 2,
        grid=(2,),
        in_specs=[own_rows] + [by_half] * 3 + [whole(8, width)],
        out_specs=[whole(block, width)] * 2,
    )
    *late_came, x0, x1, early_other = together(*late_came, x0, x1, early_other)
    x_turns = [
        lax.ppermute(out, ("fsdp", "seq"), [(b, a) for a, b in slot_pairs(turn)])
        for turn, out in enumerate((x0, x1))
    ]
    late_keep, late_send = chip_sum(meta, [late_parts[0]] + late_came, "late_chips")
    g_up_rows, g_down = kernel_call(
        early_out_body,
        "early_out",
        meta,
        [early_mine, early_other],
        [((rows, 2 * width), bf), ((unit, width), f32)],
    )
    late_pair = (late_keep + swap_seq(late_send, 1).astype(f32)).astype(bf)
    late_came, g_up_rows, g_down, *x_turns = together(swap_seq(late_pair, 2), g_up_rows, g_down, *x_turns)
    late_mine = (late_pair.astype(f32) + late_came.astype(f32)).astype(bf)
    output, grad_x = kernel_call(
        place_body,
        "place",
        meta,
        y_turns + x_turns,
        [((2, block, width), bf), ((2, block, width), f32)],
    )
    late_other, output, grad_x = together(swap_seq(late_mine, 1), output, grad_x)
    late, g_w_out, send = kernel_call(
        late_pack_body,
        "late_pack",
        meta,
        [g_up_rows, late_mine, late_other],
        [((rows, 2 * width), bf), ((shard, width), f32), ((shard + 8, 4 * width), bf)],
    )
    g_up, g_qkv, g_rel, vecs = kernel_call(
        late_out_body,
        "late_out",
        meta,
        [g_up_rows, late, swap_core(send)],
        [((shard, 2 * mine_ff), f32), ((shard, 6 * cols), f32), ((shard, 2 * cols), f32), ((8, unit), f32)],
    )
    small = lambda row: vecs[row, :shard]
    return (
        output,
        grad_x,
        small(0),
        small(1),
        g_qkv,
        g_rel,
        small(2),
        small(3),
        g_w_out,
        small(4),
        small(5),
        g_up,
        vecs[7],
        g_down,
        small(6),
    )


def per_device(*args):
    one_slot_a_chip = lax.axis_size("fsdp") == 8 and lax.axis_size("seq") == 4
    if one_slot_a_chip and args[0].shape[0] == 2:
        return slot_split_device(*args)
    return head_split_device(*args)


def solution(mesh):
    placed = (
        P("fsdp", "seq", None),
        P("fsdp"),
        P("fsdp"),
        P("fsdp"),
        P("fsdp", None),
        P("fsdp", None),
        P("fsdp"),
        P("fsdp"),
        P("fsdp", None),
        P("fsdp"),
        P("fsdp"),
        P("fsdp", None),
        P("fsdp"),
        P("fsdp", None),
        P("fsdp"),
        P("fsdp", "seq", None),
    )
    return jax.shard_map(
        per_device,
        mesh=mesh,
        in_specs=placed,
        out_specs=(
            P("fsdp", "seq", None),
            P("fsdp", "seq", None),
            P("fsdp"),
            P("fsdp"),
            P("fsdp", None),
            P("fsdp", None),
            P("fsdp"),
            P("fsdp"),
            P("fsdp", None),
            P("fsdp"),
            P("fsdp"),
            P("fsdp", None),
            P("fsdp"),
            P("fsdp", None),
            P("fsdp"),
        ),
        check_vma=False,
    )
```

```python
import functools
import math

import jax
import jax.numpy as jnp
from jax import lax
from jax.experimental import pallas as pl
from jax.experimental.pallas import tpu as pltpu
from jax.sharding import PartitionSpec as P

H = 8
HEAD_DIM = 64


NEG_FILL = -1e30
NORM_EPS = 1e-05


bf, f32 = jnp.bfloat16, jnp.float32
NEG = NEG_FILL
HD = HEAD_DIM
NT = (((1,), (1,)), ((), ()))
NN = (((1,), (0,)), ((), ()))


def dot(a, b, dims):
    return lax.dot_general(a, b, dims, preferred_element_type=f32)


def masked_tail(s, keep, block):
    tail = jnp.where(keep, s[:, s.shape[1] - block :], NEG)
    if s.shape[1] == block:
        return tail
    return jnp.concatenate([s[:, : s.shape[1] - block], tail], axis=1)


def scores(qu, qv, keys, rel_rev, keep, block):
    span = keys.shape[0]
    rel = dot(qv, rel_rev, NT)
    rel = pltpu.roll(rel, (span - block + 1) % span, 1, stride=1, stride_axis=0)
    return masked_tail(dot(qu, keys, NT) + rel, keep, block)


def attn_fwd_body(len_ref, q_ref, k_ref, v_ref, r_ref, bu_ref, bv_ref, o_ref, lse_ref, *, block):
    full = q_ref.shape[0]
    lane = lax.broadcasted_iota(jnp.int32, (block, 2 * HD), 1)
    sides = (lane < HD, lane >= HD)
    length = len_ref[0]
    col = lax.broadcasted_iota(jnp.int32, (1, full), 1)
    bias = jnp.where(col < length, 0.0, NEG)
    tri = lax.broadcasted_iota(jnp.int32, (block, block), 1) <= lax.broadcasted_iota(
        jnp.int32, (block, block), 0
    )
    for first in range(0, full, block):
        span = first + block
        q = q_ref[first:span, :].astype(f32)
        qu = (q + bu_ref[...]).astype(bf).astype(f32) * 0.125
        qv = (q + bv_ref[...]).astype(bf).astype(f32) * 0.125
        outs = []
        for head, side in enumerate(sides):
            s = scores(
                jnp.where(side, qu, 0.0).astype(bf),
                jnp.where(side, qv, 0.0).astype(bf),
                k_ref[:span, :],
                r_ref[full - span :, :],
                tri,
                block,
            )
            s = s + bias[:, :span]
            top = jnp.max(s, axis=1, keepdims=True)
            e = jnp.exp(s - top)
            total = jnp.sum(e, axis=1, keepdims=True)
            outs.append(dot(e.astype(bf), v_ref[:span, :], NN) / total)
            lse_ref[head, first:span, :] = top + jnp.log(total)
        o_ref[first:span, :] = jnp.where(sides[0], outs[0], outs[1]).astype(bf)


def attn_fwd(length, qkv, rel_rev, bias_u, bias_v, *, block=256):
    full, cols = rel_rev.shape
    pairs = cols // (2 * HD)
    at = lambda part: pl.BlockSpec((full, 2 * HD), lambda pair, _: (0, part * pairs + pair))
    row = pl.BlockSpec((1, 2 * HD), lambda pair, _: (0, pair))
    return pl.pallas_call(
        functools.partial(attn_fwd_body, block=block),
        out_shape=(
            jax.ShapeDtypeStruct((full, cols), bf),
            jax.ShapeDtypeStruct((2 * pairs, full, 1), f32),
        ),
        grid_spec=pltpu.PrefetchScalarGridSpec(
            num_scalar_prefetch=1,
            grid=(pairs,),
            in_specs=[at(0), at(1), at(2), at(0), row, row],
            out_specs=(at(0), pl.BlockSpec((2, full, 1), lambda pair, _: (pair, 0, 0))),
        ),
        cost_estimate=pl.CostEstimate(flops=0, bytes_accessed=0, transcendentals=0),
        compiler_params=pltpu.CompilerParams(vmem_limit_bytes=32 << 20),
        name="attn_fwd",
    )(length, qkv, qkv, qkv, rel_rev, bias_u, bias_v)


def attn_bwd_body(len_ref, q_ref, k_ref, v_ref, r_ref, bu_ref, bv_ref, lse_ref, do_ref, *refs, block):
    dq_ref, dk_ref, dv_ref, dr_ref, gu_ref, gv_ref, dk_t, dv_t, dr_t = refs
    full = q_ref.shape[0]
    length = len_ref[0]
    lane = lax.broadcasted_iota(jnp.int32, (block, 2 * HD), 1)
    sides = (lane < HD, lane >= HD)
    rows = lax.broadcasted_iota(jnp.int32, (block, block), 0)
    cols = lax.broadcasted_iota(jnp.int32, (block, block), 1)
    tri = cols <= rows
    flip = jnp.where(rows + cols == block - 1, 1.0, 0.0).astype(bf)
    row = lax.broadcasted_iota(jnp.int32, (block, 1), 0)
    for ref in (dk_t, dv_t, dr_t, dq_ref, gu_ref, gv_ref):
        ref[...] = jnp.zeros_like(ref)
    for first in range(0, full, block):
        span = first + block

        @pl.when(first < length)
        def _():
            q = q_ref[first:span, :].astype(f32)
            qu = (q + bu_ref[...]).astype(bf).astype(f32) * 0.125
            qv = (q + bv_ref[...]).astype(bf).astype(f32) * 0.125
            do = do_ref[first:span, :].astype(f32)
            qu_t = jnp.transpose(qu).astype(bf)
            do_t = jnp.transpose(do).astype(bf)
            qv_t = jnp.transpose(dot(flip, qv.astype(bf), NN)).astype(bf)
            dqu, dqv = [], []
            for head, side in enumerate(sides):
                at = slice(head * HD, (head + 1) * HD)
                s = scores(
                    jnp.where(side, qu, 0.0).astype(bf),
                    jnp.where(side, qv, 0.0).astype(bf),
                    k_ref[:span, :],
                    r_ref[full - span :, :],
                    tri,
                    block,
                )
                lse = jnp.where(first + row < length, lse_ref[head, first:span, :], -NEG)
                p = jnp.exp(s - lse)
                dp = dot(jnp.where(side, do, 0.0).astype(bf), v_ref[:span, :], NT)
                t = p * dp
                ds = (t - p * jnp.sum(t, axis=1, keepdims=True)).astype(bf)
                dv_t[at, :span] += dot(do_t[at], p.astype(bf), NN)
                both = dot(jnp.concatenate([qu_t[at], flip], axis=0), ds, NN)
                dk_t[at, :span] += both[:HD]
                dqu.append(dot(ds, k_ref[:span, :], NN))
                ds_rev = pltpu.roll(both[HD:], 0, 1, stride=1, stride_axis=0).astype(bf)
                dr_t[at, full - span :] += dot(qv_t[at], ds_rev, NN)
                dqv.append(dot(ds_rev, r_ref[full - span :, :], NN))
            dqu = jnp.where(sides[0], dqu[0], dqu[1]) * 0.125
            dqv = jnp.where(sides[0], dqv[0], dqv[1]) * 0.125
            gu_ref[...] += jnp.sum(dqu, axis=0, keepdims=True)
            gv_ref[...] += jnp.sum(dqv, axis=0, keepdims=True)
            dq_ref[first:span, :] = (dqu + dot(flip, dqv.astype(bf), NN)).astype(bf)

    dk_ref[...] = jnp.transpose(dk_t[...]).astype(bf)
    dv_ref[...] = jnp.transpose(dv_t[...]).astype(bf)
    dr_ref[...] = jnp.transpose(dr_t[...]).astype(bf)


def attn_bwd(length, qkv, rel_rev, bias_u, bias_v, lse, d_out, *, pair, block=256):
    full, cols = rel_rev.shape
    pairs = cols // (2 * HD)
    at = lambda part: pl.BlockSpec((full, 2 * HD), lambda i, _: (0, part * pairs + pair))
    row = pl.BlockSpec((1, 2 * HD), lambda i, _: (0, pair))
    out = pl.BlockSpec((full, 2 * HD), lambda i, _: (0, 0))
    out_row = pl.BlockSpec((1, 2 * HD), lambda i, _: (0, 0))
    return pl.pallas_call(
        functools.partial(attn_bwd_body, block=block),
        out_shape=(jax.ShapeDtypeStruct((full, 2 * HD), bf),) * 4
        + (jax.ShapeDtypeStruct((1, 2 * HD), f32),) * 2,
        grid_spec=pltpu.PrefetchScalarGridSpec(
            num_scalar_prefetch=1,
            grid=(1,),
            in_specs=[at(0), at(1), at(2), at(0), row, row]
            + [pl.BlockSpec((2, full, 1), lambda i, _: (pair, 0, 0)), at(0)],
            out_specs=(out,) * 4 + (out_row, out_row),
            scratch_shapes=[pltpu.VMEM((2 * HD, full), f32)] * 3,
        ),
        cost_estimate=pl.CostEstimate(flops=0, bytes_accessed=0, transcendentals=0),
        compiler_params=pltpu.CompilerParams(vmem_limit_bytes=32 << 20),
        name="attn_bwd",
    )(length, qkv, qkv, qkv, rel_rev, bias_u, bias_v, lse, d_out)


def norm_parts(values):
    mean_val = jnp.mean(values, axis=-1, keepdims=True)
    centered = values - mean_val
    inv_std = lax.rsqrt(jnp.mean(centered * centered, axis=-1, keepdims=True) + NORM_EPS)
    return (centered * inv_std, inv_std)


def norm_back(grad_norm, x_hat, inv_std):
    first_mean = jnp.mean(grad_norm, axis=-1, keepdims=True)
    second_mean = jnp.mean(grad_norm * x_hat, axis=-1, keepdims=True)
    return inv_std * (grad_norm - first_mean - x_hat * second_mean)


def position_table(count_rows, feature_count):
    steps = lax.iota(jnp.float32, count_rows)
    half_count = feature_count // 2
    inv_freq = jnp.exp(
        lax.iota(jnp.float32, half_count) * (-2.0 * math.log(10000.0) / feature_count)
    )
    angles = steps[:, None] * inv_freq[None, :]
    return jnp.concatenate([jnp.sin(angles), jnp.cos(angles)], axis=1)


def skew_rows(matrix):
    leading = matrix.shape[:-2]
    row_count, col_count = matrix.shape[-2:]
    flattened = matrix.reshape(leading + (row_count * col_count,))
    picked = flattened[..., row_count - 1 : row_count - 1 + row_count * (col_count - 1)]
    return picked.reshape(leading + (row_count, col_count - 1))[..., : col_count - row_count]


def unskew_rows(matrix):
    leading = matrix.shape[:-2]
    row_count, key_count = matrix.shape[-2:]
    axis_pos = len(leading)
    widened = jnp.pad(matrix, [(0, 0)] * axis_pos + [(0, 0), (0, row_count - 1)])
    flattened = widened.reshape(leading + (row_count * (key_count + row_count - 1),))
    flattened = jnp.pad(flattened, [(0, 0)] * axis_pos + [(row_count - 1, 1)])
    return flattened.reshape(leading + (row_count, key_count + row_count))


def head_split_device(
    layer_input,
    lengths,
    ln1_gain,
    ln1_bias,
    w_qkv,
    w_rel,
    bias_u,
    bias_v,
    w_out,
    ln2_gain,
    ln2_bias,
    w_up,
    up_bias,
    w_down,
    down_bias,
    grad_out,
):
    weights = (
        lax.all_gather(ln1_gain, "fsdp", axis=0, tiled=True),
        lax.all_gather(ln1_bias, "fsdp", axis=0, tiled=True),
        lax.all_gather(w_qkv, "fsdp", axis=0, tiled=True),
        lax.all_gather(w_rel, "fsdp", axis=0, tiled=True),
        lax.all_gather(bias_u, "fsdp", axis=0, tiled=True),
        lax.all_gather(bias_v, "fsdp", axis=0, tiled=True),
        lax.all_gather(w_out, "fsdp", axis=0, tiled=True),
        lax.all_gather(ln2_gain, "fsdp", axis=0, tiled=True),
        lax.all_gather(ln2_bias, "fsdp", axis=0, tiled=True),
        lax.all_gather(w_up, "fsdp", axis=0, tiled=True),
        lax.all_gather(up_bias, "fsdp", axis=0, tiled=True),
        lax.all_gather(w_down, "fsdp", axis=0, tiled=True),
        lax.all_gather(down_bias, "fsdp", axis=0, tiled=True),
    )
    (
        gain_one,
        shift_one,
        query_key_value_matrix,
        rel_weight,
        first_bias,
        second_bias,
        output_matrix,
        gain_two,
        shift_two,
        up_matrix,
        up_shift,
        down_matrix,
        down_shift,
    ) = weights
    gain_one = gain_one.astype(jnp.float32)
    shift_one = shift_one.astype(jnp.float32)
    gain_two = gain_two.astype(jnp.float32)
    shift_two = shift_two.astype(jnp.float32)
    up_shift = up_shift.astype(jnp.float32)
    down_shift = down_shift.astype(jnp.float32)
    slots, block_len, width = layer_input.shape
    seq_count = lax.axis_size("seq")
    seq_rank = lax.axis_index("seq")
    head_dim = HEAD_DIM
    group = H // seq_count
    full_len = block_len * seq_count
    score_scale = 1.0 / math.sqrt(head_dim)
    q_block = 512
    num_blocks = full_len // q_block
    win_len = full_len + q_block
    x_float = layer_input.astype(jnp.float32)
    x_hat_one, inv_std_one = norm_parts(x_float)
    first_normalized = (x_hat_one * gain_one + shift_one).astype(jnp.bfloat16)
    qkv_local = jnp.einsum(
        "mcr,rk->mck", first_normalized, query_key_value_matrix, preferred_element_type=jnp.float32
    ).astype(jnp.bfloat16)
    qkv_heads = lax.all_to_all(qkv_local, "seq", split_axis=2, concat_axis=1, tiled=True)
    qkv_heads = qkv_heads.reshape(slots, full_len, group, 3, head_dim)
    queries = qkv_heads[:, :, :, 0]
    keys = qkv_heads[:, :, :, 1]
    values = qkv_heads[:, :, :, 2]
    head_start = seq_rank * group
    head_bias_u = lax.dynamic_slice_in_dim(
        first_bias.astype(jnp.float32).reshape(H, head_dim), head_start, group, 0
    )
    head_bias_v = lax.dynamic_slice_in_dim(
        second_bias.astype(jnp.float32).reshape(H, head_dim), head_start, group, 0
    )
    query_u = (queries.astype(jnp.float32) + head_bias_u).astype(jnp.bfloat16)
    query_v = (queries.astype(jnp.float32) + head_bias_v).astype(jnp.bfloat16)
    table_rev = position_table(full_len, width).astype(jnp.bfloat16)[::-1]
    rel_cols = lax.dynamic_slice_in_dim(rel_weight, head_start * head_dim, group * head_dim, 1)
    rel_rev = jnp.dot(table_rev, rel_cols, preferred_element_type=jnp.float32).astype(jnp.bfloat16)
    rel_ext = jnp.concatenate([rel_rev, jnp.zeros_like(rel_rev)], axis=0).reshape(
        2 * full_len, group, head_dim
    )
    col_ids = lax.iota(jnp.int32, full_len)

    def scores_block(first_row):
        qu_part = lax.dynamic_slice_in_dim(query_u, first_row, q_block, 1)
        qv_part = lax.dynamic_slice_in_dim(query_v, first_row, q_block, 1)
        window_start = full_len - q_block - first_row
        rel_win = lax.dynamic_slice_in_dim(rel_ext, window_start, win_len, 0)
        content = jnp.einsum("sqhe,skhe->shqk", qu_part, keys, preferred_element_type=jnp.float32)
        rel_raw = jnp.einsum("sqhe,the->shqt", qv_part, rel_win, preferred_element_type=jnp.float32)
        rel_part = skew_rows(rel_raw)
        row_ids = first_row + lax.iota(jnp.int32, q_block)
        causal = col_ids[None, :] <= row_ids[:, None]
        inside = col_ids[None, :] < lengths[:, None]
        allowed = causal[None, None, :, :] & inside[:, None, None, :]
        scores = jnp.where(allowed, (content + rel_part) * score_scale, NEG_FILL)
        return (scores, qu_part, qv_part, rel_win, window_start)

    def forward_block(block_index):
        first_row = block_index * q_block
        scores, qu_part, qv_part, rel_win, window_start = scores_block(first_row)
        top = jnp.max(scores, axis=-1, keepdims=True)
        expo = jnp.exp(scores - top)
        total = jnp.sum(expo, axis=-1, keepdims=True)
        probs = (expo / total).astype(jnp.bfloat16)
        out_part = jnp.einsum(
            "shqk,skhe->sqhe", probs, values, preferred_element_type=jnp.float32
        ).astype(jnp.bfloat16)
        return (out_part, top[..., 0] + jnp.log(total[..., 0]))

    block_outs, block_lse = lax.map(forward_block, jnp.arange(num_blocks, dtype=jnp.int32))
    attn_heads = jnp.moveaxis(block_outs, 0, 1).reshape(slots, full_len, group * head_dim)
    attention_sequence = lax.all_to_all(attn_heads, "seq", split_axis=1, concat_axis=2, tiled=True)
    attention_projected = jnp.einsum(
        "mcr,rk->mck", attention_sequence, output_matrix, preferred_element_type=jnp.float32
    )
    resid = x_float + attention_projected
    x_hat_two, inv_std_two = norm_parts(resid)
    second_normalized = (x_hat_two * gain_two + shift_two).astype(jnp.bfloat16)
    pre_act = (
        jnp.einsum("oka,ac->okc", second_normalized, up_matrix, preferred_element_type=jnp.float32)
        + up_shift
    )
    normal_cdf = 0.5 * (1.0 + lax.erf(pre_act * (1.0 / math.sqrt(2.0))))
    hidden_state = (pre_act * normal_cdf).astype(jnp.bfloat16)
    down_proj = (
        jnp.einsum("zcp,pr->zcr", hidden_state, down_matrix, preferred_element_type=jnp.float32)
        + down_shift
    )
    output = (resid + down_proj).astype(jnp.bfloat16)
    positions = seq_rank * block_len + lax.iota(jnp.int32, block_len)
    live = (positions[None, :] < lengths[:, None]).astype(jnp.bfloat16)
    result_gradient = grad_out * live[:, :, None]
    grad_y_float = result_gradient.astype(jnp.float32)
    g_down_shift = jnp.sum(grad_y_float, axis=(0, 1))
    down_gradient = jnp.einsum(
        "hki,hku->iu", hidden_state, result_gradient, preferred_element_type=jnp.float32
    )
    hidden_gradient = jnp.einsum(
        "gvu,ju->gvj", result_gradient, down_matrix, preferred_element_type=jnp.float32
    )
    deriv = normal_cdf + pre_act * jnp.exp(-0.5 * pre_act * pre_act) * (
        1.0 / math.sqrt(2.0 * math.pi)
    )
    preactivation_gradient = (hidden_gradient * deriv).astype(jnp.bfloat16)
    g_up_shift = jnp.sum(preactivation_gradient.astype(jnp.float32), axis=(0, 1))
    up_gradient = jnp.einsum(
        "oiz,oix->zx", second_normalized, preactivation_gradient, preferred_element_type=jnp.float32
    )
    second_norm_gradient = jnp.einsum(
        "rau,ku->rak", preactivation_gradient, up_matrix, preferred_element_type=jnp.float32
    )
    g_gain_two = jnp.sum(second_norm_gradient * x_hat_two, axis=(0, 1))
    g_shift_two = jnp.sum(second_norm_gradient, axis=(0, 1))
    g_resid = grad_y_float + norm_back(second_norm_gradient * gain_two, x_hat_two, inv_std_two)
    attention_gradient = g_resid.astype(jnp.bfloat16)
    output_gradient = jnp.einsum(
        "zau,zam->um", attention_sequence, attention_gradient, preferred_element_type=jnp.float32
    )
    g_attn_seq = jnp.einsum(
        "urz,jz->urj", attention_gradient, output_matrix, preferred_element_type=jnp.float32
    ).astype(jnp.bfloat16)
    g_attn_heads = lax.all_to_all(
        g_attn_seq, "seq", split_axis=2, concat_axis=1, tiled=True
    ).reshape(slots, full_len, group, head_dim)

    def backward_block(carry, block_index):
        g_keys, g_vals, g_ext = carry
        first_row = block_index * q_block
        scores, qu_part, qv_part, rel_win, window_start = scores_block(first_row)
        probs = jnp.exp(scores - block_lse[block_index][..., None])
        d_out = lax.dynamic_slice_in_dim(g_attn_heads, first_row, q_block, 1)
        g_vals = g_vals + jnp.einsum(
            "shqk,sqhe->skhe", probs.astype(jnp.bfloat16), d_out, preferred_element_type=jnp.float32
        )
        g_probs = jnp.einsum("sqhe,skhe->shqk", d_out, values, preferred_element_type=jnp.float32)
        inner = jnp.sum(probs * g_probs, axis=-1, keepdims=True)
        g_scores = (probs * (g_probs - inner)).astype(jnp.bfloat16)
        g_qu = (
            jnp.einsum("shqk,skhe->sqhe", g_scores, keys, preferred_element_type=jnp.float32)
            * score_scale
        )
        g_keys = (
            g_keys
            + jnp.einsum("shqk,sqhe->skhe", g_scores, qu_part, preferred_element_type=jnp.float32)
            * score_scale
        )
        g_wide = unskew_rows(g_scores)
        g_qv = (
            jnp.einsum("shqt,the->sqhe", g_wide, rel_win, preferred_element_type=jnp.float32)
            * score_scale
        )
        g_win = (
            jnp.einsum("shqt,sqhe->sthe", g_wide, qv_part, preferred_element_type=jnp.float32)
            * score_scale
        )
        g_old = lax.dynamic_slice_in_dim(g_ext, window_start, win_len, 1)
        g_ext = lax.dynamic_update_slice_in_dim(g_ext, g_old + g_win, window_start, 1)
        return ((g_keys, g_vals, g_ext), (g_qu, g_qv))

    zero_heads = jnp.zeros((slots, full_len, group, head_dim), jnp.float32)
    zero_ext = jnp.zeros((slots, 2 * full_len, group, head_dim), jnp.float32)
    (g_keys, g_vals, g_ext), (g_qu_blocks, g_qv_blocks) = lax.scan(
        backward_block, (zero_heads, zero_heads, zero_ext), jnp.arange(num_blocks, dtype=jnp.int32)
    )
    g_qu = jnp.moveaxis(g_qu_blocks, 0, 1).reshape(slots, full_len, group, head_dim)
    g_qv = jnp.moveaxis(g_qv_blocks, 0, 1).reshape(slots, full_len, group, head_dim)
    g_queries = g_qu + g_qv
    g_bias_u_heads = jnp.sum(g_qu, axis=(0, 1))
    g_bias_v_heads = jnp.sum(g_qv, axis=(0, 1))
    g_qkv_heads = (
        jnp.stack([g_queries, g_keys, g_vals], axis=3)
        .astype(jnp.bfloat16)
        .reshape(slots, full_len, group * 3 * head_dim)
    )
    query_key_value_gradient = lax.all_to_all(
        g_qkv_heads, "seq", split_axis=1, concat_axis=2, tiled=True
    )
    g_rel_low = g_ext[:, :full_len].astype(jnp.bfloat16)
    g_rel_heads = jnp.einsum(
        "td,sthe->dhe", table_rev, g_rel_low, preferred_element_type=jnp.float32
    ).reshape(width, group * head_dim)
    g_rel_weight = lax.dynamic_update_slice_in_dim(
        jnp.zeros((width, width), jnp.float32), g_rel_heads, head_start * head_dim, 1
    )
    g_bias_u = lax.dynamic_update_slice_in_dim(
        jnp.zeros((H, head_dim), jnp.float32), g_bias_u_heads, head_start, 0
    ).reshape(width)
    g_bias_v = lax.dynamic_update_slice_in_dim(
        jnp.zeros((H, head_dim), jnp.float32), g_bias_v_heads, head_start, 0
    ).reshape(width)
    query_key_value_weight_gradient = jnp.einsum(
        "zau,zam->um",
        first_normalized,
        query_key_value_gradient,
        preferred_element_type=jnp.float32,
    )
    first_norm_gradient = jnp.einsum(
        "urz,jz->urj",
        query_key_value_gradient,
        query_key_value_matrix,
        preferred_element_type=jnp.float32,
    )
    g_gain_one = jnp.sum(first_norm_gradient * x_hat_one, axis=(0, 1))
    g_shift_one = jnp.sum(first_norm_gradient, axis=(0, 1))
    g_input = g_resid + norm_back(first_norm_gradient * gain_one, x_hat_one, inv_std_one)
    partial_shards = (
        lax.psum_scatter(g_gain_one, "fsdp", scatter_dimension=0, tiled=True),
        lax.psum_scatter(g_shift_one, "fsdp", scatter_dimension=0, tiled=True),
        lax.psum_scatter(query_key_value_weight_gradient, "fsdp", scatter_dimension=0, tiled=True),
        lax.psum_scatter(g_rel_weight, "fsdp", scatter_dimension=0, tiled=True),
        lax.psum_scatter(g_bias_u, "fsdp", scatter_dimension=0, tiled=True),
        lax.psum_scatter(g_bias_v, "fsdp", scatter_dimension=0, tiled=True),
        lax.psum_scatter(output_gradient, "fsdp", scatter_dimension=0, tiled=True),
        lax.psum_scatter(g_gain_two, "fsdp", scatter_dimension=0, tiled=True),
        lax.psum_scatter(g_shift_two, "fsdp", scatter_dimension=0, tiled=True),
        lax.psum_scatter(up_gradient, "fsdp", scatter_dimension=0, tiled=True),
        lax.psum_scatter(g_up_shift, "fsdp", scatter_dimension=0, tiled=True),
        lax.psum_scatter(down_gradient, "fsdp", scatter_dimension=0, tiled=True),
        lax.psum_scatter(g_down_shift, "fsdp", scatter_dimension=0, tiled=True),
    )
    shards = lax.psum(
        (
            partial_shards[0],
            partial_shards[1],
            partial_shards[2],
            partial_shards[3],
            partial_shards[4],
            partial_shards[5],
            partial_shards[6],
            partial_shards[7],
            partial_shards[8],
            partial_shards[9],
            partial_shards[10],
            partial_shards[11],
            partial_shards[12],
        ),
        "seq",
    )
    return (
        output,
        g_input,
        shards[0],
        shards[1],
        shards[2],
        shards[3],
        shards[4],
        shards[5],
        shards[6],
        shards[7],
        shards[8],
        shards[9],
        shards[10],
        shards[11],
        shards[12],
    )


def swap_core(values):
    size = lax.axis_size("fsdp")
    return lax.ppermute(values, "fsdp", [(i, i ^ 1) for i in range(size)])


def swap_chip(values, mask):
    size = lax.axis_size("fsdp")
    return lax.ppermute(values, "fsdp", [(i, i ^ (2 * mask)) for i in range(size)])


def swap_axis(values, turn):
    size = lax.axis_size("fsdp")
    return lax.ppermute(values, "fsdp", [(i, i ^ (2 << ((i & 1) ^ turn))) for i in range(size)])


def swap_seq(values, mask):
    size = lax.axis_size("seq")
    return lax.ppermute(values, "seq", [(i, i ^ mask) for i in range(size)])


def slot_pairs(turn):
    seq, pairs = lax.axis_size("seq"), []
    for f in range(lax.axis_size("fsdp")):
        for z in range(seq):
            to_f, to_z = (f & ~1) | (z & 1), 2 * (f & 1) + (turn ^ (z >> 1))
            pairs.append((f * seq + z, to_f * seq + to_z))
    return pairs


def to_slots(values, seq_rank):
    return [
        lax.ppermute(
            lax.dynamic_index_in_dim(values, turn ^ (seq_rank >> 1), 0, keepdims=False),
            ("fsdp", "seq"),
            slot_pairs(turn),
        )
        for turn in (0, 1)
    ]


def together(*values):
    return lax.optimization_barrier(values)


def whole(*shape):
    return pl.BlockSpec(shape, lambda *_: (0,) * len(shape))


def kernel_call(body, name, meta, args, outs, *, grid=(1,), in_specs=None, out_specs=None, scratch=(), flops=0, vmem=32):
    in_specs = in_specs or [whole(*a.shape) for a in args]
    out_specs = out_specs or [whole(*shape) for shape, _ in outs]
    moved = sum(a.size * a.dtype.itemsize for a in args)
    moved += sum(math.prod(shape) * jnp.dtype(kind).itemsize for shape, kind in outs)
    return pl.pallas_call(
        body,
        out_shape=[jax.ShapeDtypeStruct(shape, kind) for shape, kind in outs],
        grid_spec=pltpu.PrefetchScalarGridSpec(
            num_scalar_prefetch=1,
            grid=grid,
            in_specs=in_specs,
            out_specs=out_specs,
            scratch_shapes=scratch,
        ),
        compiler_params=pltpu.CompilerParams(vmem_limit_bytes=vmem << 20),
        cost_estimate=pl.CostEstimate(flops=0, bytes_accessed=0, transcendentals=0),
        name=name,
    )(meta, *args)


TN = (((0,), (0,)), ((), ()))
CORE, CHIP, RANK, LIVE = range(4)
DIGIT = 128


def aligned(index, size):
    return pl.multiple_of(index * size, size)


def own_place():
    device = lax.axis_index("fsdp")
    return device & 1, device >> 1, lax.axis_index("seq")


def pack_body(lengths_ref, qkv_ref, rel_ref, up_ref, out_ref, down_ref, *refs):
    small, (attn_ref, feed_ref, send_ref) = refs[:8], refs[8:]
    core, _, _ = own_place()
    shard = qkv_ref.shape[0]
    qkv, rel, up, out, down = qkv_ref[...], rel_ref[...], up_ref[...], out_ref[...], down_ref[...]
    heads, hd = rel.shape[1] // HEAD_DIM // 2, HEAD_DIM
    unit = up.shape[1] // 8
    packs, ups = [], []
    row = jnp.concatenate([ref[i : i + 1] for ref in small for i in range(ref.shape[0])], axis=1)
    lane = lax.broadcasted_iota(jnp.int32, (1, 4 * heads * hd - row.shape[1]), 1)
    digits = jnp.zeros(lane.shape, f32)
    for slot in range(lengths_ref.shape[0]):
        high = lengths_ref[slot] // DIGIT
        for at, digit in ((2 * slot, high), (2 * slot + 1, lengths_ref[slot] - high * DIGIT)):
            digits = jnp.where(lane == at, digit.astype(f32), digits)
    row = jnp.concatenate([row, digits.astype(row.dtype)], axis=1)
    rows = jnp.broadcast_to(row, (8, row.shape[1]))
    for side in (0, 1):
        parts = [
            qkv[:, ((2 * j + side) * 3 + t) * hd : ((2 * j + side) * 3 + t + 1) * hd]
            for t in range(3)
            for j in range(heads)
        ]
        parts += [rel[:, (2 * j + side) * hd : (2 * j + side + 1) * hd] for j in range(heads)]
        packs.append(jnp.concatenate(parts, axis=1))
        ups.append(
            jnp.concatenate([up[:, (2 * j + side) * unit : (2 * j + side + 1) * unit] for j in range(4)], axis=1)
        )
    first = core == 0
    folded = jnp.concatenate([out[: shard // 2], out[shard // 2 :]], axis=1)
    attn_ref[:shard] = jnp.where(first, packs[0], packs[1])
    attn_ref[shard:] = rows
    send_ref[:shard] = jnp.where(first, packs[1], packs[0])
    send_ref[shard : shard + 8] = rows
    send_ref[shard + 8 : 2 * shard + 8] = jnp.where(first, ups[1], ups[0])
    send_ref[2 * shard + 8 :] = folded
    feed_ref[:shard] = jnp.where(first, ups[0], ups[1])
    feed_ref[shard : shard + shard // 2] = folded
    feed_ref[shard + shard // 2 :] = jnp.concatenate([down[: 2 * shard], down[2 * shard :]], axis=1)


def ordered(core, own, other):
    first = core == 0
    return jnp.concatenate([jnp.where(first, own, other), jnp.where(first, other, own)], axis=0)


def slot_block(core, rank, step, own, other, store):
    turn = (step >> 1) ^ (rank & 1)
    local = (step & 1) == core
    for t in (0, 1):
        pl.when(local & (turn == t))(functools.partial(store, own[t]))
        pl.when(jnp.logical_not(local) & (turn == t))(functools.partial(store, other[t]))


def norm_rows(values):
    mean_val = jnp.mean(values, axis=1, keepdims=True)
    centered = values - mean_val
    inv_std = lax.rsqrt(jnp.mean(centered * centered, axis=1, keepdims=True) + NORM_EPS)
    return centered * inv_std, inv_std


def project_body(_, *refs):
    packs, own_x, other_x = refs[0:4], refs[4:6], refs[6:8]
    table_ref, qkv_ref, h_ref, x_ref, rel_ref, w_ref, vec_ref, up_ref, *bias_refs = refs[8:18]
    step, (core, chip, rank) = pl.program_id(0), own_place()
    width = w_ref.shape[0]
    shard = width // 8
    span = qkv_ref.shape[1]
    cols = span // 3

    @pl.when(step == 0)
    def _():
        first = core == 0
        vec_ref[...] = jnp.zeros_like(vec_ref)
        own_rows = []
        for k in range(4):
            at = pl.ds(aligned(chip ^ k, 2 * shard), 2 * shard)
            own, other = packs[k][: shard + 8], packs[k][shard + 8 :]
            w_ref[at, :] = ordered(core, own[:shard], other[:shard])
            own_row, other_row = own[shard : shard + 1].astype(f32), other[shard : shard + 1].astype(f32)
            own_rows.append(own_row)
            low, high = jnp.where(first, own_row, other_row), jnp.where(first, other_row, own_row)
            for row, source in enumerate((0, 1, 4, 5, 6)):
                piece = slice(source * shard, (source + 1) * shard)
                vec_ref[row : row + 1, at] = jnp.concatenate([low[:, piece], high[:, piece]], axis=1)
            unit = up_ref.shape[1] // 4
            up_ref[:, pl.ds(aligned(chip ^ k, unit), unit)] = own_row[:, 7 * shard : 7 * shard + unit]
        even = chip & 1 == 0
        for k in (0, 2):
            at = pl.ds(aligned((chip ^ k) >> 1, 2 * shard), 2 * shard)
            low = jnp.where(even, own_rows[k], own_rows[k + 1])
            high = jnp.where(even, own_rows[k + 1], own_rows[k])
            for row, source in enumerate((2, 3)):
                piece = slice(source * shard, (source + 1) * shard)
                bias_refs[row][:, at] = jnp.concatenate([low[:, piece], high[:, piece]], axis=1)

    def copy(ref):
        x_ref[...] = ref[...]

    slot_block(core, rank, step, own_x, other_x, copy)
    x_hat, _ = norm_rows(x_ref[...].astype(f32))
    h = (x_hat * vec_ref[0:1, :] + vec_ref[1:2, :]).astype(bf)
    h_ref[...] = h
    qkv_ref[...] = dot(h, w_ref[:, :span], NN).astype(bf)
    rel_ref[...] = dot(table_ref[...], w_ref[:, span:], NN).astype(bf)


def feed_body(meta, *refs):
    packs, own_g, other_g = refs[0:4], refs[4:6], refs[6:8]
    x_ref, o_own, o_other, vec_ref, bias_ref = refs[8:13]
    dy_ref, x_hat_ref, rstd_ref, y_keep, dh_ref, y_send, wo_mine = refs[13:20]
    outs = refs[20:24]
    up_w, down_w, wo_theirs, up_acc, down_acc, sums = refs[24:30]
    step, chip, core = pl.program_id(0), meta[CHIP], meta[CORE]
    width = up_w.shape[0]
    shard, unit, block = width // 8, down_w.shape[0] // 4, x_ref.shape[0]
    fold = shard // 2
    unfold = lambda rows: jnp.concatenate([rows[:, :width], rows[:, width:]], axis=0)

    @pl.when(step == 0)
    def _():
        sums[...] = jnp.zeros_like(sums)
        up_acc[...] = jnp.zeros_like(up_acc)
        down_acc[...] = jnp.zeros_like(down_acc)
        masks = (0, 1 + core, 2 - core, 3)
        for pack_ref, k in zip(packs, masks):
            pack, other = pack_ref[: 3 * shard + fold], pack_ref[3 * shard + fold :]
            up_w[pl.ds(aligned(chip ^ k, 2 * shard), 2 * shard), :] = ordered(core, pack[:shard], other[:shard])
            at = pl.ds(aligned(chip ^ k, shard), shard)
            wo_mine[at, :] = unfold(pack[shard : shard + fold])
            wo_theirs[at, :] = unfold(other[shard:])
            down_w[pl.ds(aligned(chip ^ k, unit), unit), :] = unfold(pack[shard + fold :])

    at = step * block + lax.broadcasted_iota(jnp.int32, (block, 1), 0)

    def load(ref):
        dy_ref[...] = jnp.where(at < meta[LIVE], ref[...].astype(f32), 0.0).astype(bf)

    slot_block(core, meta[RANK], step, own_g, other_g, load)
    y1 = x_ref[...].astype(f32) + (dot(o_own[...], wo_mine[...], NN) + dot(o_other[...], wo_theirs[...], NN))
    x_hat, inv_std = norm_rows(y1)
    x_hat_ref[...] = x_hat.astype(bf)
    rstd_ref[...] = inv_std
    h = (x_hat * vec_ref[2:3, :] + vec_ref[3:4, :]).astype(bf)
    f = dot(h, up_w[...], NN) + bias_ref[...]
    cdf = 0.5 * (1.0 + lax.erf(f * (1.0 / math.sqrt(2.0))))
    g = (f * cdf).astype(bf)
    dy = dy_ref[...]
    dg = dot(dy, down_w[...], NT)
    df = (dg * (cdf + f * jnp.exp(-0.5 * f * f) * (1.0 / math.sqrt(2.0 * math.pi)))).astype(bf)
    z = dot(g, down_w[...], NN)
    dh = dot(df, up_w[...], NT)
    dh_ref[...] = dh.astype(bf)
    up_acc[...] += dot(h, df, TN)
    down_acc[...] += dot(g, dy, TN)
    sums[0:1, :width] += jnp.sum(dh * x_hat, axis=0, keepdims=True)
    sums[1:2, :width] += jnp.sum(dh, axis=0, keepdims=True)
    sums[3:4, :] += jnp.sum(df.astype(f32), axis=0, keepdims=True)
    local = (step & 1) == core

    @pl.when(local)
    def _():
        y_keep[...] = y1 + z + vec_ref[4:5, :]
        sums[2:3, :width] += jnp.sum(dy.astype(f32), axis=0, keepdims=True)

    @pl.when(jnp.logical_not(local))
    def _():
        y_send[...] = z.astype(bf)

    @pl.when(step == pl.num_programs(0) - 1)
    def _():
        rows = 2 * shard
        for k, out in enumerate(outs):
            at = pl.ds(aligned(chip ^ k, rows), rows)
            units = pl.ds(aligned(chip ^ k, unit), unit)
            tail = [sums[0:1, at], sums[1:2, at], sums[2:3, at], sums[3:4, units]]
            tail = jnp.concatenate(tail + [jnp.zeros((1, sums.shape[1] - 3 * rows - unit), f32)], axis=1)
            out[:rows] = up_acc[at, :].astype(out.dtype)
            out[rows : rows + 8] = jnp.broadcast_to(tail, (8, tail.shape[1])).astype(out.dtype)
            down = down_acc[units, :]
            half = unit // 2
            out[rows + 8 :] = jnp.concatenate([down[:half], down[half:]], axis=1).astype(out.dtype)


def norm_two_body(meta, x_hat_ref, rstd_ref, dh_ref, dh_came, dy_ref, vec_ref, y_keep, y_came, wo_ref, o_ref, *refs):
    out0, out1, resid_ref, do_ref, go_ref = refs
    step = pl.program_id(0)

    @pl.when(step == 0)
    def _():
        go_ref[...] = jnp.zeros_like(go_ref)

    x_hat = x_hat_ref[...].astype(f32)
    e = (dh_ref[...].astype(f32) + dh_came[...].astype(f32)) * vec_ref[2:3, :]
    first = jnp.mean(e, axis=1, keepdims=True)
    second = jnp.mean(e * x_hat, axis=1, keepdims=True)
    grad = dy_ref[...].astype(f32) + rstd_ref[...] * (e - first - x_hat * second)
    da = grad.astype(bf)
    do_ref[...] = dot(da, wo_ref[...], NT).astype(bf)
    go_ref[...] += dot(o_ref[...], da, TN)
    turn = (step >> 1) ^ (meta[RANK] & 1)
    local = (step & 1) == meta[CORE]

    @pl.when(local)
    def _():
        resid_ref[...] = grad
        y = (y_keep[...] + y_came[...].astype(f32)).astype(bf)

        @pl.when(turn == 0)
        def _():
            out0[...] = y

        @pl.when(turn == 1)
        def _():
            out1[...] = y


def qkv_back_body(meta, *refs):
    grads, rels = refs[:6], refs[6:8]
    w_ref, x_ref, h_ref, table_ref = refs[8:12]
    gu_refs, gv_refs, go_ref = refs[12:14], refs[14:16], refs[16]
    keep_ref, send_ref = refs[17:19]
    outs, acc, sums = refs[19:23], refs[23], refs[24]
    step, chip = pl.program_id(0), meta[CHIP]
    width = x_ref.shape[1]
    rows = width // 4

    @pl.when(step == 0)
    def _():
        sums[...] = jnp.zeros_like(sums)
        acc[...] = jnp.zeros_like(acc)

    dqkv = jnp.concatenate([ref[...] for ref in grads], axis=1)
    drel = jnp.concatenate([ref[...] for ref in rels], axis=1)
    span = dqkv.shape[1]
    acc[:, :span] += dot(h_ref[...], dqkv, TN)
    acc[:, span:] += dot(table_ref[...], drel, TN)
    dh = dot(dqkv, w_ref[:, :span], NT)
    x_hat, _ = norm_rows(x_ref[...].astype(f32))
    sums[0:1, :] += jnp.sum(dh * x_hat, axis=0, keepdims=True)
    sums[1:2, :] += jnp.sum(dh, axis=0, keepdims=True)
    local = (step & 1) == meta[CORE]

    @pl.when(local)
    def _():
        keep_ref[...] = dh

    @pl.when(jnp.logical_not(local))
    def _():
        send_ref[...] = dh.astype(bf)

    @pl.when(step == pl.num_programs(0) - 1)
    def _():
        for k, out in enumerate(outs):
            at = pl.ds(aligned(chip ^ k, rows), rows)
            low = (chip ^ k) >> 1 == 0
            tail = [sums[0:1, at], sums[1:2, at]]
            tail += [jnp.where(low, a[...], b[...]) for a, b in (gu_refs, gv_refs)]
            tail = jnp.concatenate(tail + [jnp.zeros((1, acc.shape[1] - 4 * rows), f32)], axis=1)
            out[:rows] = acc[at, :].astype(out.dtype)
            out[rows : rows + 8] = jnp.broadcast_to(tail, (8, tail.shape[1])).astype(out.dtype)
            shard = rows // 2
            lines = go_ref[pl.ds(aligned(chip ^ k, shard), shard), :]
            lines = jnp.concatenate([lines[: shard // 2], lines[shard // 2 :]], axis=1)
            out[rows + 8 :] = lines.astype(out.dtype)


def norm_one_body(meta, x_ref, dh_keep, dh_came, resid_ref, vec_ref, out0, out1):
    turn = pl.program_id(0) ^ (meta[RANK] & 1)
    x_hat, inv_std = norm_rows(x_ref[...].astype(f32))
    e = (dh_keep[...] + dh_came[...].astype(f32)) * vec_ref[0:1, :]
    first = jnp.mean(e, axis=1, keepdims=True)
    second = jnp.mean(e * x_hat, axis=1, keepdims=True)
    grad = (resid_ref[...] + inv_std * (e - first - x_hat * second)).astype(bf)

    @pl.when(turn == 0)
    def _():
        out0[...] = grad

    @pl.when(turn == 1)
    def _():
        out1[...] = grad


def rank_bit(meta, bit):
    return (meta[RANK] >> bit) & 1


def chip_sum_body(meta, own, *refs, bit):
    *came, keep, send = refs
    half = keep.shape[1]
    for out, side in ((keep, rank_bit(meta, bit)), (send, 1 - rank_bit(meta, bit))):
        at = pl.ds(aligned(side, half), half)
        total = own[:, at]
        for ref in came:
            total = total + ref[:, at].astype(f32)
        out[...] = total.astype(out.dtype)


def chip_sum(meta, parts, name, bit):
    rows, size = parts[0].shape
    return kernel_call(functools.partial(chip_sum_body, bit=bit), name, meta, parts, [((rows, size // 2), f32), ((rows, size // 2), bf)])


def own_rows_first(total, core, shard):
    theirs = lax.dynamic_slice_in_dim(total, (1 - core) * shard, shard, 0)
    mine = lax.dynamic_slice_in_dim(total, core * shard, shard, 0)
    came = swap_core(jnp.concatenate([theirs, total[2 * shard : 2 * shard + 8]], axis=0))
    return jnp.concatenate([mine, came, total[2 * shard :]], axis=0)


def halves(meta, mine, other, bit):
    low = rank_bit(meta, bit) == 0
    return jnp.concatenate([jnp.where(low, mine, other), jnp.where(low, other, mine)], axis=1)


def both_cores(meta, own, came):
    own, came = own.astype(f32), came.astype(f32)
    return own, own + came, meta[CORE] == 0


def store_half(ref, source, at, low):
    size = 2 * ref.shape[1]
    piece = source[:, at * size : (at + 1) * size]
    ref[...] = jnp.where(low, piece[:, : size // 2], piece[:, size // 2 :])


def early_out_body(meta, mine, other, came_ref, g_up, g_down, *vec_refs):
    rows = halves(meta, mine[...], other[...], 0)
    came_rows = halves(meta, came_ref[0], came_ref[1], 0)
    shard, width = g_up.shape[0], g_down.shape[1]
    first, unit = meta[CORE] == 0, rows.shape[1] // 4
    own, came = jnp.where(first, rows[:shard], rows[shard : 2 * shard]), came_rows[:shard]
    pair = (jnp.where(first, own, came), jnp.where(first, came, own))
    for j in range(4):
        for side in (0, 1):
            at = (2 * j + side) * unit
            g_up[:, at : at + unit] = pair[side][:, j * unit : (j + 1) * unit].astype(f32)
    down = rows[2 * shard + 8 :].astype(f32)
    g_down[...] = jnp.concatenate([down[:, :width], down[:, width:]], axis=0)
    own, total, low = both_cores(meta, rows[2 * shard : 2 * shard + 1], came_rows[shard : shard + 1])
    for at, ref in enumerate(vec_refs[:3]):
        store_half(ref, total, at, low)
    vec_refs[3][...] = own[:, 6 * shard : 6 * shard + unit]


def late_out_body(meta, mine, other, g_qkv, g_rel, g_out, *vec_refs):
    rows = halves(meta, mine[...], other[...], 0)
    shard, width = g_qkv.shape[0], g_out.shape[1]
    first, hd, heads = meta[CORE] == 0, HEAD_DIM, H // 2
    own, came = rows[:shard], rows[shard : 2 * shard]
    pair = (jnp.where(first, own, came), jnp.where(first, came, own))
    cols = heads * hd
    piece = lambda h, t: pair[h & 1][:, t * cols + (h >> 1) * hd : t * cols + ((h >> 1) + 1) * hd]
    g_qkv[...] = jnp.concatenate([piece(h, t) for h in range(2 * heads) for t in range(3)], axis=1).astype(f32)
    g_rel[...] = jnp.concatenate([piece(h, 3) for h in range(2 * heads)], axis=1).astype(f32)
    out = rows[2 * shard + 16 :].astype(f32)
    g_out[...] = jnp.concatenate([out[:, :width], out[:, width:]], axis=0)
    own, total, low = both_cores(meta, rows[2 * shard + 8 : 2 * shard + 9], rows[2 * shard : 2 * shard + 1])
    even = meta[CHIP] & 1 == 0
    for at, ref in enumerate(vec_refs):
        store_half(ref, total if at < 2 else own, at, low if at < 2 else even)


def place_body(meta, y0, y1, x0, x1, y_ref, x_ref):
    high = meta[RANK] >> 1 == 1
    y_ref[0] = jnp.where(high, y1[...], y0[...])
    y_ref[1] = jnp.where(high, y0[...], y1[...])
    x_ref[0] = jnp.where(high, x1[...], x0[...]).astype(f32)
    x_ref[1] = jnp.where(high, x0[...], x1[...]).astype(f32)


def slot_split_device(
    layer_input,
    lengths,
    ln1_gain,
    ln1_bias,
    w_qkv,
    w_rel,
    bias_u,
    bias_v,
    w_out,
    ln2_gain,
    ln2_bias,
    w_up,
    up_bias,
    w_down,
    down_bias,
    grad_out,
):
    slots, block, width = layer_input.shape
    rank, device = lax.axis_index("seq"), lax.axis_index("fsdp")
    core, chip = device & 1, device >> 1
    full, heads = 4 * block, H // 2
    cols, shard, unit = heads * HEAD_DIM, width // 8, up_bias.shape[0]
    mine_ff = 4 * unit

    none = jnp.zeros((4,), jnp.int32)
    x_own = to_slots(layer_input, rank)
    vectors = (ln1_gain, ln1_bias, bias_u, bias_v, ln2_gain, ln2_bias, down_bias, up_bias)
    attn_rows, fold = shard + 8, shard // 2
    attn_pack, feed_pack, pack_send = kernel_call(
        pack_body,
        "pack",
        lengths,
        [w_qkv, w_rel, w_up, w_out, w_down] + [v.reshape(-1, min(128, v.size)) for v in vectors],
        [((attn_rows, 4 * cols), bf), ((3 * shard + fold, 4 * cols), bf), ((attn_rows + shard + fold, 4 * cols), bf)],
        vmem=60,
    )
    pack_came = swap_core(pack_send)
    attn_pack = jnp.concatenate([attn_pack, pack_came[:attn_rows]], axis=0)
    attn_packs = [attn_pack] + [swap_chip(attn_pack, k) for k in (1, 2, 3)]
    feed_pack = jnp.concatenate([feed_pack, pack_came[attn_rows:]], axis=0)
    digits_at = 7 * shard + unit
    digits = pack_came[shard, digits_at : digits_at + 2 * slots].astype(jnp.int32)
    lengths = jnp.where(core == rank >> 1, lengths, digits[0::2] * DIGIT + digits[1::2])
    length = jnp.where(rank & 1 == 0, lengths[0], lengths[1])
    meta = jnp.stack([core, chip, rank, length]).astype(jnp.int32)
    length_arr = length.reshape(1)
    feed_pack, meta, length_arr, grad_out, *rest = together(
        feed_pack, meta, length_arr, grad_out, *x_own, *attn_packs
    )
    grad_own = to_slots(grad_out, rank)
    x_own, attn_packs = rest[:2], rest[2:]
    x_other = [swap_core(x) for x in x_own]
    feed_pack, x_other[0] = together(feed_pack, x_other[0])
    feed_first = swap_axis(feed_pack, 0)

    fine = 32
    inv_freq = jnp.exp(lax.iota(f32, width // 2) * (-2.0 * math.log(10000.0) / width))
    high = (full - 1 - fine * lax.iota(jnp.int32, full // fine)).astype(f32)[:, None] * inv_freq
    low = lax.iota(f32, fine)[:, None] * inv_freq
    high_sin, high_cos, low_sin, low_cos = together(jnp.sin(high), jnp.cos(high), jnp.sin(low), jnp.cos(low))
    high_sin, high_cos = high_sin[:, None], high_cos[:, None]
    table = jnp.concatenate(
        [high_sin * low_cos - high_cos * low_sin, high_cos * low_cos + high_sin * low_sin], axis=2
    )
    table = table.astype(bf).reshape(full, width)

    by_step = lambda width: pl.BlockSpec((block, width), lambda i, _: (i, 0))
    qkv, h1, x_slot, rel, w_own, vecs, up_b, own_u, own_v = kernel_call(
        project_body,
        "project",
        none,
        [pltpu.with_memory_space_constraint(v, pltpu.HBM) for v in attn_packs + x_own + x_other + [table]],
        [((full, 3 * cols), bf), ((full, width), bf), ((full, width), bf), ((full, cols), bf)]
        + [((width, 4 * cols), bf), ((8, width), f32), ((1, mine_ff), f32), ((1, cols), f32), ((1, cols), f32)],
        grid=(4,),
        in_specs=[whole(2 * attn_rows, 4 * cols)] * 4 + [whole(block, width)] * 4 + [by_step(width)],
        out_specs=[by_step(3 * cols), by_step(width), by_step(width), by_step(cols)]
        + [whole(width, 4 * cols), whole(8, width), whole(1, mine_ff), whole(1, cols), whole(1, cols)],
        flops=2 * full * width * 4 * cols,
        vmem=32,
    )
    qkv, feed_later, feed_first = together(qkv, feed_pack, feed_first)
    feed_second = swap_axis(feed_later, 1)
    feed_third = swap_axis(feed_first, 1)
    attn, lse = attn_fwd(length_arr, qkv, rel, own_u, own_v)
    attn, feed_second, feed_third, *grad_own = together(attn, feed_second, feed_third, *grad_own)
    grad_other = [swap_core(g) for g in grad_own]
    feed_packs = [feed_pack, feed_first, feed_second, feed_third]

    attn_other = swap_core(attn)
    kept = lambda width: pl.BlockSpec((block, width), lambda i, _: (i >> 1, 0))
    half, rows = full // 2, 2 * shard + 8
    blocks = lambda rows: [((rows, 2 * width), f32)] + [((rows, 2 * width), bf)] * 3
    dy, x_hat, rstd, y_keep, dh, y_send, wo_mine, *early_parts = kernel_call(
        feed_body,
        "feed",
        meta,
        feed_packs + grad_own + grad_other + [x_slot, attn, attn_other, vecs, up_b],
        [((full, width), bf), ((full, width), bf), ((full, 1), f32), ((half, width), f32)]
        + [((full, width), bf), ((half, width), bf), ((cols, width), bf)]
        + blocks(rows + unit // 2),
        grid=(4,),
        in_specs=[whole(*feed_pack.shape)] * 4 + [whole(block, width)] * 4
        + [by_step(width), by_step(cols), by_step(cols), whole(8, width), whole(1, mine_ff)],
        out_specs=[by_step(width), by_step(width), by_step(1), kept(width)]
        + [by_step(width), kept(width), whole(cols, width)]
        + [whole(rows + unit // 2, 2 * width)] * 4,
        scratch=[
            pltpu.VMEM((width, mine_ff), bf),
            pltpu.VMEM((mine_ff, width), bf),
            pltpu.VMEM((cols, width), bf),
            pltpu.VMEM((width, mine_ff), f32),
            pltpu.VMEM((mine_ff, width), f32),
            pltpu.VMEM((8, mine_ff), f32),
        ],
        flops=12 * full * width * mine_ff,
    )
    dh_came = swap_core(dh)
    y_came = swap_core(y_send)
    early_came = [swap_chip(early_parts[k], k) for k in (1, 2, 3)]
    out0, out1, g_resid, d_attn, g_out = kernel_call(
        norm_two_body,
        "norm_two",
        meta,
        [x_hat, rstd, dh, dh_came, dy, vecs, y_keep, y_came, wo_mine, attn],
        [((block, width), bf)] * 2 + [((half, width), f32), ((full, cols), bf), ((cols, width), f32)],
        grid=(4,),
        in_specs=[by_step(width), by_step(1)] + [by_step(width)] * 3 + [whole(8, width)] + [kept(width)] * 2
        + [whole(cols, width), by_step(cols)],
        out_specs=[whole(block, width)] * 2 + [kept(width), by_step(cols), whole(cols, width)],
        flops=4 * full * width * cols,
    )
    home = lambda outs: [
        lax.ppermute(out, ("fsdp", "seq"), [(b, a) for a, b in slot_pairs(turn)])
        for turn, out in enumerate(outs)
    ]
    y_turns = home((out0, out1))
    back = lambda pair: attn_bwd(length_arr, qkv, rel, own_u, own_v, lse, d_attn, pair=pair)
    first_pair = back(0)
    d_attn, *first_pair = together(d_attn, *first_pair)
    *second_pair, y0, y1, e1, e2, e3 = together(*back(1), *y_turns, *early_came)
    q0, k0, v0, r0, u0, b0 = first_pair
    q1, k1, v1, r1, u1, b1 = second_pair
    early_keep, early_send = chip_sum(meta, [early_parts[0], e1, e2, e3], "early_chips", 0)
    early_send, q1 = together(early_send, q1)
    early_came = swap_seq(early_send, 1)
    pair_step = pl.BlockSpec((block, 2 * HEAD_DIM), lambda i, _: (i, 0))
    pair_row = whole(1, 2 * HEAD_DIM)
    dh1_keep, dh1_send, *late_parts = kernel_call(
        qkv_back_body,
        "qkv_back",
        meta,
        [q0, q1, k0, k1, v0, v1, r0, r1, w_own, x_slot, h1, table, u0, u1, b0, b1, g_out],
        [((half, width), f32), ((half, width), bf)] + blocks(rows + fold),
        grid=(4,),
        in_specs=[pair_step] * 8 + [whole(width, 4 * cols)] + [by_step(width)] * 3
        + [pair_row] * 4 + [whole(cols, width)],
        out_specs=[kept(width)] * 2 + [whole(rows + fold, 2 * width)] * 4,
        scratch=[pltpu.VMEM((width, 4 * cols), f32), pltpu.VMEM((8, width), f32)],
        flops=14 * full * width * cols,
    )
    dh1_send, early_came, *late_parts = together(dh1_send, early_came, *late_parts)
    dh1_came = swap_core(dh1_send)
    early_pair = (early_keep + early_came.astype(f32)).astype(bf)
    early_came = swap_seq(early_pair, 2)
    late_came = [swap_chip(late_parts[k], k) for k in (1, 2, 3)]
    by_half = pl.BlockSpec((block, width), lambda i, _: (i, 0))
    own_rows = pl.BlockSpec((block, width), lambda i, m: (2 * i + m[CORE], 0))
    x0, x1 = kernel_call(
        norm_one_body,
        "norm_one",
        meta,
        [x_slot, dh1_keep, dh1_came, g_resid, vecs],
        [((block, width), bf)] * 2,
        grid=(2,),
        in_specs=[own_rows] + [by_half] * 3 + [whole(8, width)],
        out_specs=[whole(block, width)] * 2,
        vmem=60,
    )
    x_turns = home((x0, x1))
    *late_came, early_came, _, _ = together(*late_came, early_came, x0, x1)
    early_mine = (early_pair.astype(f32) + early_came.astype(f32)).astype(bf)
    late_keep, late_send = chip_sum(meta, [late_parts[0]] + late_came, "late_chips", 0)
    small = lambda size: ((1, size), f32)
    late_came, g0, g1, early_mine = together(swap_seq(late_send, 1), *x_turns, early_mine)
    early_other = swap_seq(early_mine, 1)
    theirs = lambda rows: jnp.concatenate(
        [
            lax.dynamic_slice_in_dim(rows, (1 - core) * shard, shard, 0),
            rows[2 * shard : 2 * shard + 8],
        ],
        axis=0,
    )
    early_core = swap_core(jnp.stack([theirs(early_mine), theirs(early_other)]))
    g_up, g_down, g_gain_two, g_shift_two, g_down_shift, g_up_shift = kernel_call(
        early_out_body,
        "early_out",
        meta,
        [early_mine, early_other, early_core],
        [((shard, 2 * mine_ff), f32), ((unit, width), f32)] + [small(shard)] * 3 + [small(unit)],
    )
    late_pair = (late_keep + late_came.astype(f32)).astype(bf)
    output, grad_x = kernel_call(
        place_body,
        "place",
        meta,
        [y0, y1, g0, g1],
        [((2, block, width), bf), ((2, block, width), f32)],
    )
    late_came, output, grad_x, g_up = together(swap_seq(late_pair, 2), output, grad_x, g_up)
    late_total = (late_pair.astype(f32) + late_came.astype(f32)).astype(bf)
    late_mine = own_rows_first(late_total, core, shard)
    g_qkv, g_rel, g_w_out, *late_vectors = kernel_call(
        late_out_body,
        "late_out",
        meta,
        [late_mine, swap_seq(late_mine, 1)],
        [((shard, 6 * cols), f32), ((shard, 2 * cols), f32), ((shard, width), f32)] + [small(shard)] * 4,
    )
    g_gain_one, g_shift_one, g_bias_u, g_bias_v = [v.reshape(-1) for v in late_vectors]
    return (
        output,
        grad_x,
        g_gain_one,
        g_shift_one,
        g_qkv,
        g_rel,
        g_bias_u,
        g_bias_v,
        g_w_out,
        g_gain_two.reshape(-1),
        g_shift_two.reshape(-1),
        g_up,
        g_up_shift.reshape(-1),
        g_down,
        g_down_shift.reshape(-1),
    )


def per_device(*args):
    one_slot_a_chip = lax.axis_size("fsdp") == 8 and lax.axis_size("seq") == 4
    if one_slot_a_chip and args[0].shape[0] == 2:
        return slot_split_device(*args)
    return head_split_device(*args)


def solution(mesh):
    placed = (
        P("fsdp", "seq", None),
        P("fsdp"),
        P("fsdp"),
        P("fsdp"),
        P("fsdp", None),
        P("fsdp", None),
        P("fsdp"),
        P("fsdp"),
        P("fsdp", None),
        P("fsdp"),
        P("fsdp"),
        P("fsdp", None),
        P("fsdp"),
        P("fsdp", None),
        P("fsdp"),
        P("fsdp", "seq", None),
    )
    return jax.shard_map(
        per_device,
        mesh=mesh,
        in_specs=placed,
        out_specs=(
            P("fsdp", "seq", None),
            P("fsdp", "seq", None),
            P("fsdp"),
            P("fsdp"),
            P("fsdp", None),
            P("fsdp", None),
            P("fsdp"),
            P("fsdp"),
            P("fsdp", None),
            P("fsdp"),
            P("fsdp"),
            P("fsdp", None),
            P("fsdp"),
            P("fsdp", None),
            P("fsdp"),
        ),
        check_vma=False,
    )
```

```python
import functools
import math

import jax
import jax.numpy as jnp
from jax import lax
from jax.experimental import pallas as pl
from jax.experimental.pallas import tpu as pltpu
from jax.sharding import PartitionSpec as P

H = 8
HEAD_DIM = 64


NEG_FILL = -1e30
NORM_EPS = 1e-05


bf, f32 = jnp.bfloat16, jnp.float32
NEG = NEG_FILL
HD = HEAD_DIM
NT = (((1,), (1,)), ((), ()))
NN = (((1,), (0,)), ((), ()))


def dot(a, b, dims):
    return lax.dot_general(a, b, dims, preferred_element_type=f32)


def masked_tail(s, keep, block):
    tail = jnp.where(keep, s[:, s.shape[1] - block :], NEG)
    if s.shape[1] == block:
        return tail
    return jnp.concatenate([s[:, : s.shape[1] - block], tail], axis=1)


def scores(qu, qv, keys, rel_rev, keep, block):
    span = keys.shape[0]
    rel = dot(qv, rel_rev, NT)
    rel = pltpu.roll(rel, (span - block + 1) % span, 1, stride=1, stride_axis=0)
    return masked_tail(dot(qu, keys, NT) + rel, keep, block)


def attn_fwd_body(len_ref, q_ref, k_ref, v_ref, r_ref, bu_ref, bv_ref, o_ref, lse_ref, *, block):
    full = q_ref.shape[0]
    lane = lax.broadcasted_iota(jnp.int32, (block, 2 * HD), 1)
    sides = (lane < HD, lane >= HD)
    length = len_ref[0]
    col = lax.broadcasted_iota(jnp.int32, (1, full), 1)
    bias = jnp.where(col < length, 0.0, NEG)
    tri = lax.broadcasted_iota(jnp.int32, (block, block), 1) <= lax.broadcasted_iota(
        jnp.int32, (block, block), 0
    )
    for first in range(0, full, block):
        span = first + block
        q = q_ref[first:span, :].astype(f32)
        qu = (q + bu_ref[...]).astype(bf).astype(f32) * 0.125
        qv = (q + bv_ref[...]).astype(bf).astype(f32) * 0.125
        outs = []
        for head, side in enumerate(sides):
            s = scores(
                jnp.where(side, qu, 0.0).astype(bf),
                jnp.where(side, qv, 0.0).astype(bf),
                k_ref[:span, :],
                r_ref[full - span :, :],
                tri,
                block,
            )
            s = s + bias[:, :span]
            top = jnp.max(s, axis=1, keepdims=True)
            e = jnp.exp(s - top)
            total = jnp.sum(e, axis=1, keepdims=True)
            outs.append(dot(e.astype(bf), v_ref[:span, :], NN) / total)
            lse_ref[head, first:span, :] = top + jnp.log(total)
        o_ref[first:span, :] = jnp.where(sides[0], outs[0], outs[1]).astype(bf)


def attn_fwd(length, qkv, rel_rev, bias_u, bias_v, *, block=256):
    full, cols = rel_rev.shape
    pairs = cols // (2 * HD)
    at = lambda part: pl.BlockSpec((full, 2 * HD), lambda pair, _: (0, part * pairs + pair))
    row = pl.BlockSpec((1, 2 * HD), lambda pair, _: (0, pair))
    return pl.pallas_call(
        functools.partial(attn_fwd_body, block=block),
        out_shape=(
            jax.ShapeDtypeStruct((full, cols), bf),
            jax.ShapeDtypeStruct((2 * pairs, full, 1), f32),
        ),
        grid_spec=pltpu.PrefetchScalarGridSpec(
            num_scalar_prefetch=1,
            grid=(pairs,),
            in_specs=[at(0), at(1), at(2), at(0), row, row],
            out_specs=(at(0), pl.BlockSpec((2, full, 1), lambda pair, _: (pair, 0, 0))),
        ),
        cost_estimate=pl.CostEstimate(flops=0, bytes_accessed=0, transcendentals=0),
        compiler_params=pltpu.CompilerParams(vmem_limit_bytes=32 << 20),
        name="attn_fwd",
    )(length, qkv, qkv, qkv, rel_rev, bias_u, bias_v)


def attn_bwd_body(len_ref, q_ref, k_ref, v_ref, r_ref, bu_ref, bv_ref, lse_ref, do_ref, *refs, block, heads):
    dq_ref, dk_ref, dv_ref, dr_ref, gu_ref, gv_ref, dk_t, dv_t, dr_t = refs
    full = q_ref.shape[0]
    length = len_ref[0]
    lane = lax.broadcasted_iota(jnp.int32, (block, 2 * HD), 1)
    sides = (lane < HD, lane >= HD)
    rows = lax.broadcasted_iota(jnp.int32, (block, block), 0)
    cols = lax.broadcasted_iota(jnp.int32, (block, block), 1)
    tri = cols <= rows
    flip = jnp.where(rows + cols == block - 1, 1.0, 0.0).astype(bf)
    row = lax.broadcasted_iota(jnp.int32, (block, 1), 0)
    for ref in (dk_t, dv_t, dr_t, dq_ref, gu_ref, gv_ref):
        ref[...] = jnp.zeros_like(ref)
    for first in range(0, full, block):
        span = first + block

        @pl.when(first < length)
        def _():
            q = q_ref[first:span, :].astype(f32)
            qu = (q + bu_ref[...]).astype(bf).astype(f32) * 0.125
            qv = (q + bv_ref[...]).astype(bf).astype(f32) * 0.125
            do = do_ref[first:span, :].astype(f32)
            qu_t = jnp.transpose(qu).astype(bf)
            do_t = jnp.transpose(do).astype(bf)
            qv_t = jnp.transpose(dot(flip, qv.astype(bf), NN)).astype(bf)
            dqu, dqv = [0.0, 0.0], [0.0, 0.0]
            for head in heads:
                side = sides[head]
                at = slice(head * HD, (head + 1) * HD)
                s = scores(
                    jnp.where(side, qu, 0.0).astype(bf),
                    jnp.where(side, qv, 0.0).astype(bf),
                    k_ref[:span, :],
                    r_ref[full - span :, :],
                    tri,
                    block,
                )
                lse = jnp.where(first + row < length, lse_ref[head, first:span, :], -NEG)
                p = jnp.exp(s - lse)
                dp = dot(jnp.where(side, do, 0.0).astype(bf), v_ref[:span, :], NT)
                t = p * dp
                ds = (t - p * jnp.sum(t, axis=1, keepdims=True)).astype(bf)
                dv_t[at, :span] += dot(do_t[at], p.astype(bf), NN)
                both = dot(jnp.concatenate([qu_t[at], flip], axis=0), ds, NN)
                dk_t[at, :span] += both[:HD]
                dqu[head] = dot(ds, k_ref[:span, :], NN)
                ds_rev = pltpu.roll(both[HD:], 0, 1, stride=1, stride_axis=0).astype(bf)
                dr_t[at, full - span :] += dot(qv_t[at], ds_rev, NN)
                dqv[head] = dot(ds_rev, r_ref[full - span :, :], NN)
            dqu = jnp.where(sides[0], dqu[0], dqu[1]) * 0.125
            dqv = jnp.where(sides[0], dqv[0], dqv[1]) * 0.125
            gu_ref[...] += jnp.sum(dqu, axis=0, keepdims=True)
            gv_ref[...] += jnp.sum(dqv, axis=0, keepdims=True)
            dq_ref[first:span, :] = (dqu + dot(flip, dqv.astype(bf), NN)).astype(bf)

    dk_ref[...] = jnp.transpose(dk_t[...]).astype(bf)
    dv_ref[...] = jnp.transpose(dv_t[...]).astype(bf)
    dr_ref[...] = jnp.transpose(dr_t[...]).astype(bf)


def attn_bwd(length, qkv, rel_rev, bias_u, bias_v, lse, d_out, *, pair, heads=(0, 1), block=256):
    full, cols = rel_rev.shape
    pairs = cols // (2 * HD)
    at = lambda part: pl.BlockSpec((full, 2 * HD), lambda i, _: (0, part * pairs + pair))
    row = pl.BlockSpec((1, 2 * HD), lambda i, _: (0, pair))
    out = pl.BlockSpec((full, 2 * HD), lambda i, _: (0, 0))
    out_row = pl.BlockSpec((1, 2 * HD), lambda i, _: (0, 0))
    return pl.pallas_call(
        functools.partial(attn_bwd_body, block=block, heads=heads),
        out_shape=(jax.ShapeDtypeStruct((full, 2 * HD), bf),) * 4
        + (jax.ShapeDtypeStruct((1, 2 * HD), f32),) * 2,
        grid_spec=pltpu.PrefetchScalarGridSpec(
            num_scalar_prefetch=1,
            grid=(1,),
            in_specs=[at(0), at(1), at(2), at(0), row, row]
            + [pl.BlockSpec((2, full, 1), lambda i, _: (pair, 0, 0)), at(0)],
            out_specs=(out,) * 4 + (out_row, out_row),
            scratch_shapes=[pltpu.VMEM((2 * HD, full), f32)] * 3,
        ),
        cost_estimate=pl.CostEstimate(flops=0, bytes_accessed=0, transcendentals=0),
        compiler_params=pltpu.CompilerParams(vmem_limit_bytes=32 << 20),
        name="attn_bwd",
    )(length, qkv, qkv, qkv, rel_rev, bias_u, bias_v, lse, d_out)


def norm_parts(values):
    mean_val = jnp.mean(values, axis=-1, keepdims=True)
    centered = values - mean_val
    inv_std = lax.rsqrt(jnp.mean(centered * centered, axis=-1, keepdims=True) + NORM_EPS)
    return (centered * inv_std, inv_std)


def norm_back(grad_norm, x_hat, inv_std):
    first_mean = jnp.mean(grad_norm, axis=-1, keepdims=True)
    second_mean = jnp.mean(grad_norm * x_hat, axis=-1, keepdims=True)
    return inv_std * (grad_norm - first_mean - x_hat * second_mean)


def position_table(count_rows, feature_count):
    steps = lax.iota(jnp.float32, count_rows)
    half_count = feature_count // 2
    inv_freq = jnp.exp(
        lax.iota(jnp.float32, half_count) * (-2.0 * math.log(10000.0) / feature_count)
    )
    angles = steps[:, None] * inv_freq[None, :]
    return jnp.concatenate([jnp.sin(angles), jnp.cos(angles)], axis=1)


def skew_rows(matrix):
    leading = matrix.shape[:-2]
    row_count, col_count = matrix.shape[-2:]
    flattened = matrix.reshape(leading + (row_count * col_count,))
    picked = flattened[..., row_count - 1 : row_count - 1 + row_count * (col_count - 1)]
    return picked.reshape(leading + (row_count, col_count - 1))[..., : col_count - row_count]


def unskew_rows(matrix):
    leading = matrix.shape[:-2]
    row_count, key_count = matrix.shape[-2:]
    axis_pos = len(leading)
    widened = jnp.pad(matrix, [(0, 0)] * axis_pos + [(0, 0), (0, row_count - 1)])
    flattened = widened.reshape(leading + (row_count * (key_count + row_count - 1),))
    flattened = jnp.pad(flattened, [(0, 0)] * axis_pos + [(row_count - 1, 1)])
    return flattened.reshape(leading + (row_count, key_count + row_count))


def head_split_device(
    layer_input,
    lengths,
    ln1_gain,
    ln1_bias,
    w_qkv,
    w_rel,
    bias_u,
    bias_v,
    w_out,
    ln2_gain,
    ln2_bias,
    w_up,
    up_bias,
    w_down,
    down_bias,
    grad_out,
):
    weights = (
        lax.all_gather(ln1_gain, "fsdp", axis=0, tiled=True),
        lax.all_gather(ln1_bias, "fsdp", axis=0, tiled=True),
        lax.all_gather(w_qkv, "fsdp", axis=0, tiled=True),
        lax.all_gather(w_rel, "fsdp", axis=0, tiled=True),
        lax.all_gather(bias_u, "fsdp", axis=0, tiled=True),
        lax.all_gather(bias_v, "fsdp", axis=0, tiled=True),
        lax.all_gather(w_out, "fsdp", axis=0, tiled=True),
        lax.all_gather(ln2_gain, "fsdp", axis=0, tiled=True),
        lax.all_gather(ln2_bias, "fsdp", axis=0, tiled=True),
        lax.all_gather(w_up, "fsdp", axis=0, tiled=True),
        lax.all_gather(up_bias, "fsdp", axis=0, tiled=True),
        lax.all_gather(w_down, "fsdp", axis=0, tiled=True),
        lax.all_gather(down_bias, "fsdp", axis=0, tiled=True),
    )
    (
        gain_one,
        shift_one,
        query_key_value_matrix,
        rel_weight,
        first_bias,
        second_bias,
        output_matrix,
        gain_two,
        shift_two,
        up_matrix,
        up_shift,
        down_matrix,
        down_shift,
    ) = weights
    gain_one = gain_one.astype(jnp.float32)
    shift_one = shift_one.astype(jnp.float32)
    gain_two = gain_two.astype(jnp.float32)
    shift_two = shift_two.astype(jnp.float32)
    up_shift = up_shift.astype(jnp.float32)
    down_shift = down_shift.astype(jnp.float32)
    slots, block_len, width = layer_input.shape
    seq_count = lax.axis_size("seq")
    seq_rank = lax.axis_index("seq")
    head_dim = HEAD_DIM
    group = H // seq_count
    full_len = block_len * seq_count
    score_scale = 1.0 / math.sqrt(head_dim)
    q_block = 512
    num_blocks = full_len // q_block
    win_len = full_len + q_block
    x_float = layer_input.astype(jnp.float32)
    x_hat_one, inv_std_one = norm_parts(x_float)
    first_normalized = (x_hat_one * gain_one + shift_one).astype(jnp.bfloat16)
    qkv_local = jnp.einsum(
        "mcr,rk->mck", first_normalized, query_key_value_matrix, preferred_element_type=jnp.float32
    ).astype(jnp.bfloat16)
    qkv_heads = lax.all_to_all(qkv_local, "seq", split_axis=2, concat_axis=1, tiled=True)
    qkv_heads = qkv_heads.reshape(slots, full_len, group, 3, head_dim)
    queries = qkv_heads[:, :, :, 0]
    keys = qkv_heads[:, :, :, 1]
    values = qkv_heads[:, :, :, 2]
    head_start = seq_rank * group
    head_bias_u = lax.dynamic_slice_in_dim(
        first_bias.astype(jnp.float32).reshape(H, head_dim), head_start, group, 0
    )
    head_bias_v = lax.dynamic_slice_in_dim(
        second_bias.astype(jnp.float32).reshape(H, head_dim), head_start, group, 0
    )
    query_u = (queries.astype(jnp.float32) + head_bias_u).astype(jnp.bfloat16)
    query_v = (queries.astype(jnp.float32) + head_bias_v).astype(jnp.bfloat16)
    table_rev = position_table(full_len, width).astype(jnp.bfloat16)[::-1]
    rel_cols = lax.dynamic_slice_in_dim(rel_weight, head_start * head_dim, group * head_dim, 1)
    rel_rev = jnp.dot(table_rev, rel_cols, preferred_element_type=jnp.float32).astype(jnp.bfloat16)
    rel_ext = jnp.concatenate([rel_rev, jnp.zeros_like(rel_rev)], axis=0).reshape(
        2 * full_len, group, head_dim
    )
    col_ids = lax.iota(jnp.int32, full_len)

    def scores_block(first_row):
        qu_part = lax.dynamic_slice_in_dim(query_u, first_row, q_block, 1)
        qv_part = lax.dynamic_slice_in_dim(query_v, first_row, q_block, 1)
        window_start = full_len - q_block - first_row
        rel_win = lax.dynamic_slice_in_dim(rel_ext, window_start, win_len, 0)
        content = jnp.einsum("sqhe,skhe->shqk", qu_part, keys, preferred_element_type=jnp.float32)
        rel_raw = jnp.einsum("sqhe,the->shqt", qv_part, rel_win, preferred_element_type=jnp.float32)
        rel_part = skew_rows(rel_raw)
        row_ids = first_row + lax.iota(jnp.int32, q_block)
        causal = col_ids[None, :] <= row_ids[:, None]
        inside = col_ids[None, :] < lengths[:, None]
        allowed = causal[None, None, :, :] & inside[:, None, None, :]
        scores = jnp.where(allowed, (content + rel_part) * score_scale, NEG_FILL)
        return (scores, qu_part, qv_part, rel_win, window_start)

    def forward_block(block_index):
        first_row = block_index * q_block
        scores, qu_part, qv_part, rel_win, window_start = scores_block(first_row)
        top = jnp.max(scores, axis=-1, keepdims=True)
        expo = jnp.exp(scores - top)
        total = jnp.sum(expo, axis=-1, keepdims=True)
        probs = (expo / total).astype(jnp.bfloat16)
        out_part = jnp.einsum(
            "shqk,skhe->sqhe", probs, values, preferred_element_type=jnp.float32
        ).astype(jnp.bfloat16)
        return (out_part, top[..., 0] + jnp.log(total[..., 0]))

    block_outs, block_lse = lax.map(forward_block, jnp.arange(num_blocks, dtype=jnp.int32))
    attn_heads = jnp.moveaxis(block_outs, 0, 1).reshape(slots, full_len, group * head_dim)
    attention_sequence = lax.all_to_all(attn_heads, "seq", split_axis=1, concat_axis=2, tiled=True)
    attention_projected = jnp.einsum(
        "mcr,rk->mck", attention_sequence, output_matrix, preferred_element_type=jnp.float32
    )
    resid = x_float + attention_projected
    x_hat_two, inv_std_two = norm_parts(resid)
    second_normalized = (x_hat_two * gain_two + shift_two).astype(jnp.bfloat16)
    pre_act = (
        jnp.einsum("oka,ac->okc", second_normalized, up_matrix, preferred_element_type=jnp.float32)
        + up_shift
    )
    normal_cdf = 0.5 * (1.0 + lax.erf(pre_act * (1.0 / math.sqrt(2.0))))
    hidden_state = (pre_act * normal_cdf).astype(jnp.bfloat16)
    down_proj = (
        jnp.einsum("zcp,pr->zcr", hidden_state, down_matrix, preferred_element_type=jnp.float32)
        + down_shift
    )
    output = (resid + down_proj).astype(jnp.bfloat16)
    positions = seq_rank * block_len + lax.iota(jnp.int32, block_len)
    live = (positions[None, :] < lengths[:, None]).astype(jnp.bfloat16)
    result_gradient = grad_out * live[:, :, None]
    grad_y_float = result_gradient.astype(jnp.float32)
    g_down_shift = jnp.sum(grad_y_float, axis=(0, 1))
    down_gradient = jnp.einsum(
        "hki,hku->iu", hidden_state, result_gradient, preferred_element_type=jnp.float32
    )
    hidden_gradient = jnp.einsum(
        "gvu,ju->gvj", result_gradient, down_matrix, preferred_element_type=jnp.float32
    )
    deriv = normal_cdf + pre_act * jnp.exp(-0.5 * pre_act * pre_act) * (
        1.0 / math.sqrt(2.0 * math.pi)
    )
    preactivation_gradient = (hidden_gradient * deriv).astype(jnp.bfloat16)
    g_up_shift = jnp.sum(preactivation_gradient.astype(jnp.float32), axis=(0, 1))
    up_gradient = jnp.einsum(
        "oiz,oix->zx", second_normalized, preactivation_gradient, preferred_element_type=jnp.float32
    )
    second_norm_gradient = jnp.einsum(
        "rau,ku->rak", preactivation_gradient, up_matrix, preferred_element_type=jnp.float32
    )
    g_gain_two = jnp.sum(second_norm_gradient * x_hat_two, axis=(0, 1))
    g_shift_two = jnp.sum(second_norm_gradient, axis=(0, 1))
    g_resid = grad_y_float + norm_back(second_norm_gradient * gain_two, x_hat_two, inv_std_two)
    attention_gradient = g_resid.astype(jnp.bfloat16)
    output_gradient = jnp.einsum(
        "zau,zam->um", attention_sequence, attention_gradient, preferred_element_type=jnp.float32
    )
    g_attn_seq = jnp.einsum(
        "urz,jz->urj", attention_gradient, output_matrix, preferred_element_type=jnp.float32
    ).astype(jnp.bfloat16)
    g_attn_heads = lax.all_to_all(
        g_attn_seq, "seq", split_axis=2, concat_axis=1, tiled=True
    ).reshape(slots, full_len, group, head_dim)

    def backward_block(carry, block_index):
        g_keys, g_vals, g_ext = carry
        first_row = block_index * q_block
        scores, qu_part, qv_part, rel_win, window_start = scores_block(first_row)
        probs = jnp.exp(scores - block_lse[block_index][..., None])
        d_out = lax.dynamic_slice_in_dim(g_attn_heads, first_row, q_block, 1)
        g_vals = g_vals + jnp.einsum(
            "shqk,sqhe->skhe", probs.astype(jnp.bfloat16), d_out, preferred_element_type=jnp.float32
        )
        g_probs = jnp.einsum("sqhe,skhe->shqk", d_out, values, preferred_element_type=jnp.float32)
        inner = jnp.sum(probs * g_probs, axis=-1, keepdims=True)
        g_scores = (probs * (g_probs - inner)).astype(jnp.bfloat16)
        g_qu = (
            jnp.einsum("shqk,skhe->sqhe", g_scores, keys, preferred_element_type=jnp.float32)
            * score_scale
        )
        g_keys = (
            g_keys
            + jnp.einsum("shqk,sqhe->skhe", g_scores, qu_part, preferred_element_type=jnp.float32)
            * score_scale
        )
        g_wide = unskew_rows(g_scores)
        g_qv = (
            jnp.einsum("shqt,the->sqhe", g_wide, rel_win, preferred_element_type=jnp.float32)
            * score_scale
        )
        g_win = (
            jnp.einsum("shqt,sqhe->sthe", g_wide, qv_part, preferred_element_type=jnp.float32)
            * score_scale
        )
        g_old = lax.dynamic_slice_in_dim(g_ext, window_start, win_len, 1)
        g_ext = lax.dynamic_update_slice_in_dim(g_ext, g_old + g_win, window_start, 1)
        return ((g_keys, g_vals, g_ext), (g_qu, g_qv))

    zero_heads = jnp.zeros((slots, full_len, group, head_dim), jnp.float32)
    zero_ext = jnp.zeros((slots, 2 * full_len, group, head_dim), jnp.float32)
    (g_keys, g_vals, g_ext), (g_qu_blocks, g_qv_blocks) = lax.scan(
        backward_block, (zero_heads, zero_heads, zero_ext), jnp.arange(num_blocks, dtype=jnp.int32)
    )
    g_qu = jnp.moveaxis(g_qu_blocks, 0, 1).reshape(slots, full_len, group, head_dim)
    g_qv = jnp.moveaxis(g_qv_blocks, 0, 1).reshape(slots, full_len, group, head_dim)
    g_queries = g_qu + g_qv
    g_bias_u_heads = jnp.sum(g_qu, axis=(0, 1))
    g_bias_v_heads = jnp.sum(g_qv, axis=(0, 1))
    g_qkv_heads = (
        jnp.stack([g_queries, g_keys, g_vals], axis=3)
        .astype(jnp.bfloat16)
        .reshape(slots, full_len, group * 3 * head_dim)
    )
    query_key_value_gradient = lax.all_to_all(
        g_qkv_heads, "seq", split_axis=1, concat_axis=2, tiled=True
    )
    g_rel_low = g_ext[:, :full_len].astype(jnp.bfloat16)
    g_rel_heads = jnp.einsum(
        "td,sthe->dhe", table_rev, g_rel_low, preferred_element_type=jnp.float32
    ).reshape(width, group * head_dim)
    g_rel_weight = lax.dynamic_update_slice_in_dim(
        jnp.zeros((width, width), jnp.float32), g_rel_heads, head_start * head_dim, 1
    )
    g_bias_u = lax.dynamic_update_slice_in_dim(
        jnp.zeros((H, head_dim), jnp.float32), g_bias_u_heads, head_start, 0
    ).reshape(width)
    g_bias_v = lax.dynamic_update_slice_in_dim(
        jnp.zeros((H, head_dim), jnp.float32), g_bias_v_heads, head_start, 0
    ).reshape(width)
    query_key_value_weight_gradient = jnp.einsum(
        "zau,zam->um",
        first_normalized,
        query_key_value_gradient,
        preferred_element_type=jnp.float32,
    )
    first_norm_gradient = jnp.einsum(
        "urz,jz->urj",
        query_key_value_gradient,
        query_key_value_matrix,
        preferred_element_type=jnp.float32,
    )
    g_gain_one = jnp.sum(first_norm_gradient * x_hat_one, axis=(0, 1))
    g_shift_one = jnp.sum(first_norm_gradient, axis=(0, 1))
    g_input = g_resid + norm_back(first_norm_gradient * gain_one, x_hat_one, inv_std_one)
    partial_shards = (
        lax.psum_scatter(g_gain_one, "fsdp", scatter_dimension=0, tiled=True),
        lax.psum_scatter(g_shift_one, "fsdp", scatter_dimension=0, tiled=True),
        lax.psum_scatter(query_key_value_weight_gradient, "fsdp", scatter_dimension=0, tiled=True),
        lax.psum_scatter(g_rel_weight, "fsdp", scatter_dimension=0, tiled=True),
        lax.psum_scatter(g_bias_u, "fsdp", scatter_dimension=0, tiled=True),
        lax.psum_scatter(g_bias_v, "fsdp", scatter_dimension=0, tiled=True),
        lax.psum_scatter(output_gradient, "fsdp", scatter_dimension=0, tiled=True),
        lax.psum_scatter(g_gain_two, "fsdp", scatter_dimension=0, tiled=True),
        lax.psum_scatter(g_shift_two, "fsdp", scatter_dimension=0, tiled=True),
        lax.psum_scatter(up_gradient, "fsdp", scatter_dimension=0, tiled=True),
        lax.psum_scatter(g_up_shift, "fsdp", scatter_dimension=0, tiled=True),
        lax.psum_scatter(down_gradient, "fsdp", scatter_dimension=0, tiled=True),
        lax.psum_scatter(g_down_shift, "fsdp", scatter_dimension=0, tiled=True),
    )
    shards = lax.psum(
        (
            partial_shards[0],
            partial_shards[1],
            partial_shards[2],
            partial_shards[3],
            partial_shards[4],
            partial_shards[5],
            partial_shards[6],
            partial_shards[7],
            partial_shards[8],
            partial_shards[9],
            partial_shards[10],
            partial_shards[11],
            partial_shards[12],
        ),
        "seq",
    )
    return (
        output,
        g_input,
        shards[0],
        shards[1],
        shards[2],
        shards[3],
        shards[4],
        shards[5],
        shards[6],
        shards[7],
        shards[8],
        shards[9],
        shards[10],
        shards[11],
        shards[12],
    )


def swap_core(values):
    size = lax.axis_size("fsdp")
    return lax.ppermute(values, "fsdp", [(i, i ^ 1) for i in range(size)])


def swap_chip(values, mask):
    size = lax.axis_size("fsdp")
    return lax.ppermute(values, "fsdp", [(i, i ^ (2 * mask)) for i in range(size)])


def swap_axis(values, turn):
    size = lax.axis_size("fsdp")
    return lax.ppermute(values, "fsdp", [(i, i ^ (2 << ((i & 1) ^ turn))) for i in range(size)])


def swap_seq(values, mask):
    size = lax.axis_size("seq")
    return lax.ppermute(values, "seq", [(i, i ^ mask) for i in range(size)])


def slot_pairs(turn):
    seq, pairs = lax.axis_size("seq"), []
    for f in range(lax.axis_size("fsdp")):
        for z in range(seq):
            to_f, to_z = (f & ~1) | (z & 1), 2 * (f & 1) + (turn ^ (z >> 1))
            pairs.append((f * seq + z, to_f * seq + to_z))
    return pairs


def to_slots(values, seq_rank):
    return [
        lax.ppermute(
            lax.dynamic_index_in_dim(values, turn ^ (seq_rank >> 1), 0, keepdims=False),
            ("fsdp", "seq"),
            slot_pairs(turn),
        )
        for turn in (0, 1)
    ]


def together(*values):
    return lax.optimization_barrier(values)


def whole(*shape):
    return pl.BlockSpec(shape, lambda *_: (0,) * len(shape))


def kernel_call(body, name, meta, args, outs, *, grid=(1,), in_specs=None, out_specs=None, scratch=(), flops=0, vmem=32):
    in_specs = in_specs or [whole(*a.shape) for a in args]
    out_specs = out_specs or [whole(*shape) for shape, _ in outs]
    moved = sum(a.size * a.dtype.itemsize for a in args)
    moved += sum(math.prod(shape) * jnp.dtype(kind).itemsize for shape, kind in outs)
    return pl.pallas_call(
        body,
        out_shape=[jax.ShapeDtypeStruct(shape, kind) for shape, kind in outs],
        grid_spec=pltpu.PrefetchScalarGridSpec(
            num_scalar_prefetch=1,
            grid=grid,
            in_specs=in_specs,
            out_specs=out_specs,
            scratch_shapes=scratch,
        ),
        compiler_params=pltpu.CompilerParams(vmem_limit_bytes=vmem << 20),
        cost_estimate=pl.CostEstimate(flops=0, bytes_accessed=0, transcendentals=0),
        name=name,
    )(meta, *args)


TN = (((0,), (0,)), ((), ()))
CORE, CHIP, RANK, LIVE = range(4)
DIGIT = 128


def aligned(index, size):
    return pl.multiple_of(index * size, size)


def own_place():
    device = lax.axis_index("fsdp")
    return device & 1, device >> 1, lax.axis_index("seq")


def pack_body(lengths_ref, qkv_ref, rel_ref, up_ref, out_ref, down_ref, *refs):
    small, (attn_ref, feed_ref, send_ref) = refs[:8], refs[8:]
    core, _, _ = own_place()
    shard = qkv_ref.shape[0]
    qkv, rel, up, out, down = qkv_ref[...], rel_ref[...], up_ref[...], out_ref[...], down_ref[...]
    heads, hd = rel.shape[1] // HEAD_DIM // 2, HEAD_DIM
    unit = up.shape[1] // 8
    packs, ups = [], []
    row = jnp.concatenate([ref[i : i + 1] for ref in small for i in range(ref.shape[0])], axis=1)
    lane = lax.broadcasted_iota(jnp.int32, (1, 4 * heads * hd - row.shape[1]), 1)
    digits = jnp.zeros(lane.shape, f32)
    for slot in range(lengths_ref.shape[0]):
        high = lengths_ref[slot] // DIGIT
        for at, digit in ((2 * slot, high), (2 * slot + 1, lengths_ref[slot] - high * DIGIT)):
            digits = jnp.where(lane == at, digit.astype(f32), digits)
    row = jnp.concatenate([row, digits.astype(row.dtype)], axis=1)
    rows = jnp.broadcast_to(row, (8, row.shape[1]))
    for side in (0, 1):
        parts = [
            qkv[:, ((2 * j + side) * 3 + t) * hd : ((2 * j + side) * 3 + t + 1) * hd]
            for t in range(3)
            for j in range(heads)
        ]
        parts += [rel[:, (2 * j + side) * hd : (2 * j + side + 1) * hd] for j in range(heads)]
        packs.append(jnp.concatenate(parts, axis=1))
        ups.append(
            jnp.concatenate([up[:, (2 * j + side) * unit : (2 * j + side + 1) * unit] for j in range(4)], axis=1)
        )
    first = core == 0
    folded = jnp.concatenate([out[: shard // 2], out[shard // 2 :]], axis=1)
    attn_ref[:shard] = jnp.where(first, packs[0], packs[1])
    attn_ref[shard:] = rows
    send_ref[:shard] = jnp.where(first, packs[1], packs[0])
    send_ref[shard : shard + 8] = rows
    send_ref[shard + 8 : 2 * shard + 8] = jnp.where(first, ups[1], ups[0])
    send_ref[2 * shard + 8 :] = folded
    feed_ref[:shard] = jnp.where(first, ups[0], ups[1])
    feed_ref[shard : shard + shard // 2] = folded
    feed_ref[shard + shard // 2 :] = jnp.concatenate([down[: 2 * shard], down[2 * shard :]], axis=1)


def ordered(core, own, other):
    first = core == 0
    return jnp.concatenate([jnp.where(first, own, other), jnp.where(first, other, own)], axis=0)


def slot_block(core, rank, step, own, other, store):
    turn = (step >> 1) ^ (rank & 1)
    local = (step & 1) == core
    for t in (0, 1):
        pl.when(local & (turn == t))(functools.partial(store, own[t]))
        pl.when(jnp.logical_not(local) & (turn == t))(functools.partial(store, other[t]))


def norm_rows(values):
    mean_val = jnp.mean(values, axis=1, keepdims=True)
    centered = values - mean_val
    inv_std = lax.rsqrt(jnp.mean(centered * centered, axis=1, keepdims=True) + NORM_EPS)
    return centered * inv_std, inv_std


def project_body(_, *refs):
    packs, own_x, other_x = refs[0:4], refs[4:6], refs[6:8]
    table_ref, qkv_ref, h_ref, x_ref, rel_ref, w_ref, vec_ref, up_ref, *bias_refs = refs[8:18]
    step, (core, chip, rank) = pl.program_id(0), own_place()
    width = w_ref.shape[0]
    shard = width // 8
    span = qkv_ref.shape[1]
    cols = span // 3

    @pl.when(step == 0)
    def _():
        first = core == 0
        vec_ref[...] = jnp.zeros_like(vec_ref)
        own_rows = []
        for k in range(4):
            at = pl.ds(aligned(chip ^ k, 2 * shard), 2 * shard)
            own, other = packs[k][: shard + 8], packs[k][shard + 8 :]
            w_ref[at, :] = ordered(core, own[:shard], other[:shard])
            own_row, other_row = own[shard : shard + 1].astype(f32), other[shard : shard + 1].astype(f32)
            own_rows.append(own_row)
            low, high = jnp.where(first, own_row, other_row), jnp.where(first, other_row, own_row)
            for row, source in enumerate((0, 1, 4, 5, 6)):
                piece = slice(source * shard, (source + 1) * shard)
                vec_ref[row : row + 1, at] = jnp.concatenate([low[:, piece], high[:, piece]], axis=1)
            unit = up_ref.shape[1] // 4
            up_ref[:, pl.ds(aligned(chip ^ k, unit), unit)] = own_row[:, 7 * shard : 7 * shard + unit]
        even = chip & 1 == 0
        for k in (0, 2):
            at = pl.ds(aligned((chip ^ k) >> 1, 2 * shard), 2 * shard)
            low = jnp.where(even, own_rows[k], own_rows[k + 1])
            high = jnp.where(even, own_rows[k + 1], own_rows[k])
            for row, source in enumerate((2, 3)):
                piece = slice(source * shard, (source + 1) * shard)
                bias_refs[row][:, at] = jnp.concatenate([low[:, piece], high[:, piece]], axis=1)

    def copy(ref):
        x_ref[...] = ref[...]

    slot_block(core, rank, step, own_x, other_x, copy)
    x_hat, _ = norm_rows(x_ref[...].astype(f32))
    h = (x_hat * vec_ref[0:1, :] + vec_ref[1:2, :]).astype(bf)
    h_ref[...] = h
    qkv_ref[...] = dot(h, w_ref[:, :span], NN).astype(bf)
    rel_ref[...] = dot(table_ref[...], w_ref[:, span:], NN).astype(bf)


def feed_body(meta, *refs):
    packs, own_g, other_g = refs[0:4], refs[4:6], refs[6:8]
    x_ref, o_own, o_other, vec_ref, bias_ref = refs[8:13]
    dy_ref, x_hat_ref, rstd_ref, y_keep, dh_ref, y_send, wo_mine = refs[13:20]
    outs = refs[20:24]
    up_w, down_w, wo_theirs, up_acc, down_acc, sums = refs[24:30]
    step, chip, core = pl.program_id(0), meta[CHIP], meta[CORE]
    width = up_w.shape[0]
    shard, unit, block = width // 8, down_w.shape[0] // 4, x_ref.shape[0]
    fold = shard // 2
    unfold = lambda rows: jnp.concatenate([rows[:, :width], rows[:, width:]], axis=0)

    @pl.when(step == 0)
    def _():
        sums[...] = jnp.zeros_like(sums)
        up_acc[...] = jnp.zeros_like(up_acc)
        down_acc[...] = jnp.zeros_like(down_acc)
        masks = (0, 1 + core, 2 - core, 3)
        for pack_ref, k in zip(packs, masks):
            pack, other = pack_ref[: 3 * shard + fold], pack_ref[3 * shard + fold :]
            up_w[pl.ds(aligned(chip ^ k, 2 * shard), 2 * shard), :] = ordered(core, pack[:shard], other[:shard])
            at = pl.ds(aligned(chip ^ k, shard), shard)
            wo_mine[at, :] = unfold(pack[shard : shard + fold])
            wo_theirs[at, :] = unfold(other[shard:])
            down_w[pl.ds(aligned(chip ^ k, unit), unit), :] = unfold(pack[shard + fold :])

    at = step * block + lax.broadcasted_iota(jnp.int32, (block, 1), 0)

    def load(ref):
        dy_ref[...] = jnp.where(at < meta[LIVE], ref[...].astype(f32), 0.0).astype(bf)

    slot_block(core, meta[RANK], step, own_g, other_g, load)
    y1 = x_ref[...].astype(f32) + (dot(o_own[...], wo_mine[...], NN) + dot(o_other[...], wo_theirs[...], NN))
    x_hat, inv_std = norm_rows(y1)
    x_hat_ref[...] = x_hat.astype(bf)
    rstd_ref[...] = inv_std
    h = (x_hat * vec_ref[2:3, :] + vec_ref[3:4, :]).astype(bf)
    f = dot(h, up_w[...], NN) + bias_ref[...]
    cdf = 0.5 * (1.0 + lax.erf(f * (1.0 / math.sqrt(2.0))))
    g = (f * cdf).astype(bf)
    dy = dy_ref[...]
    dg = dot(dy, down_w[...], NT)
    df = (dg * (cdf + f * jnp.exp(-0.5 * f * f) * (1.0 / math.sqrt(2.0 * math.pi)))).astype(bf)
    z = dot(g, down_w[...], NN)
    dh = dot(df, up_w[...], NT)
    dh_ref[...] = dh.astype(bf)
    up_acc[...] += dot(h, df, TN)
    down_acc[...] += dot(g, dy, TN)
    sums[0:1, :width] += jnp.sum(dh * x_hat, axis=0, keepdims=True)
    sums[1:2, :width] += jnp.sum(dh, axis=0, keepdims=True)
    sums[3:4, :] += jnp.sum(df.astype(f32), axis=0, keepdims=True)
    local = (step & 1) == core

    @pl.when(local)
    def _():
        y_keep[...] = y1 + z + vec_ref[4:5, :]
        sums[2:3, :width] += jnp.sum(dy.astype(f32), axis=0, keepdims=True)

    @pl.when(jnp.logical_not(local))
    def _():
        y_send[...] = z.astype(bf)

    @pl.when(step == pl.num_programs(0) - 1)
    def _():
        rows = 2 * shard
        for k, out in enumerate(outs):
            at = pl.ds(aligned(chip ^ k, rows), rows)
            units = pl.ds(aligned(chip ^ k, unit), unit)
            tail = [sums[0:1, at], sums[1:2, at], sums[2:3, at], sums[3:4, units]]
            tail = jnp.concatenate(tail + [jnp.zeros((1, sums.shape[1] - 3 * rows - unit), f32)], axis=1)
            out[:rows] = up_acc[at, :].astype(out.dtype)
            out[rows : rows + 8] = jnp.broadcast_to(tail, (8, tail.shape[1])).astype(out.dtype)
            down = down_acc[units, :]
            half = unit // 2
            out[rows + 8 :] = jnp.concatenate([down[:half], down[half:]], axis=1).astype(out.dtype)


def norm_two_body(meta, x_hat_ref, rstd_ref, dh_ref, dh_came, dy_ref, vec_ref, y_keep, y_came, wo_ref, o_ref, *refs):
    out0, out1, resid_ref, do_ref, go_ref = refs
    step = pl.program_id(0)

    @pl.when(step == 0)
    def _():
        go_ref[...] = jnp.zeros_like(go_ref)

    x_hat = x_hat_ref[...].astype(f32)
    e = (dh_ref[...].astype(f32) + dh_came[...].astype(f32)) * vec_ref[2:3, :]
    first = jnp.mean(e, axis=1, keepdims=True)
    second = jnp.mean(e * x_hat, axis=1, keepdims=True)
    grad = dy_ref[...].astype(f32) + rstd_ref[...] * (e - first - x_hat * second)
    da = grad.astype(bf)
    do_ref[...] = dot(da, wo_ref[...], NT).astype(bf)
    go_ref[...] += dot(o_ref[...], da, TN)
    turn = (step >> 1) ^ (meta[RANK] & 1)
    local = (step & 1) == meta[CORE]

    @pl.when(local)
    def _():
        resid_ref[...] = grad
        y = (y_keep[...] + y_came[...].astype(f32)).astype(bf)

        @pl.when(turn == 0)
        def _():
            out0[...] = y

        @pl.when(turn == 1)
        def _():
            out1[...] = y


def qkv_back_body(meta, *refs):
    grads_a, grads_b, grads_c = refs[:6], refs[6:12], refs[12:18]
    w_ref, x_ref, h_ref, table_ref, go_ref = refs[18:23]
    keep_ref, send_ref = refs[23:25]
    outs, acc, sums = refs[25:29], refs[29], refs[30]
    step, chip = pl.program_id(0), meta[CHIP]
    width = x_ref.shape[1]
    rows = width // 4

    @pl.when(step == 0)
    def _():
        sums[...] = jnp.zeros_like(sums)
        acc[...] = jnp.zeros_like(acc)

    both = lambda i: [grads_a[i][...], grads_b[i][...] + grads_c[i][...]]
    dqkv = jnp.concatenate(both(0) + both(1) + both(2), axis=1)
    drel = jnp.concatenate(both(3), axis=1)
    span = dqkv.shape[1]
    acc[:, :span] += dot(h_ref[...], dqkv, TN)
    acc[:, span:] += dot(table_ref[...], drel, TN)
    dh = dot(dqkv, w_ref[:, :span], NT)
    x_hat, _ = norm_rows(x_ref[...].astype(f32))
    sums[0:1, :] += jnp.sum(dh * x_hat, axis=0, keepdims=True)
    sums[1:2, :] += jnp.sum(dh, axis=0, keepdims=True)
    local = (step & 1) == meta[CORE]

    @pl.when(local)
    def _():
        keep_ref[...] = dh

    @pl.when(jnp.logical_not(local))
    def _():
        send_ref[...] = dh.astype(bf)

    @pl.when(step == pl.num_programs(0) - 1)
    def _():
        for k, out in enumerate(outs):
            at = pl.ds(aligned(chip ^ k, rows), rows)
            low = (chip ^ k) >> 1 == 0
            tail = [sums[0:1, at], sums[1:2, at]]
            tail += [jnp.where(low, *both(i)) for i in (4, 5)]
            tail = jnp.concatenate(tail + [jnp.zeros((1, acc.shape[1] - 4 * rows), f32)], axis=1)
            out[:rows] = acc[at, :].astype(out.dtype)
            out[rows : rows + 8] = jnp.broadcast_to(tail, (8, tail.shape[1])).astype(out.dtype)
            shard = rows // 2
            lines = go_ref[pl.ds(aligned(chip ^ k, shard), shard), :]
            lines = jnp.concatenate([lines[: shard // 2], lines[shard // 2 :]], axis=1)
            out[rows + 8 :] = lines.astype(out.dtype)


def norm_one_body(meta, x_ref, dh_keep, dh_came, resid_ref, vec_ref, out0, out1):
    turn = pl.program_id(0) ^ (meta[RANK] & 1)
    x_hat, inv_std = norm_rows(x_ref[...].astype(f32))
    e = (dh_keep[...] + dh_came[...].astype(f32)) * vec_ref[0:1, :]
    first = jnp.mean(e, axis=1, keepdims=True)
    second = jnp.mean(e * x_hat, axis=1, keepdims=True)
    grad = (resid_ref[...] + inv_std * (e - first - x_hat * second)).astype(bf)

    @pl.when(turn == 0)
    def _():
        out0[...] = grad

    @pl.when(turn == 1)
    def _():
        out1[...] = grad


def rank_bit(meta, bit):
    return (meta[RANK] >> bit) & 1


def chip_sum_body(meta, own, *refs, bit):
    *came, keep, send = refs
    half = keep.shape[1]
    for out, side in ((keep, rank_bit(meta, bit)), (send, 1 - rank_bit(meta, bit))):
        at = pl.ds(aligned(side, half), half)
        total = own[:, at]
        for ref in came:
            total = total + ref[:, at].astype(f32)
        out[...] = total.astype(out.dtype)


def chip_sum(meta, parts, name, bit):
    rows, size = parts[0].shape
    return kernel_call(functools.partial(chip_sum_body, bit=bit), name, meta, parts, [((rows, size // 2), f32), ((rows, size // 2), bf)])


def own_rows_first(total, core, shard):
    theirs = lax.dynamic_slice_in_dim(total, (1 - core) * shard, shard, 0)
    mine = lax.dynamic_slice_in_dim(total, core * shard, shard, 0)
    came = swap_core(jnp.concatenate([theirs, total[2 * shard : 2 * shard + 8]], axis=0))
    return jnp.concatenate([mine, came, total[2 * shard :]], axis=0)


def halves(meta, mine, other, bit):
    low = rank_bit(meta, bit) == 0
    return jnp.concatenate([jnp.where(low, mine, other), jnp.where(low, other, mine)], axis=1)


def both_cores(meta, own, came):
    own, came = own.astype(f32), came.astype(f32)
    return own, own + came, meta[CORE] == 0


def store_half(ref, source, at, low):
    size = 2 * ref.shape[1]
    piece = source[:, at * size : (at + 1) * size]
    ref[...] = jnp.where(low, piece[:, : size // 2], piece[:, size // 2 :])


def early_out_body(meta, mine, other, came_ref, g_up, g_down, *vec_refs):
    rows = halves(meta, mine[...], other[...], 0)
    came_rows = halves(meta, came_ref[0], came_ref[1], 0)
    shard, width = g_up.shape[0], g_down.shape[1]
    first, unit = meta[CORE] == 0, rows.shape[1] // 4
    own, came = jnp.where(first, rows[:shard], rows[shard : 2 * shard]), came_rows[:shard]
    pair = (jnp.where(first, own, came), jnp.where(first, came, own))
    for j in range(4):
        for side in (0, 1):
            at = (2 * j + side) * unit
            g_up[:, at : at + unit] = pair[side][:, j * unit : (j + 1) * unit].astype(f32)
    down = rows[2 * shard + 8 :].astype(f32)
    g_down[...] = jnp.concatenate([down[:, :width], down[:, width:]], axis=0)
    own, total, low = both_cores(meta, rows[2 * shard : 2 * shard + 1], came_rows[shard : shard + 1])
    for at, ref in enumerate(vec_refs[:3]):
        store_half(ref, total, at, low)
    vec_refs[3][...] = own[:, 6 * shard : 6 * shard + unit]


def late_out_body(meta, mine, other, g_qkv, g_rel, g_out, *vec_refs):
    rows = halves(meta, mine[...], other[...], 0)
    shard, width = g_qkv.shape[0], g_out.shape[1]
    first, hd, heads = meta[CORE] == 0, HEAD_DIM, H // 2
    own, came = rows[:shard], rows[shard : 2 * shard]
    pair = (jnp.where(first, own, came), jnp.where(first, came, own))
    cols = heads * hd
    piece = lambda h, t: pair[h & 1][:, t * cols + (h >> 1) * hd : t * cols + ((h >> 1) + 1) * hd]
    g_qkv[...] = jnp.concatenate([piece(h, t) for h in range(2 * heads) for t in range(3)], axis=1).astype(f32)
    g_rel[...] = jnp.concatenate([piece(h, 3) for h in range(2 * heads)], axis=1).astype(f32)
    out = rows[2 * shard + 16 :].astype(f32)
    g_out[...] = jnp.concatenate([out[:, :width], out[:, width:]], axis=0)
    own, total, low = both_cores(meta, rows[2 * shard + 8 : 2 * shard + 9], rows[2 * shard : 2 * shard + 1])
    even = meta[CHIP] & 1 == 0
    for at, ref in enumerate(vec_refs):
        store_half(ref, total if at < 2 else own, at, low if at < 2 else even)


def place_body(meta, y0, y1, x0, x1, y_ref, x_ref):
    high = meta[RANK] >> 1 == 1
    y_ref[0] = jnp.where(high, y1[...], y0[...])
    y_ref[1] = jnp.where(high, y0[...], y1[...])
    x_ref[0] = jnp.where(high, x1[...], x0[...]).astype(f32)
    x_ref[1] = jnp.where(high, x0[...], x1[...]).astype(f32)


def slot_split_device(
    layer_input,
    lengths,
    ln1_gain,
    ln1_bias,
    w_qkv,
    w_rel,
    bias_u,
    bias_v,
    w_out,
    ln2_gain,
    ln2_bias,
    w_up,
    up_bias,
    w_down,
    down_bias,
    grad_out,
):
    slots, block, width = layer_input.shape
    rank, device = lax.axis_index("seq"), lax.axis_index("fsdp")
    core, chip = device & 1, device >> 1
    full, heads = 4 * block, H // 2
    cols, shard, unit = heads * HEAD_DIM, width // 8, up_bias.shape[0]
    mine_ff = 4 * unit

    none = jnp.zeros((4,), jnp.int32)
    x_own = to_slots(jnp.concatenate([layer_input, grad_out], axis=2), rank)
    vectors = (ln1_gain, ln1_bias, bias_u, bias_v, ln2_gain, ln2_bias, down_bias, up_bias)
    attn_rows, fold = shard + 8, shard // 2
    attn_pack, feed_pack, pack_send = kernel_call(
        pack_body,
        "pack",
        lengths,
        [
            pltpu.with_memory_space_constraint(v, pltpu.HBM)
            for v in [w_qkv, w_rel, w_up, w_out, w_down] + [v.reshape(-1, min(128, v.size)) for v in vectors]
        ],
        [((attn_rows, 4 * cols), bf), ((3 * shard + fold, 4 * cols), bf), ((attn_rows + shard + fold, 4 * cols), bf)],
        vmem=32,
    )
    pack_came = swap_core(pack_send)
    attn_pack = jnp.concatenate([attn_pack, pack_came[:attn_rows]], axis=0)
    attn_packs = [attn_pack] + [swap_chip(attn_pack, k) for k in (1, 2, 3)]
    feed_pack = jnp.concatenate([feed_pack, pack_came[attn_rows:]], axis=0)
    digits_at = 7 * shard + unit
    digits = pack_came[shard, digits_at : digits_at + 2 * slots].astype(jnp.int32)
    lengths = jnp.where(core == rank >> 1, lengths, digits[0::2] * DIGIT + digits[1::2])
    length = jnp.where(rank & 1 == 0, lengths[0], lengths[1])
    meta = jnp.stack([core, chip, rank, length]).astype(jnp.int32)
    length_arr = length.reshape(1)
    fine = 32
    inv_freq = jnp.exp(lax.iota(f32, width // 2) * (-2.0 * math.log(10000.0) / width))
    high = (full - 1 - fine * lax.iota(jnp.int32, full // fine)).astype(f32)[:, None] * inv_freq
    low = lax.iota(f32, fine)[:, None] * inv_freq
    high_sin, high_cos, low_sin, low_cos = together(jnp.sin(high), jnp.cos(high), jnp.sin(low), jnp.cos(low))
    high_sin, high_cos = high_sin[:, None], high_cos[:, None]
    table = jnp.concatenate(
        [high_sin * low_cos - high_cos * low_sin, high_cos * low_cos + high_sin * low_sin], axis=2
    )
    table = table.astype(bf).reshape(full, width)

    feed_pack, meta, length_arr, table, *attn_packs = together(feed_pack, meta, length_arr, table, *attn_packs)
    rest = list(together(*x_own, *attn_packs))
    x_own, attn_packs = rest[:2], rest[2:]
    x_other = [swap_core(x) for x in x_own]
    feed_first = swap_axis(feed_pack, 0)
    feed_pack, x_other[1] = together(feed_pack, x_other[1])
    feed_second = swap_axis(feed_pack, 1)

    side = lambda at: pl.BlockSpec((block, width), lambda i, _: (0, at))
    by_step = lambda width: pl.BlockSpec((block, width), lambda i, _: (i, 0))
    qkv, h1, x_slot, rel, w_own, vecs, up_b, own_u, own_v = kernel_call(
        project_body,
        "project",
        none,
        [pltpu.with_memory_space_constraint(v, pltpu.HBM) for v in attn_packs + x_own + x_other + [table]],
        [((full, 3 * cols), bf), ((full, width), bf), ((full, width), bf), ((full, cols), bf)]
        + [((width, 4 * cols), bf), ((8, width), f32), ((1, mine_ff), f32), ((1, cols), f32), ((1, cols), f32)],
        grid=(4,),
        in_specs=[whole(2 * attn_rows, 4 * cols)] * 4 + [side(0)] * 4 + [by_step(width)],
        out_specs=[by_step(3 * cols), by_step(width), by_step(width), by_step(cols)]
        + [whole(width, 4 * cols), whole(8, width), whole(1, mine_ff), whole(1, cols), whole(1, cols)],
        flops=2 * full * width * 4 * cols,
        vmem=32,
    )
    qkv, feed_first = together(qkv, feed_first)
    feed_third = swap_axis(feed_first, 1)
    attn, lse = attn_fwd(length_arr, qkv, rel, own_u, own_v)
    attn, feed_second, feed_third = together(attn, feed_second, feed_third)
    feed_packs = [feed_pack, feed_first, feed_second, feed_third]

    attn_other = swap_core(attn)
    kept = lambda width: pl.BlockSpec((block, width), lambda i, _: (i >> 1, 0))
    half, rows = full // 2, 2 * shard + 8
    blocks = lambda rows: [((rows, 2 * width), f32)] + [((rows, 2 * width), bf)] * 3
    dy, x_hat, rstd, y_keep, dh, y_send, wo_mine, *early_parts = kernel_call(
        feed_body,
        "feed",
        meta,
        feed_packs + x_own + x_other + [x_slot, attn, attn_other, vecs, up_b],
        [((full, width), bf), ((full, width), bf), ((full, 1), f32), ((half, width), f32)]
        + [((full, width), bf), ((half, width), bf), ((cols, width), bf)]
        + blocks(rows + unit // 2),
        grid=(4,),
        in_specs=[whole(*feed_pack.shape)] * 4 + [side(1)] * 4
        + [by_step(width), by_step(cols), by_step(cols), whole(8, width), whole(1, mine_ff)],
        out_specs=[by_step(width), by_step(width), by_step(1), kept(width)]
        + [by_step(width), kept(width), whole(cols, width)]
        + [whole(rows + unit // 2, 2 * width)] * 4,
        scratch=[
            pltpu.VMEM((width, mine_ff), bf),
            pltpu.VMEM((mine_ff, width), bf),
            pltpu.VMEM((cols, width), bf),
            pltpu.VMEM((width, mine_ff), f32),
            pltpu.VMEM((mine_ff, width), f32),
            pltpu.VMEM((8, mine_ff), f32),
        ],
        flops=12 * full * width * mine_ff,
    )
    dh_came = swap_core(dh)
    y_came = swap_core(y_send)
    early_came = [swap_chip(early_parts[k], k) for k in (1, 2, 3)]
    out0, out1, g_resid, d_attn, g_out = kernel_call(
        norm_two_body,
        "norm_two",
        meta,
        [x_hat, rstd, dh, dh_came, dy, vecs, y_keep, y_came, wo_mine, attn],
        [((block, width), bf)] * 2 + [((half, width), f32), ((full, cols), bf), ((cols, width), f32)],
        grid=(4,),
        in_specs=[by_step(width), by_step(1)] + [by_step(width)] * 3 + [whole(8, width)] + [kept(width)] * 2
        + [whole(cols, width), by_step(cols)],
        out_specs=[whole(block, width)] * 2 + [kept(width), by_step(cols), whole(cols, width)],
        flops=4 * full * width * cols,
    )
    home = lambda outs: [
        lax.ppermute(out, ("fsdp", "seq"), [(b, a) for a, b in slot_pairs(turn)])
        for turn, out in enumerate(outs)
    ]
    y_turns = home((out0, out1))
    back = lambda pair, heads, d_out: attn_bwd(
        length_arr, qkv, rel, own_u, own_v, lse, d_out, pair=pair, heads=heads
    )
    d_attn, *grads_a = together(d_attn, *back(0, (0, 1), d_attn))
    *grads_b, y0, y1, e1, e2, e3 = together(*back(1, (0,), d_attn), *y_turns, *early_came)
    early_keep, early_send = chip_sum(meta, [early_parts[0], e1, e2, e3], "early_chips", 0)
    d_attn, early_send, early_keep = together(d_attn, early_send, early_keep)
    *grads_c, early_came = together(*back(1, (1,), d_attn), swap_seq(early_send, 1))
    early_pair = (early_keep + early_came.astype(f32)).astype(bf)
    early_pair, *grads_c = together(early_pair, *grads_c)
    early_came = swap_seq(early_pair, 2)
    pair_step = pl.BlockSpec((block, 2 * HEAD_DIM), lambda i, _: (i, 0))
    pair_row = whole(1, 2 * HEAD_DIM)
    dh1_keep, dh1_send, *late_parts = kernel_call(
        qkv_back_body,
        "qkv_back",
        meta,
        [*grads_a, *grads_b, *grads_c, w_own, x_slot, h1, table, g_out],
        [((half, width), f32), ((half, width), bf)] + blocks(rows + fold),
        grid=(4,),
        in_specs=([pair_step] * 4 + [pair_row] * 2) * 3
        + [whole(width, 4 * cols)] + [by_step(width)] * 3 + [whole(cols, width)],
        out_specs=[kept(width)] * 2 + [whole(rows + fold, 2 * width)] * 4,
        scratch=[pltpu.VMEM((width, 4 * cols), f32), pltpu.VMEM((8, width), f32)],
        flops=14 * full * width * cols,
    )
    dh1_send, *late_parts = together(dh1_send, *late_parts)
    dh1_came = swap_core(dh1_send)
    late_came = [swap_chip(late_parts[k], k) for k in (1, 2, 3)]
    by_half = pl.BlockSpec((block, width), lambda i, _: (i, 0))
    own_rows = pl.BlockSpec((block, width), lambda i, m: (2 * i + m[CORE], 0))
    x0, x1 = kernel_call(
        norm_one_body,
        "norm_one",
        meta,
        [x_slot, dh1_keep, dh1_came, g_resid, vecs],
        [((block, width), bf)] * 2,
        grid=(2,),
        in_specs=[own_rows] + [by_half] * 3 + [whole(8, width)],
        out_specs=[whole(block, width)] * 2,
    )
    x_turns = home((x0, x1))
    *late_came, early_came, _, _ = together(*late_came, early_came, x0, x1)
    early_mine = (early_pair.astype(f32) + early_came.astype(f32)).astype(bf)
    late_keep, late_send = chip_sum(meta, [late_parts[0]] + late_came, "late_chips", 0)
    small = lambda size: ((1, size), f32)
    late_came, early_mine = together(swap_seq(late_send, 1), early_mine)
    late_pair = (late_keep + late_came.astype(f32)).astype(bf)
    late_came = swap_seq(late_pair, 2)
    early_other = swap_seq(early_mine, 1)
    late_total = (late_pair.astype(f32) + late_came.astype(f32)).astype(bf)
    late_mine = own_rows_first(late_total, core, shard)
    late_other = swap_seq(late_mine, 1)
    late_mine, g0, g1, early_other = together(late_mine, *x_turns, early_other)
    theirs = lambda rows: jnp.concatenate(
        [
            lax.dynamic_slice_in_dim(rows, (1 - core) * shard, shard, 0),
            rows[2 * shard : 2 * shard + 8],
        ],
        axis=0,
    )
    early_core = swap_core(jnp.stack([theirs(early_mine), theirs(early_other)]))
    output, grad_x = kernel_call(
        place_body,
        "place",
        meta,
        [y0, y1, g0, g1],
        [((2, block, width), bf), ((2, block, width), f32)],
    )
    g_up, g_down, g_gain_two, g_shift_two, g_down_shift, g_up_shift = kernel_call(
        early_out_body,
        "early_out",
        meta,
        [early_mine, early_other, early_core],
        [((shard, 2 * mine_ff), f32), ((unit, width), f32)] + [small(shard)] * 3 + [small(unit)],
    )
    late_other, output, grad_x, g_up = together(late_other, output, grad_x, g_up)
    g_qkv, g_rel, g_w_out, *late_vectors = kernel_call(
        late_out_body,
        "late_out",
        meta,
        [late_mine, late_other],
        [((shard, 6 * cols), f32), ((shard, 2 * cols), f32), ((shard, width), f32)] + [small(shard)] * 4,
    )
    g_gain_one, g_shift_one, g_bias_u, g_bias_v = [v.reshape(-1) for v in late_vectors]
    return (
        output,
        grad_x,
        g_gain_one,
        g_shift_one,
        g_qkv,
        g_rel,
        g_bias_u,
        g_bias_v,
        g_w_out,
        g_gain_two.reshape(-1),
        g_shift_two.reshape(-1),
        g_up,
        g_up_shift.reshape(-1),
        g_down,
        g_down_shift.reshape(-1),
    )


def per_device(*args):
    one_slot_a_chip = lax.axis_size("fsdp") == 8 and lax.axis_size("seq") == 4
    if one_slot_a_chip and args[0].shape[0] == 2:
        return slot_split_device(*args)
    return head_split_device(*args)


def solution(mesh):
    placed = (
        P("fsdp", "seq", None),
        P("fsdp"),
        P("fsdp"),
        P("fsdp"),
        P("fsdp", None),
        P("fsdp", None),
        P("fsdp"),
        P("fsdp"),
        P("fsdp", None),
        P("fsdp"),
        P("fsdp"),
        P("fsdp", None),
        P("fsdp"),
        P("fsdp", None),
        P("fsdp"),
        P("fsdp", "seq", None),
    )
    return jax.shard_map(
        per_device,
        mesh=mesh,
        in_specs=placed,
        out_specs=(
            P("fsdp", "seq", None),
            P("fsdp", "seq", None),
            P("fsdp"),
            P("fsdp"),
            P("fsdp", None),
            P("fsdp", None),
            P("fsdp"),
            P("fsdp"),
            P("fsdp", None),
            P("fsdp"),
            P("fsdp"),
            P("fsdp", None),
            P("fsdp"),
            P("fsdp", None),
            P("fsdp"),
        ),
        check_vma=False,
    )
```

```python
import functools
import math

import jax
import jax.numpy as jnp
from jax import lax
from jax.experimental import pallas as pl
from jax.experimental.pallas import tpu as pltpu
from jax.sharding import PartitionSpec as P

H = 8
HEAD_DIM = 64


NEG_FILL = -1e30
NORM_EPS = 1e-05


bf, f32 = jnp.bfloat16, jnp.float32
NEG = NEG_FILL
HD = HEAD_DIM
NT = (((1,), (1,)), ((), ()))
NN = (((1,), (0,)), ((), ()))


def dot(a, b, dims):
    return lax.dot_general(a, b, dims, preferred_element_type=f32)


def masked_tail(s, keep, block):
    tail = jnp.where(keep, s[:, s.shape[1] - block :], NEG)
    if s.shape[1] == block:
        return tail
    return jnp.concatenate([s[:, : s.shape[1] - block], tail], axis=1)


def scores(qu, qv, keys, rel_rev, keep, block):
    span = keys.shape[0]
    rel = dot(qv, rel_rev, NT)
    rel = pltpu.roll(rel, (span - block + 1) % span, 1, stride=1, stride_axis=0)
    return masked_tail(dot(qu, keys, NT) + rel, keep, block)


def attn_fwd_body(len_ref, q_ref, k_ref, v_ref, r_ref, bu_ref, bv_ref, o_ref, *p_refs, block):
    full = q_ref.shape[0]
    lane = lax.broadcasted_iota(jnp.int32, (block, 2 * HD), 1)
    sides = (lane < HD, lane >= HD)
    length = len_ref[0]
    col = lax.broadcasted_iota(jnp.int32, (1, full), 1)
    bias = jnp.where(col < length, 0.0, NEG)
    tri = lax.broadcasted_iota(jnp.int32, (block, block), 1) <= lax.broadcasted_iota(
        jnp.int32, (block, block), 0
    )
    for first in range(0, full, block):
        span = first + block
        q = q_ref[first:span, :].astype(f32)
        qu = (q + bu_ref[...]).astype(bf).astype(f32) * 0.125
        qv = (q + bv_ref[...]).astype(bf).astype(f32) * 0.125
        outs = []
        for head, side in enumerate(sides):
            s = scores(
                jnp.where(side, qu, 0.0).astype(bf),
                jnp.where(side, qv, 0.0).astype(bf),
                k_ref[:span, :],
                r_ref[full - span :, :],
                tri,
                block,
            )
            s = s + bias[:, :span]
            top = jnp.max(s, axis=1, keepdims=True)
            e = jnp.exp(s - top)
            total = jnp.sum(e, axis=1, keepdims=True)
            p = (e * (1.0 / total)).astype(bf)
            p_refs[first // block][head] = p
            outs.append(dot(p, v_ref[:span, :], NN))
        o_ref[first:span, :] = jnp.where(sides[0], outs[0], outs[1]).astype(bf)


def attn_fwd(length, qkv, rel_rev, bias_u, bias_v, *, block=256):
    full, cols = rel_rev.shape
    spans = range(block, full + 1, block)
    pairs = cols // (2 * HD)
    at = lambda part: pl.BlockSpec((full, 2 * HD), lambda pair, _: (0, part * pairs + pair))
    row = pl.BlockSpec((1, 2 * HD), lambda pair, _: (0, pair))
    return pl.pallas_call(
        functools.partial(attn_fwd_body, block=block),
        out_shape=(
            jax.ShapeDtypeStruct((full, cols), bf),
            *(jax.ShapeDtypeStruct((2 * pairs, block, span), bf) for span in spans),
        ),
        grid_spec=pltpu.PrefetchScalarGridSpec(
            num_scalar_prefetch=1,
            grid=(pairs,),
            in_specs=[at(0), at(1), at(2), at(0), row, row],
            out_specs=(
                at(0),
                *(pl.BlockSpec((2, block, span), lambda pair, _: (pair, 0, 0)) for span in spans),
            ),
        ),
        cost_estimate=pl.CostEstimate(flops=0, bytes_accessed=0, transcendentals=0),
        compiler_params=pltpu.CompilerParams(vmem_limit_bytes=32 << 20),
        name="attn_fwd",
    )(length, qkv, qkv, qkv, rel_rev, bias_u, bias_v)


def attn_bwd_body(len_ref, q_ref, k_ref, v_ref, r_ref, bu_ref, bv_ref, do_ref, *refs, block, heads):
    full = q_ref.shape[0]
    p_refs, refs = refs[: full // block], refs[full // block :]
    dq_ref, dk_ref, dv_ref, dr_ref, gu_ref, gv_ref, dk_t, dv_t, dr_t = refs
    length = len_ref[0]
    lane = lax.broadcasted_iota(jnp.int32, (block, 2 * HD), 1)
    sides = (lane < HD, lane >= HD)
    rows = lax.broadcasted_iota(jnp.int32, (block, block), 0)
    cols = lax.broadcasted_iota(jnp.int32, (block, block), 1)
    flip = jnp.where(rows + cols == block - 1, 1.0, 0.0).astype(bf)
    for ref in (dk_t, dv_t, dr_t, dq_ref, gu_ref, gv_ref):
        ref[...] = jnp.zeros_like(ref)
    for first in range(0, full, block):
        span = first + block

        @pl.when(first < length)
        def _():
            q = q_ref[first:span, :].astype(f32)
            qu = (q + bu_ref[...]).astype(bf).astype(f32) * 0.125
            qv = (q + bv_ref[...]).astype(bf).astype(f32) * 0.125
            do = do_ref[first:span, :].astype(f32)
            qu_t = jnp.transpose(qu).astype(bf)
            do_t = jnp.transpose(do).astype(bf)
            qv_t = jnp.transpose(dot(flip, qv.astype(bf), NN)).astype(bf)
            dqu, dqv = [0.0, 0.0], [0.0, 0.0]
            for head in heads:
                side = sides[head]
                at = slice(head * HD, (head + 1) * HD)
                rounded = p_refs[first // block][head - heads[0]]
                p = rounded.astype(f32)
                dp = dot(jnp.where(side, do, 0.0).astype(bf), v_ref[:span, :], NT)
                t = p * dp
                ds = (t - p * jnp.sum(t, axis=1, keepdims=True)).astype(bf)
                dv_t[at, :span] += dot(do_t[at], rounded, NN)
                both = dot(jnp.concatenate([qu_t[at], flip], axis=0), ds, NN)
                dk_t[at, :span] += both[:HD]
                dqu[head] = dot(ds, k_ref[:span, :], NN)
                ds_rev = pltpu.roll(both[HD:], 0, 1, stride=1, stride_axis=0).astype(bf)
                dr_t[at, full - span :] += dot(qv_t[at], ds_rev, NN)
                dqv[head] = dot(ds_rev, r_ref[full - span :, :], NN)
            dqu = jnp.where(sides[0], dqu[0], dqu[1]) * 0.125
            dqv = jnp.where(sides[0], dqv[0], dqv[1]) * 0.125
            gu_ref[...] += jnp.sum(dqu, axis=0, keepdims=True)
            gv_ref[...] += jnp.sum(dqv, axis=0, keepdims=True)
            dq_ref[first:span, :] = (dqu + dot(flip, dqv.astype(bf), NN)).astype(bf)

    dk_ref[...] = jnp.transpose(dk_t[...]).astype(bf)
    dv_ref[...] = jnp.transpose(dv_t[...]).astype(bf)
    dr_ref[...] = jnp.transpose(dr_t[...]).astype(bf)


def attn_bwd(length, qkv, rel_rev, bias_u, bias_v, probs, d_out, *, pair, heads=(0, 1), block=256):
    full, cols = rel_rev.shape
    pairs = cols // (2 * HD)
    at = lambda part: pl.BlockSpec((full, 2 * HD), lambda i, _: (0, part * pairs + pair))
    row = pl.BlockSpec((1, 2 * HD), lambda i, _: (0, pair))
    out = pl.BlockSpec((full, 2 * HD), lambda i, _: (0, 0))
    out_row = pl.BlockSpec((1, 2 * HD), lambda i, _: (0, 0))
    return pl.pallas_call(
        functools.partial(attn_bwd_body, block=block, heads=heads),
        out_shape=(jax.ShapeDtypeStruct((full, 2 * HD), bf),) * 4
        + (jax.ShapeDtypeStruct((1, 2 * HD), f32),) * 2,
        grid_spec=pltpu.PrefetchScalarGridSpec(
            num_scalar_prefetch=1,
            grid=(1,),
            in_specs=[at(0), at(1), at(2), at(0), row, row]
            + [at(0)]
            + [
                pl.BlockSpec((len(heads),) + p.shape[1:], lambda i, _: ((2 * pair + heads[0]) // len(heads), 0, 0))
                for p in probs
            ],
            out_specs=(out,) * 4 + (out_row, out_row),
            scratch_shapes=[pltpu.VMEM((2 * HD, full), f32)] * 3,
        ),
        cost_estimate=pl.CostEstimate(flops=0, bytes_accessed=0, transcendentals=0),
        compiler_params=pltpu.CompilerParams(vmem_limit_bytes=32 << 20),
        name="attn_bwd",
    )(length, qkv, qkv, qkv, rel_rev, bias_u, bias_v, d_out, *probs)


def norm_parts(values):
    mean_val = jnp.mean(values, axis=-1, keepdims=True)
    centered = values - mean_val
    inv_std = lax.rsqrt(jnp.mean(centered * centered, axis=-1, keepdims=True) + NORM_EPS)
    return (centered * inv_std, inv_std)


def norm_back(grad_norm, x_hat, inv_std):
    first_mean = jnp.mean(grad_norm, axis=-1, keepdims=True)
    second_mean = jnp.mean(grad_norm * x_hat, axis=-1, keepdims=True)
    return inv_std * (grad_norm - first_mean - x_hat * second_mean)


def position_table(count_rows, feature_count):
    steps = lax.iota(jnp.float32, count_rows)
    half_count = feature_count // 2
    inv_freq = jnp.exp(
        lax.iota(jnp.float32, half_count) * (-2.0 * math.log(10000.0) / feature_count)
    )
    angles = steps[:, None] * inv_freq[None, :]
    return jnp.concatenate([jnp.sin(angles), jnp.cos(angles)], axis=1)


def skew_rows(matrix):
    leading = matrix.shape[:-2]
    row_count, col_count = matrix.shape[-2:]
    flattened = matrix.reshape(leading + (row_count * col_count,))
    picked = flattened[..., row_count - 1 : row_count - 1 + row_count * (col_count - 1)]
    return picked.reshape(leading + (row_count, col_count - 1))[..., : col_count - row_count]


def unskew_rows(matrix):
    leading = matrix.shape[:-2]
    row_count, key_count = matrix.shape[-2:]
    axis_pos = len(leading)
    widened = jnp.pad(matrix, [(0, 0)] * axis_pos + [(0, 0), (0, row_count - 1)])
    flattened = widened.reshape(leading + (row_count * (key_count + row_count - 1),))
    flattened = jnp.pad(flattened, [(0, 0)] * axis_pos + [(row_count - 1, 1)])
    return flattened.reshape(leading + (row_count, key_count + row_count))


def head_split_device(
    layer_input,
    lengths,
    ln1_gain,
    ln1_bias,
    w_qkv,
    w_rel,
    bias_u,
    bias_v,
    w_out,
    ln2_gain,
    ln2_bias,
    w_up,
    up_bias,
    w_down,
    down_bias,
    grad_out,
):
    weights = (
        lax.all_gather(ln1_gain, "fsdp", axis=0, tiled=True),
        lax.all_gather(ln1_bias, "fsdp", axis=0, tiled=True),
        lax.all_gather(w_qkv, "fsdp", axis=0, tiled=True),
        lax.all_gather(w_rel, "fsdp", axis=0, tiled=True),
        lax.all_gather(bias_u, "fsdp", axis=0, tiled=True),
        lax.all_gather(bias_v, "fsdp", axis=0, tiled=True),
        lax.all_gather(w_out, "fsdp", axis=0, tiled=True),
        lax.all_gather(ln2_gain, "fsdp", axis=0, tiled=True),
        lax.all_gather(ln2_bias, "fsdp", axis=0, tiled=True),
        lax.all_gather(w_up, "fsdp", axis=0, tiled=True),
        lax.all_gather(up_bias, "fsdp", axis=0, tiled=True),
        lax.all_gather(w_down, "fsdp", axis=0, tiled=True),
        lax.all_gather(down_bias, "fsdp", axis=0, tiled=True),
    )
    (
        gain_one,
        shift_one,
        query_key_value_matrix,
        rel_weight,
        first_bias,
        second_bias,
        output_matrix,
        gain_two,
        shift_two,
        up_matrix,
        up_shift,
        down_matrix,
        down_shift,
    ) = weights
    gain_one = gain_one.astype(jnp.float32)
    shift_one = shift_one.astype(jnp.float32)
    gain_two = gain_two.astype(jnp.float32)
    shift_two = shift_two.astype(jnp.float32)
    up_shift = up_shift.astype(jnp.float32)
    down_shift = down_shift.astype(jnp.float32)
    slots, block_len, width = layer_input.shape
    seq_count = lax.axis_size("seq")
    seq_rank = lax.axis_index("seq")
    head_dim = HEAD_DIM
    group = H // seq_count
    full_len = block_len * seq_count
    score_scale = 1.0 / math.sqrt(head_dim)
    q_block = 512
    num_blocks = full_len // q_block
    win_len = full_len + q_block
    x_float = layer_input.astype(jnp.float32)
    x_hat_one, inv_std_one = norm_parts(x_float)
    first_normalized = (x_hat_one * gain_one + shift_one).astype(jnp.bfloat16)
    qkv_local = jnp.einsum(
        "mcr,rk->mck", first_normalized, query_key_value_matrix, preferred_element_type=jnp.float32
    ).astype(jnp.bfloat16)
    qkv_heads = lax.all_to_all(qkv_local, "seq", split_axis=2, concat_axis=1, tiled=True)
    qkv_heads = qkv_heads.reshape(slots, full_len, group, 3, head_dim)
    queries = qkv_heads[:, :, :, 0]
    keys = qkv_heads[:, :, :, 1]
    values = qkv_heads[:, :, :, 2]
    head_start = seq_rank * group
    head_bias_u = lax.dynamic_slice_in_dim(
        first_bias.astype(jnp.float32).reshape(H, head_dim), head_start, group, 0
    )
    head_bias_v = lax.dynamic_slice_in_dim(
        second_bias.astype(jnp.float32).reshape(H, head_dim), head_start, group, 0
    )
    query_u = (queries.astype(jnp.float32) + head_bias_u).astype(jnp.bfloat16)
    query_v = (queries.astype(jnp.float32) + head_bias_v).astype(jnp.bfloat16)
    table_rev = position_table(full_len, width).astype(jnp.bfloat16)[::-1]
    rel_cols = lax.dynamic_slice_in_dim(rel_weight, head_start * head_dim, group * head_dim, 1)
    rel_rev = jnp.dot(table_rev, rel_cols, preferred_element_type=jnp.float32).astype(jnp.bfloat16)
    rel_ext = jnp.concatenate([rel_rev, jnp.zeros_like(rel_rev)], axis=0).reshape(
        2 * full_len, group, head_dim
    )
    col_ids = lax.iota(jnp.int32, full_len)

    def scores_block(first_row):
        qu_part = lax.dynamic_slice_in_dim(query_u, first_row, q_block, 1)
        qv_part = lax.dynamic_slice_in_dim(query_v, first_row, q_block, 1)
        window_start = full_len - q_block - first_row
        rel_win = lax.dynamic_slice_in_dim(rel_ext, window_start, win_len, 0)
        content = jnp.einsum("sqhe,skhe->shqk", qu_part, keys, preferred_element_type=jnp.float32)
        rel_raw = jnp.einsum("sqhe,the->shqt", qv_part, rel_win, preferred_element_type=jnp.float32)
        rel_part = skew_rows(rel_raw)
        row_ids = first_row + lax.iota(jnp.int32, q_block)
        causal = col_ids[None, :] <= row_ids[:, None]
        inside = col_ids[None, :] < lengths[:, None]
        allowed = causal[None, None, :, :] & inside[:, None, None, :]
        scores = jnp.where(allowed, (content + rel_part) * score_scale, NEG_FILL)
        return (scores, qu_part, qv_part, rel_win, window_start)

    def forward_block(block_index):
        first_row = block_index * q_block
        scores, qu_part, qv_part, rel_win, window_start = scores_block(first_row)
        top = jnp.max(scores, axis=-1, keepdims=True)
        expo = jnp.exp(scores - top)
        total = jnp.sum(expo, axis=-1, keepdims=True)
        probs = (expo / total).astype(jnp.bfloat16)
        out_part = jnp.einsum(
            "shqk,skhe->sqhe", probs, values, preferred_element_type=jnp.float32
        ).astype(jnp.bfloat16)
        return (out_part, top[..., 0] + jnp.log(total[..., 0]))

    block_outs, block_lse = lax.map(forward_block, jnp.arange(num_blocks, dtype=jnp.int32))
    attn_heads = jnp.moveaxis(block_outs, 0, 1).reshape(slots, full_len, group * head_dim)
    attention_sequence = lax.all_to_all(attn_heads, "seq", split_axis=1, concat_axis=2, tiled=True)
    attention_projected = jnp.einsum(
        "mcr,rk->mck", attention_sequence, output_matrix, preferred_element_type=jnp.float32
    )
    resid = x_float + attention_projected
    x_hat_two, inv_std_two = norm_parts(resid)
    second_normalized = (x_hat_two * gain_two + shift_two).astype(jnp.bfloat16)
    pre_act = (
        jnp.einsum("oka,ac->okc", second_normalized, up_matrix, preferred_element_type=jnp.float32)
        + up_shift
    )
    normal_cdf = 0.5 * (1.0 + lax.erf(pre_act * (1.0 / math.sqrt(2.0))))
    hidden_state = (pre_act * normal_cdf).astype(jnp.bfloat16)
    down_proj = (
        jnp.einsum("zcp,pr->zcr", hidden_state, down_matrix, preferred_element_type=jnp.float32)
        + down_shift
    )
    output = (resid + down_proj).astype(jnp.bfloat16)
    positions = seq_rank * block_len + lax.iota(jnp.int32, block_len)
    live = (positions[None, :] < lengths[:, None]).astype(jnp.bfloat16)
    result_gradient = grad_out * live[:, :, None]
    grad_y_float = result_gradient.astype(jnp.float32)
    g_down_shift = jnp.sum(grad_y_float, axis=(0, 1))
    down_gradient = jnp.einsum(
        "hki,hku->iu", hidden_state, result_gradient, preferred_element_type=jnp.float32
    )
    hidden_gradient = jnp.einsum(
        "gvu,ju->gvj", result_gradient, down_matrix, preferred_element_type=jnp.float32
    )
    deriv = normal_cdf + pre_act * jnp.exp(-0.5 * pre_act * pre_act) * (
        1.0 / math.sqrt(2.0 * math.pi)
    )
    preactivation_gradient = (hidden_gradient * deriv).astype(jnp.bfloat16)
    g_up_shift = jnp.sum(preactivation_gradient.astype(jnp.float32), axis=(0, 1))
    up_gradient = jnp.einsum(
        "oiz,oix->zx", second_normalized, preactivation_gradient, preferred_element_type=jnp.float32
    )
    second_norm_gradient = jnp.einsum(
        "rau,ku->rak", preactivation_gradient, up_matrix, preferred_element_type=jnp.float32
    )
    g_gain_two = jnp.sum(second_norm_gradient * x_hat_two, axis=(0, 1))
    g_shift_two = jnp.sum(second_norm_gradient, axis=(0, 1))
    g_resid = grad_y_float + norm_back(second_norm_gradient * gain_two, x_hat_two, inv_std_two)
    attention_gradient = g_resid.astype(jnp.bfloat16)
    output_gradient = jnp.einsum(
        "zau,zam->um", attention_sequence, attention_gradient, preferred_element_type=jnp.float32
    )
    g_attn_seq = jnp.einsum(
        "urz,jz->urj", attention_gradient, output_matrix, preferred_element_type=jnp.float32
    ).astype(jnp.bfloat16)
    g_attn_heads = lax.all_to_all(
        g_attn_seq, "seq", split_axis=2, concat_axis=1, tiled=True
    ).reshape(slots, full_len, group, head_dim)

    def backward_block(carry, block_index):
        g_keys, g_vals, g_ext = carry
        first_row = block_index * q_block
        scores, qu_part, qv_part, rel_win, window_start = scores_block(first_row)
        probs = jnp.exp(scores - block_lse[block_index][..., None])
        d_out = lax.dynamic_slice_in_dim(g_attn_heads, first_row, q_block, 1)
        g_vals = g_vals + jnp.einsum(
            "shqk,sqhe->skhe", probs.astype(jnp.bfloat16), d_out, preferred_element_type=jnp.float32
        )
        g_probs = jnp.einsum("sqhe,skhe->shqk", d_out, values, preferred_element_type=jnp.float32)
        inner = jnp.sum(probs * g_probs, axis=-1, keepdims=True)
        g_scores = (probs * (g_probs - inner)).astype(jnp.bfloat16)
        g_qu = (
            jnp.einsum("shqk,skhe->sqhe", g_scores, keys, preferred_element_type=jnp.float32)
            * score_scale
        )
        g_keys = (
            g_keys
            + jnp.einsum("shqk,sqhe->skhe", g_scores, qu_part, preferred_element_type=jnp.float32)
            * score_scale
        )
        g_wide = unskew_rows(g_scores)
        g_qv = (
            jnp.einsum("shqt,the->sqhe", g_wide, rel_win, preferred_element_type=jnp.float32)
            * score_scale
        )
        g_win = (
            jnp.einsum("shqt,sqhe->sthe", g_wide, qv_part, preferred_element_type=jnp.float32)
            * score_scale
        )
        g_old = lax.dynamic_slice_in_dim(g_ext, window_start, win_len, 1)
        g_ext = lax.dynamic_update_slice_in_dim(g_ext, g_old + g_win, window_start, 1)
        return ((g_keys, g_vals, g_ext), (g_qu, g_qv))

    zero_heads = jnp.zeros((slots, full_len, group, head_dim), jnp.float32)
    zero_ext = jnp.zeros((slots, 2 * full_len, group, head_dim), jnp.float32)
    (g_keys, g_vals, g_ext), (g_qu_blocks, g_qv_blocks) = lax.scan(
        backward_block, (zero_heads, zero_heads, zero_ext), jnp.arange(num_blocks, dtype=jnp.int32)
    )
    g_qu = jnp.moveaxis(g_qu_blocks, 0, 1).reshape(slots, full_len, group, head_dim)
    g_qv = jnp.moveaxis(g_qv_blocks, 0, 1).reshape(slots, full_len, group, head_dim)
    g_queries = g_qu + g_qv
    g_bias_u_heads = jnp.sum(g_qu, axis=(0, 1))
    g_bias_v_heads = jnp.sum(g_qv, axis=(0, 1))
    g_qkv_heads = (
        jnp.stack([g_queries, g_keys, g_vals], axis=3)
        .astype(jnp.bfloat16)
        .reshape(slots, full_len, group * 3 * head_dim)
    )
    query_key_value_gradient = lax.all_to_all(
        g_qkv_heads, "seq", split_axis=1, concat_axis=2, tiled=True
    )
    g_rel_low = g_ext[:, :full_len].astype(jnp.bfloat16)
    g_rel_heads = jnp.einsum(
        "td,sthe->dhe", table_rev, g_rel_low, preferred_element_type=jnp.float32
    ).reshape(width, group * head_dim)
    g_rel_weight = lax.dynamic_update_slice_in_dim(
        jnp.zeros((width, width), jnp.float32), g_rel_heads, head_start * head_dim, 1
    )
    g_bias_u = lax.dynamic_update_slice_in_dim(
        jnp.zeros((H, head_dim), jnp.float32), g_bias_u_heads, head_start, 0
    ).reshape(width)
    g_bias_v = lax.dynamic_update_slice_in_dim(
        jnp.zeros((H, head_dim), jnp.float32), g_bias_v_heads, head_start, 0
    ).reshape(width)
    query_key_value_weight_gradient = jnp.einsum(
        "zau,zam->um",
        first_normalized,
        query_key_value_gradient,
        preferred_element_type=jnp.float32,
    )
    first_norm_gradient = jnp.einsum(
        "urz,jz->urj",
        query_key_value_gradient,
        query_key_value_matrix,
        preferred_element_type=jnp.float32,
    )
    g_gain_one = jnp.sum(first_norm_gradient * x_hat_one, axis=(0, 1))
    g_shift_one = jnp.sum(first_norm_gradient, axis=(0, 1))
    g_input = g_resid + norm_back(first_norm_gradient * gain_one, x_hat_one, inv_std_one)
    partial_shards = (
        lax.psum_scatter(g_gain_one, "fsdp", scatter_dimension=0, tiled=True),
        lax.psum_scatter(g_shift_one, "fsdp", scatter_dimension=0, tiled=True),
        lax.psum_scatter(query_key_value_weight_gradient, "fsdp", scatter_dimension=0, tiled=True),
        lax.psum_scatter(g_rel_weight, "fsdp", scatter_dimension=0, tiled=True),
        lax.psum_scatter(g_bias_u, "fsdp", scatter_dimension=0, tiled=True),
        lax.psum_scatter(g_bias_v, "fsdp", scatter_dimension=0, tiled=True),
        lax.psum_scatter(output_gradient, "fsdp", scatter_dimension=0, tiled=True),
        lax.psum_scatter(g_gain_two, "fsdp", scatter_dimension=0, tiled=True),
        lax.psum_scatter(g_shift_two, "fsdp", scatter_dimension=0, tiled=True),
        lax.psum_scatter(up_gradient, "fsdp", scatter_dimension=0, tiled=True),
        lax.psum_scatter(g_up_shift, "fsdp", scatter_dimension=0, tiled=True),
        lax.psum_scatter(down_gradient, "fsdp", scatter_dimension=0, tiled=True),
        lax.psum_scatter(g_down_shift, "fsdp", scatter_dimension=0, tiled=True),
    )
    shards = lax.psum(
        (
            partial_shards[0],
            partial_shards[1],
            partial_shards[2],
            partial_shards[3],
            partial_shards[4],
            partial_shards[5],
            partial_shards[6],
            partial_shards[7],
            partial_shards[8],
            partial_shards[9],
            partial_shards[10],
            partial_shards[11],
            partial_shards[12],
        ),
        "seq",
    )
    return (
        output,
        g_input,
        shards[0],
        shards[1],
        shards[2],
        shards[3],
        shards[4],
        shards[5],
        shards[6],
        shards[7],
        shards[8],
        shards[9],
        shards[10],
        shards[11],
        shards[12],
    )


def swap_core(values):
    size = lax.axis_size("fsdp")
    return lax.ppermute(values, "fsdp", [(i, i ^ 1) for i in range(size)])


def swap_chip(values, mask):
    size = lax.axis_size("fsdp")
    return lax.ppermute(values, "fsdp", [(i, i ^ (2 * mask)) for i in range(size)])


def swap_axis(values, turn):
    size = lax.axis_size("fsdp")
    return lax.ppermute(values, "fsdp", [(i, i ^ (2 << ((i & 1) ^ turn))) for i in range(size)])


def swap_seq(values, mask):
    size = lax.axis_size("seq")
    return lax.ppermute(values, "seq", [(i, i ^ mask) for i in range(size)])


def slot_pairs(turn):
    seq, pairs = lax.axis_size("seq"), []
    for f in range(lax.axis_size("fsdp")):
        for z in range(seq):
            to_f, to_z = (f & ~1) | (z & 1), 2 * (f & 1) + (turn ^ (z >> 1))
            pairs.append((f * seq + z, to_f * seq + to_z))
    return pairs


def to_slots(values, seq_rank):
    return [
        lax.ppermute(
            lax.dynamic_index_in_dim(values, turn ^ (seq_rank >> 1), 0, keepdims=False),
            ("fsdp", "seq"),
            slot_pairs(turn),
        )
        for turn in (0, 1)
    ]


def together(*values):
    return lax.optimization_barrier(values)


def whole(*shape):
    return pl.BlockSpec(shape, lambda *_: (0,) * len(shape))


def kernel_call(body, name, meta, args, outs, *, grid=(1,), in_specs=None, out_specs=None, scratch=(), flops=0, vmem=32):
    in_specs = in_specs or [whole(*a.shape) for a in args]
    out_specs = out_specs or [whole(*shape) for shape, _ in outs]
    moved = sum(a.size * a.dtype.itemsize for a in args)
    moved += sum(math.prod(shape) * jnp.dtype(kind).itemsize for shape, kind in outs)
    return pl.pallas_call(
        body,
        out_shape=[jax.ShapeDtypeStruct(shape, kind) for shape, kind in outs],
        grid_spec=pltpu.PrefetchScalarGridSpec(
            num_scalar_prefetch=1,
            grid=grid,
            in_specs=in_specs,
            out_specs=out_specs,
            scratch_shapes=scratch,
        ),
        compiler_params=pltpu.CompilerParams(vmem_limit_bytes=vmem << 20),
        cost_estimate=pl.CostEstimate(flops=0, bytes_accessed=0, transcendentals=0),
        name=name,
    )(meta, *args)


TN = (((0,), (0,)), ((), ()))
CORE, CHIP, RANK, LIVE = range(4)
DIGIT = 128


def aligned(index, size):
    return pl.multiple_of(index * size, size)


def own_place():
    device = lax.axis_index("fsdp")
    return device & 1, device >> 1, lax.axis_index("seq")


def pack_body(lengths_ref, qkv_ref, rel_ref, up_ref, out_ref, down_ref, *refs):
    small, (attn_ref, feed_ref, send_ref) = refs[:8], refs[8:]
    core, _, _ = own_place()
    shard = qkv_ref.shape[0]
    qkv, rel, up, out, down = qkv_ref[...], rel_ref[...], up_ref[...], out_ref[...], down_ref[...]
    heads, hd = rel.shape[1] // HEAD_DIM // 2, HEAD_DIM
    unit = up.shape[1] // 8
    packs, ups = [], []
    row = jnp.concatenate([ref[i : i + 1] for ref in small for i in range(ref.shape[0])], axis=1)
    lane = lax.broadcasted_iota(jnp.int32, (1, 4 * heads * hd - row.shape[1]), 1)
    digits = jnp.zeros(lane.shape, f32)
    for slot in range(lengths_ref.shape[0]):
        high = lengths_ref[slot] // DIGIT
        for at, digit in ((2 * slot, high), (2 * slot + 1, lengths_ref[slot] - high * DIGIT)):
            digits = jnp.where(lane == at, digit.astype(f32), digits)
    row = jnp.concatenate([row, digits.astype(row.dtype)], axis=1)
    rows = jnp.broadcast_to(row, (8, row.shape[1]))
    for side in (0, 1):
        parts = [
            qkv[:, ((2 * j + side) * 3 + t) * hd : ((2 * j + side) * 3 + t + 1) * hd]
            for t in range(3)
            for j in range(heads)
        ]
        parts += [rel[:, (2 * j + side) * hd : (2 * j + side + 1) * hd] for j in range(heads)]
        packs.append(jnp.concatenate(parts, axis=1))
        ups.append(
            jnp.concatenate([up[:, (2 * j + side) * unit : (2 * j + side + 1) * unit] for j in range(4)], axis=1)
        )
    first = core == 0
    folded = jnp.concatenate([out[: shard // 2], out[shard // 2 :]], axis=1)
    attn_ref[:shard] = jnp.where(first, packs[0], packs[1])
    attn_ref[shard:] = rows
    send_ref[:shard] = jnp.where(first, packs[1], packs[0])
    send_ref[shard : shard + 8] = rows
    send_ref[shard + 8 : 2 * shard + 8] = jnp.where(first, ups[1], ups[0])
    send_ref[2 * shard + 8 :] = folded
    feed_ref[:shard] = jnp.where(first, ups[0], ups[1])
    feed_ref[shard : shard + shard // 2] = folded
    feed_ref[shard + shard // 2 :] = jnp.concatenate([down[: 2 * shard], down[2 * shard :]], axis=1)


def ordered(core, own, other):
    first = core == 0
    return jnp.concatenate([jnp.where(first, own, other), jnp.where(first, other, own)], axis=0)


def slot_block(core, rank, step, own, other, store):
    turn = (step >> 1) ^ (rank & 1)
    local = (step & 1) == core
    for t in (0, 1):
        pl.when(local & (turn == t))(functools.partial(store, own[t]))
        pl.when(jnp.logical_not(local) & (turn == t))(functools.partial(store, other[t]))


def norm_rows(values):
    mean_val = jnp.mean(values, axis=1, keepdims=True)
    centered = values - mean_val
    inv_std = lax.rsqrt(jnp.mean(centered * centered, axis=1, keepdims=True) + NORM_EPS)
    return centered * inv_std, inv_std


def project_body(_, *refs):
    packs, own_x, other_x = refs[0:4], refs[4:6], refs[6:8]
    table_ref, qkv_ref, h_ref, x_ref, rel_ref, w_ref, vec_ref, up_ref, *bias_refs = refs[8:18]
    step, (core, chip, rank) = pl.program_id(0), own_place()
    width = w_ref.shape[0]
    shard = width // 8
    span = qkv_ref.shape[1]
    cols = span // 3

    @pl.when(step == 0)
    def _():
        first = core == 0
        vec_ref[...] = jnp.zeros_like(vec_ref)
        own_rows = []
        for k in range(4):
            at = pl.ds(aligned(chip ^ k, 2 * shard), 2 * shard)
            own, other = packs[k][: shard + 8], packs[k][shard + 8 :]
            w_ref[at, :] = ordered(core, own[:shard], other[:shard])
            own_row, other_row = own[shard : shard + 1].astype(f32), other[shard : shard + 1].astype(f32)
            own_rows.append(own_row)
            low, high = jnp.where(first, own_row, other_row), jnp.where(first, other_row, own_row)
            for row, source in enumerate((0, 1, 4, 5, 6)):
                piece = slice(source * shard, (source + 1) * shard)
                vec_ref[row : row + 1, at] = jnp.concatenate([low[:, piece], high[:, piece]], axis=1)
            unit = up_ref.shape[1] // 4
            up_ref[:, pl.ds(aligned(chip ^ k, unit), unit)] = own_row[:, 7 * shard : 7 * shard + unit]
        even = chip & 1 == 0
        for k in (0, 2):
            at = pl.ds(aligned((chip ^ k) >> 1, 2 * shard), 2 * shard)
            low = jnp.where(even, own_rows[k], own_rows[k + 1])
            high = jnp.where(even, own_rows[k + 1], own_rows[k])
            for row, source in enumerate((2, 3)):
                piece = slice(source * shard, (source + 1) * shard)
                bias_refs[row][:, at] = jnp.concatenate([low[:, piece], high[:, piece]], axis=1)

    def copy(ref):
        x_ref[...] = ref[...]

    slot_block(core, rank, step, own_x, other_x, copy)
    x_hat, _ = norm_rows(x_ref[...].astype(f32))
    h = (x_hat * vec_ref[0:1, :] + vec_ref[1:2, :]).astype(bf)
    h_ref[...] = h
    qkv_ref[...] = dot(h, w_ref[:, :span], NN).astype(bf)
    rel_ref[...] = dot(table_ref[...], w_ref[:, span:], NN).astype(bf)


def feed_body(meta, *refs):
    packs, own_g, other_g = refs[0:4], refs[4:6], refs[6:8]
    x_ref, o_own, o_other, vec_ref, bias_ref = refs[8:13]
    dy_ref, x_hat_ref, rstd_ref, y_keep, dh_ref, y_send, wo_mine = refs[13:20]
    outs = refs[20:24]
    up_w, down_w, wo_theirs, up_acc, down_acc, sums = refs[24:30]
    step, chip, core = pl.program_id(0), meta[CHIP], meta[CORE]
    width = up_w.shape[0]
    shard, unit, block = width // 8, down_w.shape[0] // 4, x_ref.shape[0]
    fold = shard // 2
    unfold = lambda rows: jnp.concatenate([rows[:, :width], rows[:, width:]], axis=0)

    @pl.when(step == 0)
    def _():
        sums[...] = jnp.zeros_like(sums)
        up_acc[...] = jnp.zeros_like(up_acc)
        down_acc[...] = jnp.zeros_like(down_acc)
        masks = (0, 1 + core, 2 - core, 3)
        for pack_ref, k in zip(packs, masks):
            pack, other = pack_ref[: 3 * shard + fold], pack_ref[3 * shard + fold :]
            up_w[pl.ds(aligned(chip ^ k, 2 * shard), 2 * shard), :] = ordered(core, pack[:shard], other[:shard])
            at = pl.ds(aligned(chip ^ k, shard), shard)
            wo_mine[at, :] = unfold(pack[shard : shard + fold])
            wo_theirs[at, :] = unfold(other[shard:])
            down_w[pl.ds(aligned(chip ^ k, unit), unit), :] = unfold(pack[shard + fold :])

    at = step * block + lax.broadcasted_iota(jnp.int32, (block, 1), 0)

    def load(ref):
        dy_ref[...] = jnp.where(at < meta[LIVE], ref[...].astype(f32), 0.0).astype(bf)

    slot_block(core, meta[RANK], step, own_g, other_g, load)
    y1 = x_ref[...].astype(f32) + (dot(o_own[...], wo_mine[...], NN) + dot(o_other[...], wo_theirs[...], NN))
    x_hat, inv_std = norm_rows(y1)
    x_hat_ref[...] = x_hat.astype(bf)
    rstd_ref[...] = inv_std
    h = (x_hat * vec_ref[2:3, :] + vec_ref[3:4, :]).astype(bf)
    f = dot(h, up_w[...], NN) + bias_ref[...]
    cdf = 0.5 * (1.0 + lax.erf(f * (1.0 / math.sqrt(2.0))))
    g = (f * cdf).astype(bf)
    dy = dy_ref[...]
    dg = dot(dy, down_w[...], NT)
    df = (dg * (cdf + f * jnp.exp(-0.5 * f * f) * (1.0 / math.sqrt(2.0 * math.pi)))).astype(bf)
    z = dot(g, down_w[...], NN)
    dh = dot(df, up_w[...], NT)
    dh_ref[...] = dh.astype(bf)
    up_acc[...] += dot(h, df, TN)
    down_acc[...] += dot(g, dy, TN)
    sums[0:1, :width] += jnp.sum(dh * x_hat, axis=0, keepdims=True)
    sums[1:2, :width] += jnp.sum(dh, axis=0, keepdims=True)
    sums[3:4, :] += jnp.sum(df.astype(f32), axis=0, keepdims=True)
    local = (step & 1) == core

    @pl.when(local)
    def _():
        y_keep[...] = y1 + z + vec_ref[4:5, :]
        sums[2:3, :width] += jnp.sum(dy.astype(f32), axis=0, keepdims=True)

    @pl.when(jnp.logical_not(local))
    def _():
        y_send[...] = z.astype(bf)

    @pl.when(step == pl.num_programs(0) - 1)
    def _():
        rows = 2 * shard
        for k, out in enumerate(outs):
            at = pl.ds(aligned(chip ^ k, rows), rows)
            units = pl.ds(aligned(chip ^ k, unit), unit)
            tail = [sums[0:1, at], sums[1:2, at], sums[2:3, at], sums[3:4, units]]
            tail = jnp.concatenate(tail + [jnp.zeros((1, sums.shape[1] - 3 * rows - unit), f32)], axis=1)
            out[:rows] = up_acc[at, :].astype(out.dtype)
            out[rows : rows + 8] = jnp.broadcast_to(tail, (8, tail.shape[1])).astype(out.dtype)
            down = down_acc[units, :]
            half = unit // 2
            out[rows + 8 :] = jnp.concatenate([down[:half], down[half:]], axis=1).astype(out.dtype)


def norm_two_body(meta, x_hat_ref, rstd_ref, dh_ref, dh_came, dy_ref, vec_ref, y_keep, y_came, wo_ref, o_ref, *refs):
    out0, out1, resid_ref, do_ref, go_ref = refs
    step = pl.program_id(0)

    @pl.when(step == 0)
    def _():
        go_ref[...] = jnp.zeros_like(go_ref)

    x_hat = x_hat_ref[...].astype(f32)
    e = (dh_ref[...].astype(f32) + dh_came[...].astype(f32)) * vec_ref[2:3, :]
    first = jnp.mean(e, axis=1, keepdims=True)
    second = jnp.mean(e * x_hat, axis=1, keepdims=True)
    grad = dy_ref[...].astype(f32) + rstd_ref[...] * (e - first - x_hat * second)
    da = grad.astype(bf)
    do_ref[...] = dot(da, wo_ref[...], NT).astype(bf)
    go_ref[...] += dot(o_ref[...], da, TN)
    turn = (step >> 1) ^ (meta[RANK] & 1)
    local = (step & 1) == meta[CORE]

    @pl.when(local)
    def _():
        resid_ref[...] = grad
        y = (y_keep[...] + y_came[...].astype(f32)).astype(bf)

        @pl.when(turn == 0)
        def _():
            out0[...] = y

        @pl.when(turn == 1)
        def _():
            out1[...] = y


def qkv_back_body(meta, *refs):
    grads_a, grads_b = refs[:6], refs[6:12]
    w_ref, x_ref, h_ref, table_ref, go_ref = refs[12:17]
    keep_ref, send_ref = refs[17:19]
    outs, acc, sums = refs[19:23], refs[23], refs[24]
    step, chip = pl.program_id(0), meta[CHIP]
    width = x_ref.shape[1]
    rows = width // 4

    @pl.when(step == 0)
    def _():
        sums[...] = jnp.zeros_like(sums)
        acc[...] = jnp.zeros_like(acc)

    both = lambda i: [grads_a[i][...], grads_b[i][...]]
    dqkv = jnp.concatenate(both(0) + both(1) + both(2), axis=1)
    drel = jnp.concatenate(both(3), axis=1)
    span = dqkv.shape[1]
    acc[:, :span] += dot(h_ref[...], dqkv, TN)
    acc[:, span:] += dot(table_ref[...], drel, TN)
    dh = dot(dqkv, w_ref[:, :span], NT)
    x_hat, _ = norm_rows(x_ref[...].astype(f32))
    sums[0:1, :] += jnp.sum(dh * x_hat, axis=0, keepdims=True)
    sums[1:2, :] += jnp.sum(dh, axis=0, keepdims=True)
    local = (step & 1) == meta[CORE]

    @pl.when(local)
    def _():
        keep_ref[...] = dh

    @pl.when(jnp.logical_not(local))
    def _():
        send_ref[...] = dh.astype(bf)

    @pl.when(step == pl.num_programs(0) - 1)
    def _():
        for k, out in enumerate(outs):
            at = pl.ds(aligned(chip ^ k, rows), rows)
            low = (chip ^ k) >> 1 == 0
            tail = [sums[0:1, at], sums[1:2, at]]
            tail += [jnp.where(low, *both(i)) for i in (4, 5)]
            tail = jnp.concatenate(tail + [jnp.zeros((1, acc.shape[1] - 4 * rows), f32)], axis=1)
            out[:rows] = acc[at, :].astype(out.dtype)
            out[rows : rows + 8] = jnp.broadcast_to(tail, (8, tail.shape[1])).astype(out.dtype)
            shard = rows // 2
            lines = go_ref[pl.ds(aligned(chip ^ k, shard), shard), :]
            lines = jnp.concatenate([lines[: shard // 2], lines[shard // 2 :]], axis=1)
            out[rows + 8 :] = lines.astype(out.dtype)


def norm_one_body(meta, x_ref, dh_keep, dh_came, resid_ref, vec_ref, out0, out1):
    turn = pl.program_id(0) ^ (meta[RANK] & 1)
    x_hat, inv_std = norm_rows(x_ref[...].astype(f32))
    e = (dh_keep[...] + dh_came[...].astype(f32)) * vec_ref[0:1, :]
    first = jnp.mean(e, axis=1, keepdims=True)
    second = jnp.mean(e * x_hat, axis=1, keepdims=True)
    grad = (resid_ref[...] + inv_std * (e - first - x_hat * second)).astype(bf)

    @pl.when(turn == 0)
    def _():
        out0[...] = grad

    @pl.when(turn == 1)
    def _():
        out1[...] = grad


def rank_bit(meta, bit):
    return (meta[RANK] >> bit) & 1


def chip_sum_body(meta, own, *refs, bit):
    *came, keep, send = refs
    half = keep.shape[1]
    for out, side in ((keep, rank_bit(meta, bit)), (send, 1 - rank_bit(meta, bit))):
        at = pl.ds(aligned(side, half), half)
        total = own[:, at]
        for ref in came:
            total = total + ref[:, at].astype(f32)
        out[...] = total.astype(out.dtype)


def chip_sum(meta, parts, name, bit):
    rows, size = parts[0].shape
    return kernel_call(functools.partial(chip_sum_body, bit=bit), name, meta, parts, [((rows, size // 2), f32), ((rows, size // 2), bf)])


def own_rows_first(total, core, shard):
    theirs = lax.dynamic_slice_in_dim(total, (1 - core) * shard, shard, 0)
    mine = lax.dynamic_slice_in_dim(total, core * shard, shard, 0)
    came = swap_core(jnp.concatenate([theirs, total[2 * shard : 2 * shard + 8]], axis=0))
    return jnp.concatenate([mine, came, total[2 * shard :]], axis=0)


def halves(meta, mine, other, bit):
    low = rank_bit(meta, bit) == 0
    return jnp.concatenate([jnp.where(low, mine, other), jnp.where(low, other, mine)], axis=1)


def both_cores(meta, own, came):
    own, came = own.astype(f32), came.astype(f32)
    return own, own + came, meta[CORE] == 0


def store_half(ref, source, at, low):
    size = 2 * ref.shape[1]
    piece = source[:, at * size : (at + 1) * size]
    ref[...] = jnp.where(low, piece[:, : size // 2], piece[:, size // 2 :])


def early_out_body(meta, mine, other, came_ref, g_up, g_down, *vec_refs):
    rows = halves(meta, mine[...], other[...], 0)
    came_rows = halves(meta, came_ref[0], came_ref[1], 0)
    shard, width = g_up.shape[0], g_down.shape[1]
    first, unit = meta[CORE] == 0, rows.shape[1] // 4
    own, came = jnp.where(first, rows[:shard], rows[shard : 2 * shard]), came_rows[:shard]
    pair = (jnp.where(first, own, came), jnp.where(first, came, own))
    for j in range(4):
        for side in (0, 1):
            at = (2 * j + side) * unit
            g_up[:, at : at + unit] = pair[side][:, j * unit : (j + 1) * unit].astype(f32)
    down = rows[2 * shard + 8 :].astype(f32)
    g_down[...] = jnp.concatenate([down[:, :width], down[:, width:]], axis=0)
    own, total, low = both_cores(meta, rows[2 * shard : 2 * shard + 1], came_rows[shard : shard + 1])
    for at, ref in enumerate(vec_refs[:3]):
        store_half(ref, total, at, low)
    vec_refs[3][...] = own[:, 6 * shard : 6 * shard + unit]


def late_out_body(meta, mine, other, g_qkv, g_rel, g_out, *vec_refs):
    rows = halves(meta, mine[...], other[...], 0)
    shard, width = g_qkv.shape[0], g_out.shape[1]
    first, hd, heads = meta[CORE] == 0, HEAD_DIM, H // 2
    own, came = rows[:shard], rows[shard : 2 * shard]
    pair = (jnp.where(first, own, came), jnp.where(first, came, own))
    cols = heads * hd
    piece = lambda h, t: pair[h & 1][:, t * cols + (h >> 1) * hd : t * cols + ((h >> 1) + 1) * hd]
    g_qkv[...] = jnp.concatenate([piece(h, t) for h in range(2 * heads) for t in range(3)], axis=1).astype(f32)
    g_rel[...] = jnp.concatenate([piece(h, 3) for h in range(2 * heads)], axis=1).astype(f32)
    out = rows[2 * shard + 16 :].astype(f32)
    g_out[...] = jnp.concatenate([out[:, :width], out[:, width:]], axis=0)
    own, total, low = both_cores(meta, rows[2 * shard + 8 : 2 * shard + 9], rows[2 * shard : 2 * shard + 1])
    even = meta[CHIP] & 1 == 0
    for at, ref in enumerate(vec_refs):
        store_half(ref, total if at < 2 else own, at, low if at < 2 else even)


def place_body(meta, y0, y1, x0, x1, y_ref, x_ref):
    high = meta[RANK] >> 1 == 1
    y_ref[0] = jnp.where(high, y1[...], y0[...])
    y_ref[1] = jnp.where(high, y0[...], y1[...])
    x_ref[0] = jnp.where(high, x1[...], x0[...]).astype(f32)
    x_ref[1] = jnp.where(high, x0[...], x1[...]).astype(f32)


def slot_split_device(
    layer_input,
    lengths,
    ln1_gain,
    ln1_bias,
    w_qkv,
    w_rel,
    bias_u,
    bias_v,
    w_out,
    ln2_gain,
    ln2_bias,
    w_up,
    up_bias,
    w_down,
    down_bias,
    grad_out,
):
    slots, block, width = layer_input.shape
    rank, device = lax.axis_index("seq"), lax.axis_index("fsdp")
    core, chip = device & 1, device >> 1
    full, heads = 4 * block, H // 2
    cols, shard, unit = heads * HEAD_DIM, width // 8, up_bias.shape[0]
    mine_ff = 4 * unit

    none = jnp.zeros((4,), jnp.int32)
    x_own = to_slots(jnp.concatenate([layer_input, grad_out], axis=2), rank)
    vectors = (ln1_gain, ln1_bias, bias_u, bias_v, ln2_gain, ln2_bias, down_bias, up_bias)
    attn_rows, fold = shard + 8, shard // 2
    attn_pack, feed_pack, pack_send = kernel_call(
        pack_body,
        "pack",
        lengths,
        [
            pltpu.with_memory_space_constraint(v, pltpu.HBM)
            for v in [w_qkv, w_rel, w_up, w_out, w_down] + [v.reshape(-1, min(128, v.size)) for v in vectors]
        ],
        [((attn_rows, 4 * cols), bf), ((3 * shard + fold, 4 * cols), bf), ((attn_rows + shard + fold, 4 * cols), bf)],
        vmem=32,
    )
    pack_came = swap_core(pack_send)
    attn_pack = jnp.concatenate([attn_pack, pack_came[:attn_rows]], axis=0)
    attn_packs = [attn_pack] + [swap_chip(attn_pack, k) for k in (1, 2, 3)]
    feed_pack = jnp.concatenate([feed_pack, pack_came[attn_rows:]], axis=0)
    digits_at = 7 * shard + unit
    digits = pack_came[shard, digits_at : digits_at + 2 * slots].astype(jnp.int32)
    lengths = jnp.where(core == rank >> 1, lengths, digits[0::2] * DIGIT + digits[1::2])
    length = jnp.where(rank & 1 == 0, lengths[0], lengths[1])
    meta = jnp.stack([core, chip, rank, length]).astype(jnp.int32)
    length_arr = length.reshape(1)
    fine = 32
    inv_freq = jnp.exp(lax.iota(f32, width // 2) * (-2.0 * math.log(10000.0) / width))
    high = (full - 1 - fine * lax.iota(jnp.int32, full // fine)).astype(f32)[:, None] * inv_freq
    low = lax.iota(f32, fine)[:, None] * inv_freq
    high_sin, high_cos, low_sin, low_cos = together(jnp.sin(high), jnp.cos(high), jnp.sin(low), jnp.cos(low))
    high_sin, high_cos = high_sin[:, None], high_cos[:, None]
    table = jnp.concatenate(
        [high_sin * low_cos - high_cos * low_sin, high_cos * low_cos + high_sin * low_sin], axis=2
    )
    table = table.astype(bf).reshape(full, width)

    feed_pack, meta, length_arr, table, *attn_packs = together(feed_pack, meta, length_arr, table, *attn_packs)
    rest = list(together(*x_own, *attn_packs))
    x_own, attn_packs = rest[:2], rest[2:]
    x_other = [swap_core(x) for x in x_own]
    feed_first = swap_axis(feed_pack, 0)
    feed_pack, x_other[1] = together(feed_pack, x_other[1])
    feed_second = swap_axis(feed_pack, 1)

    side = lambda at: pl.BlockSpec((block, width), lambda i, _: (0, at))
    by_step = lambda width: pl.BlockSpec((block, width), lambda i, _: (i, 0))
    qkv, h1, x_slot, rel, w_own, vecs, up_b, own_u, own_v = kernel_call(
        project_body,
        "project",
        none,
        [pltpu.with_memory_space_constraint(v, pltpu.HBM) for v in attn_packs + x_own + x_other + [table]],
        [((full, 3 * cols), bf), ((full, width), bf), ((full, width), bf), ((full, cols), bf)]
        + [((width, 4 * cols), bf), ((8, width), f32), ((1, mine_ff), f32), ((1, cols), f32), ((1, cols), f32)],
        grid=(4,),
        in_specs=[whole(2 * attn_rows, 4 * cols)] * 4 + [side(0)] * 4 + [by_step(width)],
        out_specs=[by_step(3 * cols), by_step(width), by_step(width), by_step(cols)]
        + [whole(width, 4 * cols), whole(8, width), whole(1, mine_ff), whole(1, cols), whole(1, cols)],
        flops=2 * full * width * 4 * cols,
        vmem=32,
    )
    qkv, feed_first = together(qkv, feed_first)
    feed_third = swap_axis(feed_first, 1)
    attn, *probs = attn_fwd(length_arr, qkv, rel, own_u, own_v)
    attn, feed_second, feed_third = together(attn, feed_second, feed_third)
    feed_packs = [feed_pack, feed_first, feed_second, feed_third]

    attn_other = swap_core(attn)
    kept = lambda width: pl.BlockSpec((block, width), lambda i, _: (i >> 1, 0))
    half, rows = full // 2, 2 * shard + 8
    blocks = lambda rows: [((rows, 2 * width), f32)] + [((rows, 2 * width), bf)] * 3
    dy, x_hat, rstd, y_keep, dh, y_send, wo_mine, *early_parts = kernel_call(
        feed_body,
        "feed",
        meta,
        feed_packs + x_own + x_other + [x_slot, attn, attn_other, vecs, up_b],
        [((full, width), bf), ((full, width), bf), ((full, 1), f32), ((half, width), f32)]
        + [((full, width), bf), ((half, width), bf), ((cols, width), bf)]
        + blocks(rows + unit // 2),
        grid=(4,),
        in_specs=[whole(*feed_pack.shape)] * 4 + [side(1)] * 4
        + [by_step(width), by_step(cols), by_step(cols), whole(8, width), whole(1, mine_ff)],
        out_specs=[by_step(width), by_step(width), by_step(1), kept(width)]
        + [by_step(width), kept(width), whole(cols, width)]
        + [whole(rows + unit // 2, 2 * width)] * 4,
        scratch=[
            pltpu.VMEM((width, mine_ff), bf),
            pltpu.VMEM((mine_ff, width), bf),
            pltpu.VMEM((cols, width), bf),
            pltpu.VMEM((width, mine_ff), f32),
            pltpu.VMEM((mine_ff, width), f32),
            pltpu.VMEM((8, mine_ff), f32),
        ],
        flops=12 * full * width * mine_ff,
    )
    dh_came = swap_core(dh)
    y_came = swap_core(y_send)
    early_came = [swap_chip(early_parts[k], k) for k in (1, 2, 3)]
    out0, out1, g_resid, d_attn, g_out = kernel_call(
        norm_two_body,
        "norm_two",
        meta,
        [x_hat, rstd, dh, dh_came, dy, vecs, y_keep, y_came, wo_mine, attn],
        [((block, width), bf)] * 2 + [((half, width), f32), ((full, cols), bf), ((cols, width), f32)],
        grid=(4,),
        in_specs=[by_step(width), by_step(1)] + [by_step(width)] * 3 + [whole(8, width)] + [kept(width)] * 2
        + [whole(cols, width), by_step(cols)],
        out_specs=[whole(block, width)] * 2 + [kept(width), by_step(cols), whole(cols, width)],
        flops=4 * full * width * cols,
    )
    home = lambda outs: [
        lax.ppermute(out, ("fsdp", "seq"), [(b, a) for a, b in slot_pairs(turn)])
        for turn, out in enumerate(outs)
    ]
    y_turns = home((out0, out1))
    back = lambda pair, d_out: attn_bwd(length_arr, qkv, rel, own_u, own_v, probs, d_out, pair=pair)
    d_attn, *grads_a = together(d_attn, *back(0, d_attn))
    *grads_b, y0, y1, e1, e2, e3 = together(*back(1, d_attn), *y_turns, *early_came)
    early_keep, early_send = chip_sum(meta, [early_parts[0], e1, e2, e3], "early_chips", 0)
    early_send, *grads_b = together(early_send, *grads_b)
    early_came = swap_seq(early_send, 1)
    pair_step = pl.BlockSpec((block, 2 * HEAD_DIM), lambda i, _: (i, 0))
    pair_row = whole(1, 2 * HEAD_DIM)
    dh1_keep, dh1_send, *late_parts = kernel_call(
        qkv_back_body,
        "qkv_back",
        meta,
        [*grads_a, *grads_b, w_own, x_slot, h1, table, g_out],
        [((half, width), f32), ((half, width), bf)] + blocks(rows + fold),
        grid=(4,),
        in_specs=([pair_step] * 4 + [pair_row] * 2) * 2
        + [whole(width, 4 * cols)] + [by_step(width)] * 3 + [whole(cols, width)],
        out_specs=[kept(width)] * 2 + [whole(rows + fold, 2 * width)] * 4,
        scratch=[pltpu.VMEM((width, 4 * cols), f32), pltpu.VMEM((8, width), f32)],
        flops=14 * full * width * cols,
    )
    dh1_send, *late_parts = together(dh1_send, *late_parts)
    dh1_came, early_came = together(swap_core(dh1_send), early_came)
    late_came = [swap_chip(late_parts[k], k) for k in (1, 2, 3)]
    by_half = pl.BlockSpec((block, width), lambda i, _: (i, 0))
    own_rows = pl.BlockSpec((block, width), lambda i, m: (2 * i + m[CORE], 0))
    x0, x1 = kernel_call(
        norm_one_body,
        "norm_one",
        meta,
        [x_slot, dh1_keep, dh1_came, g_resid, vecs],
        [((block, width), bf)] * 2,
        grid=(2,),
        in_specs=[own_rows] + [by_half] * 3 + [whole(8, width)],
        out_specs=[whole(block, width)] * 2,
    )
    x_turns = home((x0, x1))
    *late_came, _, _ = together(*late_came, x0, x1)
    early_pair = (early_keep + early_came.astype(f32)).astype(bf)
    early_came = swap_seq(early_pair, 2)
    late_keep, late_send = chip_sum(meta, [late_parts[0]] + late_came, "late_chips", 0)
    small = lambda size: ((1, size), f32)
    late_came, early_came, x_turns[0] = together(swap_seq(late_send, 1), early_came, x_turns[0])
    early_mine = (early_pair.astype(f32) + early_came.astype(f32)).astype(bf)
    late_pair = (late_keep + late_came.astype(f32)).astype(bf)
    late_came = swap_seq(late_pair, 2)
    early_other = swap_seq(early_mine, 1)
    late_total = (late_pair.astype(f32) + late_came.astype(f32)).astype(bf)
    late_mine = own_rows_first(late_total, core, shard)
    late_other = swap_seq(late_mine, 1)
    late_mine, g0, g1, early_other = together(late_mine, *x_turns, early_other)
    theirs = lambda rows: jnp.concatenate(
        [
            lax.dynamic_slice_in_dim(rows, (1 - core) * shard, shard, 0),
            rows[2 * shard : 2 * shard + 8],
        ],
        axis=0,
    )
    early_core = swap_core(jnp.stack([theirs(early_mine), theirs(early_other)]))
    output, grad_x = kernel_call(
        place_body,
        "place",
        meta,
        [y0, y1, g0, g1],
        [((2, block, width), bf), ((2, block, width), f32)],
    )
    g_up, g_down, g_gain_two, g_shift_two, g_down_shift, g_up_shift = kernel_call(
        early_out_body,
        "early_out",
        meta,
        [early_mine, early_other, early_core],
        [((shard, 2 * mine_ff), f32), ((unit, width), f32)] + [small(shard)] * 3 + [small(unit)],
    )
    late_other, output, grad_x, g_up = together(late_other, output, grad_x, g_up)
    g_qkv, g_rel, g_w_out, *late_vectors = kernel_call(
        late_out_body,
        "late_out",
        meta,
        [late_mine, late_other],
        [((shard, 6 * cols), f32), ((shard, 2 * cols), f32), ((shard, width), f32)] + [small(shard)] * 4,
    )
    g_gain_one, g_shift_one, g_bias_u, g_bias_v = [v.reshape(-1) for v in late_vectors]
    return (
        output,
        grad_x,
        g_gain_one,
        g_shift_one,
        g_qkv,
        g_rel,
        g_bias_u,
        g_bias_v,
        g_w_out,
        g_gain_two.reshape(-1),
        g_shift_two.reshape(-1),
        g_up,
        g_up_shift.reshape(-1),
        g_down,
        g_down_shift.reshape(-1),
    )


def per_device(*args):
    one_slot_a_chip = lax.axis_size("fsdp") == 8 and lax.axis_size("seq") == 4
    if one_slot_a_chip and args[0].shape[0] == 2:
        return slot_split_device(*args)
    return head_split_device(*args)


def solution(mesh):
    placed = (
        P("fsdp", "seq", None),
        P("fsdp"),
        P("fsdp"),
        P("fsdp"),
        P("fsdp", None),
        P("fsdp", None),
        P("fsdp"),
        P("fsdp"),
        P("fsdp", None),
        P("fsdp"),
        P("fsdp"),
        P("fsdp", None),
        P("fsdp"),
        P("fsdp", None),
        P("fsdp"),
        P("fsdp", "seq", None),
    )
    return jax.shard_map(
        per_device,
        mesh=mesh,
        in_specs=placed,
        out_specs=(
            P("fsdp", "seq", None),
            P("fsdp", "seq", None),
            P("fsdp"),
            P("fsdp"),
            P("fsdp", None),
            P("fsdp", None),
            P("fsdp"),
            P("fsdp"),
            P("fsdp", None),
            P("fsdp"),
            P("fsdp"),
            P("fsdp", None),
            P("fsdp"),
            P("fsdp", None),
            P("fsdp"),
        ),
        check_vma=False,
    )
```

```python
import functools
import math

import jax
import jax.numpy as jnp
from jax import lax
from jax.experimental import pallas as pl
from jax.experimental.pallas import tpu as pltpu
from jax.sharding import PartitionSpec as P

H = 8
HEAD_DIM = 64


NEG_FILL = -1e30
NORM_EPS = 1e-05


bf, f32 = jnp.bfloat16, jnp.float32
NEG = NEG_FILL
HD = HEAD_DIM
NT = (((1,), (1,)), ((), ()))
NN = (((1,), (0,)), ((), ()))


def dot(a, b, dims):
    return lax.dot_general(a, b, dims, preferred_element_type=f32)


def masked_tail(s, keep, block):
    tail = jnp.where(keep, s[:, s.shape[1] - block :], NEG)
    if s.shape[1] == block:
        return tail
    return jnp.concatenate([s[:, : s.shape[1] - block], tail], axis=1)


def scores(qu, qv, keys, rel_rev, keep, block):
    span = keys.shape[0]
    rel = dot(qv, rel_rev, NT)
    rel = pltpu.roll(rel, (span - block + 1) % span, 1, stride=1, stride_axis=0)
    return masked_tail(dot(qu, keys, NT) + rel, keep, block)


def attn_fwd_body(len_ref, q_ref, k_ref, v_ref, r_ref, bu_ref, bv_ref, o_ref, *p_refs, block):
    full = q_ref.shape[0]
    lane = lax.broadcasted_iota(jnp.int32, (block, 2 * HD), 1)
    sides = (lane < HD, lane >= HD)
    length = len_ref[0]
    col = lax.broadcasted_iota(jnp.int32, (1, full), 1)
    bias = jnp.where(col < length, 0.0, NEG)
    tri = lax.broadcasted_iota(jnp.int32, (block, block), 1) <= lax.broadcasted_iota(
        jnp.int32, (block, block), 0
    )
    for first in range(0, full, block):
        span = first + block
        q = q_ref[first:span, :].astype(f32)
        qu = (q + bu_ref[...]).astype(bf).astype(f32) * 0.125
        qv = (q + bv_ref[...]).astype(bf).astype(f32) * 0.125
        outs = []
        for head, side in enumerate(sides):
            s = scores(
                jnp.where(side, qu, 0.0).astype(bf),
                jnp.where(side, qv, 0.0).astype(bf),
                k_ref[:span, :],
                r_ref[full - span :, :],
                tri,
                block,
            )
            s = s + bias[:, :span]
            top = jnp.max(s, axis=1, keepdims=True)
            e = jnp.exp(s - top)
            total = jnp.sum(e, axis=1, keepdims=True)
            p = (e * (1.0 / total)).astype(bf)
            p_refs[first // block][head] = p
            outs.append(dot(p, v_ref[:span, :], NN))
        o_ref[first:span, :] = jnp.where(sides[0], outs[0], outs[1]).astype(bf)


def attn_fwd(length, qkv, rel_rev, bias_u, bias_v, *, block=256):
    full, cols = rel_rev.shape
    spans = range(block, full + 1, block)
    pairs = cols // (2 * HD)
    at = lambda part: pl.BlockSpec((full, 2 * HD), lambda pair, _: (0, part * pairs + pair))
    row = pl.BlockSpec((1, 2 * HD), lambda pair, _: (0, pair))
    return pl.pallas_call(
        functools.partial(attn_fwd_body, block=block),
        out_shape=(
            jax.ShapeDtypeStruct((full, cols), bf),
            *(jax.ShapeDtypeStruct((2 * pairs, block, span), bf) for span in spans),
        ),
        grid_spec=pltpu.PrefetchScalarGridSpec(
            num_scalar_prefetch=1,
            grid=(pairs,),
            in_specs=[at(0), at(1), at(2), at(0), row, row],
            out_specs=(
                at(0),
                *(pl.BlockSpec((2, block, span), lambda pair, _: (pair, 0, 0)) for span in spans),
            ),
        ),
        cost_estimate=pl.CostEstimate(flops=0, bytes_accessed=0, transcendentals=0),
        compiler_params=pltpu.CompilerParams(vmem_limit_bytes=32 << 20),
        name="attn_fwd",
    )(length, qkv, qkv, qkv, rel_rev, bias_u, bias_v)


def attn_bwd_body(len_ref, q_ref, k_ref, v_ref, r_ref, bu_ref, bv_ref, do_ref, *refs, block, heads):
    full = q_ref.shape[0]
    p_refs, refs = refs[: full // block], refs[full // block :]
    dq_ref, dk_ref, dv_ref, dr_ref, gu_ref, gv_ref, dk_t, dv_t, dr_t = refs
    length = len_ref[0]
    lane = lax.broadcasted_iota(jnp.int32, (block, 2 * HD), 1)
    sides = (lane < HD, lane >= HD)
    rows = lax.broadcasted_iota(jnp.int32, (block, block), 0)
    cols = lax.broadcasted_iota(jnp.int32, (block, block), 1)
    flip = jnp.where(rows + cols == block - 1, 1.0, 0.0).astype(bf)
    for ref in (dk_t, dv_t, dr_t, dq_ref, gu_ref, gv_ref):
        ref[...] = jnp.zeros_like(ref)
    for first in range(0, full, block):
        span = first + block

        @pl.when(first < length)
        def _():
            q = q_ref[first:span, :].astype(f32)
            qu = (q + bu_ref[...]).astype(bf).astype(f32) * 0.125
            qv = (q + bv_ref[...]).astype(bf).astype(f32) * 0.125
            do = do_ref[first:span, :].astype(f32)
            qu_t = jnp.transpose(qu).astype(bf)
            do_t = jnp.transpose(do).astype(bf)
            qv_t = jnp.transpose(dot(flip, qv.astype(bf), NN)).astype(bf)
            dqu, dqv = [0.0, 0.0], [0.0, 0.0]
            for head in heads:
                side = sides[head]
                at = slice(head * HD, (head + 1) * HD)
                rounded = p_refs[first // block][head - heads[0]]
                p = rounded.astype(f32)
                dp = dot(jnp.where(side, do, 0.0).astype(bf), v_ref[:span, :], NT)
                t = p * dp
                ds = (t - p * jnp.sum(t, axis=1, keepdims=True)).astype(bf)
                dv_t[at, :span] += dot(do_t[at], rounded, NN)
                both = dot(jnp.concatenate([qu_t[at], flip], axis=0), ds, NN)
                dk_t[at, :span] += both[:HD]
                dqu[head] = dot(ds, k_ref[:span, :], NN)
                ds_rev = pltpu.roll(both[HD:], 0, 1, stride=1, stride_axis=0).astype(bf)
                dr_t[at, full - span :] += dot(qv_t[at], ds_rev, NN)
                dqv[head] = dot(ds_rev, r_ref[full - span :, :], NN)
            dqu = jnp.where(sides[0], dqu[0], dqu[1]) * 0.125
            dqv = jnp.where(sides[0], dqv[0], dqv[1]) * 0.125
            gu_ref[...] += jnp.sum(dqu, axis=0, keepdims=True)
            gv_ref[...] += jnp.sum(dqv, axis=0, keepdims=True)
            dq_ref[first:span, :] = (dqu + dot(flip, dqv.astype(bf), NN)).astype(bf)

    dk_ref[...] = jnp.transpose(dk_t[...]).astype(bf)
    dv_ref[...] = jnp.transpose(dv_t[...]).astype(bf)
    dr_ref[...] = jnp.transpose(dr_t[...]).astype(bf)


def attn_bwd(length, qkv, rel_rev, bias_u, bias_v, probs, d_out, *, pair, heads=(0, 1), block=256):
    full, cols = rel_rev.shape
    pairs = cols // (2 * HD)
    at = lambda part: pl.BlockSpec((full, 2 * HD), lambda i, _: (0, part * pairs + pair))
    row = pl.BlockSpec((1, 2 * HD), lambda i, _: (0, pair))
    out = pl.BlockSpec((full, 2 * HD), lambda i, _: (0, 0))
    out_row = pl.BlockSpec((1, 2 * HD), lambda i, _: (0, 0))
    return pl.pallas_call(
        functools.partial(attn_bwd_body, block=block, heads=heads),
        out_shape=(jax.ShapeDtypeStruct((full, 2 * HD), bf),) * 4
        + (jax.ShapeDtypeStruct((1, 2 * HD), f32),) * 2,
        grid_spec=pltpu.PrefetchScalarGridSpec(
            num_scalar_prefetch=1,
            grid=(1,),
            in_specs=[at(0), at(1), at(2), at(0), row, row]
            + [at(0)]
            + [
                pl.BlockSpec((len(heads),) + p.shape[1:], lambda i, _: ((2 * pair + heads[0]) // len(heads), 0, 0))
                for p in probs
            ],
            out_specs=(out,) * 4 + (out_row, out_row),
            scratch_shapes=[pltpu.VMEM((2 * HD, full), f32)] * 3,
        ),
        cost_estimate=pl.CostEstimate(flops=0, bytes_accessed=0, transcendentals=0),
        compiler_params=pltpu.CompilerParams(vmem_limit_bytes=32 << 20),
        name="attn_bwd",
    )(length, qkv, qkv, qkv, rel_rev, bias_u, bias_v, d_out, *probs)


def norm_parts(values):
    mean_val = jnp.mean(values, axis=-1, keepdims=True)
    centered = values - mean_val
    inv_std = lax.rsqrt(jnp.mean(centered * centered, axis=-1, keepdims=True) + NORM_EPS)
    return (centered * inv_std, inv_std)


def norm_back(grad_norm, x_hat, inv_std):
    first_mean = jnp.mean(grad_norm, axis=-1, keepdims=True)
    second_mean = jnp.mean(grad_norm * x_hat, axis=-1, keepdims=True)
    return inv_std * (grad_norm - first_mean - x_hat * second_mean)


def position_table(count_rows, feature_count):
    steps = lax.iota(jnp.float32, count_rows)
    half_count = feature_count // 2
    inv_freq = jnp.exp(
        lax.iota(jnp.float32, half_count) * (-2.0 * math.log(10000.0) / feature_count)
    )
    angles = steps[:, None] * inv_freq[None, :]
    return jnp.concatenate([jnp.sin(angles), jnp.cos(angles)], axis=1)


def skew_rows(matrix):
    leading = matrix.shape[:-2]
    row_count, col_count = matrix.shape[-2:]
    flattened = matrix.reshape(leading + (row_count * col_count,))
    picked = flattened[..., row_count - 1 : row_count - 1 + row_count * (col_count - 1)]
    return picked.reshape(leading + (row_count, col_count - 1))[..., : col_count - row_count]


def unskew_rows(matrix):
    leading = matrix.shape[:-2]
    row_count, key_count = matrix.shape[-2:]
    axis_pos = len(leading)
    widened = jnp.pad(matrix, [(0, 0)] * axis_pos + [(0, 0), (0, row_count - 1)])
    flattened = widened.reshape(leading + (row_count * (key_count + row_count - 1),))
    flattened = jnp.pad(flattened, [(0, 0)] * axis_pos + [(row_count - 1, 1)])
    return flattened.reshape(leading + (row_count, key_count + row_count))


def head_split_device(
    layer_input,
    lengths,
    ln1_gain,
    ln1_bias,
    w_qkv,
    w_rel,
    bias_u,
    bias_v,
    w_out,
    ln2_gain,
    ln2_bias,
    w_up,
    up_bias,
    w_down,
    down_bias,
    grad_out,
):
    weights = (
        lax.all_gather(ln1_gain, "fsdp", axis=0, tiled=True),
        lax.all_gather(ln1_bias, "fsdp", axis=0, tiled=True),
        lax.all_gather(w_qkv, "fsdp", axis=0, tiled=True),
        lax.all_gather(w_rel, "fsdp", axis=0, tiled=True),
        lax.all_gather(bias_u, "fsdp", axis=0, tiled=True),
        lax.all_gather(bias_v, "fsdp", axis=0, tiled=True),
        lax.all_gather(w_out, "fsdp", axis=0, tiled=True),
        lax.all_gather(ln2_gain, "fsdp", axis=0, tiled=True),
        lax.all_gather(ln2_bias, "fsdp", axis=0, tiled=True),
        lax.all_gather(w_up, "fsdp", axis=0, tiled=True),
        lax.all_gather(up_bias, "fsdp", axis=0, tiled=True),
        lax.all_gather(w_down, "fsdp", axis=0, tiled=True),
        lax.all_gather(down_bias, "fsdp", axis=0, tiled=True),
    )
    (
        gain_one,
        shift_one,
        query_key_value_matrix,
        rel_weight,
        first_bias,
        second_bias,
        output_matrix,
        gain_two,
        shift_two,
        up_matrix,
        up_shift,
        down_matrix,
        down_shift,
    ) = weights
    gain_one = gain_one.astype(jnp.float32)
    shift_one = shift_one.astype(jnp.float32)
    gain_two = gain_two.astype(jnp.float32)
    shift_two = shift_two.astype(jnp.float32)
    up_shift = up_shift.astype(jnp.float32)
    down_shift = down_shift.astype(jnp.float32)
    slots, block_len, width = layer_input.shape
    seq_count = lax.axis_size("seq")
    seq_rank = lax.axis_index("seq")
    head_dim = HEAD_DIM
    group = H // seq_count
    full_len = block_len * seq_count
    score_scale = 1.0 / math.sqrt(head_dim)
    q_block = 512
    num_blocks = full_len // q_block
    win_len = full_len + q_block
    x_float = layer_input.astype(jnp.float32)
    x_hat_one, inv_std_one = norm_parts(x_float)
    first_normalized = (x_hat_one * gain_one + shift_one).astype(jnp.bfloat16)
    qkv_local = jnp.einsum(
        "mcr,rk->mck", first_normalized, query_key_value_matrix, preferred_element_type=jnp.float32
    ).astype(jnp.bfloat16)
    qkv_heads = lax.all_to_all(qkv_local, "seq", split_axis=2, concat_axis=1, tiled=True)
    qkv_heads = qkv_heads.reshape(slots, full_len, group, 3, head_dim)
    queries = qkv_heads[:, :, :, 0]
    keys = qkv_heads[:, :, :, 1]
    values = qkv_heads[:, :, :, 2]
    head_start = seq_rank * group
    head_bias_u = lax.dynamic_slice_in_dim(
        first_bias.astype(jnp.float32).reshape(H, head_dim), head_start, group, 0
    )
    head_bias_v = lax.dynamic_slice_in_dim(
        second_bias.astype(jnp.float32).reshape(H, head_dim), head_start, group, 0
    )
    query_u = (queries.astype(jnp.float32) + head_bias_u).astype(jnp.bfloat16)
    query_v = (queries.astype(jnp.float32) + head_bias_v).astype(jnp.bfloat16)
    table_rev = position_table(full_len, width).astype(jnp.bfloat16)[::-1]
    rel_cols = lax.dynamic_slice_in_dim(rel_weight, head_start * head_dim, group * head_dim, 1)
    rel_rev = jnp.dot(table_rev, rel_cols, preferred_element_type=jnp.float32).astype(jnp.bfloat16)
    rel_ext = jnp.concatenate([rel_rev, jnp.zeros_like(rel_rev)], axis=0).reshape(
        2 * full_len, group, head_dim
    )
    col_ids = lax.iota(jnp.int32, full_len)

    def scores_block(first_row):
        qu_part = lax.dynamic_slice_in_dim(query_u, first_row, q_block, 1)
        qv_part = lax.dynamic_slice_in_dim(query_v, first_row, q_block, 1)
        window_start = full_len - q_block - first_row
        rel_win = lax.dynamic_slice_in_dim(rel_ext, window_start, win_len, 0)
        content = jnp.einsum("sqhe,skhe->shqk", qu_part, keys, preferred_element_type=jnp.float32)
        rel_raw = jnp.einsum("sqhe,the->shqt", qv_part, rel_win, preferred_element_type=jnp.float32)
        rel_part = skew_rows(rel_raw)
        row_ids = first_row + lax.iota(jnp.int32, q_block)
        causal = col_ids[None, :] <= row_ids[:, None]
        inside = col_ids[None, :] < lengths[:, None]
        allowed = causal[None, None, :, :] & inside[:, None, None, :]
        scores = jnp.where(allowed, (content + rel_part) * score_scale, NEG_FILL)
        return (scores, qu_part, qv_part, rel_win, window_start)

    def forward_block(block_index):
        first_row = block_index * q_block
        scores, qu_part, qv_part, rel_win, window_start = scores_block(first_row)
        top = jnp.max(scores, axis=-1, keepdims=True)
        expo = jnp.exp(scores - top)
        total = jnp.sum(expo, axis=-1, keepdims=True)
        probs = (expo / total).astype(jnp.bfloat16)
        out_part = jnp.einsum(
            "shqk,skhe->sqhe", probs, values, preferred_element_type=jnp.float32
        ).astype(jnp.bfloat16)
        return (out_part, top[..., 0] + jnp.log(total[..., 0]))

    block_outs, block_lse = lax.map(forward_block, jnp.arange(num_blocks, dtype=jnp.int32))
    attn_heads = jnp.moveaxis(block_outs, 0, 1).reshape(slots, full_len, group * head_dim)
    attention_sequence = lax.all_to_all(attn_heads, "seq", split_axis=1, concat_axis=2, tiled=True)
    attention_projected = jnp.einsum(
        "mcr,rk->mck", attention_sequence, output_matrix, preferred_element_type=jnp.float32
    )
    resid = x_float + attention_projected
    x_hat_two, inv_std_two = norm_parts(resid)
    second_normalized = (x_hat_two * gain_two + shift_two).astype(jnp.bfloat16)
    pre_act = (
        jnp.einsum("oka,ac->okc", second_normalized, up_matrix, preferred_element_type=jnp.float32)
        + up_shift
    )
    normal_cdf = 0.5 * (1.0 + lax.erf(pre_act * (1.0 / math.sqrt(2.0))))
    hidden_state = (pre_act * normal_cdf).astype(jnp.bfloat16)
    down_proj = (
        jnp.einsum("zcp,pr->zcr", hidden_state, down_matrix, preferred_element_type=jnp.float32)
        + down_shift
    )
    output = (resid + down_proj).astype(jnp.bfloat16)
    positions = seq_rank * block_len + lax.iota(jnp.int32, block_len)
    live = (positions[None, :] < lengths[:, None]).astype(jnp.bfloat16)
    result_gradient = grad_out * live[:, :, None]
    grad_y_float = result_gradient.astype(jnp.float32)
    g_down_shift = jnp.sum(grad_y_float, axis=(0, 1))
    down_gradient = jnp.einsum(
        "hki,hku->iu", hidden_state, result_gradient, preferred_element_type=jnp.float32
    )
    hidden_gradient = jnp.einsum(
        "gvu,ju->gvj", result_gradient, down_matrix, preferred_element_type=jnp.float32
    )
    deriv = normal_cdf + pre_act * jnp.exp(-0.5 * pre_act * pre_act) * (
        1.0 / math.sqrt(2.0 * math.pi)
    )
    preactivation_gradient = (hidden_gradient * deriv).astype(jnp.bfloat16)
    g_up_shift = jnp.sum(preactivation_gradient.astype(jnp.float32), axis=(0, 1))
    up_gradient = jnp.einsum(
        "oiz,oix->zx", second_normalized, preactivation_gradient, preferred_element_type=jnp.float32
    )
    second_norm_gradient = jnp.einsum(
        "rau,ku->rak", preactivation_gradient, up_matrix, preferred_element_type=jnp.float32
    )
    g_gain_two = jnp.sum(second_norm_gradient * x_hat_two, axis=(0, 1))
    g_shift_two = jnp.sum(second_norm_gradient, axis=(0, 1))
    g_resid = grad_y_float + norm_back(second_norm_gradient * gain_two, x_hat_two, inv_std_two)
    attention_gradient = g_resid.astype(jnp.bfloat16)
    output_gradient = jnp.einsum(
        "zau,zam->um", attention_sequence, attention_gradient, preferred_element_type=jnp.float32
    )
    g_attn_seq = jnp.einsum(
        "urz,jz->urj", attention_gradient, output_matrix, preferred_element_type=jnp.float32
    ).astype(jnp.bfloat16)
    g_attn_heads = lax.all_to_all(
        g_attn_seq, "seq", split_axis=2, concat_axis=1, tiled=True
    ).reshape(slots, full_len, group, head_dim)

    def backward_block(carry, block_index):
        g_keys, g_vals, g_ext = carry
        first_row = block_index * q_block
        scores, qu_part, qv_part, rel_win, window_start = scores_block(first_row)
        probs = jnp.exp(scores - block_lse[block_index][..., None])
        d_out = lax.dynamic_slice_in_dim(g_attn_heads, first_row, q_block, 1)
        g_vals = g_vals + jnp.einsum(
            "shqk,sqhe->skhe", probs.astype(jnp.bfloat16), d_out, preferred_element_type=jnp.float32
        )
        g_probs = jnp.einsum("sqhe,skhe->shqk", d_out, values, preferred_element_type=jnp.float32)
        inner = jnp.sum(probs * g_probs, axis=-1, keepdims=True)
        g_scores = (probs * (g_probs - inner)).astype(jnp.bfloat16)
        g_qu = (
            jnp.einsum("shqk,skhe->sqhe", g_scores, keys, preferred_element_type=jnp.float32)
            * score_scale
        )
        g_keys = (
            g_keys
            + jnp.einsum("shqk,sqhe->skhe", g_scores, qu_part, preferred_element_type=jnp.float32)
            * score_scale
        )
        g_wide = unskew_rows(g_scores)
        g_qv = (
            jnp.einsum("shqt,the->sqhe", g_wide, rel_win, preferred_element_type=jnp.float32)
            * score_scale
        )
        g_win = (
            jnp.einsum("shqt,sqhe->sthe", g_wide, qv_part, preferred_element_type=jnp.float32)
            * score_scale
        )
        g_old = lax.dynamic_slice_in_dim(g_ext, window_start, win_len, 1)
        g_ext = lax.dynamic_update_slice_in_dim(g_ext, g_old + g_win, window_start, 1)
        return ((g_keys, g_vals, g_ext), (g_qu, g_qv))

    zero_heads = jnp.zeros((slots, full_len, group, head_dim), jnp.float32)
    zero_ext = jnp.zeros((slots, 2 * full_len, group, head_dim), jnp.float32)
    (g_keys, g_vals, g_ext), (g_qu_blocks, g_qv_blocks) = lax.scan(
        backward_block, (zero_heads, zero_heads, zero_ext), jnp.arange(num_blocks, dtype=jnp.int32)
    )
    g_qu = jnp.moveaxis(g_qu_blocks, 0, 1).reshape(slots, full_len, group, head_dim)
    g_qv = jnp.moveaxis(g_qv_blocks, 0, 1).reshape(slots, full_len, group, head_dim)
    g_queries = g_qu + g_qv
    g_bias_u_heads = jnp.sum(g_qu, axis=(0, 1))
    g_bias_v_heads = jnp.sum(g_qv, axis=(0, 1))
    g_qkv_heads = (
        jnp.stack([g_queries, g_keys, g_vals], axis=3)
        .astype(jnp.bfloat16)
        .reshape(slots, full_len, group * 3 * head_dim)
    )
    query_key_value_gradient = lax.all_to_all(
        g_qkv_heads, "seq", split_axis=1, concat_axis=2, tiled=True
    )
    g_rel_low = g_ext[:, :full_len].astype(jnp.bfloat16)
    g_rel_heads = jnp.einsum(
        "td,sthe->dhe", table_rev, g_rel_low, preferred_element_type=jnp.float32
    ).reshape(width, group * head_dim)
    g_rel_weight = lax.dynamic_update_slice_in_dim(
        jnp.zeros((width, width), jnp.float32), g_rel_heads, head_start * head_dim, 1
    )
    g_bias_u = lax.dynamic_update_slice_in_dim(
        jnp.zeros((H, head_dim), jnp.float32), g_bias_u_heads, head_start, 0
    ).reshape(width)
    g_bias_v = lax.dynamic_update_slice_in_dim(
        jnp.zeros((H, head_dim), jnp.float32), g_bias_v_heads, head_start, 0
    ).reshape(width)
    query_key_value_weight_gradient = jnp.einsum(
        "zau,zam->um",
        first_normalized,
        query_key_value_gradient,
        preferred_element_type=jnp.float32,
    )
    first_norm_gradient = jnp.einsum(
        "urz,jz->urj",
        query_key_value_gradient,
        query_key_value_matrix,
        preferred_element_type=jnp.float32,
    )
    g_gain_one = jnp.sum(first_norm_gradient * x_hat_one, axis=(0, 1))
    g_shift_one = jnp.sum(first_norm_gradient, axis=(0, 1))
    g_input = g_resid + norm_back(first_norm_gradient * gain_one, x_hat_one, inv_std_one)
    partial_shards = (
        lax.psum_scatter(g_gain_one, "fsdp", scatter_dimension=0, tiled=True),
        lax.psum_scatter(g_shift_one, "fsdp", scatter_dimension=0, tiled=True),
        lax.psum_scatter(query_key_value_weight_gradient, "fsdp", scatter_dimension=0, tiled=True),
        lax.psum_scatter(g_rel_weight, "fsdp", scatter_dimension=0, tiled=True),
        lax.psum_scatter(g_bias_u, "fsdp", scatter_dimension=0, tiled=True),
        lax.psum_scatter(g_bias_v, "fsdp", scatter_dimension=0, tiled=True),
        lax.psum_scatter(output_gradient, "fsdp", scatter_dimension=0, tiled=True),
        lax.psum_scatter(g_gain_two, "fsdp", scatter_dimension=0, tiled=True),
        lax.psum_scatter(g_shift_two, "fsdp", scatter_dimension=0, tiled=True),
        lax.psum_scatter(up_gradient, "fsdp", scatter_dimension=0, tiled=True),
        lax.psum_scatter(g_up_shift, "fsdp", scatter_dimension=0, tiled=True),
        lax.psum_scatter(down_gradient, "fsdp", scatter_dimension=0, tiled=True),
        lax.psum_scatter(g_down_shift, "fsdp", scatter_dimension=0, tiled=True),
    )
    shards = lax.psum(
        (
            partial_shards[0],
            partial_shards[1],
            partial_shards[2],
            partial_shards[3],
            partial_shards[4],
            partial_shards[5],
            partial_shards[6],
            partial_shards[7],
            partial_shards[8],
            partial_shards[9],
            partial_shards[10],
            partial_shards[11],
            partial_shards[12],
        ),
        "seq",
    )
    return (
        output,
        g_input,
        shards[0],
        shards[1],
        shards[2],
        shards[3],
        shards[4],
        shards[5],
        shards[6],
        shards[7],
        shards[8],
        shards[9],
        shards[10],
        shards[11],
        shards[12],
    )


def swap_core(values):
    size = lax.axis_size("fsdp")
    return lax.ppermute(values, "fsdp", [(i, i ^ 1) for i in range(size)])


def swap_chip(values, mask):
    size = lax.axis_size("fsdp")
    return lax.ppermute(values, "fsdp", [(i, i ^ (2 * mask)) for i in range(size)])


def swap_axis(values, turn):
    size = lax.axis_size("fsdp")
    return lax.ppermute(values, "fsdp", [(i, i ^ (2 << ((i & 1) ^ turn))) for i in range(size)])


def swap_seq(values, mask):
    size = lax.axis_size("seq")
    return lax.ppermute(values, "seq", [(i, i ^ mask) for i in range(size)])


def slot_pairs(turn):
    seq, pairs = lax.axis_size("seq"), []
    for f in range(lax.axis_size("fsdp")):
        for z in range(seq):
            to_f, to_z = (f & ~1) | (z & 1), 2 * (f & 1) + (turn ^ (z >> 1))
            pairs.append((f * seq + z, to_f * seq + to_z))
    return pairs


def to_slots(values, seq_rank):
    return [
        lax.ppermute(
            lax.dynamic_index_in_dim(values, turn ^ (seq_rank >> 1), 0, keepdims=False),
            ("fsdp", "seq"),
            slot_pairs(turn),
        )
        for turn in (0, 1)
    ]


def together(*values):
    return lax.optimization_barrier(values)


def whole(*shape):
    return pl.BlockSpec(shape, lambda *_: (0,) * len(shape))


def kernel_call(body, name, meta, args, outs, *, grid=(1,), in_specs=None, out_specs=None, scratch=(), flops=0, vmem=32):
    in_specs = in_specs or [whole(*a.shape) for a in args]
    out_specs = out_specs or [whole(*shape) for shape, _ in outs]
    moved = sum(a.size * a.dtype.itemsize for a in args)
    moved += sum(math.prod(shape) * jnp.dtype(kind).itemsize for shape, kind in outs)
    return pl.pallas_call(
        body,
        out_shape=[jax.ShapeDtypeStruct(shape, kind) for shape, kind in outs],
        grid_spec=pltpu.PrefetchScalarGridSpec(
            num_scalar_prefetch=1,
            grid=grid,
            in_specs=in_specs,
            out_specs=out_specs,
            scratch_shapes=scratch,
        ),
        compiler_params=pltpu.CompilerParams(vmem_limit_bytes=vmem << 20),
        cost_estimate=pl.CostEstimate(flops=0, bytes_accessed=0, transcendentals=0),
        name=name,
    )(meta, *args)


TN = (((0,), (0,)), ((), ()))
CORE, CHIP, RANK, LIVE = range(4)
DIGIT = 128


def aligned(index, size):
    return pl.multiple_of(index * size, size)


def own_place():
    device = lax.axis_index("fsdp")
    return device & 1, device >> 1, lax.axis_index("seq")


def pack_body(lengths_ref, qkv_ref, rel_ref, up_ref, out_ref, down_ref, *refs):
    small, (attn_ref, feed_ref, send_ref) = refs[:8], refs[8:]
    core, _, _ = own_place()
    shard = qkv_ref.shape[0]
    qkv, rel, up, out, down = qkv_ref[...], rel_ref[...], up_ref[...], out_ref[...], down_ref[...]
    heads, hd = rel.shape[1] // HEAD_DIM // 2, HEAD_DIM
    unit = up.shape[1] // 8
    packs, ups = [], []
    row = jnp.concatenate([ref[i : i + 1] for ref in small for i in range(ref.shape[0])], axis=1)
    lane = lax.broadcasted_iota(jnp.int32, (1, 4 * heads * hd - row.shape[1]), 1)
    digits = jnp.zeros(lane.shape, f32)
    for slot in range(lengths_ref.shape[0]):
        high = lengths_ref[slot] // DIGIT
        for at, digit in ((2 * slot, high), (2 * slot + 1, lengths_ref[slot] - high * DIGIT)):
            digits = jnp.where(lane == at, digit.astype(f32), digits)
    row = jnp.concatenate([row, digits.astype(row.dtype)], axis=1)
    rows = jnp.broadcast_to(row, (8, row.shape[1]))
    for side in (0, 1):
        parts = [
            qkv[:, ((2 * j + side) * 3 + t) * hd : ((2 * j + side) * 3 + t + 1) * hd]
            for t in range(3)
            for j in range(heads)
        ]
        parts += [rel[:, (2 * j + side) * hd : (2 * j + side + 1) * hd] for j in range(heads)]
        packs.append(jnp.concatenate(parts, axis=1))
        ups.append(
            jnp.concatenate([up[:, (2 * j + side) * unit : (2 * j + side + 1) * unit] for j in range(4)], axis=1)
        )
    first = core == 0
    folded = jnp.concatenate([out[: shard // 2], out[shard // 2 :]], axis=1)
    attn_ref[:shard] = jnp.where(first, packs[0], packs[1])
    attn_ref[shard:] = rows
    send_ref[:shard] = jnp.where(first, packs[1], packs[0])
    send_ref[shard : shard + 8] = rows
    send_ref[shard + 8 : 2 * shard + 8] = jnp.where(first, ups[1], ups[0])
    send_ref[2 * shard + 8 :] = folded
    feed_ref[:shard] = jnp.where(first, ups[0], ups[1])
    feed_ref[shard : shard + shard // 2] = folded
    feed_ref[shard + shard // 2 :] = jnp.concatenate([down[: 2 * shard], down[2 * shard :]], axis=1)


def ordered(core, own, other):
    first = core == 0
    return jnp.concatenate([jnp.where(first, own, other), jnp.where(first, other, own)], axis=0)


def slot_block(core, rank, step, own, other, store):
    turn = (step >> 1) ^ (rank & 1)
    local = (step & 1) == core
    for t in (0, 1):
        pl.when(local & (turn == t))(functools.partial(store, own[t]))
        pl.when(jnp.logical_not(local) & (turn == t))(functools.partial(store, other[t]))


def norm_rows(values):
    mean_val = jnp.mean(values, axis=1, keepdims=True)
    centered = values - mean_val
    inv_std = lax.rsqrt(jnp.mean(centered * centered, axis=1, keepdims=True) + NORM_EPS)
    return centered * inv_std, inv_std


def project_body(_, *refs):
    packs, own_x, other_x = refs[0:4], refs[4:6], refs[6:8]
    table_ref, qkv_ref, h_ref, x_ref, rel_ref, w_ref, vec_ref, up_ref, *bias_refs = refs[8:18]
    step, (core, chip, rank) = pl.program_id(0), own_place()
    width = w_ref.shape[0]
    shard = width // 8
    span = qkv_ref.shape[1]
    cols = span // 3

    @pl.when(step == 0)
    def _():
        first = core == 0
        vec_ref[...] = jnp.zeros_like(vec_ref)
        own_rows = []
        for k in range(4):
            at = pl.ds(aligned(chip ^ k, 2 * shard), 2 * shard)
            own, other = packs[k][: shard + 8], packs[k][shard + 8 :]
            w_ref[at, :] = ordered(core, own[:shard], other[:shard])
            own_row, other_row = own[shard : shard + 1].astype(f32), other[shard : shard + 1].astype(f32)
            own_rows.append(own_row)
            low, high = jnp.where(first, own_row, other_row), jnp.where(first, other_row, own_row)
            for row, source in enumerate((0, 1, 4, 5, 6)):
                piece = slice(source * shard, (source + 1) * shard)
                vec_ref[row : row + 1, at] = jnp.concatenate([low[:, piece], high[:, piece]], axis=1)
            unit = up_ref.shape[1] // 4
            up_ref[:, pl.ds(aligned(chip ^ k, unit), unit)] = own_row[:, 7 * shard : 7 * shard + unit]
        even = chip & 1 == 0
        for k in (0, 2):
            at = pl.ds(aligned((chip ^ k) >> 1, 2 * shard), 2 * shard)
            low = jnp.where(even, own_rows[k], own_rows[k + 1])
            high = jnp.where(even, own_rows[k + 1], own_rows[k])
            for row, source in enumerate((2, 3)):
                piece = slice(source * shard, (source + 1) * shard)
                bias_refs[row][:, at] = jnp.concatenate([low[:, piece], high[:, piece]], axis=1)

    def copy(ref):
        x_ref[...] = ref[...]

    slot_block(core, rank, step, own_x, other_x, copy)
    x_hat, _ = norm_rows(x_ref[...].astype(f32))
    h = (x_hat * vec_ref[0:1, :] + vec_ref[1:2, :]).astype(bf)
    h_ref[...] = h
    qkv_ref[...] = dot(h, w_ref[:, :span], NN).astype(bf)
    rel_ref[...] = dot(table_ref[...], w_ref[:, span:], NN).astype(bf)


def feed_body(meta, *refs):
    packs, own_g, other_g = refs[0:4], refs[4:6], refs[6:8]
    x_ref, o_own, o_other, vec_ref, bias_ref = refs[8:13]
    dy_ref, x_hat_ref, rstd_ref, y_keep, dh_ref, y_send, wo_mine = refs[13:20]
    outs = refs[20:24]
    up_w, down_w, wo_theirs, up_acc, down_acc, sums = refs[24:30]
    step, chip, core = pl.program_id(0), meta[CHIP], meta[CORE]
    width = up_w.shape[0]
    shard, unit, block = width // 8, down_w.shape[0] // 4, x_ref.shape[0]
    fold = shard // 2
    unfold = lambda rows: jnp.concatenate([rows[:, :width], rows[:, width:]], axis=0)

    @pl.when(step == 0)
    def _():
        sums[...] = jnp.zeros_like(sums)
        up_acc[...] = jnp.zeros_like(up_acc)
        down_acc[...] = jnp.zeros_like(down_acc)
        masks = (0, 1 + core, 2 - core, 3)
        for pack_ref, k in zip(packs, masks):
            pack, other = pack_ref[: 3 * shard + fold], pack_ref[3 * shard + fold :]
            up_w[pl.ds(aligned(chip ^ k, 2 * shard), 2 * shard), :] = ordered(core, pack[:shard], other[:shard])
            at = pl.ds(aligned(chip ^ k, shard), shard)
            wo_mine[at, :] = unfold(pack[shard : shard + fold])
            wo_theirs[at, :] = unfold(other[shard:])
            down_w[pl.ds(aligned(chip ^ k, unit), unit), :] = unfold(pack[shard + fold :])

    at = step * block + lax.broadcasted_iota(jnp.int32, (block, 1), 0)

    def load(ref):
        dy_ref[...] = jnp.where(at < meta[LIVE], ref[...].astype(f32), 0.0).astype(bf)

    slot_block(core, meta[RANK], step, own_g, other_g, load)
    y1 = x_ref[...].astype(f32) + (dot(o_own[...], wo_mine[...], NN) + dot(o_other[...], wo_theirs[...], NN))
    x_hat, inv_std = norm_rows(y1)
    x_hat_ref[...] = x_hat.astype(bf)
    rstd_ref[...] = inv_std
    h = (x_hat * vec_ref[2:3, :] + vec_ref[3:4, :]).astype(bf)
    f = dot(h, up_w[...], NN) + bias_ref[...]
    cdf = 0.5 * (1.0 + lax.erf(f * (1.0 / math.sqrt(2.0))))
    g = (f * cdf).astype(bf)
    dy = dy_ref[...]
    dg = dot(dy, down_w[...], NT)
    df = (dg * (cdf + f * jnp.exp(-0.5 * f * f) * (1.0 / math.sqrt(2.0 * math.pi)))).astype(bf)
    z = dot(g, down_w[...], NN)
    dh = dot(df, up_w[...], NT)
    dh_ref[...] = dh.astype(bf)
    up_acc[...] += dot(h, df, TN)
    down_acc[...] += dot(g, dy, TN)
    sums[0:1, :width] += jnp.sum(dh * x_hat, axis=0, keepdims=True)
    sums[1:2, :width] += jnp.sum(dh, axis=0, keepdims=True)
    sums[3:4, :] += jnp.sum(df.astype(f32), axis=0, keepdims=True)
    local = (step & 1) == core

    @pl.when(local)
    def _():
        y_keep[...] = y1 + z + vec_ref[4:5, :]
        sums[2:3, :width] += jnp.sum(dy.astype(f32), axis=0, keepdims=True)

    @pl.when(jnp.logical_not(local))
    def _():
        y_send[...] = z.astype(bf)

    @pl.when(step == pl.num_programs(0) - 1)
    def _():
        rows = 2 * shard
        for k, out in enumerate(outs):
            at = pl.ds(aligned(chip ^ k, rows), rows)
            units = pl.ds(aligned(chip ^ k, unit), unit)
            tail = [sums[0:1, at], sums[1:2, at], sums[2:3, at], sums[3:4, units]]
            tail = jnp.concatenate(tail + [jnp.zeros((1, sums.shape[1] - 3 * rows - unit), f32)], axis=1)
            out[:rows] = up_acc[at, :].astype(out.dtype)
            out[rows : rows + 8] = jnp.broadcast_to(tail, (8, tail.shape[1])).astype(out.dtype)
            down = down_acc[units, :]
            half = unit // 2
            out[rows + 8 :] = jnp.concatenate([down[:half], down[half:]], axis=1).astype(out.dtype)


def norm_two_body(meta, x_hat_ref, rstd_ref, dh_ref, dh_came, dy_ref, vec_ref, y_keep, y_came, wo_ref, o_ref, *refs):
    out0, out1, resid_ref, do_ref, go_ref = refs
    step = pl.program_id(0)

    @pl.when(step == 0)
    def _():
        go_ref[...] = jnp.zeros_like(go_ref)

    x_hat = x_hat_ref[...].astype(f32)
    e = (dh_ref[...].astype(f32) + dh_came[...].astype(f32)) * vec_ref[2:3, :]
    first = jnp.mean(e, axis=1, keepdims=True)
    second = jnp.mean(e * x_hat, axis=1, keepdims=True)
    grad = dy_ref[...].astype(f32) + rstd_ref[...] * (e - first - x_hat * second)
    da = grad.astype(bf)
    do_ref[...] = dot(da, wo_ref[...], NT).astype(bf)
    go_ref[...] += dot(o_ref[...], da, TN)
    turn = (step >> 1) ^ (meta[RANK] & 1)
    local = (step & 1) == meta[CORE]

    @pl.when(local)
    def _():
        resid_ref[...] = grad
        y = (y_keep[...] + y_came[...].astype(f32)).astype(bf)

        @pl.when(turn == 0)
        def _():
            out0[...] = y

        @pl.when(turn == 1)
        def _():
            out1[...] = y


def qkv_back_body(meta, *refs):
    grads_a, grads_b = refs[:6], refs[6:12]
    w_ref, x_ref, h_ref, table_ref, go_ref = refs[12:17]
    keep_ref, send_ref = refs[17:19]
    outs, acc, sums = refs[19:23], refs[23], refs[24]
    step, chip = pl.program_id(0), meta[CHIP]
    width = x_ref.shape[1]
    rows = width // 4

    @pl.when(step == 0)
    def _():
        sums[...] = jnp.zeros_like(sums)
        acc[...] = jnp.zeros_like(acc)

    both = lambda i: [grads_a[i][...], grads_b[i][...]]
    dqkv = jnp.concatenate(both(0) + both(1) + both(2), axis=1)
    drel = jnp.concatenate(both(3), axis=1)
    span = dqkv.shape[1]
    acc[:, :span] += dot(h_ref[...], dqkv, TN)
    acc[:, span:] += dot(table_ref[...], drel, TN)
    dh = dot(dqkv, w_ref[:, :span], NT)
    x_hat, _ = norm_rows(x_ref[...].astype(f32))
    sums[0:1, :] += jnp.sum(dh * x_hat, axis=0, keepdims=True)
    sums[1:2, :] += jnp.sum(dh, axis=0, keepdims=True)
    local = (step & 1) == meta[CORE]

    @pl.when(local)
    def _():
        keep_ref[...] = dh

    @pl.when(jnp.logical_not(local))
    def _():
        send_ref[...] = dh.astype(bf)

    @pl.when(step == pl.num_programs(0) - 1)
    def _():
        for k, out in enumerate(outs):
            at = pl.ds(aligned(chip ^ k, rows), rows)
            low = (chip ^ k) >> 1 == 0
            tail = [sums[0:1, at], sums[1:2, at]]
            tail += [jnp.where(low, *both(i)) for i in (4, 5)]
            tail = jnp.concatenate(tail + [jnp.zeros((1, acc.shape[1] - 4 * rows), f32)], axis=1)
            out[:rows] = acc[at, :].astype(out.dtype)
            out[rows : rows + 8] = jnp.broadcast_to(tail, (8, tail.shape[1])).astype(out.dtype)
            shard = rows // 2
            lines = go_ref[pl.ds(aligned(chip ^ k, shard), shard), :]
            lines = jnp.concatenate([lines[: shard // 2], lines[shard // 2 :]], axis=1)
            out[rows + 8 :] = lines.astype(out.dtype)


def norm_one_body(meta, x_ref, dh_keep, dh_came, resid_ref, vec_ref, out0, out1):
    turn = pl.program_id(0) ^ (meta[RANK] & 1)
    x_hat, inv_std = norm_rows(x_ref[...].astype(f32))
    e = (dh_keep[...] + dh_came[...].astype(f32)) * vec_ref[0:1, :]
    first = jnp.mean(e, axis=1, keepdims=True)
    second = jnp.mean(e * x_hat, axis=1, keepdims=True)
    grad = (resid_ref[...] + inv_std * (e - first - x_hat * second)).astype(bf)

    @pl.when(turn == 0)
    def _():
        out0[...] = grad

    @pl.when(turn == 1)
    def _():
        out1[...] = grad


def rank_bit(meta, bit):
    return (meta[RANK] >> bit) & 1


def chip_sum_body(meta, own, *refs, bit):
    *came, keep, send = refs
    half = keep.shape[1]
    for out, side in ((keep, rank_bit(meta, bit)), (send, 1 - rank_bit(meta, bit))):
        at = pl.ds(aligned(side, half), half)
        total = own[:, at]
        for ref in came:
            total = total + ref[:, at].astype(f32)
        out[...] = total.astype(out.dtype)


def chip_sum(meta, parts, name, bit):
    rows, size = parts[0].shape
    return kernel_call(functools.partial(chip_sum_body, bit=bit), name, meta, parts, [((rows, size // 2), f32), ((rows, size // 2), bf)])


def own_rows_first(total, core, shard):
    theirs = lax.dynamic_slice_in_dim(total, (1 - core) * shard, shard, 0)
    mine = lax.dynamic_slice_in_dim(total, core * shard, shard, 0)
    came = swap_core(jnp.concatenate([theirs, total[2 * shard : 2 * shard + 8]], axis=0))
    return jnp.concatenate([mine, came, total[2 * shard :]], axis=0)


def halves(meta, mine, other, bit):
    low = rank_bit(meta, bit) == 0
    return jnp.concatenate([jnp.where(low, mine, other), jnp.where(low, other, mine)], axis=1)


def both_cores(meta, own, came):
    own, came = own.astype(f32), came.astype(f32)
    return own, own + came, meta[CORE] == 0


def store_half(ref, source, at, low):
    size = 2 * ref.shape[1]
    piece = source[:, at * size : (at + 1) * size]
    ref[...] = jnp.where(low, piece[:, : size // 2], piece[:, size // 2 :])


def early_out_body(meta, mine, other, came_ref, g_up, g_down, *vec_refs):
    rows = halves(meta, mine[...], other[...], 0)
    came_rows = halves(meta, came_ref[0], came_ref[1], 0)
    shard, width = g_up.shape[0], g_down.shape[1]
    first, unit = meta[CORE] == 0, rows.shape[1] // 4
    own, came = jnp.where(first, rows[:shard], rows[shard : 2 * shard]), came_rows[:shard]
    pair = (jnp.where(first, own, came), jnp.where(first, came, own))
    for j in range(4):
        for side in (0, 1):
            at = (2 * j + side) * unit
            g_up[:, at : at + unit] = pair[side][:, j * unit : (j + 1) * unit].astype(f32)
    down = rows[2 * shard + 8 :].astype(f32)
    g_down[...] = jnp.concatenate([down[:, :width], down[:, width:]], axis=0)
    own, total, low = both_cores(meta, rows[2 * shard : 2 * shard + 1], came_rows[shard : shard + 1])
    for at, ref in enumerate(vec_refs[:3]):
        store_half(ref, total, at, low)
    vec_refs[3][...] = own[:, 6 * shard : 6 * shard + unit]


def late_out_body(meta, mine, other, g_qkv, g_rel, g_out, *vec_refs):
    rows = halves(meta, mine[...], other[...], 0)
    shard, width = g_qkv.shape[0], g_out.shape[1]
    first, hd, heads = meta[CORE] == 0, HEAD_DIM, H // 2
    own, came = rows[:shard], rows[shard : 2 * shard]
    pair = (jnp.where(first, own, came), jnp.where(first, came, own))
    cols = heads * hd
    piece = lambda h, t: pair[h & 1][:, t * cols + (h >> 1) * hd : t * cols + ((h >> 1) + 1) * hd]
    g_qkv[...] = jnp.concatenate([piece(h, t) for h in range(2 * heads) for t in range(3)], axis=1).astype(f32)
    g_rel[...] = jnp.concatenate([piece(h, 3) for h in range(2 * heads)], axis=1).astype(f32)
    out = rows[2 * shard + 16 :].astype(f32)
    g_out[...] = jnp.concatenate([out[:, :width], out[:, width:]], axis=0)
    own, total, low = both_cores(meta, rows[2 * shard + 8 : 2 * shard + 9], rows[2 * shard : 2 * shard + 1])
    even = meta[CHIP] & 1 == 0
    for at, ref in enumerate(vec_refs):
        store_half(ref, total if at < 2 else own, at, low if at < 2 else even)


def place_body(meta, y0, y1, x0, x1, y_ref, x_ref):
    high = meta[RANK] >> 1 == 1
    y_ref[0] = jnp.where(high, y1[...], y0[...])
    y_ref[1] = jnp.where(high, y0[...], y1[...])
    x_ref[0] = jnp.where(high, x1[...], x0[...]).astype(f32)
    x_ref[1] = jnp.where(high, x0[...], x1[...]).astype(f32)


def slot_split_device(
    layer_input,
    lengths,
    ln1_gain,
    ln1_bias,
    w_qkv,
    w_rel,
    bias_u,
    bias_v,
    w_out,
    ln2_gain,
    ln2_bias,
    w_up,
    up_bias,
    w_down,
    down_bias,
    grad_out,
):
    slots, block, width = layer_input.shape
    rank, device = lax.axis_index("seq"), lax.axis_index("fsdp")
    core, chip = device & 1, device >> 1
    full, heads = 4 * block, H // 2
    cols, shard, unit = heads * HEAD_DIM, width // 8, up_bias.shape[0]
    mine_ff = 4 * unit

    none = jnp.zeros((4,), jnp.int32)
    x_own = to_slots(jnp.concatenate([layer_input, grad_out], axis=2), rank)
    vectors = (ln1_gain, ln1_bias, bias_u, bias_v, ln2_gain, ln2_bias, down_bias, up_bias)
    attn_rows, fold = shard + 8, shard // 2
    attn_pack, feed_pack, pack_send = kernel_call(
        pack_body,
        "pack",
        pltpu.with_memory_space_constraint(lengths, pltpu.HBM),
        [
            pltpu.with_memory_space_constraint(v, pltpu.HBM)
            for v in [w_qkv, w_rel, w_up, w_out, w_down] + [v.reshape(-1, min(128, v.size)) for v in vectors]
        ],
        [((attn_rows, 4 * cols), bf), ((3 * shard + fold, 4 * cols), bf), ((attn_rows + shard + fold, 4 * cols), bf)],
        vmem=32,
    )
    pack_came = swap_core(pack_send)
    attn_pack = jnp.concatenate([attn_pack, pack_came[:attn_rows]], axis=0)
    attn_packs = [attn_pack] + [swap_chip(attn_pack, k) for k in (1, 2, 3)]
    feed_pack = jnp.concatenate([feed_pack, pack_came[attn_rows:]], axis=0)
    digits_at = 7 * shard + unit
    digits = pack_came[shard, digits_at : digits_at + 2 * slots].astype(jnp.int32)
    lengths = jnp.where(core == rank >> 1, lengths, digits[0::2] * DIGIT + digits[1::2])
    length = jnp.where(rank & 1 == 0, lengths[0], lengths[1])
    meta = jnp.stack([core, chip, rank, length]).astype(jnp.int32)
    length_arr = length.reshape(1)
    fine = 32
    inv_freq = jnp.exp(lax.iota(f32, width // 2) * (-2.0 * math.log(10000.0) / width))
    high = (full - 1 - fine * lax.iota(jnp.int32, full // fine)).astype(f32)[:, None] * inv_freq
    low = lax.iota(f32, fine)[:, None] * inv_freq
    high_sin, high_cos, low_sin, low_cos = together(jnp.sin(high), jnp.cos(high), jnp.sin(low), jnp.cos(low))
    high_sin, high_cos = high_sin[:, None], high_cos[:, None]
    table = jnp.concatenate(
        [high_sin * low_cos - high_cos * low_sin, high_cos * low_cos + high_sin * low_sin], axis=2
    )
    table = table.astype(bf).reshape(full, width)

    feed_pack, meta, length_arr, table, *attn_packs = together(feed_pack, meta, length_arr, table, *attn_packs)
    rest = list(together(*x_own, *attn_packs))
    x_own, attn_packs = rest[:2], rest[2:]
    x_other = [swap_core(x) for x in x_own]
    feed_first = swap_axis(feed_pack, 0)
    feed_second = swap_axis(feed_pack, 1)

    side = lambda at: pl.BlockSpec((block, width), lambda i, _: (0, at))
    by_step = lambda width: pl.BlockSpec((block, width), lambda i, _: (i, 0))
    qkv, h1, x_slot, rel, w_own, vecs, up_b, own_u, own_v = kernel_call(
        project_body,
        "project",
        none,
        [pltpu.with_memory_space_constraint(v, pltpu.HBM) for v in attn_packs] + x_own + x_other + [table],
        [((full, 3 * cols), bf), ((full, width), bf), ((full, width), bf), ((full, cols), bf)]
        + [((width, 4 * cols), bf), ((8, width), f32), ((1, mine_ff), f32), ((1, cols), f32), ((1, cols), f32)],
        grid=(4,),
        in_specs=[whole(2 * attn_rows, 4 * cols)] * 4 + [side(0)] * 4 + [by_step(width)],
        out_specs=[by_step(3 * cols), by_step(width), by_step(width), by_step(cols)]
        + [whole(width, 4 * cols), whole(8, width), whole(1, mine_ff), whole(1, cols), whole(1, cols)],
        flops=2 * full * width * 4 * cols,
        vmem=32,
    )
    qkv, feed_first = together(qkv, feed_first)
    feed_third = swap_axis(feed_first, 1)
    attn, *probs = attn_fwd(length_arr, qkv, rel, own_u, own_v)
    attn, feed_second, feed_third = together(attn, feed_second, feed_third)
    feed_packs = [feed_pack, feed_first, feed_second, feed_third]

    attn_other = swap_core(attn)
    kept = lambda width: pl.BlockSpec((block, width), lambda i, _: (i >> 1, 0))
    half, rows = full // 2, 2 * shard + 8
    blocks = lambda rows: [((rows, 2 * width), f32)] + [((rows, 2 * width), bf)] * 3
    dy, x_hat, rstd, y_keep, dh, y_send, wo_mine, *early_parts = kernel_call(
        feed_body,
        "feed",
        meta,
        feed_packs + x_own + x_other + [x_slot, attn, attn_other, vecs, up_b],
        [((full, width), bf), ((full, width), bf), ((full, 1), f32), ((half, width), f32)]
        + [((full, width), bf), ((half, width), bf), ((cols, width), bf)]
        + blocks(rows + unit // 2),
        grid=(4,),
        in_specs=[whole(*feed_pack.shape)] * 4 + [side(1)] * 4
        + [by_step(width), by_step(cols), by_step(cols), whole(8, width), whole(1, mine_ff)],
        out_specs=[by_step(width), by_step(width), by_step(1), kept(width)]
        + [by_step(width), kept(width), whole(cols, width)]
        + [whole(rows + unit // 2, 2 * width)] * 4,
        scratch=[
            pltpu.VMEM((width, mine_ff), bf),
            pltpu.VMEM((mine_ff, width), bf),
            pltpu.VMEM((cols, width), bf),
            pltpu.VMEM((width, mine_ff), f32),
            pltpu.VMEM((mine_ff, width), f32),
            pltpu.VMEM((8, mine_ff), f32),
        ],
        flops=12 * full * width * mine_ff,
    )
    dh_came = swap_core(dh)
    y_came = swap_core(y_send)
    early_came = [swap_chip(early_parts[k], k) for k in (1, 2, 3)]
    out0, out1, g_resid, d_attn, g_out = kernel_call(
        norm_two_body,
        "norm_two",
        meta,
        [x_hat, rstd, dh, dh_came, dy, vecs, y_keep, y_came, wo_mine, attn],
        [((block, width), bf)] * 2 + [((half, width), f32), ((full, cols), bf), ((cols, width), f32)],
        grid=(4,),
        in_specs=[by_step(width), by_step(1)] + [by_step(width)] * 3 + [whole(8, width)] + [kept(width)] * 2
        + [whole(cols, width), by_step(cols)],
        out_specs=[whole(block, width)] * 2 + [kept(width), by_step(cols), whole(cols, width)],
        flops=4 * full * width * cols,
    )
    home = lambda outs: [
        lax.ppermute(out, ("fsdp", "seq"), [(b, a) for a, b in slot_pairs(turn)])
        for turn, out in enumerate(outs)
    ]
    y_turns = home((out0, out1))
    back = lambda pair, d_out: attn_bwd(length_arr, qkv, rel, own_u, own_v, probs, d_out, pair=pair)
    d_attn, *grads_a = together(d_attn, *back(0, d_attn))
    *grads_b, y0, y1, e1, e2, e3 = together(*back(1, d_attn), *y_turns, *early_came)
    early_keep, early_send = chip_sum(meta, [early_parts[0], e1, e2, e3], "early_chips", 0)
    early_send, *grads_b = together(early_send, *grads_b)
    early_came = swap_seq(early_send, 1)
    pair_step = pl.BlockSpec((block, 2 * HEAD_DIM), lambda i, _: (i, 0))
    pair_row = whole(1, 2 * HEAD_DIM)
    dh1_keep, dh1_send, *late_parts = kernel_call(
        qkv_back_body,
        "qkv_back",
        meta,
        [*grads_a, *grads_b, w_own, x_slot, h1, table, g_out],
        [((half, width), f32), ((half, width), bf)] + blocks(rows + fold),
        grid=(4,),
        in_specs=([pair_step] * 4 + [pair_row] * 2) * 2
        + [whole(width, 4 * cols)] + [by_step(width)] * 3 + [whole(cols, width)],
        out_specs=[kept(width)] * 2 + [whole(rows + fold, 2 * width)] * 4,
        scratch=[pltpu.VMEM((width, 4 * cols), f32), pltpu.VMEM((8, width), f32)],
        flops=14 * full * width * cols,
    )
    dh1_send, *late_parts = together(dh1_send, *late_parts)
    early_pair = (early_keep + early_came.astype(f32)).astype(bf)
    dh1_came = swap_core(dh1_send)
    early_came = swap_seq(early_pair, 2)
    late_came = [swap_chip(late_parts[k], k) for k in (1, 2, 3)]
    by_half = pl.BlockSpec((block, width), lambda i, _: (i, 0))
    own_rows = pl.BlockSpec((block, width), lambda i, m: (2 * i + m[CORE], 0))
    x0, x1 = kernel_call(
        norm_one_body,
        "norm_one",
        meta,
        [x_slot, dh1_keep, dh1_came, g_resid, vecs],
        [((block, width), bf)] * 2,
        grid=(2,),
        in_specs=[own_rows] + [by_half] * 3 + [whole(8, width)],
        out_specs=[whole(block, width)] * 2,
    )
    x_turns = home((x0, x1))
    late_keep, late_send = chip_sum(meta, [late_parts[0]] + late_came, "late_chips", 0)
    small = lambda size: ((1, size), f32)
    late_came, early_came, x_turns[0] = together(swap_seq(late_send, 1), early_came, x_turns[0])
    early_mine = (early_pair.astype(f32) + early_came.astype(f32)).astype(bf)
    late_pair = (late_keep + late_came.astype(f32)).astype(bf)
    late_came = swap_seq(late_pair, 2)
    early_other = swap_seq(early_mine, 1)
    late_total = (late_pair.astype(f32) + late_came.astype(f32)).astype(bf)
    late_mine = own_rows_first(late_total, core, shard)
    late_other = swap_seq(late_mine, 1)
    late_mine, g0, g1, early_other = together(late_mine, *x_turns, early_other)
    theirs = lambda rows: jnp.concatenate(
        [
            lax.dynamic_slice_in_dim(rows, (1 - core) * shard, shard, 0),
            rows[2 * shard : 2 * shard + 8],
        ],
        axis=0,
    )
    early_core = swap_core(jnp.stack([theirs(early_mine), theirs(early_other)]))
    output, grad_x = kernel_call(
        place_body,
        "place",
        meta,
        [y0, y1, g0, g1],
        [((2, block, width), bf), ((2, block, width), f32)],
    )
    g_up, g_down, g_gain_two, g_shift_two, g_down_shift, g_up_shift = kernel_call(
        early_out_body,
        "early_out",
        meta,
        [early_mine, early_other, early_core],
        [((shard, 2 * mine_ff), f32), ((unit, width), f32)] + [small(shard)] * 3 + [small(unit)],
    )
    late_other, output, grad_x, g_up = together(late_other, output, grad_x, g_up)
    g_qkv, g_rel, g_w_out, *late_vectors = kernel_call(
        late_out_body,
        "late_out",
        meta,
        [late_mine, late_other],
        [((shard, 6 * cols), f32), ((shard, 2 * cols), f32), ((shard, width), f32)] + [small(shard)] * 4,
    )
    g_gain_one, g_shift_one, g_bias_u, g_bias_v = [v.reshape(-1) for v in late_vectors]
    return (
        output,
        grad_x,
        g_gain_one,
        g_shift_one,
        g_qkv,
        g_rel,
        g_bias_u,
        g_bias_v,
        g_w_out,
        g_gain_two.reshape(-1),
        g_shift_two.reshape(-1),
        g_up,
        g_up_shift.reshape(-1),
        g_down,
        g_down_shift.reshape(-1),
    )


def per_device(*args):
    one_slot_a_chip = lax.axis_size("fsdp") == 8 and lax.axis_size("seq") == 4
    if one_slot_a_chip and args[0].shape[0] == 2:
        return slot_split_device(*args)
    return head_split_device(*args)


def solution(mesh):
    placed = (
        P("fsdp", "seq", None),
        P("fsdp"),
        P("fsdp"),
        P("fsdp"),
        P("fsdp", None),
        P("fsdp", None),
        P("fsdp"),
        P("fsdp"),
        P("fsdp", None),
        P("fsdp"),
        P("fsdp"),
        P("fsdp", None),
        P("fsdp"),
        P("fsdp", None),
        P("fsdp"),
        P("fsdp", "seq", None),
    )
    return jax.shard_map(
        per_device,
        mesh=mesh,
        in_specs=placed,
        out_specs=(
            P("fsdp", "seq", None),
            P("fsdp", "seq", None),
            P("fsdp"),
            P("fsdp"),
            P("fsdp", None),
            P("fsdp", None),
            P("fsdp"),
            P("fsdp"),
            P("fsdp", None),
            P("fsdp"),
            P("fsdp"),
            P("fsdp", None),
            P("fsdp"),
            P("fsdp", None),
            P("fsdp"),
        ),
        check_vma=False,
    )
```

```python
import functools
import math

import jax
import jax.numpy as jnp
from jax import lax
from jax.experimental import pallas as pl
from jax.experimental.pallas import tpu as pltpu
from jax.sharding import PartitionSpec as P

H = 8
HEAD_DIM = 64


NEG_FILL = -1e30
NORM_EPS = 1e-05


bf, f32 = jnp.bfloat16, jnp.float32
NEG = NEG_FILL
HD = HEAD_DIM
NT = (((1,), (1,)), ((), ()))
NN = (((1,), (0,)), ((), ()))


def dot(a, b, dims):
    return lax.dot_general(a, b, dims, preferred_element_type=f32)


def masked_tail(s, keep, block):
    tail = jnp.where(keep, s[:, s.shape[1] - block :], NEG)
    if s.shape[1] == block:
        return tail
    return jnp.concatenate([s[:, : s.shape[1] - block], tail], axis=1)


def scores(qu, qv, keys, rel_rev, keep, block):
    span = keys.shape[0]
    rel = dot(qv, rel_rev, NT)
    rel = pltpu.roll(rel, (span - block + 1) % span, 1, stride=1, stride_axis=0)
    return masked_tail(dot(qu, keys, NT) + rel, keep, block)


def attn_fwd_body(len_ref, q_ref, k_ref, v_ref, r_ref, bu_ref, bv_ref, o_ref, *p_refs, block):
    full = q_ref.shape[0]
    lane = lax.broadcasted_iota(jnp.int32, (block, 2 * HD), 1)
    sides = (lane < HD, lane >= HD)
    length = len_ref[0]
    col = lax.broadcasted_iota(jnp.int32, (1, full), 1)
    bias = jnp.where(col < length, 0.0, NEG)
    tri = lax.broadcasted_iota(jnp.int32, (block, block), 1) <= lax.broadcasted_iota(
        jnp.int32, (block, block), 0
    )
    for first in range(0, full, block):
        span = first + block
        q = q_ref[first:span, :].astype(f32)
        qu = (q + bu_ref[...]).astype(bf).astype(f32) * 0.125
        qv = (q + bv_ref[...]).astype(bf).astype(f32) * 0.125
        outs = []
        for head, side in enumerate(sides):
            s = scores(
                jnp.where(side, qu, 0.0).astype(bf),
                jnp.where(side, qv, 0.0).astype(bf),
                k_ref[:span, :],
                r_ref[full - span :, :],
                tri,
                block,
            )
            if span > full // 2:
                s = s + bias[:, :span]
            top = jnp.max(s, axis=1, keepdims=True)
            e = jnp.exp(s - top)
            total = jnp.sum(e, axis=1, keepdims=True)
            p = (e * (1.0 / total)).astype(bf)
            p_refs[first // block][head] = p
            outs.append(dot(p, v_ref[:span, :], NN))
        o_ref[first:span, :] = jnp.where(sides[0], outs[0], outs[1]).astype(bf)


def attn_fwd(length, qkv, rel_rev, bias_u, bias_v, *, block=256):
    full, cols = rel_rev.shape
    spans = range(block, full + 1, block)
    pairs = cols // (2 * HD)
    at = lambda part: pl.BlockSpec((full, 2 * HD), lambda pair, _: (0, part * pairs + pair))
    row = pl.BlockSpec((1, 2 * HD), lambda pair, _: (0, pair))
    return pl.pallas_call(
        functools.partial(attn_fwd_body, block=block),
        out_shape=(
            jax.ShapeDtypeStruct((full, cols), bf),
            *(jax.ShapeDtypeStruct((2 * pairs, block, span), bf) for span in spans),
        ),
        grid_spec=pltpu.PrefetchScalarGridSpec(
            num_scalar_prefetch=1,
            grid=(pairs,),
            in_specs=[at(0), at(1), at(2), at(0), row, row],
            out_specs=(
                at(0),
                *(pl.BlockSpec((2, block, span), lambda pair, _: (pair, 0, 0)) for span in spans),
            ),
        ),
        cost_estimate=pl.CostEstimate(flops=0, bytes_accessed=0, transcendentals=0),
        compiler_params=pltpu.CompilerParams(vmem_limit_bytes=32 << 20),
        name="attn_fwd",
    )(length, qkv, qkv, qkv, rel_rev, bias_u, bias_v)


def attn_bwd_body(len_ref, q_ref, k_ref, v_ref, r_ref, bu_ref, bv_ref, do_ref, *refs, block, heads):
    full = q_ref.shape[0]
    p_refs, refs = refs[: full // block], refs[full // block :]
    dq_ref, dk_ref, dv_ref, dr_ref, gu_ref, gv_ref, dk_t, dv_t, dr_t = refs
    length = len_ref[0]
    lane = lax.broadcasted_iota(jnp.int32, (block, 2 * HD), 1)
    sides = (lane < HD, lane >= HD)
    rows = lax.broadcasted_iota(jnp.int32, (block, block), 0)
    cols = lax.broadcasted_iota(jnp.int32, (block, block), 1)
    flip = jnp.where(rows + cols == block - 1, 1.0, 0.0).astype(bf)
    for ref in (dk_t, dv_t, dr_t, dq_ref, gu_ref, gv_ref):
        ref[...] = jnp.zeros_like(ref)
    for first in range(0, full, block):
        span = first + block

        def one_block(first=first, span=span):
            q = q_ref[first:span, :].astype(f32)
            qu = (q + bu_ref[...]).astype(bf).astype(f32) * 0.125
            qv = (q + bv_ref[...]).astype(bf).astype(f32) * 0.125
            do = do_ref[first:span, :].astype(f32)
            qu_t = jnp.transpose(qu).astype(bf)
            do_t = jnp.transpose(do).astype(bf)
            qv_t = jnp.transpose(dot(flip, qv.astype(bf), NN)).astype(bf)
            dqu, dqv = [0.0, 0.0], [0.0, 0.0]
            for head in heads:
                side = sides[head]
                at = slice(head * HD, (head + 1) * HD)
                rounded = p_refs[first // block][head - heads[0]]
                p = rounded.astype(f32)
                dp = dot(jnp.where(side, do, 0.0).astype(bf), v_ref[:span, :], NT)
                t = p * dp
                ds = (t - p * jnp.sum(t, axis=1, keepdims=True)).astype(bf)
                dv_t[at, :span] += dot(do_t[at], rounded, NN)
                both = dot(jnp.concatenate([qu_t[at], flip], axis=0), ds, NN)
                dk_t[at, :span] += both[:HD]
                dqu[head] = dot(ds, k_ref[:span, :], NN)
                ds_rev = pltpu.roll(both[HD:], 0, 1, stride=1, stride_axis=0).astype(bf)
                dr_t[at, full - span :] += dot(qv_t[at], ds_rev, NN)
                dqv[head] = dot(ds_rev, r_ref[full - span :, :], NN)
            dqu = jnp.where(sides[0], dqu[0], dqu[1]) * 0.125
            dqv = jnp.where(sides[0], dqv[0], dqv[1]) * 0.125
            gu_ref[...] += jnp.sum(dqu, axis=0, keepdims=True)
            gv_ref[...] += jnp.sum(dqv, axis=0, keepdims=True)
            dq_ref[first:span, :] = (dqu + dot(flip, dqv.astype(bf), NN)).astype(bf)

        if first < full // 2:
            one_block()
        else:
            pl.when(first < length)(one_block)

    dk_ref[...] = jnp.transpose(dk_t[...]).astype(bf)
    dv_ref[...] = jnp.transpose(dv_t[...]).astype(bf)
    dr_ref[...] = jnp.transpose(dr_t[...]).astype(bf)


def attn_bwd(length, qkv, rel_rev, bias_u, bias_v, probs, d_out, *, pair, heads=(0, 1), block=256):
    full, cols = rel_rev.shape
    pairs = cols // (2 * HD)
    at = lambda part: pl.BlockSpec((full, 2 * HD), lambda i, _: (0, part * pairs + pair))
    row = pl.BlockSpec((1, 2 * HD), lambda i, _: (0, pair))
    out = pl.BlockSpec((full, 2 * HD), lambda i, _: (0, 0))
    out_row = pl.BlockSpec((1, 2 * HD), lambda i, _: (0, 0))
    return pl.pallas_call(
        functools.partial(attn_bwd_body, block=block, heads=heads),
        out_shape=(jax.ShapeDtypeStruct((full, 2 * HD), bf),) * 4
        + (jax.ShapeDtypeStruct((1, 2 * HD), f32),) * 2,
        grid_spec=pltpu.PrefetchScalarGridSpec(
            num_scalar_prefetch=1,
            grid=(1,),
            in_specs=[at(0), at(1), at(2), at(0), row, row]
            + [at(0)]
            + [
                pl.BlockSpec((len(heads),) + p.shape[1:], lambda i, _: ((2 * pair + heads[0]) // len(heads), 0, 0))
                for p in probs
            ],
            out_specs=(out,) * 4 + (out_row, out_row),
            scratch_shapes=[pltpu.VMEM((2 * HD, full), f32)] * 3,
        ),
        cost_estimate=pl.CostEstimate(flops=0, bytes_accessed=0, transcendentals=0),
        compiler_params=pltpu.CompilerParams(vmem_limit_bytes=32 << 20),
        name="attn_bwd",
    )(length, qkv, qkv, qkv, rel_rev, bias_u, bias_v, d_out, *probs)


def norm_parts(values):
    mean_val = jnp.mean(values, axis=-1, keepdims=True)
    centered = values - mean_val
    inv_std = lax.rsqrt(jnp.mean(centered * centered, axis=-1, keepdims=True) + NORM_EPS)
    return (centered * inv_std, inv_std)


def norm_back(grad_norm, x_hat, inv_std):
    first_mean = jnp.mean(grad_norm, axis=-1, keepdims=True)
    second_mean = jnp.mean(grad_norm * x_hat, axis=-1, keepdims=True)
    return inv_std * (grad_norm - first_mean - x_hat * second_mean)


def position_table(count_rows, feature_count):
    steps = lax.iota(jnp.float32, count_rows)
    half_count = feature_count // 2
    inv_freq = jnp.exp(
        lax.iota(jnp.float32, half_count) * (-2.0 * math.log(10000.0) / feature_count)
    )
    angles = steps[:, None] * inv_freq[None, :]
    return jnp.concatenate([jnp.sin(angles), jnp.cos(angles)], axis=1)


def skew_rows(matrix):
    leading = matrix.shape[:-2]
    row_count, col_count = matrix.shape[-2:]
    flattened = matrix.reshape(leading + (row_count * col_count,))
    picked = flattened[..., row_count - 1 : row_count - 1 + row_count * (col_count - 1)]
    return picked.reshape(leading + (row_count, col_count - 1))[..., : col_count - row_count]


def unskew_rows(matrix):
    leading = matrix.shape[:-2]
    row_count, key_count = matrix.shape[-2:]
    axis_pos = len(leading)
    widened = jnp.pad(matrix, [(0, 0)] * axis_pos + [(0, 0), (0, row_count - 1)])
    flattened = widened.reshape(leading + (row_count * (key_count + row_count - 1),))
    flattened = jnp.pad(flattened, [(0, 0)] * axis_pos + [(row_count - 1, 1)])
    return flattened.reshape(leading + (row_count, key_count + row_count))


def head_split_device(
    layer_input,
    lengths,
    ln1_gain,
    ln1_bias,
    w_qkv,
    w_rel,
    bias_u,
    bias_v,
    w_out,
    ln2_gain,
    ln2_bias,
    w_up,
    up_bias,
    w_down,
    down_bias,
    grad_out,
):
    weights = (
        lax.all_gather(ln1_gain, "fsdp", axis=0, tiled=True),
        lax.all_gather(ln1_bias, "fsdp", axis=0, tiled=True),
        lax.all_gather(w_qkv, "fsdp", axis=0, tiled=True),
        lax.all_gather(w_rel, "fsdp", axis=0, tiled=True),
        lax.all_gather(bias_u, "fsdp", axis=0, tiled=True),
        lax.all_gather(bias_v, "fsdp", axis=0, tiled=True),
        lax.all_gather(w_out, "fsdp", axis=0, tiled=True),
        lax.all_gather(ln2_gain, "fsdp", axis=0, tiled=True),
        lax.all_gather(ln2_bias, "fsdp", axis=0, tiled=True),
        lax.all_gather(w_up, "fsdp", axis=0, tiled=True),
        lax.all_gather(up_bias, "fsdp", axis=0, tiled=True),
        lax.all_gather(w_down, "fsdp", axis=0, tiled=True),
        lax.all_gather(down_bias, "fsdp", axis=0, tiled=True),
    )
    (
        gain_one,
        shift_one,
        query_key_value_matrix,
        rel_weight,
        first_bias,
        second_bias,
        output_matrix,
        gain_two,
        shift_two,
        up_matrix,
        up_shift,
        down_matrix,
        down_shift,
    ) = weights
    gain_one = gain_one.astype(jnp.float32)
    shift_one = shift_one.astype(jnp.float32)
    gain_two = gain_two.astype(jnp.float32)
    shift_two = shift_two.astype(jnp.float32)
    up_shift = up_shift.astype(jnp.float32)
    down_shift = down_shift.astype(jnp.float32)
    slots, block_len, width = layer_input.shape
    seq_count = lax.axis_size("seq")
    seq_rank = lax.axis_index("seq")
    head_dim = HEAD_DIM
    group = H // seq_count
    full_len = block_len * seq_count
    score_scale = 1.0 / math.sqrt(head_dim)
    q_block = 512
    num_blocks = full_len // q_block
    win_len = full_len + q_block
    x_float = layer_input.astype(jnp.float32)
    x_hat_one, inv_std_one = norm_parts(x_float)
    first_normalized = (x_hat_one * gain_one + shift_one).astype(jnp.bfloat16)
    qkv_local = jnp.einsum(
        "mcr,rk->mck", first_normalized, query_key_value_matrix, preferred_element_type=jnp.float32
    ).astype(jnp.bfloat16)
    qkv_heads = lax.all_to_all(qkv_local, "seq", split_axis=2, concat_axis=1, tiled=True)
    qkv_heads = qkv_heads.reshape(slots, full_len, group, 3, head_dim)
    queries = qkv_heads[:, :, :, 0]
    keys = qkv_heads[:, :, :, 1]
    values = qkv_heads[:, :, :, 2]
    head_start = seq_rank * group
    head_bias_u = lax.dynamic_slice_in_dim(
        first_bias.astype(jnp.float32).reshape(H, head_dim), head_start, group, 0
    )
    head_bias_v = lax.dynamic_slice_in_dim(
        second_bias.astype(jnp.float32).reshape(H, head_dim), head_start, group, 0
    )
    query_u = (queries.astype(jnp.float32) + head_bias_u).astype(jnp.bfloat16)
    query_v = (queries.astype(jnp.float32) + head_bias_v).astype(jnp.bfloat16)
    table_rev = position_table(full_len, width).astype(jnp.bfloat16)[::-1]
    rel_cols = lax.dynamic_slice_in_dim(rel_weight, head_start * head_dim, group * head_dim, 1)
    rel_rev = jnp.dot(table_rev, rel_cols, preferred_element_type=jnp.float32).astype(jnp.bfloat16)
    rel_ext = jnp.concatenate([rel_rev, jnp.zeros_like(rel_rev)], axis=0).reshape(
        2 * full_len, group, head_dim
    )
    col_ids = lax.iota(jnp.int32, full_len)

    def scores_block(first_row):
        qu_part = lax.dynamic_slice_in_dim(query_u, first_row, q_block, 1)
        qv_part = lax.dynamic_slice_in_dim(query_v, first_row, q_block, 1)
        window_start = full_len - q_block - first_row
        rel_win = lax.dynamic_slice_in_dim(rel_ext, window_start, win_len, 0)
        content = jnp.einsum("sqhe,skhe->shqk", qu_part, keys, preferred_element_type=jnp.float32)
        rel_raw = jnp.einsum("sqhe,the->shqt", qv_part, rel_win, preferred_element_type=jnp.float32)
        rel_part = skew_rows(rel_raw)
        row_ids = first_row + lax.iota(jnp.int32, q_block)
        causal = col_ids[None, :] <= row_ids[:, None]
        inside = col_ids[None, :] < lengths[:, None]
        allowed = causal[None, None, :, :] & inside[:, None, None, :]
        scores = jnp.where(allowed, (content + rel_part) * score_scale, NEG_FILL)
        return (scores, qu_part, qv_part, rel_win, window_start)

    def forward_block(block_index):
        first_row = block_index * q_block
        scores, qu_part, qv_part, rel_win, window_start = scores_block(first_row)
        top = jnp.max(scores, axis=-1, keepdims=True)
        expo = jnp.exp(scores - top)
        total = jnp.sum(expo, axis=-1, keepdims=True)
        probs = (expo / total).astype(jnp.bfloat16)
        out_part = jnp.einsum(
            "shqk,skhe->sqhe", probs, values, preferred_element_type=jnp.float32
        ).astype(jnp.bfloat16)
        return (out_part, top[..., 0] + jnp.log(total[..., 0]))

    block_outs, block_lse = lax.map(forward_block, jnp.arange(num_blocks, dtype=jnp.int32))
    attn_heads = jnp.moveaxis(block_outs, 0, 1).reshape(slots, full_len, group * head_dim)
    attention_sequence = lax.all_to_all(attn_heads, "seq", split_axis=1, concat_axis=2, tiled=True)
    attention_projected = jnp.einsum(
        "mcr,rk->mck", attention_sequence, output_matrix, preferred_element_type=jnp.float32
    )
    resid = x_float + attention_projected
    x_hat_two, inv_std_two = norm_parts(resid)
    second_normalized = (x_hat_two * gain_two + shift_two).astype(jnp.bfloat16)
    pre_act = (
        jnp.einsum("oka,ac->okc", second_normalized, up_matrix, preferred_element_type=jnp.float32)
        + up_shift
    )
    normal_cdf = 0.5 * (1.0 + lax.erf(pre_act * (1.0 / math.sqrt(2.0))))
    hidden_state = (pre_act * normal_cdf).astype(jnp.bfloat16)
    down_proj = (
        jnp.einsum("zcp,pr->zcr", hidden_state, down_matrix, preferred_element_type=jnp.float32)
        + down_shift
    )
    output = (resid + down_proj).astype(jnp.bfloat16)
    positions = seq_rank * block_len + lax.iota(jnp.int32, block_len)
    live = (positions[None, :] < lengths[:, None]).astype(jnp.bfloat16)
    result_gradient = grad_out * live[:, :, None]
    grad_y_float = result_gradient.astype(jnp.float32)
    g_down_shift = jnp.sum(grad_y_float, axis=(0, 1))
    down_gradient = jnp.einsum(
        "hki,hku->iu", hidden_state, result_gradient, preferred_element_type=jnp.float32
    )
    hidden_gradient = jnp.einsum(
        "gvu,ju->gvj", result_gradient, down_matrix, preferred_element_type=jnp.float32
    )
    deriv = normal_cdf + pre_act * jnp.exp(-0.5 * pre_act * pre_act) * (
        1.0 / math.sqrt(2.0 * math.pi)
    )
    preactivation_gradient = (hidden_gradient * deriv).astype(jnp.bfloat16)
    g_up_shift = jnp.sum(preactivation_gradient.astype(jnp.float32), axis=(0, 1))
    up_gradient = jnp.einsum(
        "oiz,oix->zx", second_normalized, preactivation_gradient, preferred_element_type=jnp.float32
    )
    second_norm_gradient = jnp.einsum(
        "rau,ku->rak", preactivation_gradient, up_matrix, preferred_element_type=jnp.float32
    )
    g_gain_two = jnp.sum(second_norm_gradient * x_hat_two, axis=(0, 1))
    g_shift_two = jnp.sum(second_norm_gradient, axis=(0, 1))
    g_resid = grad_y_float + norm_back(second_norm_gradient * gain_two, x_hat_two, inv_std_two)
    attention_gradient = g_resid.astype(jnp.bfloat16)
    output_gradient = jnp.einsum(
        "zau,zam->um", attention_sequence, attention_gradient, preferred_element_type=jnp.float32
    )
    g_attn_seq = jnp.einsum(
        "urz,jz->urj", attention_gradient, output_matrix, preferred_element_type=jnp.float32
    ).astype(jnp.bfloat16)
    g_attn_heads = lax.all_to_all(
        g_attn_seq, "seq", split_axis=2, concat_axis=1, tiled=True
    ).reshape(slots, full_len, group, head_dim)

    def backward_block(carry, block_index):
        g_keys, g_vals, g_ext = carry
        first_row = block_index * q_block
        scores, qu_part, qv_part, rel_win, window_start = scores_block(first_row)
        probs = jnp.exp(scores - block_lse[block_index][..., None])
        d_out = lax.dynamic_slice_in_dim(g_attn_heads, first_row, q_block, 1)
        g_vals = g_vals + jnp.einsum(
            "shqk,sqhe->skhe", probs.astype(jnp.bfloat16), d_out, preferred_element_type=jnp.float32
        )
        g_probs = jnp.einsum("sqhe,skhe->shqk", d_out, values, preferred_element_type=jnp.float32)
        inner = jnp.sum(probs * g_probs, axis=-1, keepdims=True)
        g_scores = (probs * (g_probs - inner)).astype(jnp.bfloat16)
        g_qu = (
            jnp.einsum("shqk,skhe->sqhe", g_scores, keys, preferred_element_type=jnp.float32)
            * score_scale
        )
        g_keys = (
            g_keys
            + jnp.einsum("shqk,sqhe->skhe", g_scores, qu_part, preferred_element_type=jnp.float32)
            * score_scale
        )
        g_wide = unskew_rows(g_scores)
        g_qv = (
            jnp.einsum("shqt,the->sqhe", g_wide, rel_win, preferred_element_type=jnp.float32)
            * score_scale
        )
        g_win = (
            jnp.einsum("shqt,sqhe->sthe", g_wide, qv_part, preferred_element_type=jnp.float32)
            * score_scale
        )
        g_old = lax.dynamic_slice_in_dim(g_ext, window_start, win_len, 1)
        g_ext = lax.dynamic_update_slice_in_dim(g_ext, g_old + g_win, window_start, 1)
        return ((g_keys, g_vals, g_ext), (g_qu, g_qv))

    zero_heads = jnp.zeros((slots, full_len, group, head_dim), jnp.float32)
    zero_ext = jnp.zeros((slots, 2 * full_len, group, head_dim), jnp.float32)
    (g_keys, g_vals, g_ext), (g_qu_blocks, g_qv_blocks) = lax.scan(
        backward_block, (zero_heads, zero_heads, zero_ext), jnp.arange(num_blocks, dtype=jnp.int32)
    )
    g_qu = jnp.moveaxis(g_qu_blocks, 0, 1).reshape(slots, full_len, group, head_dim)
    g_qv = jnp.moveaxis(g_qv_blocks, 0, 1).reshape(slots, full_len, group, head_dim)
    g_queries = g_qu + g_qv
    g_bias_u_heads = jnp.sum(g_qu, axis=(0, 1))
    g_bias_v_heads = jnp.sum(g_qv, axis=(0, 1))
    g_qkv_heads = (
        jnp.stack([g_queries, g_keys, g_vals], axis=3)
        .astype(jnp.bfloat16)
        .reshape(slots, full_len, group * 3 * head_dim)
    )
    query_key_value_gradient = lax.all_to_all(
        g_qkv_heads, "seq", split_axis=1, concat_axis=2, tiled=True
    )
    g_rel_low = g_ext[:, :full_len].astype(jnp.bfloat16)
    g_rel_heads = jnp.einsum(
        "td,sthe->dhe", table_rev, g_rel_low, preferred_element_type=jnp.float32
    ).reshape(width, group * head_dim)
    g_rel_weight = lax.dynamic_update_slice_in_dim(
        jnp.zeros((width, width), jnp.float32), g_rel_heads, head_start * head_dim, 1
    )
    g_bias_u = lax.dynamic_update_slice_in_dim(
        jnp.zeros((H, head_dim), jnp.float32), g_bias_u_heads, head_start, 0
    ).reshape(width)
    g_bias_v = lax.dynamic_update_slice_in_dim(
        jnp.zeros((H, head_dim), jnp.float32), g_bias_v_heads, head_start, 0
    ).reshape(width)
    query_key_value_weight_gradient = jnp.einsum(
        "zau,zam->um",
        first_normalized,
        query_key_value_gradient,
        preferred_element_type=jnp.float32,
    )
    first_norm_gradient = jnp.einsum(
        "urz,jz->urj",
        query_key_value_gradient,
        query_key_value_matrix,
        preferred_element_type=jnp.float32,
    )
    g_gain_one = jnp.sum(first_norm_gradient * x_hat_one, axis=(0, 1))
    g_shift_one = jnp.sum(first_norm_gradient, axis=(0, 1))
    g_input = g_resid + norm_back(first_norm_gradient * gain_one, x_hat_one, inv_std_one)
    partial_shards = (
        lax.psum_scatter(g_gain_one, "fsdp", scatter_dimension=0, tiled=True),
        lax.psum_scatter(g_shift_one, "fsdp", scatter_dimension=0, tiled=True),
        lax.psum_scatter(query_key_value_weight_gradient, "fsdp", scatter_dimension=0, tiled=True),
        lax.psum_scatter(g_rel_weight, "fsdp", scatter_dimension=0, tiled=True),
        lax.psum_scatter(g_bias_u, "fsdp", scatter_dimension=0, tiled=True),
        lax.psum_scatter(g_bias_v, "fsdp", scatter_dimension=0, tiled=True),
        lax.psum_scatter(output_gradient, "fsdp", scatter_dimension=0, tiled=True),
        lax.psum_scatter(g_gain_two, "fsdp", scatter_dimension=0, tiled=True),
        lax.psum_scatter(g_shift_two, "fsdp", scatter_dimension=0, tiled=True),
        lax.psum_scatter(up_gradient, "fsdp", scatter_dimension=0, tiled=True),
        lax.psum_scatter(g_up_shift, "fsdp", scatter_dimension=0, tiled=True),
        lax.psum_scatter(down_gradient, "fsdp", scatter_dimension=0, tiled=True),
        lax.psum_scatter(g_down_shift, "fsdp", scatter_dimension=0, tiled=True),
    )
    shards = lax.psum(
        (
            partial_shards[0],
            partial_shards[1],
            partial_shards[2],
            partial_shards[3],
            partial_shards[4],
            partial_shards[5],
            partial_shards[6],
            partial_shards[7],
            partial_shards[8],
            partial_shards[9],
            partial_shards[10],
            partial_shards[11],
            partial_shards[12],
        ),
        "seq",
    )
    return (
        output,
        g_input,
        shards[0],
        shards[1],
        shards[2],
        shards[3],
        shards[4],
        shards[5],
        shards[6],
        shards[7],
        shards[8],
        shards[9],
        shards[10],
        shards[11],
        shards[12],
    )


def swap_core(values):
    size = lax.axis_size("fsdp")
    return lax.ppermute(values, "fsdp", [(i, i ^ 1) for i in range(size)])


def swap_chip(values, mask):
    size = lax.axis_size("fsdp")
    return lax.ppermute(values, "fsdp", [(i, i ^ (2 * mask)) for i in range(size)])


def swap_axis(values, turn):
    size = lax.axis_size("fsdp")
    return lax.ppermute(values, "fsdp", [(i, i ^ (2 << ((i & 1) ^ turn))) for i in range(size)])


def swap_seq(values, mask):
    size = lax.axis_size("seq")
    return lax.ppermute(values, "seq", [(i, i ^ mask) for i in range(size)])


def slot_pairs(turn):
    seq, pairs = lax.axis_size("seq"), []
    for f in range(lax.axis_size("fsdp")):
        for z in range(seq):
            to_f, to_z = (f & ~1) | (z & 1), 2 * (f & 1) + (turn ^ (z >> 1))
            pairs.append((f * seq + z, to_f * seq + to_z))
    return pairs


def to_slots(values, seq_rank):
    return [
        lax.ppermute(
            lax.dynamic_index_in_dim(values, turn ^ (seq_rank >> 1), 0, keepdims=False),
            ("fsdp", "seq"),
            slot_pairs(turn),
        )
        for turn in (0, 1)
    ]


def together(*values):
    return lax.optimization_barrier(values)


def whole(*shape):
    return pl.BlockSpec(shape, lambda *_: (0,) * len(shape))


def kernel_call(body, name, meta, args, outs, *, grid=(1,), in_specs=None, out_specs=None, scratch=(), flops=0, vmem=32):
    in_specs = in_specs or [whole(*a.shape) for a in args]
    out_specs = out_specs or [whole(*shape) for shape, _ in outs]
    moved = sum(a.size * a.dtype.itemsize for a in args)
    moved += sum(math.prod(shape) * jnp.dtype(kind).itemsize for shape, kind in outs)
    return pl.pallas_call(
        body,
        out_shape=[jax.ShapeDtypeStruct(shape, kind) for shape, kind in outs],
        grid_spec=pltpu.PrefetchScalarGridSpec(
            num_scalar_prefetch=1,
            grid=grid,
            in_specs=in_specs,
            out_specs=out_specs,
            scratch_shapes=scratch,
        ),
        compiler_params=pltpu.CompilerParams(vmem_limit_bytes=vmem << 20),
        cost_estimate=pl.CostEstimate(flops=0, bytes_accessed=0, transcendentals=0),
        name=name,
    )(meta, *args)


TN = (((0,), (0,)), ((), ()))
CORE, CHIP, RANK, LIVE = range(4)
DIGIT = 128


def aligned(index, size):
    return pl.multiple_of(index * size, size)


def own_place():
    device = lax.axis_index("fsdp")
    return device & 1, device >> 1, lax.axis_index("seq")


def pack_body(lengths_ref, qkv_ref, rel_ref, up_ref, out_ref, down_ref, *refs):
    small, (attn_ref, feed_ref, send_ref) = refs[:8], refs[8:]
    core, _, _ = own_place()
    shard = qkv_ref.shape[0]
    qkv, rel, up, out, down = qkv_ref[...], rel_ref[...], up_ref[...], out_ref[...], down_ref[...]
    heads, hd = rel.shape[1] // HEAD_DIM // 2, HEAD_DIM
    unit = up.shape[1] // 8
    packs, ups = [], []
    row = jnp.concatenate([ref[i : i + 1] for ref in small for i in range(ref.shape[0])], axis=1)
    lane = lax.broadcasted_iota(jnp.int32, (1, 4 * heads * hd - row.shape[1]), 1)
    digits = jnp.zeros(lane.shape, f32)
    for slot in range(lengths_ref.shape[0]):
        high = lengths_ref[slot] // DIGIT
        for at, digit in ((2 * slot, high), (2 * slot + 1, lengths_ref[slot] - high * DIGIT)):
            digits = jnp.where(lane == at, digit.astype(f32), digits)
    row = jnp.concatenate([row, digits.astype(row.dtype)], axis=1)
    rows = jnp.broadcast_to(row, (8, row.shape[1]))
    for side in (0, 1):
        parts = [
            qkv[:, ((2 * j + side) * 3 + t) * hd : ((2 * j + side) * 3 + t + 1) * hd]
            for t in range(3)
            for j in range(heads)
        ]
        parts += [rel[:, (2 * j + side) * hd : (2 * j + side + 1) * hd] for j in range(heads)]
        packs.append(jnp.concatenate(parts, axis=1))
        ups.append(
            jnp.concatenate([up[:, (2 * j + side) * unit : (2 * j + side + 1) * unit] for j in range(4)], axis=1)
        )
    first = core == 0
    folded = jnp.concatenate([out[: shard // 2], out[shard // 2 :]], axis=1)
    attn_ref[:shard] = jnp.where(first, packs[0], packs[1])
    attn_ref[shard:] = rows
    send_ref[:shard] = jnp.where(first, packs[1], packs[0])
    send_ref[shard : shard + 8] = rows
    send_ref[shard + 8 : 2 * shard + 8] = jnp.where(first, ups[1], ups[0])
    send_ref[2 * shard + 8 :] = folded
    feed_ref[:shard] = jnp.where(first, ups[0], ups[1])
    feed_ref[shard : shard + shard // 2] = folded
    feed_ref[shard + shard // 2 :] = jnp.concatenate([down[: 2 * shard], down[2 * shard :]], axis=1)


def ordered(core, own, other):
    first = core == 0
    return jnp.concatenate([jnp.where(first, own, other), jnp.where(first, other, own)], axis=0)


def slot_block(core, rank, step, own, other, store):
    turn = (step >> 1) ^ (rank & 1)
    local = (step & 1) == core
    for t in (0, 1):
        pl.when(local & (turn == t))(functools.partial(store, own[t]))
        pl.when(jnp.logical_not(local) & (turn == t))(functools.partial(store, other[t]))


def norm_rows(values):
    mean_val = jnp.mean(values, axis=1, keepdims=True)
    centered = values - mean_val
    inv_std = lax.rsqrt(jnp.mean(centered * centered, axis=1, keepdims=True) + NORM_EPS)
    return centered * inv_std, inv_std


def weights_body(_, *refs):
    packs, table_ref = refs[0:4], refs[4]
    rel_ref, w_ref, vec_ref, up_ref, *bias_refs = refs[5:11]
    step, (core, chip, _) = pl.program_id(0), own_place()
    width = w_ref.shape[0]
    shard = width // 8
    span = w_ref.shape[1] - rel_ref.shape[1]

    @pl.when(step == 0)
    def _():
        first = core == 0
        vec_ref[...] = jnp.zeros_like(vec_ref)
        own_rows = []
        for k in range(4):
            at = pl.ds(aligned(chip ^ k, 2 * shard), 2 * shard)
            own, other = packs[k][: shard + 8], packs[k][shard + 8 :]
            w_ref[at, :] = ordered(core, own[:shard], other[:shard])
            own_row, other_row = own[shard : shard + 1].astype(f32), other[shard : shard + 1].astype(f32)
            own_rows.append(own_row)
            low, high = jnp.where(first, own_row, other_row), jnp.where(first, other_row, own_row)
            for row, source in enumerate((0, 1, 4, 5, 6)):
                piece = slice(source * shard, (source + 1) * shard)
                vec_ref[row : row + 1, at] = jnp.concatenate([low[:, piece], high[:, piece]], axis=1)
            unit = up_ref.shape[1] // 4
            up_ref[:, pl.ds(aligned(chip ^ k, unit), unit)] = own_row[:, 7 * shard : 7 * shard + unit]
        even = chip & 1 == 0
        for k in (0, 2):
            at = pl.ds(aligned((chip ^ k) >> 1, 2 * shard), 2 * shard)
            low = jnp.where(even, own_rows[k], own_rows[k + 1])
            high = jnp.where(even, own_rows[k + 1], own_rows[k])
            for row, source in enumerate((2, 3)):
                piece = slice(source * shard, (source + 1) * shard)
                bias_refs[row][:, at] = jnp.concatenate([low[:, piece], high[:, piece]], axis=1)

    rel_ref[...] = dot(table_ref[...], w_ref[:, span:], NN).astype(bf)


def project_body(_, *refs):
    own_x, other_x = refs[0:2], refs[2:4]
    w_ref, vec_ref, qkv_ref, h_ref, x_ref = refs[4:9]
    step, (core, _, rank) = pl.program_id(0), own_place()

    def copy(ref):
        x_ref[...] = ref[...]

    slot_block(core, rank, step, own_x, other_x, copy)
    x_hat, _ = norm_rows(x_ref[...].astype(f32))
    h = (x_hat * vec_ref[0:1, :] + vec_ref[1:2, :]).astype(bf)
    h_ref[...] = h
    qkv_ref[...] = dot(h, w_ref[:, : qkv_ref.shape[1]], NN).astype(bf)


def feed_body(meta, *refs):
    packs, own_g, other_g = refs[0:4], refs[4:6], refs[6:8]
    x_ref, o_own, o_other, vec_ref, bias_ref = refs[8:13]
    dy_ref, x_hat_ref, rstd_ref, y_keep, dh_ref, y_send, wo_mine = refs[13:20]
    outs = refs[20:24]
    up_w, down_w, wo_theirs, up_acc, down_acc, sums = refs[24:30]
    step, chip, core = pl.program_id(0), meta[CHIP], meta[CORE]
    width = up_w.shape[0]
    shard, unit, block = width // 8, down_w.shape[0] // 4, x_ref.shape[0]
    fold = shard // 2
    unfold = lambda rows: jnp.concatenate([rows[:, :width], rows[:, width:]], axis=0)

    @pl.when(step == 0)
    def _():
        sums[...] = jnp.zeros_like(sums)
        up_acc[...] = jnp.zeros_like(up_acc)
        down_acc[...] = jnp.zeros_like(down_acc)
        masks = (0, 1 + core, 2 - core, 3)
        for pack_ref, k in zip(packs, masks):
            pack, other = pack_ref[: 3 * shard + fold], pack_ref[3 * shard + fold :]
            up_w[pl.ds(aligned(chip ^ k, 2 * shard), 2 * shard), :] = ordered(core, pack[:shard], other[:shard])
            at = pl.ds(aligned(chip ^ k, shard), shard)
            wo_mine[at, :] = unfold(pack[shard : shard + fold])
            wo_theirs[at, :] = unfold(other[shard:])
            down_w[pl.ds(aligned(chip ^ k, unit), unit), :] = unfold(pack[shard + fold :])

    at = step * block + lax.broadcasted_iota(jnp.int32, (block, 1), 0)

    def load(ref):
        dy_ref[...] = jnp.where(at < meta[LIVE], ref[...].astype(f32), 0.0).astype(bf)

    slot_block(core, meta[RANK], step, own_g, other_g, load)
    y1 = x_ref[...].astype(f32) + (dot(o_own[...], wo_mine[...], NN) + dot(o_other[...], wo_theirs[...], NN))
    x_hat, inv_std = norm_rows(y1)
    x_hat_ref[...] = x_hat.astype(bf)
    rstd_ref[...] = inv_std
    h = (x_hat * vec_ref[2:3, :] + vec_ref[3:4, :]).astype(bf)
    f = dot(h, up_w[...], NN) + bias_ref[...]
    cdf = 0.5 * (1.0 + lax.erf(f * (1.0 / math.sqrt(2.0))))
    g = (f * cdf).astype(bf)
    dy = dy_ref[...]
    dg = dot(dy, down_w[...], NT)
    df = (dg * (cdf + f * jnp.exp(-0.5 * f * f) * (1.0 / math.sqrt(2.0 * math.pi)))).astype(bf)
    z = dot(g, down_w[...], NN)
    dh = dot(df, up_w[...], NT)
    dh_ref[...] = dh.astype(bf)
    up_acc[...] += dot(h, df, TN)
    down_acc[...] += dot(g, dy, TN)
    sums[0:1, :width] += jnp.sum(dh * x_hat, axis=0, keepdims=True)
    sums[1:2, :width] += jnp.sum(dh, axis=0, keepdims=True)
    sums[3:4, :] += jnp.sum(df.astype(f32), axis=0, keepdims=True)
    local = (step & 1) == core

    @pl.when(local)
    def _():
        y_keep[...] = y1 + z + vec_ref[4:5, :]
        sums[2:3, :width] += jnp.sum(dy.astype(f32), axis=0, keepdims=True)

    @pl.when(jnp.logical_not(local))
    def _():
        y_send[...] = z.astype(bf)

    @pl.when(step == pl.num_programs(0) - 1)
    def _():
        rows = 2 * shard
        for k, out in enumerate(outs):
            at = pl.ds(aligned(chip ^ k, rows), rows)
            units = pl.ds(aligned(chip ^ k, unit), unit)
            tail = [sums[0:1, at], sums[1:2, at], sums[2:3, at], sums[3:4, units]]
            tail = jnp.concatenate(tail + [jnp.zeros((1, sums.shape[1] - 3 * rows - unit), f32)], axis=1)
            out[:rows] = up_acc[at, :].astype(out.dtype)
            out[rows : rows + 8] = jnp.broadcast_to(tail, (8, tail.shape[1])).astype(out.dtype)
            down = down_acc[units, :]
            half = unit // 2
            out[rows + 8 :] = jnp.concatenate([down[:half], down[half:]], axis=1).astype(out.dtype)


def norm_two_body(meta, x_hat_ref, rstd_ref, dh_ref, dh_came, dy_ref, vec_ref, y_keep, y_came, wo_ref, o_ref, *refs):
    out0, out1, resid_ref, do_ref, go_ref = refs
    step = pl.program_id(0)

    @pl.when(step == 0)
    def _():
        go_ref[...] = jnp.zeros_like(go_ref)

    x_hat = x_hat_ref[...].astype(f32)
    e = (dh_ref[...].astype(f32) + dh_came[...].astype(f32)) * vec_ref[2:3, :]
    first = jnp.mean(e, axis=1, keepdims=True)
    second = jnp.mean(e * x_hat, axis=1, keepdims=True)
    grad = dy_ref[...].astype(f32) + rstd_ref[...] * (e - first - x_hat * second)
    da = grad.astype(bf)
    do_ref[...] = dot(da, wo_ref[...], NT).astype(bf)
    go_ref[...] += dot(o_ref[...], da, TN)
    turn = (step >> 1) ^ (meta[RANK] & 1)
    local = (step & 1) == meta[CORE]

    @pl.when(local)
    def _():
        resid_ref[...] = grad
        y = (y_keep[...] + y_came[...].astype(f32)).astype(bf)

        @pl.when(turn == 0)
        def _():
            out0[...] = y

        @pl.when(turn == 1)
        def _():
            out1[...] = y


def qkv_back_body(meta, *refs):
    grads_a, grads_b = refs[:6], refs[6:12]
    w_ref, x_ref, h_ref, table_ref, go_ref = refs[12:17]
    keep_ref, send_ref = refs[17:19]
    outs, acc, sums = refs[19:23], refs[23], refs[24]
    step, chip = pl.program_id(0), meta[CHIP]
    width = x_ref.shape[1]
    rows = width // 4

    @pl.when(step == 0)
    def _():
        sums[...] = jnp.zeros_like(sums)
        acc[...] = jnp.zeros_like(acc)

    both = lambda i: [grads_a[i][...], grads_b[i][...]]
    dqkv = jnp.concatenate(both(0) + both(1) + both(2), axis=1)
    drel = jnp.concatenate(both(3), axis=1)
    span = dqkv.shape[1]
    acc[:, :span] += dot(h_ref[...], dqkv, TN)
    acc[:, span:] += dot(table_ref[...], drel, TN)
    dh = dot(dqkv, w_ref[:, :span], NT)
    x_hat, _ = norm_rows(x_ref[...].astype(f32))
    sums[0:1, :] += jnp.sum(dh * x_hat, axis=0, keepdims=True)
    sums[1:2, :] += jnp.sum(dh, axis=0, keepdims=True)
    local = (step & 1) == meta[CORE]

    @pl.when(local)
    def _():
        keep_ref[...] = dh

    @pl.when(jnp.logical_not(local))
    def _():
        send_ref[...] = dh.astype(bf)

    @pl.when(step == pl.num_programs(0) - 1)
    def _():
        for k, out in enumerate(outs):
            at = pl.ds(aligned(chip ^ k, rows), rows)
            low = (chip ^ k) >> 1 == 0
            tail = [sums[0:1, at], sums[1:2, at]]
            tail += [jnp.where(low, *both(i)) for i in (4, 5)]
            tail = jnp.concatenate(tail + [jnp.zeros((1, acc.shape[1] - 4 * rows), f32)], axis=1)
            out[:rows] = acc[at, :].astype(out.dtype)
            out[rows : rows + 8] = jnp.broadcast_to(tail, (8, tail.shape[1])).astype(out.dtype)
            shard = rows // 2
            lines = go_ref[pl.ds(aligned(chip ^ k, shard), shard), :]
            lines = jnp.concatenate([lines[: shard // 2], lines[shard // 2 :]], axis=1)
            out[rows + 8 :] = lines.astype(out.dtype)


def norm_one_body(meta, x_ref, dh_keep, dh_came, resid_ref, vec_ref, out0, out1):
    turn = pl.program_id(0) ^ (meta[RANK] & 1)
    x_hat, inv_std = norm_rows(x_ref[...].astype(f32))
    e = (dh_keep[...] + dh_came[...].astype(f32)) * vec_ref[0:1, :]
    first = jnp.mean(e, axis=1, keepdims=True)
    second = jnp.mean(e * x_hat, axis=1, keepdims=True)
    grad = (resid_ref[...] + inv_std * (e - first - x_hat * second)).astype(bf)

    @pl.when(turn == 0)
    def _():
        out0[...] = grad

    @pl.when(turn == 1)
    def _():
        out1[...] = grad


def rank_bit(meta, bit):
    return (meta[RANK] >> bit) & 1


def chip_sum_body(meta, own, *refs, bit):
    *came, keep, send = refs
    half = keep.shape[1]
    for out, side in ((keep, rank_bit(meta, bit)), (send, 1 - rank_bit(meta, bit))):
        at = pl.ds(aligned(side, half), half)
        total = own[:, at]
        for ref in came:
            total = total + ref[:, at].astype(f32)
        out[...] = total.astype(out.dtype)


def chip_sum(meta, parts, name, bit):
    rows, size = parts[0].shape
    return kernel_call(functools.partial(chip_sum_body, bit=bit), name, meta, parts, [((rows, size // 2), f32), ((rows, size // 2), bf)])


def own_rows_first(total, core, shard):
    theirs = lax.dynamic_slice_in_dim(total, (1 - core) * shard, shard, 0)
    mine = lax.dynamic_slice_in_dim(total, core * shard, shard, 0)
    came = swap_core(jnp.concatenate([theirs, total[2 * shard : 2 * shard + 8]], axis=0))
    return jnp.concatenate([mine, came, total[2 * shard :]], axis=0)


def halves(meta, mine, other, bit):
    low = rank_bit(meta, bit) == 0
    return jnp.concatenate([jnp.where(low, mine, other), jnp.where(low, other, mine)], axis=1)


def both_cores(meta, own, came):
    own, came = own.astype(f32), came.astype(f32)
    return own, own + came, meta[CORE] == 0


def store_half(ref, source, at, low):
    size = 2 * ref.shape[1]
    piece = source[:, at * size : (at + 1) * size]
    ref[...] = jnp.where(low, piece[:, : size // 2], piece[:, size // 2 :])


def early_out_body(meta, mine, other, came_ref, g_up, g_down, *vec_refs):
    rows = halves(meta, mine[...], other[...], 0)
    came_rows = halves(meta, came_ref[0], came_ref[1], 0)
    shard, width = g_up.shape[0], g_down.shape[1]
    first, unit = meta[CORE] == 0, rows.shape[1] // 4
    own, came = jnp.where(first, rows[:shard], rows[shard : 2 * shard]), came_rows[:shard]
    pair = (jnp.where(first, own, came), jnp.where(first, came, own))
    for j in range(4):
        for side in (0, 1):
            at = (2 * j + side) * unit
            g_up[:, at : at + unit] = pair[side][:, j * unit : (j + 1) * unit].astype(f32)
    down = rows[2 * shard + 8 :].astype(f32)
    g_down[...] = jnp.concatenate([down[:, :width], down[:, width:]], axis=0)
    own, total, low = both_cores(meta, rows[2 * shard : 2 * shard + 1], came_rows[shard : shard + 1])
    for at, ref in enumerate(vec_refs[:3]):
        store_half(ref, total, at, low)
    vec_refs[3][...] = own[:, 6 * shard : 6 * shard + unit]


def late_out_body(meta, mine, other, g_qkv, g_rel, g_out, *vec_refs):
    rows = halves(meta, mine[...], other[...], 0)
    shard, width = g_qkv.shape[0], g_out.shape[1]
    first, hd, heads = meta[CORE] == 0, HEAD_DIM, H // 2
    own, came = rows[:shard], rows[shard : 2 * shard]
    pair = (jnp.where(first, own, came), jnp.where(first, came, own))
    cols = heads * hd
    piece = lambda h, t: pair[h & 1][:, t * cols + (h >> 1) * hd : t * cols + ((h >> 1) + 1) * hd]
    g_qkv[...] = jnp.concatenate([piece(h, t) for h in range(2 * heads) for t in range(3)], axis=1).astype(f32)
    g_rel[...] = jnp.concatenate([piece(h, 3) for h in range(2 * heads)], axis=1).astype(f32)
    out = rows[2 * shard + 16 :].astype(f32)
    g_out[...] = jnp.concatenate([out[:, :width], out[:, width:]], axis=0)
    own, total, low = both_cores(meta, rows[2 * shard + 8 : 2 * shard + 9], rows[2 * shard : 2 * shard + 1])
    even = meta[CHIP] & 1 == 0
    for at, ref in enumerate(vec_refs):
        store_half(ref, total if at < 2 else own, at, low if at < 2 else even)


def place_body(meta, y0, y1, x0, x1, y_ref, x_ref):
    high = meta[RANK] >> 1 == 1
    y_ref[0] = jnp.where(high, y1[...], y0[...])
    y_ref[1] = jnp.where(high, y0[...], y1[...])
    x_ref[0] = jnp.where(high, x1[...], x0[...]).astype(f32)
    x_ref[1] = jnp.where(high, x0[...], x1[...]).astype(f32)


def slot_split_device(
    layer_input,
    lengths,
    ln1_gain,
    ln1_bias,
    w_qkv,
    w_rel,
    bias_u,
    bias_v,
    w_out,
    ln2_gain,
    ln2_bias,
    w_up,
    up_bias,
    w_down,
    down_bias,
    grad_out,
):
    slots, block, width = layer_input.shape
    rank, device = lax.axis_index("seq"), lax.axis_index("fsdp")
    core, chip = device & 1, device >> 1
    full, heads = 4 * block, H // 2
    cols, shard, unit = heads * HEAD_DIM, width // 8, up_bias.shape[0]
    mine_ff = 4 * unit

    none = jnp.zeros((4,), jnp.int32)
    x_own = to_slots(jnp.concatenate([layer_input, grad_out], axis=2), rank)
    vectors = (ln1_gain, ln1_bias, bias_u, bias_v, ln2_gain, ln2_bias, down_bias, up_bias)
    attn_rows, fold = shard + 8, shard // 2
    attn_pack, feed_pack, pack_send = kernel_call(
        pack_body,
        "pack",
        pltpu.with_memory_space_constraint(lengths, pltpu.HBM),
        [
            pltpu.with_memory_space_constraint(v, pltpu.HBM)
            for v in [w_qkv, w_rel, w_up, w_out, w_down] + [v.reshape(-1, min(128, v.size)) for v in vectors]
        ],
        [((attn_rows, 4 * cols), bf), ((3 * shard + fold, 4 * cols), bf), ((attn_rows + shard + fold, 4 * cols), bf)],
        vmem=32,
    )
    pack_came = swap_core(pack_send)
    attn_pack = jnp.concatenate([attn_pack, pack_came[:attn_rows]], axis=0)
    attn_packs = [attn_pack] + [swap_chip(attn_pack, k) for k in (1, 2, 3)]
    feed_pack = jnp.concatenate([feed_pack, pack_came[attn_rows:]], axis=0)
    digits_at = 7 * shard + unit
    digits = pack_came[shard, digits_at : digits_at + 2 * slots].astype(jnp.int32)
    lengths = jnp.where(core == rank >> 1, lengths, digits[0::2] * DIGIT + digits[1::2])
    length = jnp.where(rank & 1 == 0, lengths[0], lengths[1])
    meta = jnp.stack([core, chip, rank, length]).astype(jnp.int32)
    length_arr = length.reshape(1)
    fine = 32
    inv_freq = jnp.exp(lax.iota(f32, width // 2) * (-2.0 * math.log(10000.0) / width))
    high = (full - 1 - fine * lax.iota(jnp.int32, full // fine)).astype(f32)[:, None] * inv_freq
    low = lax.iota(f32, fine)[:, None] * inv_freq
    high_sin, high_cos, low_sin, low_cos = together(jnp.sin(high), jnp.cos(high), jnp.sin(low), jnp.cos(low))
    high_sin, high_cos = high_sin[:, None], high_cos[:, None]
    table = jnp.concatenate(
        [high_sin * low_cos - high_cos * low_sin, high_cos * low_cos + high_sin * low_sin], axis=2
    )
    table = table.astype(bf).reshape(full, width)

    feed_pack, meta, length_arr, table, *attn_packs = together(feed_pack, meta, length_arr, table, *attn_packs)
    by_step = lambda width: pl.BlockSpec((block, width), lambda i, _: (i, 0))
    rel, w_own, vecs, up_b, own_u, own_v = kernel_call(
        weights_body,
        "weights",
        none,
        [pltpu.with_memory_space_constraint(v, pltpu.HBM) for v in attn_packs] + [table],
        [((full, cols), bf), ((width, 4 * cols), bf), ((8, width), f32), ((1, mine_ff), f32)]
        + [((1, cols), f32), ((1, cols), f32)],
        grid=(4,),
        in_specs=[whole(2 * attn_rows, 4 * cols)] * 4 + [by_step(width)],
        out_specs=[by_step(cols), whole(width, 4 * cols), whole(8, width), whole(1, mine_ff)]
        + [whole(1, cols), whole(1, cols)],
    )
    w_own, vecs, *x_own = together(w_own, vecs, *x_own)
    x_other = [swap_core(x) for x in x_own]
    feed_first = swap_axis(feed_pack, 0)
    feed_second = swap_axis(feed_pack, 1)

    side = lambda at: pl.BlockSpec((block, width), lambda i, _: (0, at))
    qkv, h1, x_slot = kernel_call(
        project_body,
        "project",
        none,
        x_own + x_other + [w_own, vecs],
        [((full, 3 * cols), bf), ((full, width), bf), ((full, width), bf)],
        grid=(4,),
        in_specs=[side(0)] * 4 + [whole(width, 4 * cols), whole(8, width)],
        out_specs=[by_step(3 * cols), by_step(width), by_step(width)],
    )
    qkv, feed_first = together(qkv, feed_first)
    feed_third = swap_axis(feed_first, 1)
    attn, *probs = attn_fwd(length_arr, qkv, rel, own_u, own_v)
    attn, feed_second, feed_third = together(attn, feed_second, feed_third)
    feed_packs = [feed_pack, feed_first, feed_second, feed_third]

    attn_other = swap_core(attn)
    kept = lambda width: pl.BlockSpec((block, width), lambda i, _: (i >> 1, 0))
    half, rows = full // 2, 2 * shard + 8
    blocks = lambda rows: [((rows, 2 * width), f32)] + [((rows, 2 * width), bf)] * 3
    dy, x_hat, rstd, y_keep, dh, y_send, wo_mine, *early_parts = kernel_call(
        feed_body,
        "feed",
        meta,
        feed_packs + x_own + x_other + [x_slot, attn, attn_other, vecs, up_b],
        [((full, width), bf), ((full, width), bf), ((full, 1), f32), ((half, width), f32)]
        + [((full, width), bf), ((half, width), bf), ((cols, width), bf)]
        + blocks(rows + unit // 2),
        grid=(4,),
        in_specs=[whole(*feed_pack.shape)] * 4 + [side(1)] * 4
        + [by_step(width), by_step(cols), by_step(cols), whole(8, width), whole(1, mine_ff)],
        out_specs=[by_step(width), by_step(width), by_step(1), kept(width)]
        + [by_step(width), kept(width), whole(cols, width)]
        + [whole(rows + unit // 2, 2 * width)] * 4,
        scratch=[
            pltpu.VMEM((width, mine_ff), bf),
            pltpu.VMEM((mine_ff, width), bf),
            pltpu.VMEM((cols, width), bf),
            pltpu.VMEM((width, mine_ff), f32),
            pltpu.VMEM((mine_ff, width), f32),
            pltpu.VMEM((8, mine_ff), f32),
        ],
        flops=12 * full * width * mine_ff,
    )
    dh_came = swap_core(dh)
    y_came = swap_core(y_send)
    early_came = [swap_chip(early_parts[k], k) for k in (1, 2, 3)]
    out0, out1, g_resid, d_attn, g_out = kernel_call(
        norm_two_body,
        "norm_two",
        meta,
        [x_hat, rstd, dh, dh_came, dy, vecs, y_keep, y_came, wo_mine, attn],
        [((block, width), bf)] * 2 + [((half, width), f32), ((full, cols), bf), ((cols, width), f32)],
        grid=(4,),
        in_specs=[by_step(width), by_step(1)] + [by_step(width)] * 3 + [whole(8, width)] + [kept(width)] * 2
        + [whole(cols, width), by_step(cols)],
        out_specs=[whole(block, width)] * 2 + [kept(width), by_step(cols), whole(cols, width)],
        flops=4 * full * width * cols,
    )
    home = lambda outs: [
        lax.ppermute(out, ("fsdp", "seq"), [(b, a) for a, b in slot_pairs(turn)])
        for turn, out in enumerate(outs)
    ]
    y_turns = home((out0, out1))
    back = lambda pair, d_out: attn_bwd(length_arr, qkv, rel, own_u, own_v, probs, d_out, pair=pair)
    d_attn, *grads_a = together(d_attn, *back(0, d_attn))
    *grads_b, y0, y1, e1, e2, e3 = together(*back(1, d_attn), *y_turns, *early_came)
    early_keep, early_send = chip_sum(meta, [early_parts[0], e1, e2, e3], "early_chips", 0)
    early_send, *grads_b = together(early_send, *grads_b)
    early_came = swap_seq(early_send, 1)
    pair_step = pl.BlockSpec((block, 2 * HEAD_DIM), lambda i, _: (i, 0))
    pair_row = whole(1, 2 * HEAD_DIM)
    dh1_keep, dh1_send, *late_parts = kernel_call(
        qkv_back_body,
        "qkv_back",
        meta,
        [*grads_a, *grads_b, w_own, x_slot, h1, table, g_out],
        [((half, width), f32), ((half, width), bf)] + blocks(rows + fold),
        grid=(4,),
        in_specs=([pair_step] * 4 + [pair_row] * 2) * 2
        + [whole(width, 4 * cols)] + [by_step(width)] * 3 + [whole(cols, width)],
        out_specs=[kept(width)] * 2 + [whole(rows + fold, 2 * width)] * 4,
        scratch=[pltpu.VMEM((width, 4 * cols), f32), pltpu.VMEM((8, width), f32)],
        flops=14 * full * width * cols,
    )
    dh1_send, *late_parts = together(dh1_send, *late_parts)
    early_pair = (early_keep + early_came.astype(f32)).astype(bf)
    dh1_came = swap_core(dh1_send)
    early_came = swap_seq(early_pair, 2)
    late_came = [swap_chip(late_parts[k], k) for k in (1, 2, 3)]
    by_half = pl.BlockSpec((block, width), lambda i, _: (i, 0))
    own_rows = pl.BlockSpec((block, width), lambda i, m: (2 * i + m[CORE], 0))
    x0, x1 = kernel_call(
        norm_one_body,
        "norm_one",
        meta,
        [x_slot, dh1_keep, dh1_came, g_resid, vecs],
        [((block, width), bf)] * 2,
        grid=(2,),
        in_specs=[own_rows] + [by_half] * 3 + [whole(8, width)],
        out_specs=[whole(block, width)] * 2,
    )
    x_turns = home((x0, x1))
    late_keep, late_send = chip_sum(meta, [late_parts[0]] + late_came, "late_chips", 0)
    small = lambda size: ((1, size), f32)
    late_came, early_came, x_turns[0] = together(swap_seq(late_send, 1), early_came, x_turns[0])
    early_mine = (early_pair.astype(f32) + early_came.astype(f32)).astype(bf)
    late_pair = (late_keep + late_came.astype(f32)).astype(bf)
    late_came = swap_seq(late_pair, 2)
    early_other = swap_seq(early_mine, 1)
    late_total = (late_pair.astype(f32) + late_came.astype(f32)).astype(bf)
    late_mine = own_rows_first(late_total, core, shard)
    late_other = swap_seq(late_mine, 1)
    late_mine, g0, g1, early_other = together(late_mine, *x_turns, early_other)
    theirs = lambda rows: jnp.concatenate(
        [
            lax.dynamic_slice_in_dim(rows, (1 - core) * shard, shard, 0),
            rows[2 * shard : 2 * shard + 8],
        ],
        axis=0,
    )
    early_core = swap_core(jnp.stack([theirs(early_mine), theirs(early_other)]))
    output, grad_x = kernel_call(
        place_body,
        "place",
        meta,
        [y0, y1, g0, g1],
        [((2, block, width), bf), ((2, block, width), f32)],
    )
    g_up, g_down, g_gain_two, g_shift_two, g_down_shift, g_up_shift = kernel_call(
        early_out_body,
        "early_out",
        meta,
        [early_mine, early_other, early_core],
        [((shard, 2 * mine_ff), f32), ((unit, width), f32)] + [small(shard)] * 3 + [small(unit)],
    )
    late_other, output, grad_x, g_up = together(late_other, output, grad_x, g_up)
    g_qkv, g_rel, g_w_out, *late_vectors = kernel_call(
        late_out_body,
        "late_out",
        meta,
        [late_mine, late_other],
        [((shard, 6 * cols), f32), ((shard, 2 * cols), f32), ((shard, width), f32)] + [small(shard)] * 4,
    )
    g_gain_one, g_shift_one, g_bias_u, g_bias_v = [v.reshape(-1) for v in late_vectors]
    return (
        output,
        grad_x,
        g_gain_one,
        g_shift_one,
        g_qkv,
        g_rel,
        g_bias_u,
        g_bias_v,
        g_w_out,
        g_gain_two.reshape(-1),
        g_shift_two.reshape(-1),
        g_up,
        g_up_shift.reshape(-1),
        g_down,
        g_down_shift.reshape(-1),
    )


def per_device(*args):
    one_slot_a_chip = lax.axis_size("fsdp") == 8 and lax.axis_size("seq") == 4
    if one_slot_a_chip and args[0].shape[0] == 2:
        return slot_split_device(*args)
    return head_split_device(*args)


def solution(mesh):
    placed = (
        P("fsdp", "seq", None),
        P("fsdp"),
        P("fsdp"),
        P("fsdp"),
        P("fsdp", None),
        P("fsdp", None),
        P("fsdp"),
        P("fsdp"),
        P("fsdp", None),
        P("fsdp"),
        P("fsdp"),
        P("fsdp", None),
        P("fsdp"),
        P("fsdp", None),
        P("fsdp"),
        P("fsdp", "seq", None),
    )
    return jax.shard_map(
        per_device,
        mesh=mesh,
        in_specs=placed,
        out_specs=(
            P("fsdp", "seq", None),
            P("fsdp", "seq", None),
            P("fsdp"),
            P("fsdp"),
            P("fsdp", None),
            P("fsdp", None),
            P("fsdp"),
            P("fsdp"),
            P("fsdp", None),
            P("fsdp"),
            P("fsdp"),
            P("fsdp", None),
            P("fsdp"),
            P("fsdp", None),
            P("fsdp"),
        ),
        check_vma=False,
    )
```

```python
import functools
import math

import jax
import jax.numpy as jnp
from jax import lax
from jax.experimental import pallas as pl
from jax.experimental.pallas import tpu as pltpu
from jax.sharding import PartitionSpec as P

H = 8
HEAD_DIM = 64


NEG_FILL = -1e30
NORM_EPS = 1e-05


bf, f32 = jnp.bfloat16, jnp.float32
NEG = NEG_FILL
HD = HEAD_DIM
NT = (((1,), (1,)), ((), ()))
NN = (((1,), (0,)), ((), ()))


def dot(a, b, dims):
    return lax.dot_general(a, b, dims, preferred_element_type=f32)


def masked_tail(s, keep, block):
    tail = jnp.where(keep, s[:, s.shape[1] - block :], NEG)
    if s.shape[1] == block:
        return tail
    return jnp.concatenate([s[:, : s.shape[1] - block], tail], axis=1)


def scores(qu, qv, keys, rel_rev, keep, block):
    span = keys.shape[0]
    rel = dot(qv, rel_rev, NT)
    rel = pltpu.roll(rel, (span - block + 1) % span, 1, stride=1, stride_axis=0)
    return masked_tail(dot(qu, keys, NT) + rel, keep, block)


def attn_fwd_body(len_ref, q_ref, k_ref, v_ref, r_ref, bu_ref, bv_ref, o_ref, wide_ref, *p_refs, block):
    full = q_ref.shape[0]
    lane = lax.broadcasted_iota(jnp.int32, (block, 2 * HD), 1)
    sides = (lane < HD, lane >= HD)
    length = len_ref[0]
    col = lax.broadcasted_iota(jnp.int32, (1, full), 1)
    bias = jnp.where(col < length, 0.0, NEG)
    tri = lax.broadcasted_iota(jnp.int32, (block, block), 1) <= lax.broadcasted_iota(
        jnp.int32, (block, block), 0
    )
    for first in range(0, full, block):
        span = first + block
        q = q_ref[first:span, :].astype(f32)
        qu = (q + bu_ref[...]).astype(bf).astype(f32) * 0.125
        qv = (q + bv_ref[...]).astype(bf).astype(f32) * 0.125
        outs = []
        for head, side in enumerate(sides):
            s = scores(
                jnp.where(side, qu, 0.0).astype(bf),
                jnp.where(side, qv, 0.0).astype(bf),
                k_ref[:span, :],
                r_ref[full - span :, :],
                tri,
                block,
            )
            if span > full // 2:
                s = s + bias[:, :span]
            top = jnp.max(s, axis=1, keepdims=True)
            e = jnp.exp(s - top)
            total = jnp.sum(e, axis=1, keepdims=True)
            p = (e * (1.0 / total)).astype(bf)
            p_refs[first // block][head] = p
            outs.append(dot(p, v_ref[:span, :], NN))
        wide = jnp.where(sides[0], outs[0], outs[1])
        wide_ref[first:span, :] = wide
        o_ref[first:span, :] = wide.astype(bf)


def attn_fwd(length, qkv, rel_rev, bias_u, bias_v, *, block=256):
    full, cols = rel_rev.shape
    spans = range(block, full + 1, block)
    pairs = cols // (2 * HD)
    at = lambda part: pl.BlockSpec((full, 2 * HD), lambda pair, _: (0, part * pairs + pair))
    row = pl.BlockSpec((1, 2 * HD), lambda pair, _: (0, pair))
    return pl.pallas_call(
        functools.partial(attn_fwd_body, block=block),
        out_shape=(
            jax.ShapeDtypeStruct((full, cols), bf),
            jax.ShapeDtypeStruct((full, cols), f32),
            *(jax.ShapeDtypeStruct((2 * pairs, block, span), bf) for span in spans),
        ),
        grid_spec=pltpu.PrefetchScalarGridSpec(
            num_scalar_prefetch=1,
            grid=(pairs,),
            in_specs=[at(0), at(1), at(2), at(0), row, row],
            out_specs=(
                at(0),
                at(0),
                *(pl.BlockSpec((2, block, span), lambda pair, _: (pair, 0, 0)) for span in spans),
            ),
        ),
        cost_estimate=pl.CostEstimate(flops=0, bytes_accessed=0, transcendentals=0),
        compiler_params=pltpu.CompilerParams(vmem_limit_bytes=32 << 20),
        name="attn_fwd",
    )(length, qkv, qkv, qkv, rel_rev, bias_u, bias_v)


def attn_bwd_body(len_ref, q_ref, k_ref, v_ref, r_ref, bu_ref, bv_ref, do_ref, o_ref, *refs, block, heads):
    full = q_ref.shape[0]
    p_refs, refs = refs[: full // block], refs[full // block :]
    dq_ref, dk_ref, dv_ref, dr_ref, gu_ref, gv_ref, dk_t, dv_t, dr_t = refs
    length = len_ref[0]
    lane = lax.broadcasted_iota(jnp.int32, (block, 2 * HD), 1)
    sides = (lane < HD, lane >= HD)
    rows = lax.broadcasted_iota(jnp.int32, (block, block), 0)
    cols = lax.broadcasted_iota(jnp.int32, (block, block), 1)
    flip = jnp.where(rows + cols == block - 1, 1.0, 0.0).astype(bf)
    for ref in (dk_t, dv_t, dr_t, dq_ref, gu_ref, gv_ref):
        ref[...] = jnp.zeros_like(ref)
    for first in range(0, full, block):
        span = first + block

        def one_block(first=first, span=span):
            q = q_ref[first:span, :].astype(f32)
            qu = (q + bu_ref[...]).astype(bf).astype(f32) * 0.125
            qv = (q + bv_ref[...]).astype(bf).astype(f32) * 0.125
            do = do_ref[first:span, :].astype(f32)
            o = o_ref[first:span, :]
            qu_t = jnp.transpose(qu).astype(bf)
            do_t = jnp.transpose(do).astype(bf)
            qv_t = jnp.transpose(dot(flip, qv.astype(bf), NN)).astype(bf)
            dqu, dqv = [0.0, 0.0], [0.0, 0.0]
            for head in heads:
                side = sides[head]
                at = slice(head * HD, (head + 1) * HD)
                rounded = p_refs[first // block][head - heads[0]]
                p = rounded.astype(f32)
                dp = dot(jnp.where(side, do, 0.0).astype(bf), v_ref[:span, :], NT)
                inner = jnp.sum(jnp.where(side, do * o, 0.0), axis=1, keepdims=True)
                ds = (p * (dp - inner)).astype(bf)
                dv_t[at, :span] += dot(do_t[at], rounded, NN)
                both = dot(jnp.concatenate([qu_t[at], flip], axis=0), ds, NN)
                dk_t[at, :span] += both[:HD]
                dqu[head] = dot(ds, k_ref[:span, :], NN)
                ds_rev = pltpu.roll(both[HD:], 0, 1, stride=1, stride_axis=0).astype(bf)
                dr_t[at, full - span :] += dot(qv_t[at], ds_rev, NN)
                dqv[head] = dot(ds_rev, r_ref[full - span :, :], NN)
            dqu = jnp.where(sides[0], dqu[0], dqu[1]) * 0.125
            dqv = jnp.where(sides[0], dqv[0], dqv[1]) * 0.125
            gu_ref[...] += jnp.sum(dqu, axis=0, keepdims=True)
            gv_ref[...] += jnp.sum(dqv, axis=0, keepdims=True)
            dq_ref[first:span, :] = (dqu + dot(flip, dqv.astype(bf), NN)).astype(bf)

        if first < full // 2:
            one_block()
        else:
            pl.when(first < length)(one_block)

    dk_ref[...] = jnp.transpose(dk_t[...]).astype(bf)
    dv_ref[...] = jnp.transpose(dv_t[...]).astype(bf)
    dr_ref[...] = jnp.transpose(dr_t[...]).astype(bf)


def attn_bwd(length, qkv, rel_rev, bias_u, bias_v, probs, d_out, out_rows, *, pair, heads=(0, 1), block=256):
    full, cols = rel_rev.shape
    pairs = cols // (2 * HD)
    at = lambda part: pl.BlockSpec((full, 2 * HD), lambda i, _: (0, part * pairs + pair))
    row = pl.BlockSpec((1, 2 * HD), lambda i, _: (0, pair))
    out = pl.BlockSpec((full, 2 * HD), lambda i, _: (0, 0))
    out_row = pl.BlockSpec((1, 2 * HD), lambda i, _: (0, 0))
    return pl.pallas_call(
        functools.partial(attn_bwd_body, block=block, heads=heads),
        out_shape=(jax.ShapeDtypeStruct((full, 2 * HD), bf),) * 4
        + (jax.ShapeDtypeStruct((1, 2 * HD), f32),) * 2,
        grid_spec=pltpu.PrefetchScalarGridSpec(
            num_scalar_prefetch=1,
            grid=(1,),
            in_specs=[at(0), at(1), at(2), at(0), row, row]
            + [at(0), at(0)]
            + [
                pl.BlockSpec((len(heads),) + p.shape[1:], lambda i, _: ((2 * pair + heads[0]) // len(heads), 0, 0))
                for p in probs
            ],
            out_specs=(out,) * 4 + (out_row, out_row),
            scratch_shapes=[pltpu.VMEM((2 * HD, full), f32)] * 3,
        ),
        cost_estimate=pl.CostEstimate(flops=0, bytes_accessed=0, transcendentals=0),
        compiler_params=pltpu.CompilerParams(vmem_limit_bytes=32 << 20),
        name="attn_bwd",
    )(length, qkv, qkv, qkv, rel_rev, bias_u, bias_v, d_out, out_rows, *probs)


def norm_parts(values):
    mean_val = jnp.mean(values, axis=-1, keepdims=True)
    centered = values - mean_val
    inv_std = lax.rsqrt(jnp.mean(centered * centered, axis=-1, keepdims=True) + NORM_EPS)
    return (centered * inv_std, inv_std)


def norm_back(grad_norm, x_hat, inv_std):
    first_mean = jnp.mean(grad_norm, axis=-1, keepdims=True)
    second_mean = jnp.mean(grad_norm * x_hat, axis=-1, keepdims=True)
    return inv_std * (grad_norm - first_mean - x_hat * second_mean)


def position_table(count_rows, feature_count):
    steps = lax.iota(jnp.float32, count_rows)
    half_count = feature_count // 2
    inv_freq = jnp.exp(
        lax.iota(jnp.float32, half_count) * (-2.0 * math.log(10000.0) / feature_count)
    )
    angles = steps[:, None] * inv_freq[None, :]
    return jnp.concatenate([jnp.sin(angles), jnp.cos(angles)], axis=1)


def skew_rows(matrix):
    leading = matrix.shape[:-2]
    row_count, col_count = matrix.shape[-2:]
    flattened = matrix.reshape(leading + (row_count * col_count,))
    picked = flattened[..., row_count - 1 : row_count - 1 + row_count * (col_count - 1)]
    return picked.reshape(leading + (row_count, col_count - 1))[..., : col_count - row_count]


def unskew_rows(matrix):
    leading = matrix.shape[:-2]
    row_count, key_count = matrix.shape[-2:]
    axis_pos = len(leading)
    widened = jnp.pad(matrix, [(0, 0)] * axis_pos + [(0, 0), (0, row_count - 1)])
    flattened = widened.reshape(leading + (row_count * (key_count + row_count - 1),))
    flattened = jnp.pad(flattened, [(0, 0)] * axis_pos + [(row_count - 1, 1)])
    return flattened.reshape(leading + (row_count, key_count + row_count))


def head_split_device(
    layer_input,
    lengths,
    ln1_gain,
    ln1_bias,
    w_qkv,
    w_rel,
    bias_u,
    bias_v,
    w_out,
    ln2_gain,
    ln2_bias,
    w_up,
    up_bias,
    w_down,
    down_bias,
    grad_out,
):
    weights = (
        lax.all_gather(ln1_gain, "fsdp", axis=0, tiled=True),
        lax.all_gather(ln1_bias, "fsdp", axis=0, tiled=True),
        lax.all_gather(w_qkv, "fsdp", axis=0, tiled=True),
        lax.all_gather(w_rel, "fsdp", axis=0, tiled=True),
        lax.all_gather(bias_u, "fsdp", axis=0, tiled=True),
        lax.all_gather(bias_v, "fsdp", axis=0, tiled=True),
        lax.all_gather(w_out, "fsdp", axis=0, tiled=True),
        lax.all_gather(ln2_gain, "fsdp", axis=0, tiled=True),
        lax.all_gather(ln2_bias, "fsdp", axis=0, tiled=True),
        lax.all_gather(w_up, "fsdp", axis=0, tiled=True),
        lax.all_gather(up_bias, "fsdp", axis=0, tiled=True),
        lax.all_gather(w_down, "fsdp", axis=0, tiled=True),
        lax.all_gather(down_bias, "fsdp", axis=0, tiled=True),
    )
    (
        gain_one,
        shift_one,
        query_key_value_matrix,
        rel_weight,
        first_bias,
        second_bias,
        output_matrix,
        gain_two,
        shift_two,
        up_matrix,
        up_shift,
        down_matrix,
        down_shift,
    ) = weights
    gain_one = gain_one.astype(jnp.float32)
    shift_one = shift_one.astype(jnp.float32)
    gain_two = gain_two.astype(jnp.float32)
    shift_two = shift_two.astype(jnp.float32)
    up_shift = up_shift.astype(jnp.float32)
    down_shift = down_shift.astype(jnp.float32)
    slots, block_len, width = layer_input.shape
    seq_count = lax.axis_size("seq")
    seq_rank = lax.axis_index("seq")
    head_dim = HEAD_DIM
    group = H // seq_count
    full_len = block_len * seq_count
    score_scale = 1.0 / math.sqrt(head_dim)
    q_block = 512
    num_blocks = full_len // q_block
    win_len = full_len + q_block
    x_float = layer_input.astype(jnp.float32)
    x_hat_one, inv_std_one = norm_parts(x_float)
    first_normalized = (x_hat_one * gain_one + shift_one).astype(jnp.bfloat16)
    qkv_local = jnp.einsum(
        "mcr,rk->mck", first_normalized, query_key_value_matrix, preferred_element_type=jnp.float32
    ).astype(jnp.bfloat16)
    qkv_heads = lax.all_to_all(qkv_local, "seq", split_axis=2, concat_axis=1, tiled=True)
    qkv_heads = qkv_heads.reshape(slots, full_len, group, 3, head_dim)
    queries = qkv_heads[:, :, :, 0]
    keys = qkv_heads[:, :, :, 1]
    values = qkv_heads[:, :, :, 2]
    head_start = seq_rank * group
    head_bias_u = lax.dynamic_slice_in_dim(
        first_bias.astype(jnp.float32).reshape(H, head_dim), head_start, group, 0
    )
    head_bias_v = lax.dynamic_slice_in_dim(
        second_bias.astype(jnp.float32).reshape(H, head_dim), head_start, group, 0
    )
    query_u = (queries.astype(jnp.float32) + head_bias_u).astype(jnp.bfloat16)
    query_v = (queries.astype(jnp.float32) + head_bias_v).astype(jnp.bfloat16)
    table_rev = position_table(full_len, width).astype(jnp.bfloat16)[::-1]
    rel_cols = lax.dynamic_slice_in_dim(rel_weight, head_start * head_dim, group * head_dim, 1)
    rel_rev = jnp.dot(table_rev, rel_cols, preferred_element_type=jnp.float32).astype(jnp.bfloat16)
    rel_ext = jnp.concatenate([rel_rev, jnp.zeros_like(rel_rev)], axis=0).reshape(
        2 * full_len, group, head_dim
    )
    col_ids = lax.iota(jnp.int32, full_len)

    def scores_block(first_row):
        qu_part = lax.dynamic_slice_in_dim(query_u, first_row, q_block, 1)
        qv_part = lax.dynamic_slice_in_dim(query_v, first_row, q_block, 1)
        window_start = full_len - q_block - first_row
        rel_win = lax.dynamic_slice_in_dim(rel_ext, window_start, win_len, 0)
        content = jnp.einsum("sqhe,skhe->shqk", qu_part, keys, preferred_element_type=jnp.float32)
        rel_raw = jnp.einsum("sqhe,the->shqt", qv_part, rel_win, preferred_element_type=jnp.float32)
        rel_part = skew_rows(rel_raw)
        row_ids = first_row + lax.iota(jnp.int32, q_block)
        causal = col_ids[None, :] <= row_ids[:, None]
        inside = col_ids[None, :] < lengths[:, None]
        allowed = causal[None, None, :, :] & inside[:, None, None, :]
        scores = jnp.where(allowed, (content + rel_part) * score_scale, NEG_FILL)
        return (scores, qu_part, qv_part, rel_win, window_start)

    def forward_block(block_index):
        first_row = block_index * q_block
        scores, qu_part, qv_part, rel_win, window_start = scores_block(first_row)
        top = jnp.max(scores, axis=-1, keepdims=True)
        expo = jnp.exp(scores - top)
        total = jnp.sum(expo, axis=-1, keepdims=True)
        probs = (expo / total).astype(jnp.bfloat16)
        out_part = jnp.einsum(
            "shqk,skhe->sqhe", probs, values, preferred_element_type=jnp.float32
        ).astype(jnp.bfloat16)
        return (out_part, top[..., 0] + jnp.log(total[..., 0]))

    block_outs, block_lse = lax.map(forward_block, jnp.arange(num_blocks, dtype=jnp.int32))
    attn_heads = jnp.moveaxis(block_outs, 0, 1).reshape(slots, full_len, group * head_dim)
    attention_sequence = lax.all_to_all(attn_heads, "seq", split_axis=1, concat_axis=2, tiled=True)
    attention_projected = jnp.einsum(
        "mcr,rk->mck", attention_sequence, output_matrix, preferred_element_type=jnp.float32
    )
    resid = x_float + attention_projected
    x_hat_two, inv_std_two = norm_parts(resid)
    second_normalized = (x_hat_two * gain_two + shift_two).astype(jnp.bfloat16)
    pre_act = (
        jnp.einsum("oka,ac->okc", second_normalized, up_matrix, preferred_element_type=jnp.float32)
        + up_shift
    )
    normal_cdf = 0.5 * (1.0 + lax.erf(pre_act * (1.0 / math.sqrt(2.0))))
    hidden_state = (pre_act * normal_cdf).astype(jnp.bfloat16)
    down_proj = (
        jnp.einsum("zcp,pr->zcr", hidden_state, down_matrix, preferred_element_type=jnp.float32)
        + down_shift
    )
    output = (resid + down_proj).astype(jnp.bfloat16)
    positions = seq_rank * block_len + lax.iota(jnp.int32, block_len)
    live = (positions[None, :] < lengths[:, None]).astype(jnp.bfloat16)
    result_gradient = grad_out * live[:, :, None]
    grad_y_float = result_gradient.astype(jnp.float32)
    g_down_shift = jnp.sum(grad_y_float, axis=(0, 1))
    down_gradient = jnp.einsum(
        "hki,hku->iu", hidden_state, result_gradient, preferred_element_type=jnp.float32
    )
    hidden_gradient = jnp.einsum(
        "gvu,ju->gvj", result_gradient, down_matrix, preferred_element_type=jnp.float32
    )
    deriv = normal_cdf + pre_act * jnp.exp(-0.5 * pre_act * pre_act) * (
        1.0 / math.sqrt(2.0 * math.pi)
    )
    preactivation_gradient = (hidden_gradient * deriv).astype(jnp.bfloat16)
    g_up_shift = jnp.sum(preactivation_gradient.astype(jnp.float32), axis=(0, 1))
    up_gradient = jnp.einsum(
        "oiz,oix->zx", second_normalized, preactivation_gradient, preferred_element_type=jnp.float32
    )
    second_norm_gradient = jnp.einsum(
        "rau,ku->rak", preactivation_gradient, up_matrix, preferred_element_type=jnp.float32
    )
    g_gain_two = jnp.sum(second_norm_gradient * x_hat_two, axis=(0, 1))
    g_shift_two = jnp.sum(second_norm_gradient, axis=(0, 1))
    g_resid = grad_y_float + norm_back(second_norm_gradient * gain_two, x_hat_two, inv_std_two)
    attention_gradient = g_resid.astype(jnp.bfloat16)
    output_gradient = jnp.einsum(
        "zau,zam->um", attention_sequence, attention_gradient, preferred_element_type=jnp.float32
    )
    g_attn_seq = jnp.einsum(
        "urz,jz->urj", attention_gradient, output_matrix, preferred_element_type=jnp.float32
    ).astype(jnp.bfloat16)
    g_attn_heads = lax.all_to_all(
        g_attn_seq, "seq", split_axis=2, concat_axis=1, tiled=True
    ).reshape(slots, full_len, group, head_dim)

    def backward_block(carry, block_index):
        g_keys, g_vals, g_ext = carry
        first_row = block_index * q_block
        scores, qu_part, qv_part, rel_win, window_start = scores_block(first_row)
        probs = jnp.exp(scores - block_lse[block_index][..., None])
        d_out = lax.dynamic_slice_in_dim(g_attn_heads, first_row, q_block, 1)
        g_vals = g_vals + jnp.einsum(
            "shqk,sqhe->skhe", probs.astype(jnp.bfloat16), d_out, preferred_element_type=jnp.float32
        )
        g_probs = jnp.einsum("sqhe,skhe->shqk", d_out, values, preferred_element_type=jnp.float32)
        inner = jnp.sum(probs * g_probs, axis=-1, keepdims=True)
        g_scores = (probs * (g_probs - inner)).astype(jnp.bfloat16)
        g_qu = (
            jnp.einsum("shqk,skhe->sqhe", g_scores, keys, preferred_element_type=jnp.float32)
            * score_scale
        )
        g_keys = (
            g_keys
            + jnp.einsum("shqk,sqhe->skhe", g_scores, qu_part, preferred_element_type=jnp.float32)
            * score_scale
        )
        g_wide = unskew_rows(g_scores)
        g_qv = (
            jnp.einsum("shqt,the->sqhe", g_wide, rel_win, preferred_element_type=jnp.float32)
            * score_scale
        )
        g_win = (
            jnp.einsum("shqt,sqhe->sthe", g_wide, qv_part, preferred_element_type=jnp.float32)
            * score_scale
        )
        g_old = lax.dynamic_slice_in_dim(g_ext, window_start, win_len, 1)
        g_ext = lax.dynamic_update_slice_in_dim(g_ext, g_old + g_win, window_start, 1)
        return ((g_keys, g_vals, g_ext), (g_qu, g_qv))

    zero_heads = jnp.zeros((slots, full_len, group, head_dim), jnp.float32)
    zero_ext = jnp.zeros((slots, 2 * full_len, group, head_dim), jnp.float32)
    (g_keys, g_vals, g_ext), (g_qu_blocks, g_qv_blocks) = lax.scan(
        backward_block, (zero_heads, zero_heads, zero_ext), jnp.arange(num_blocks, dtype=jnp.int32)
    )
    g_qu = jnp.moveaxis(g_qu_blocks, 0, 1).reshape(slots, full_len, group, head_dim)
    g_qv = jnp.moveaxis(g_qv_blocks, 0, 1).reshape(slots, full_len, group, head_dim)
    g_queries = g_qu + g_qv
    g_bias_u_heads = jnp.sum(g_qu, axis=(0, 1))
    g_bias_v_heads = jnp.sum(g_qv, axis=(0, 1))
    g_qkv_heads = (
        jnp.stack([g_queries, g_keys, g_vals], axis=3)
        .astype(jnp.bfloat16)
        .reshape(slots, full_len, group * 3 * head_dim)
    )
    query_key_value_gradient = lax.all_to_all(
        g_qkv_heads, "seq", split_axis=1, concat_axis=2, tiled=True
    )
    g_rel_low = g_ext[:, :full_len].astype(jnp.bfloat16)
    g_rel_heads = jnp.einsum(
        "td,sthe->dhe", table_rev, g_rel_low, preferred_element_type=jnp.float32
    ).reshape(width, group * head_dim)
    g_rel_weight = lax.dynamic_update_slice_in_dim(
        jnp.zeros((width, width), jnp.float32), g_rel_heads, head_start * head_dim, 1
    )
    g_bias_u = lax.dynamic_update_slice_in_dim(
        jnp.zeros((H, head_dim), jnp.float32), g_bias_u_heads, head_start, 0
    ).reshape(width)
    g_bias_v = lax.dynamic_update_slice_in_dim(
        jnp.zeros((H, head_dim), jnp.float32), g_bias_v_heads, head_start, 0
    ).reshape(width)
    query_key_value_weight_gradient = jnp.einsum(
        "zau,zam->um",
        first_normalized,
        query_key_value_gradient,
        preferred_element_type=jnp.float32,
    )
    first_norm_gradient = jnp.einsum(
        "urz,jz->urj",
        query_key_value_gradient,
        query_key_value_matrix,
        preferred_element_type=jnp.float32,
    )
    g_gain_one = jnp.sum(first_norm_gradient * x_hat_one, axis=(0, 1))
    g_shift_one = jnp.sum(first_norm_gradient, axis=(0, 1))
    g_input = g_resid + norm_back(first_norm_gradient * gain_one, x_hat_one, inv_std_one)
    partial_shards = (
        lax.psum_scatter(g_gain_one, "fsdp", scatter_dimension=0, tiled=True),
        lax.psum_scatter(g_shift_one, "fsdp", scatter_dimension=0, tiled=True),
        lax.psum_scatter(query_key_value_weight_gradient, "fsdp", scatter_dimension=0, tiled=True),
        lax.psum_scatter(g_rel_weight, "fsdp", scatter_dimension=0, tiled=True),
        lax.psum_scatter(g_bias_u, "fsdp", scatter_dimension=0, tiled=True),
        lax.psum_scatter(g_bias_v, "fsdp", scatter_dimension=0, tiled=True),
        lax.psum_scatter(output_gradient, "fsdp", scatter_dimension=0, tiled=True),
        lax.psum_scatter(g_gain_two, "fsdp", scatter_dimension=0, tiled=True),
        lax.psum_scatter(g_shift_two, "fsdp", scatter_dimension=0, tiled=True),
        lax.psum_scatter(up_gradient, "fsdp", scatter_dimension=0, tiled=True),
        lax.psum_scatter(g_up_shift, "fsdp", scatter_dimension=0, tiled=True),
        lax.psum_scatter(down_gradient, "fsdp", scatter_dimension=0, tiled=True),
        lax.psum_scatter(g_down_shift, "fsdp", scatter_dimension=0, tiled=True),
    )
    shards = lax.psum(
        (
            partial_shards[0],
            partial_shards[1],
            partial_shards[2],
            partial_shards[3],
            partial_shards[4],
            partial_shards[5],
            partial_shards[6],
            partial_shards[7],
            partial_shards[8],
            partial_shards[9],
            partial_shards[10],
            partial_shards[11],
            partial_shards[12],
        ),
        "seq",
    )
    return (
        output,
        g_input,
        shards[0],
        shards[1],
        shards[2],
        shards[3],
        shards[4],
        shards[5],
        shards[6],
        shards[7],
        shards[8],
        shards[9],
        shards[10],
        shards[11],
        shards[12],
    )


def swap_core(values):
    size = lax.axis_size("fsdp")
    return lax.ppermute(values, "fsdp", [(i, i ^ 1) for i in range(size)])


def swap_chip(values, mask):
    size = lax.axis_size("fsdp")
    return lax.ppermute(values, "fsdp", [(i, i ^ (2 * mask)) for i in range(size)])


def swap_axis(values, turn):
    size = lax.axis_size("fsdp")
    return lax.ppermute(values, "fsdp", [(i, i ^ (2 << ((i & 1) ^ turn))) for i in range(size)])


def swap_seq(values, mask):
    size = lax.axis_size("seq")
    return lax.ppermute(values, "seq", [(i, i ^ mask) for i in range(size)])


def slot_pairs(turn):
    seq, pairs = lax.axis_size("seq"), []
    for f in range(lax.axis_size("fsdp")):
        for z in range(seq):
            to_f, to_z = (f & ~1) | (z & 1), 2 * (f & 1) + (turn ^ (z >> 1))
            pairs.append((f * seq + z, to_f * seq + to_z))
    return pairs


def to_slots(values, seq_rank):
    return [
        lax.ppermute(
            lax.dynamic_index_in_dim(values, turn ^ (seq_rank >> 1), 0, keepdims=False),
            ("fsdp", "seq"),
            slot_pairs(turn),
        )
        for turn in (0, 1)
    ]


def together(*values):
    return lax.optimization_barrier(values)


def whole(*shape):
    return pl.BlockSpec(shape, lambda *_: (0,) * len(shape))


def kernel_call(body, name, meta, args, outs, *, grid=(1,), in_specs=None, out_specs=None, scratch=(), flops=0, vmem=32):
    in_specs = in_specs or [whole(*a.shape) for a in args]
    out_specs = out_specs or [whole(*shape) for shape, _ in outs]
    moved = sum(a.size * a.dtype.itemsize for a in args)
    moved += sum(math.prod(shape) * jnp.dtype(kind).itemsize for shape, kind in outs)
    return pl.pallas_call(
        body,
        out_shape=[jax.ShapeDtypeStruct(shape, kind) for shape, kind in outs],
        grid_spec=pltpu.PrefetchScalarGridSpec(
            num_scalar_prefetch=1,
            grid=grid,
            in_specs=in_specs,
            out_specs=out_specs,
            scratch_shapes=scratch,
        ),
        compiler_params=pltpu.CompilerParams(vmem_limit_bytes=vmem << 20),
        cost_estimate=pl.CostEstimate(flops=0, bytes_accessed=0, transcendentals=0),
        name=name,
    )(meta, *args)


TN = (((0,), (0,)), ((), ()))
CORE, CHIP, RANK, LIVE = range(4)
DIGIT = 128


def aligned(index, size):
    return pl.multiple_of(index * size, size)


def own_place():
    device = lax.axis_index("fsdp")
    return device & 1, device >> 1, lax.axis_index("seq")


def pack_body(lengths_ref, qkv_ref, rel_ref, up_ref, out_ref, down_ref, *refs):
    small, (attn_ref, feed_ref, send_ref) = refs[:8], refs[8:]
    core, _, _ = own_place()
    shard = qkv_ref.shape[0]
    qkv, rel, up, out, down = qkv_ref[...], rel_ref[...], up_ref[...], out_ref[...], down_ref[...]
    heads, hd = rel.shape[1] // HEAD_DIM // 2, HEAD_DIM
    unit = up.shape[1] // 8
    packs, ups = [], []
    row = jnp.concatenate([ref[i : i + 1] for ref in small for i in range(ref.shape[0])], axis=1)
    lane = lax.broadcasted_iota(jnp.int32, (1, 4 * heads * hd - row.shape[1]), 1)
    digits = jnp.zeros(lane.shape, f32)
    for slot in range(lengths_ref.shape[0]):
        high = lengths_ref[slot] // DIGIT
        for at, digit in ((2 * slot, high), (2 * slot + 1, lengths_ref[slot] - high * DIGIT)):
            digits = jnp.where(lane == at, digit.astype(f32), digits)
    row = jnp.concatenate([row, digits.astype(row.dtype)], axis=1)
    rows = jnp.broadcast_to(row, (8, row.shape[1]))
    for side in (0, 1):
        parts = [
            qkv[:, ((2 * j + side) * 3 + t) * hd : ((2 * j + side) * 3 + t + 1) * hd]
            for t in range(3)
            for j in range(heads)
        ]
        parts += [rel[:, (2 * j + side) * hd : (2 * j + side + 1) * hd] for j in range(heads)]
        packs.append(jnp.concatenate(parts, axis=1))
        ups.append(
            jnp.concatenate([up[:, (2 * j + side) * unit : (2 * j + side + 1) * unit] for j in range(4)], axis=1)
        )
    first = core == 0
    folded = jnp.concatenate([out[: shard // 2], out[shard // 2 :]], axis=1)
    attn_ref[:shard] = jnp.where(first, packs[0], packs[1])
    attn_ref[shard:] = rows
    send_ref[:shard] = jnp.where(first, packs[1], packs[0])
    send_ref[shard : shard + 8] = rows
    send_ref[shard + 8 : 2 * shard + 8] = jnp.where(first, ups[1], ups[0])
    send_ref[2 * shard + 8 :] = folded
    feed_ref[:shard] = jnp.where(first, ups[0], ups[1])
    feed_ref[shard : shard + shard // 2] = folded
    feed_ref[shard + shard // 2 :] = jnp.concatenate([down[: 2 * shard], down[2 * shard :]], axis=1)


def ordered(core, own, other):
    first = core == 0
    return jnp.concatenate([jnp.where(first, own, other), jnp.where(first, other, own)], axis=0)


def slot_block(core, rank, step, own, other, store):
    turn = (step >> 1) ^ (rank & 1)
    local = (step & 1) == core
    for t in (0, 1):
        pl.when(local & (turn == t))(functools.partial(store, own[t]))
        pl.when(jnp.logical_not(local) & (turn == t))(functools.partial(store, other[t]))


def norm_rows(values):
    mean_val = jnp.mean(values, axis=1, keepdims=True)
    centered = values - mean_val
    inv_std = lax.rsqrt(jnp.mean(centered * centered, axis=1, keepdims=True) + NORM_EPS)
    return centered * inv_std, inv_std


def weights_body(_, *refs):
    packs, table_ref = refs[0:4], refs[4]
    rel_ref, w_ref, vec_ref, up_ref, *bias_refs = refs[5:11]
    step, (core, chip, _) = pl.program_id(0), own_place()
    width = w_ref.shape[0]
    shard = width // 8
    span = w_ref.shape[1] - rel_ref.shape[1]

    @pl.when(step == 0)
    def _():
        first = core == 0
        vec_ref[...] = jnp.zeros_like(vec_ref)
        own_rows = []
        for k in range(4):
            at = pl.ds(aligned(chip ^ k, 2 * shard), 2 * shard)
            own, other = packs[k][: shard + 8], packs[k][shard + 8 :]
            w_ref[at, :] = ordered(core, own[:shard], other[:shard])
            own_row, other_row = own[shard : shard + 1].astype(f32), other[shard : shard + 1].astype(f32)
            own_rows.append(own_row)
            low, high = jnp.where(first, own_row, other_row), jnp.where(first, other_row, own_row)
            for row, source in enumerate((0, 1, 4, 5, 6)):
                piece = slice(source * shard, (source + 1) * shard)
                vec_ref[row : row + 1, at] = jnp.concatenate([low[:, piece], high[:, piece]], axis=1)
            unit = up_ref.shape[1] // 4
            up_ref[:, pl.ds(aligned(chip ^ k, unit), unit)] = own_row[:, 7 * shard : 7 * shard + unit]
        even = chip & 1 == 0
        for k in (0, 2):
            at = pl.ds(aligned((chip ^ k) >> 1, 2 * shard), 2 * shard)
            low = jnp.where(even, own_rows[k], own_rows[k + 1])
            high = jnp.where(even, own_rows[k + 1], own_rows[k])
            for row, source in enumerate((2, 3)):
                piece = slice(source * shard, (source + 1) * shard)
                bias_refs[row][:, at] = jnp.concatenate([low[:, piece], high[:, piece]], axis=1)

    rel_ref[...] = dot(table_ref[...], w_ref[:, span:], NN).astype(bf)


def project_body(_, *refs):
    own_x, other_x = refs[0:2], refs[2:4]
    w_ref, vec_ref, qkv_ref, h_ref, x_ref = refs[4:9]
    step, (core, _, rank) = pl.program_id(0), own_place()

    def copy(ref):
        x_ref[...] = ref[...]

    slot_block(core, rank, step, own_x, other_x, copy)
    x_hat, _ = norm_rows(x_ref[...].astype(f32))
    h = (x_hat * vec_ref[0:1, :] + vec_ref[1:2, :]).astype(bf)
    h_ref[...] = h
    qkv_ref[...] = dot(h, w_ref[:, : qkv_ref.shape[1]], NN).astype(bf)


def feed_body(meta, *refs):
    packs, own_g, other_g = refs[0:4], refs[4:6], refs[6:8]
    x_ref, o_own, o_other, vec_ref, bias_ref = refs[8:13]
    dy_ref, x_hat_ref, rstd_ref, y_keep, dh_ref, y_send, wo_mine = refs[13:20]
    outs = refs[20:24]
    up_w, down_w, wo_theirs, up_acc, down_acc, sums = refs[24:30]
    step, chip, core = pl.program_id(0), meta[CHIP], meta[CORE]
    width = up_w.shape[0]
    shard, unit, block = width // 8, down_w.shape[0] // 4, x_ref.shape[0]
    fold = shard // 2
    unfold = lambda rows: jnp.concatenate([rows[:, :width], rows[:, width:]], axis=0)

    @pl.when(step == 0)
    def _():
        sums[...] = jnp.zeros_like(sums)
        up_acc[...] = jnp.zeros_like(up_acc)
        down_acc[...] = jnp.zeros_like(down_acc)
        masks = (0, 1 + core, 2 - core, 3)
        for pack_ref, k in zip(packs, masks):
            pack, other = pack_ref[: 3 * shard + fold], pack_ref[3 * shard + fold :]
            up_w[pl.ds(aligned(chip ^ k, 2 * shard), 2 * shard), :] = ordered(core, pack[:shard], other[:shard])
            at = pl.ds(aligned(chip ^ k, shard), shard)
            wo_mine[at, :] = unfold(pack[shard : shard + fold])
            wo_theirs[at, :] = unfold(other[shard:])
            down_w[pl.ds(aligned(chip ^ k, unit), unit), :] = unfold(pack[shard + fold :])

    at = step * block + lax.broadcasted_iota(jnp.int32, (block, 1), 0)

    def load(ref):
        dy_ref[...] = jnp.where(at < meta[LIVE], ref[...].astype(f32), 0.0).astype(bf)

    slot_block(core, meta[RANK], step, own_g, other_g, load)
    y1 = x_ref[...].astype(f32) + (dot(o_own[...], wo_mine[...], NN) + dot(o_other[...], wo_theirs[...], NN))
    x_hat, inv_std = norm_rows(y1)
    x_hat_ref[...] = x_hat.astype(bf)
    rstd_ref[...] = inv_std
    h = (x_hat * vec_ref[2:3, :] + vec_ref[3:4, :]).astype(bf)
    f = dot(h, up_w[...], NN) + bias_ref[...]
    cdf = 0.5 * (1.0 + lax.erf(f * (1.0 / math.sqrt(2.0))))
    g = (f * cdf).astype(bf)
    dy = dy_ref[...]
    dg = dot(dy, down_w[...], NT)
    df = (dg * (cdf + f * jnp.exp(-0.5 * f * f) * (1.0 / math.sqrt(2.0 * math.pi)))).astype(bf)
    z = dot(g, down_w[...], NN)
    dh = dot(df, up_w[...], NT)
    dh_ref[...] = dh.astype(bf)
    up_acc[...] += dot(h, df, TN)
    down_acc[...] += dot(g, dy, TN)
    sums[0:1, :width] += jnp.sum(dh * x_hat, axis=0, keepdims=True)
    sums[1:2, :width] += jnp.sum(dh, axis=0, keepdims=True)
    sums[3:4, :] += jnp.sum(df.astype(f32), axis=0, keepdims=True)
    local = (step & 1) == core

    @pl.when(local)
    def _():
        y_keep[...] = y1 + z + vec_ref[4:5, :]
        sums[2:3, :width] += jnp.sum(dy.astype(f32), axis=0, keepdims=True)

    @pl.when(jnp.logical_not(local))
    def _():
        y_send[...] = z.astype(bf)

    @pl.when(step == pl.num_programs(0) - 1)
    def _():
        rows = 2 * shard
        for k, out in enumerate(outs):
            at = pl.ds(aligned(chip ^ k, rows), rows)
            units = pl.ds(aligned(chip ^ k, unit), unit)
            tail = [sums[0:1, at], sums[1:2, at], sums[2:3, at], sums[3:4, units]]
            tail = jnp.concatenate(tail + [jnp.zeros((1, sums.shape[1] - 3 * rows - unit), f32)], axis=1)
            out[:rows] = up_acc[at, :].astype(out.dtype)
            out[rows : rows + 8] = jnp.broadcast_to(tail, (8, tail.shape[1])).astype(out.dtype)
            down = down_acc[units, :]
            half = unit // 2
            out[rows + 8 :] = jnp.concatenate([down[:half], down[half:]], axis=1).astype(out.dtype)


def norm_two_body(meta, x_hat_ref, rstd_ref, dh_ref, dh_came, dy_ref, vec_ref, y_keep, y_came, wo_ref, o_ref, *refs):
    out0, out1, resid_ref, do_ref, go_ref = refs
    step = pl.program_id(0)

    @pl.when(step == 0)
    def _():
        go_ref[...] = jnp.zeros_like(go_ref)

    x_hat = x_hat_ref[...].astype(f32)
    e = (dh_ref[...].astype(f32) + dh_came[...].astype(f32)) * vec_ref[2:3, :]
    first = jnp.mean(e, axis=1, keepdims=True)
    second = jnp.mean(e * x_hat, axis=1, keepdims=True)
    grad = dy_ref[...].astype(f32) + rstd_ref[...] * (e - first - x_hat * second)
    da = grad.astype(bf)
    do_ref[...] = dot(da, wo_ref[...], NT).astype(bf)
    go_ref[...] += dot(o_ref[...], da, TN)
    turn = (step >> 1) ^ (meta[RANK] & 1)
    local = (step & 1) == meta[CORE]

    @pl.when(local)
    def _():
        resid_ref[...] = grad
        y = (y_keep[...] + y_came[...].astype(f32)).astype(bf)

        @pl.when(turn == 0)
        def _():
            out0[...] = y

        @pl.when(turn == 1)
        def _():
            out1[...] = y


def qkv_back_body(meta, *refs):
    grads_a, grads_b = refs[:6], refs[6:12]
    w_ref, x_ref, h_ref, table_ref, go_ref = refs[12:17]
    keep_ref, send_ref = refs[17:19]
    outs, acc, sums = refs[19:23], refs[23], refs[24]
    step, chip = pl.program_id(0), meta[CHIP]
    width = x_ref.shape[1]
    rows = width // 4

    @pl.when(step == 0)
    def _():
        sums[...] = jnp.zeros_like(sums)
        acc[...] = jnp.zeros_like(acc)

    both = lambda i: [grads_a[i][...], grads_b[i][...]]
    dqkv = jnp.concatenate(both(0) + both(1) + both(2), axis=1)
    drel = jnp.concatenate(both(3), axis=1)
    span = dqkv.shape[1]
    acc[:, :span] += dot(h_ref[...], dqkv, TN)
    acc[:, span:] += dot(table_ref[...], drel, TN)
    dh = dot(dqkv, w_ref[:, :span], NT)
    x_hat, _ = norm_rows(x_ref[...].astype(f32))
    sums[0:1, :] += jnp.sum(dh * x_hat, axis=0, keepdims=True)
    sums[1:2, :] += jnp.sum(dh, axis=0, keepdims=True)
    local = (step & 1) == meta[CORE]

    @pl.when(local)
    def _():
        keep_ref[...] = dh

    @pl.when(jnp.logical_not(local))
    def _():
        send_ref[...] = dh.astype(bf)

    @pl.when(step == pl.num_programs(0) - 1)
    def _():
        for k, out in enumerate(outs):
            at = pl.ds(aligned(chip ^ k, rows), rows)
            low = (chip ^ k) >> 1 == 0
            tail = [sums[0:1, at], sums[1:2, at]]
            tail += [jnp.where(low, *both(i)) for i in (4, 5)]
            tail = jnp.concatenate(tail + [jnp.zeros((1, acc.shape[1] - 4 * rows), f32)], axis=1)
            out[:rows] = acc[at, :].astype(out.dtype)
            out[rows : rows + 8] = jnp.broadcast_to(tail, (8, tail.shape[1])).astype(out.dtype)
            shard = rows // 2
            lines = go_ref[pl.ds(aligned(chip ^ k, shard), shard), :]
            lines = jnp.concatenate([lines[: shard // 2], lines[shard // 2 :]], axis=1)
            out[rows + 8 :] = lines.astype(out.dtype)


def norm_one_body(meta, x_ref, dh_keep, dh_came, resid_ref, vec_ref, out0, out1):
    turn = pl.program_id(0) ^ (meta[RANK] & 1)
    x_hat, inv_std = norm_rows(x_ref[...].astype(f32))
    e = (dh_keep[...] + dh_came[...].astype(f32)) * vec_ref[0:1, :]
    first = jnp.mean(e, axis=1, keepdims=True)
    second = jnp.mean(e * x_hat, axis=1, keepdims=True)
    grad = (resid_ref[...] + inv_std * (e - first - x_hat * second)).astype(bf)

    @pl.when(turn == 0)
    def _():
        out0[...] = grad

    @pl.when(turn == 1)
    def _():
        out1[...] = grad


def rank_bit(meta, bit):
    return (meta[RANK] >> bit) & 1


def chip_sum_body(meta, own, *refs, bit):
    *came, keep, send = refs
    half = keep.shape[1]
    for out, side in ((keep, rank_bit(meta, bit)), (send, 1 - rank_bit(meta, bit))):
        at = pl.ds(aligned(side, half), half)
        total = own[:, at]
        for ref in came:
            total = total + ref[:, at].astype(f32)
        out[...] = total.astype(out.dtype)


def chip_sum(meta, parts, name, bit):
    rows, size = parts[0].shape
    return kernel_call(functools.partial(chip_sum_body, bit=bit), name, meta, parts, [((rows, size // 2), f32), ((rows, size // 2), bf)])


def own_rows_first(total, core, shard):
    theirs = lax.dynamic_slice_in_dim(total, (1 - core) * shard, shard, 0)
    mine = lax.dynamic_slice_in_dim(total, core * shard, shard, 0)
    came = swap_core(jnp.concatenate([theirs, total[2 * shard : 2 * shard + 8]], axis=0))
    return jnp.concatenate([mine, came, total[2 * shard :]], axis=0)


def halves(meta, mine, other, bit):
    low = rank_bit(meta, bit) == 0
    return jnp.concatenate([jnp.where(low, mine, other), jnp.where(low, other, mine)], axis=1)


def both_cores(meta, own, came):
    own, came = own.astype(f32), came.astype(f32)
    return own, own + came, meta[CORE] == 0


def store_half(ref, source, at, low):
    size = 2 * ref.shape[1]
    piece = source[:, at * size : (at + 1) * size]
    ref[...] = jnp.where(low, piece[:, : size // 2], piece[:, size // 2 :])


def early_out_body(meta, mine, other, came_ref, g_up, g_down, *vec_refs):
    rows = halves(meta, mine[...], other[...], 0)
    came_rows = halves(meta, came_ref[0], came_ref[1], 0)
    shard, width = g_up.shape[0], g_down.shape[1]
    first, unit = meta[CORE] == 0, rows.shape[1] // 4
    own, came = jnp.where(first, rows[:shard], rows[shard : 2 * shard]), came_rows[:shard]
    pair = (jnp.where(first, own, came), jnp.where(first, came, own))
    for j in range(4):
        for side in (0, 1):
            at = (2 * j + side) * unit
            g_up[:, at : at + unit] = pair[side][:, j * unit : (j + 1) * unit].astype(f32)
    down = rows[2 * shard + 8 :].astype(f32)
    g_down[...] = jnp.concatenate([down[:, :width], down[:, width:]], axis=0)
    own, total, low = both_cores(meta, rows[2 * shard : 2 * shard + 1], came_rows[shard : shard + 1])
    for at, ref in enumerate(vec_refs[:3]):
        store_half(ref, total, at, low)
    vec_refs[3][...] = own[:, 6 * shard : 6 * shard + unit]


def late_out_body(meta, mine, other, g_qkv, g_rel, g_out, *vec_refs):
    rows = halves(meta, mine[...], other[...], 0)
    shard, width = g_qkv.shape[0], g_out.shape[1]
    first, hd, heads = meta[CORE] == 0, HEAD_DIM, H // 2
    own, came = rows[:shard], rows[shard : 2 * shard]
    pair = (jnp.where(first, own, came), jnp.where(first, came, own))
    cols = heads * hd
    piece = lambda h, t: pair[h & 1][:, t * cols + (h >> 1) * hd : t * cols + ((h >> 1) + 1) * hd]
    g_qkv[...] = jnp.concatenate([piece(h, t) for h in range(2 * heads) for t in range(3)], axis=1).astype(f32)
    g_rel[...] = jnp.concatenate([piece(h, 3) for h in range(2 * heads)], axis=1).astype(f32)
    out = rows[2 * shard + 16 :].astype(f32)
    g_out[...] = jnp.concatenate([out[:, :width], out[:, width:]], axis=0)
    own, total, low = both_cores(meta, rows[2 * shard + 8 : 2 * shard + 9], rows[2 * shard : 2 * shard + 1])
    even = meta[CHIP] & 1 == 0
    for at, ref in enumerate(vec_refs):
        store_half(ref, total if at < 2 else own, at, low if at < 2 else even)


def place_body(meta, y0, y1, x0, x1, y_ref, x_ref):
    high = meta[RANK] >> 1 == 1
    y_ref[0] = jnp.where(high, y1[...], y0[...])
    y_ref[1] = jnp.where(high, y0[...], y1[...])
    x_ref[0] = jnp.where(high, x1[...], x0[...]).astype(f32)
    x_ref[1] = jnp.where(high, x0[...], x1[...]).astype(f32)


def slot_split_device(
    layer_input,
    lengths,
    ln1_gain,
    ln1_bias,
    w_qkv,
    w_rel,
    bias_u,
    bias_v,
    w_out,
    ln2_gain,
    ln2_bias,
    w_up,
    up_bias,
    w_down,
    down_bias,
    grad_out,
):
    slots, block, width = layer_input.shape
    rank, device = lax.axis_index("seq"), lax.axis_index("fsdp")
    core, chip = device & 1, device >> 1
    full, heads = 4 * block, H // 2
    cols, shard, unit = heads * HEAD_DIM, width // 8, up_bias.shape[0]
    mine_ff = 4 * unit

    none = jnp.zeros((4,), jnp.int32)
    x_own = to_slots(jnp.concatenate([layer_input, grad_out], axis=2), rank)
    vectors = (ln1_gain, ln1_bias, bias_u, bias_v, ln2_gain, ln2_bias, down_bias, up_bias)
    attn_rows, fold = shard + 8, shard // 2
    attn_pack, feed_pack, pack_send = kernel_call(
        pack_body,
        "pack",
        pltpu.with_memory_space_constraint(lengths, pltpu.HBM),
        [
            pltpu.with_memory_space_constraint(v, pltpu.HBM)
            for v in [w_qkv, w_rel, w_up, w_out, w_down] + [v.reshape(-1, min(128, v.size)) for v in vectors]
        ],
        [((attn_rows, 4 * cols), bf), ((3 * shard + fold, 4 * cols), bf), ((attn_rows + shard + fold, 4 * cols), bf)],
        vmem=32,
    )
    pack_came = swap_core(pack_send)
    attn_pack = jnp.concatenate([attn_pack, pack_came[:attn_rows]], axis=0)
    attn_packs = [attn_pack] + [swap_chip(attn_pack, k) for k in (1, 2, 3)]
    feed_pack = jnp.concatenate([feed_pack, pack_came[attn_rows:]], axis=0)
    digits_at = 7 * shard + unit
    digits = pack_came[shard, digits_at : digits_at + 2 * slots].astype(jnp.int32)
    lengths = jnp.where(core == rank >> 1, lengths, digits[0::2] * DIGIT + digits[1::2])
    length = jnp.where(rank & 1 == 0, lengths[0], lengths[1])
    meta = jnp.stack([core, chip, rank, length]).astype(jnp.int32)
    length_arr = length.reshape(1)
    fine = 32
    inv_freq = jnp.exp(lax.iota(f32, width // 2) * (-2.0 * math.log(10000.0) / width))
    high = (full - 1 - fine * lax.iota(jnp.int32, full // fine)).astype(f32)[:, None] * inv_freq
    low = lax.iota(f32, fine)[:, None] * inv_freq
    high_sin, high_cos, low_sin, low_cos = together(jnp.sin(high), jnp.cos(high), jnp.sin(low), jnp.cos(low))
    high_sin, high_cos = high_sin[:, None], high_cos[:, None]
    table = jnp.concatenate(
        [high_sin * low_cos - high_cos * low_sin, high_cos * low_cos + high_sin * low_sin], axis=2
    )
    table = table.astype(bf).reshape(full, width)

    feed_pack, meta, length_arr, table, *attn_packs = together(feed_pack, meta, length_arr, table, *attn_packs)
    by_step = lambda width: pl.BlockSpec((block, width), lambda i, _: (i, 0))
    rel, w_own, vecs, up_b, own_u, own_v = kernel_call(
        weights_body,
        "weights",
        none,
        [pltpu.with_memory_space_constraint(v, pltpu.HBM) for v in attn_packs] + [table],
        [((full, cols), bf), ((width, 4 * cols), bf), ((8, width), f32), ((1, mine_ff), f32)]
        + [((1, cols), f32), ((1, cols), f32)],
        grid=(4,),
        in_specs=[whole(2 * attn_rows, 4 * cols)] * 4 + [by_step(width)],
        out_specs=[by_step(cols), whole(width, 4 * cols), whole(8, width), whole(1, mine_ff)]
        + [whole(1, cols), whole(1, cols)],
    )
    w_own, vecs, *x_own = together(w_own, vecs, *x_own)
    x_other = [swap_core(x) for x in x_own]
    feed_first = swap_axis(feed_pack, 0)
    feed_second = swap_axis(feed_pack, 1)

    side = lambda at: pl.BlockSpec((block, width), lambda i, _: (0, at))
    qkv, h1, x_slot = kernel_call(
        project_body,
        "project",
        none,
        x_own + x_other + [w_own, vecs],
        [((full, 3 * cols), bf), ((full, width), bf), ((full, width), bf)],
        grid=(4,),
        in_specs=[side(0)] * 4 + [whole(width, 4 * cols), whole(8, width)],
        out_specs=[by_step(3 * cols), by_step(width), by_step(width)],
    )
    qkv, feed_first = together(qkv, feed_first)
    feed_third = swap_axis(feed_first, 1)
    attn, attn_wide, *probs = attn_fwd(length_arr, qkv, rel, own_u, own_v)
    attn, feed_second, feed_third = together(attn, feed_second, feed_third)
    feed_packs = [feed_pack, feed_first, feed_second, feed_third]

    attn_other = swap_core(attn)
    kept = lambda width: pl.BlockSpec((block, width), lambda i, _: (i >> 1, 0))
    half, rows = full // 2, 2 * shard + 8
    blocks = lambda rows: [((rows, 2 * width), f32)] + [((rows, 2 * width), bf)] * 3
    dy, x_hat, rstd, y_keep, dh, y_send, wo_mine, *early_parts = kernel_call(
        feed_body,
        "feed",
        meta,
        feed_packs + x_own + x_other + [x_slot, attn, attn_other, vecs, up_b],
        [((full, width), bf), ((full, width), bf), ((full, 1), f32), ((half, width), f32)]
        + [((full, width), bf), ((half, width), bf), ((cols, width), bf)]
        + blocks(rows + unit // 2),
        grid=(4,),
        in_specs=[whole(*feed_pack.shape)] * 4 + [side(1)] * 4
        + [by_step(width), by_step(cols), by_step(cols), whole(8, width), whole(1, mine_ff)],
        out_specs=[by_step(width), by_step(width), by_step(1), kept(width)]
        + [by_step(width), kept(width), whole(cols, width)]
        + [whole(rows + unit // 2, 2 * width)] * 4,
        scratch=[
            pltpu.VMEM((width, mine_ff), bf),
            pltpu.VMEM((mine_ff, width), bf),
            pltpu.VMEM((cols, width), bf),
            pltpu.VMEM((width, mine_ff), f32),
            pltpu.VMEM((mine_ff, width), f32),
            pltpu.VMEM((8, mine_ff), f32),
        ],
        flops=12 * full * width * mine_ff,
    )
    dh_came = swap_core(dh)
    y_came = swap_core(y_send)
    early_came = [swap_chip(early_parts[k], k) for k in (1, 2, 3)]
    out0, out1, g_resid, d_attn, g_out = kernel_call(
        norm_two_body,
        "norm_two",
        meta,
        [x_hat, rstd, dh, dh_came, dy, vecs, y_keep, y_came, wo_mine, attn],
        [((block, width), bf)] * 2 + [((half, width), f32), ((full, cols), bf), ((cols, width), f32)],
        grid=(4,),
        in_specs=[by_step(width), by_step(1)] + [by_step(width)] * 3 + [whole(8, width)] + [kept(width)] * 2
        + [whole(cols, width), by_step(cols)],
        out_specs=[whole(block, width)] * 2 + [kept(width), by_step(cols), whole(cols, width)],
        flops=4 * full * width * cols,
    )
    home = lambda outs: [
        lax.ppermute(out, ("fsdp", "seq"), [(b, a) for a, b in slot_pairs(turn)])
        for turn, out in enumerate(outs)
    ]
    y_turns = home((out0, out1))
    back = lambda pair, d_out: attn_bwd(length_arr, qkv, rel, own_u, own_v, probs, d_out, attn_wide, pair=pair)
    d_attn, *grads_a = together(d_attn, *back(0, d_attn))
    *grads_b, y0, y1, e1, e2, e3 = together(*back(1, d_attn), *y_turns, *early_came)
    early_keep, early_send = chip_sum(meta, [early_parts[0], e1, e2, e3], "early_chips", 0)
    early_send, *grads_b = together(early_send, *grads_b)
    early_came = swap_seq(early_send, 1)
    pair_step = pl.BlockSpec((block, 2 * HEAD_DIM), lambda i, _: (i, 0))
    pair_row = whole(1, 2 * HEAD_DIM)
    dh1_keep, dh1_send, *late_parts = kernel_call(
        qkv_back_body,
        "qkv_back",
        meta,
        [*grads_a, *grads_b, w_own, x_slot, h1, table, g_out],
        [((half, width), f32), ((half, width), bf)] + blocks(rows + fold),
        grid=(4,),
        in_specs=([pair_step] * 4 + [pair_row] * 2) * 2
        + [whole(width, 4 * cols)] + [by_step(width)] * 3 + [whole(cols, width)],
        out_specs=[kept(width)] * 2 + [whole(rows + fold, 2 * width)] * 4,
        scratch=[pltpu.VMEM((width, 4 * cols), f32), pltpu.VMEM((8, width), f32)],
        flops=14 * full * width * cols,
    )
    dh1_send, *late_parts = together(dh1_send, *late_parts)
    early_pair = (early_keep + early_came.astype(f32)).astype(bf)
    dh1_came = swap_core(dh1_send)
    early_came = swap_seq(early_pair, 2)
    late_came = [swap_chip(late_parts[k], k) for k in (1, 2, 3)]
    by_half = pl.BlockSpec((block, width), lambda i, _: (i, 0))
    own_rows = pl.BlockSpec((block, width), lambda i, m: (2 * i + m[CORE], 0))
    x0, x1 = kernel_call(
        norm_one_body,
        "norm_one",
        meta,
        [x_slot, dh1_keep, dh1_came, g_resid, vecs],
        [((block, width), bf)] * 2,
        grid=(2,),
        in_specs=[own_rows] + [by_half] * 3 + [whole(8, width)],
        out_specs=[whole(block, width)] * 2,
    )
    x_turns = home((x0, x1))
    late_keep, late_send = chip_sum(meta, [late_parts[0]] + late_came, "late_chips", 0)
    small = lambda size: ((1, size), f32)
    late_came, early_came, x_turns[0] = together(swap_seq(late_send, 1), early_came, x_turns[0])
    early_mine = (early_pair.astype(f32) + early_came.astype(f32)).astype(bf)
    late_pair = (late_keep + late_came.astype(f32)).astype(bf)
    late_came = swap_seq(late_pair, 2)
    early_other = swap_seq(early_mine, 1)
    late_total = (late_pair.astype(f32) + late_came.astype(f32)).astype(bf)
    late_mine = own_rows_first(late_total, core, shard)
    late_other = swap_seq(late_mine, 1)
    late_mine, g0, g1, early_other = together(late_mine, *x_turns, early_other)
    theirs = lambda rows: jnp.concatenate(
        [
            lax.dynamic_slice_in_dim(rows, (1 - core) * shard, shard, 0),
            rows[2 * shard : 2 * shard + 8],
        ],
        axis=0,
    )
    early_core = swap_core(jnp.stack([theirs(early_mine), theirs(early_other)]))
    output, grad_x = kernel_call(
        place_body,
        "place",
        meta,
        [y0, y1, g0, g1],
        [((2, block, width), bf), ((2, block, width), f32)],
    )
    g_up, g_down, g_gain_two, g_shift_two, g_down_shift, g_up_shift = kernel_call(
        early_out_body,
        "early_out",
        meta,
        [early_mine, early_other, early_core],
        [((shard, 2 * mine_ff), f32), ((unit, width), f32)] + [small(shard)] * 3 + [small(unit)],
    )
    late_other, output, grad_x, g_up = together(late_other, output, grad_x, g_up)
    g_qkv, g_rel, g_w_out, *late_vectors = kernel_call(
        late_out_body,
        "late_out",
        meta,
        [late_mine, late_other],
        [((shard, 6 * cols), f32), ((shard, 2 * cols), f32), ((shard, width), f32)] + [small(shard)] * 4,
    )
    g_gain_one, g_shift_one, g_bias_u, g_bias_v = [v.reshape(-1) for v in late_vectors]
    return (
        output,
        grad_x,
        g_gain_one,
        g_shift_one,
        g_qkv,
        g_rel,
        g_bias_u,
        g_bias_v,
        g_w_out,
        g_gain_two.reshape(-1),
        g_shift_two.reshape(-1),
        g_up,
        g_up_shift.reshape(-1),
        g_down,
        g_down_shift.reshape(-1),
    )


def per_device(*args):
    one_slot_a_chip = lax.axis_size("fsdp") == 8 and lax.axis_size("seq") == 4
    if one_slot_a_chip and args[0].shape[0] == 2:
        return slot_split_device(*args)
    return head_split_device(*args)


def solution(mesh):
    placed = (
        P("fsdp", "seq", None),
        P("fsdp"),
        P("fsdp"),
        P("fsdp"),
        P("fsdp", None),
        P("fsdp", None),
        P("fsdp"),
        P("fsdp"),
        P("fsdp", None),
        P("fsdp"),
        P("fsdp"),
        P("fsdp", None),
        P("fsdp"),
        P("fsdp", None),
        P("fsdp"),
        P("fsdp", "seq", None),
    )
    return jax.shard_map(
        per_device,
        mesh=mesh,
        in_specs=placed,
        out_specs=(
            P("fsdp", "seq", None),
            P("fsdp", "seq", None),
            P("fsdp"),
            P("fsdp"),
            P("fsdp", None),
            P("fsdp", None),
            P("fsdp"),
            P("fsdp"),
            P("fsdp", None),
            P("fsdp"),
            P("fsdp"),
            P("fsdp", None),
            P("fsdp"),
            P("fsdp", None),
            P("fsdp"),
        ),
        check_vma=False,
    )
```

```python
import functools
import math

import jax
import jax.numpy as jnp
from jax import lax
from jax.experimental import pallas as pl
from jax.experimental.pallas import tpu as pltpu
from jax.sharding import PartitionSpec as P

H = 8
HEAD_DIM = 64


NEG_FILL = -1e30
NORM_EPS = 1e-05


bf, f32 = jnp.bfloat16, jnp.float32
NEG = NEG_FILL
HD = HEAD_DIM
NT = (((1,), (1,)), ((), ()))
NN = (((1,), (0,)), ((), ()))


def dot(a, b, dims):
    return lax.dot_general(a, b, dims, preferred_element_type=f32)


def masked_tail(s, keep, block):
    tail = jnp.where(keep, s[:, s.shape[1] - block :], NEG)
    if s.shape[1] == block:
        return tail
    return jnp.concatenate([s[:, : s.shape[1] - block], tail], axis=1)


def scores(qu, qv, keys, rel_rev, keep, block):
    span = keys.shape[0]
    rel = dot(qv, rel_rev, NT)
    rel = pltpu.roll(rel, (span - block + 1) % span, 1, stride=1, stride_axis=0)
    return masked_tail(dot(qu, keys, NT) + rel, keep, block)


def attn_fwd_body(len_ref, q_ref, k_ref, v_ref, r_ref, bu_ref, bv_ref, o_ref, wide_ref, *p_refs, block):
    full = q_ref.shape[0]
    lane = lax.broadcasted_iota(jnp.int32, (block, 2 * HD), 1)
    sides = (lane < HD, lane >= HD)
    length = len_ref[0]
    col = lax.broadcasted_iota(jnp.int32, (1, full), 1)
    bias = jnp.where(col < length, 0.0, NEG)
    tri = lax.broadcasted_iota(jnp.int32, (block, block), 1) <= lax.broadcasted_iota(
        jnp.int32, (block, block), 0
    )
    for first in reversed(range(0, full, block)):
        span = first + block
        q = q_ref[first:span, :].astype(f32)
        qu = (q + bu_ref[...]).astype(bf).astype(f32) * 0.125
        qv = (q + bv_ref[...]).astype(bf).astype(f32) * 0.125
        outs = []
        for head, side in enumerate(sides):
            s = scores(
                jnp.where(side, qu, 0.0).astype(bf),
                jnp.where(side, qv, 0.0).astype(bf),
                k_ref[:span, :],
                r_ref[full - span :, :],
                tri,
                block,
            )
            if span > full // 2:
                s = s + bias[:, :span]
            top = jnp.max(s, axis=1, keepdims=True)
            e = jnp.exp(s - top)
            total = jnp.sum(e, axis=1, keepdims=True)
            p = (e * (1.0 / total)).astype(bf)
            p_refs[first // block][head] = p
            outs.append(dot(p, v_ref[:span, :], NN))
        wide = jnp.where(sides[0], outs[0], outs[1])
        wide_ref[first:span, :] = wide
        o_ref[first:span, :] = wide.astype(bf)


def attn_fwd(length, qkv, rel_rev, bias_u, bias_v, *, block=256):
    full, cols = rel_rev.shape
    spans = range(block, full + 1, block)
    pairs = cols // (2 * HD)
    at = lambda part: pl.BlockSpec((full, 2 * HD), lambda pair, _: (0, part * pairs + pair))
    row = pl.BlockSpec((1, 2 * HD), lambda pair, _: (0, pair))
    return pl.pallas_call(
        functools.partial(attn_fwd_body, block=block),
        out_shape=(
            jax.ShapeDtypeStruct((full, cols), bf),
            jax.ShapeDtypeStruct((full, cols), f32),
            *(jax.ShapeDtypeStruct((2 * pairs, block, span), bf) for span in spans),
        ),
        grid_spec=pltpu.PrefetchScalarGridSpec(
            num_scalar_prefetch=1,
            grid=(pairs,),
            in_specs=[at(0), at(1), at(2), at(0), row, row],
            out_specs=(
                at(0),
                at(0),
                *(pl.BlockSpec((2, block, span), lambda pair, _: (pair, 0, 0)) for span in spans),
            ),
        ),
        cost_estimate=pl.CostEstimate(flops=0, bytes_accessed=0, transcendentals=0),
        compiler_params=pltpu.CompilerParams(vmem_limit_bytes=32 << 20),
        name="attn_fwd",
    )(length, qkv, qkv, qkv, rel_rev, bias_u, bias_v)


def attn_bwd_body(len_ref, q_ref, k_ref, v_ref, r_ref, bu_ref, bv_ref, do_ref, o_ref, *refs, block, heads):
    full = q_ref.shape[0]
    p_refs, refs = refs[: full // block], refs[full // block :]
    dq_ref, dk_ref, dv_ref, dr_ref, gu_ref, gv_ref, dk_t, dv_t, dr_t = refs
    length = len_ref[0]
    lane = lax.broadcasted_iota(jnp.int32, (block, 2 * HD), 1)
    sides = (lane < HD, lane >= HD)
    rows = lax.broadcasted_iota(jnp.int32, (block, block), 0)
    cols = lax.broadcasted_iota(jnp.int32, (block, block), 1)
    flip = jnp.where(rows + cols == block - 1, 1.0, 0.0).astype(bf)
    for ref in (dk_t, dv_t, dr_t, dq_ref, gu_ref, gv_ref):
        ref[...] = jnp.zeros_like(ref)
    for first in reversed(range(0, full, block)):
        span = first + block

        def one_block(first=first, span=span):
            q = q_ref[first:span, :].astype(f32)
            qu = (q + bu_ref[...]).astype(bf).astype(f32) * 0.125
            qv = (q + bv_ref[...]).astype(bf).astype(f32) * 0.125
            do = do_ref[first:span, :].astype(f32)
            o = o_ref[first:span, :]
            qu_t = jnp.transpose(qu).astype(bf)
            do_t = jnp.transpose(do).astype(bf)
            qv_t = jnp.transpose(dot(flip, qv.astype(bf), NN)).astype(bf)
            dqu, dqv = [0.0, 0.0], [0.0, 0.0]
            for head in heads:
                side = sides[head]
                at = slice(head * HD, (head + 1) * HD)
                rounded = p_refs[first // block][head - heads[0]]
                p = rounded.astype(f32)
                dp = dot(jnp.where(side, do, 0.0).astype(bf), v_ref[:span, :], NT)
                inner = jnp.sum(jnp.where(side, do * o, 0.0), axis=1, keepdims=True)
                ds = (p * (dp - inner)).astype(bf)
                dv_t[at, :span] += dot(do_t[at], rounded, NN)
                both = dot(jnp.concatenate([qu_t[at], flip], axis=0), ds, NN)
                dk_t[at, :span] += both[:HD]
                dqu[head] = dot(ds, k_ref[:span, :], NN)
                ds_rev = pltpu.roll(both[HD:], 0, 1, stride=1, stride_axis=0).astype(bf)
                dr_t[at, full - span :] += dot(qv_t[at], ds_rev, NN)
                dqv[head] = dot(ds_rev, r_ref[full - span :, :], NN)
            dqu = jnp.where(sides[0], dqu[0], dqu[1]) * 0.125
            dqv = jnp.where(sides[0], dqv[0], dqv[1]) * 0.125
            gu_ref[...] += jnp.sum(dqu, axis=0, keepdims=True)
            gv_ref[...] += jnp.sum(dqv, axis=0, keepdims=True)
            dq_ref[first:span, :] = (dqu + dot(flip, dqv.astype(bf), NN)).astype(bf)

        if first < full // 2:
            one_block()
        else:
            pl.when(first < length)(one_block)

    dk_ref[...] = jnp.transpose(dk_t[...]).astype(bf)
    dv_ref[...] = jnp.transpose(dv_t[...]).astype(bf)
    dr_ref[...] = jnp.transpose(dr_t[...]).astype(bf)


def attn_bwd(length, qkv, rel_rev, bias_u, bias_v, probs, d_out, out_rows, *, pair, heads=(0, 1), block=256):
    full, cols = rel_rev.shape
    pairs = cols // (2 * HD)
    at = lambda part: pl.BlockSpec((full, 2 * HD), lambda i, _: (0, part * pairs + pair))
    row = pl.BlockSpec((1, 2 * HD), lambda i, _: (0, pair))
    out = pl.BlockSpec((full, 2 * HD), lambda i, _: (0, 0))
    out_row = pl.BlockSpec((1, 2 * HD), lambda i, _: (0, 0))
    return pl.pallas_call(
        functools.partial(attn_bwd_body, block=block, heads=heads),
        out_shape=(jax.ShapeDtypeStruct((full, 2 * HD), bf),) * 4
        + (jax.ShapeDtypeStruct((1, 2 * HD), f32),) * 2,
        grid_spec=pltpu.PrefetchScalarGridSpec(
            num_scalar_prefetch=1,
            grid=(1,),
            in_specs=[at(0), at(1), at(2), at(0), row, row]
            + [at(0), at(0)]
            + [
                pl.BlockSpec((len(heads),) + p.shape[1:], lambda i, _: ((2 * pair + heads[0]) // len(heads), 0, 0))
                for p in probs
            ],
            out_specs=(out,) * 4 + (out_row, out_row),
            scratch_shapes=[pltpu.VMEM((2 * HD, full), f32)] * 3,
        ),
        cost_estimate=pl.CostEstimate(flops=0, bytes_accessed=0, transcendentals=0),
        compiler_params=pltpu.CompilerParams(vmem_limit_bytes=32 << 20),
        name="attn_bwd",
    )(length, qkv, qkv, qkv, rel_rev, bias_u, bias_v, d_out, out_rows, *probs)


def norm_parts(values):
    mean_val = jnp.mean(values, axis=-1, keepdims=True)
    centered = values - mean_val
    inv_std = lax.rsqrt(jnp.mean(centered * centered, axis=-1, keepdims=True) + NORM_EPS)
    return (centered * inv_std, inv_std)


def norm_back(grad_norm, x_hat, inv_std):
    first_mean = jnp.mean(grad_norm, axis=-1, keepdims=True)
    second_mean = jnp.mean(grad_norm * x_hat, axis=-1, keepdims=True)
    return inv_std * (grad_norm - first_mean - x_hat * second_mean)


def position_table(count_rows, feature_count):
    steps = lax.iota(jnp.float32, count_rows)
    half_count = feature_count // 2
    inv_freq = jnp.exp(
        lax.iota(jnp.float32, half_count) * (-2.0 * math.log(10000.0) / feature_count)
    )
    angles = steps[:, None] * inv_freq[None, :]
    return jnp.concatenate([jnp.sin(angles), jnp.cos(angles)], axis=1)


def skew_rows(matrix):
    leading = matrix.shape[:-2]
    row_count, col_count = matrix.shape[-2:]
    flattened = matrix.reshape(leading + (row_count * col_count,))
    picked = flattened[..., row_count - 1 : row_count - 1 + row_count * (col_count - 1)]
    return picked.reshape(leading + (row_count, col_count - 1))[..., : col_count - row_count]


def unskew_rows(matrix):
    leading = matrix.shape[:-2]
    row_count, key_count = matrix.shape[-2:]
    axis_pos = len(leading)
    widened = jnp.pad(matrix, [(0, 0)] * axis_pos + [(0, 0), (0, row_count - 1)])
    flattened = widened.reshape(leading + (row_count * (key_count + row_count - 1),))
    flattened = jnp.pad(flattened, [(0, 0)] * axis_pos + [(row_count - 1, 1)])
    return flattened.reshape(leading + (row_count, key_count + row_count))


def head_split_device(
    layer_input,
    lengths,
    ln1_gain,
    ln1_bias,
    w_qkv,
    w_rel,
    bias_u,
    bias_v,
    w_out,
    ln2_gain,
    ln2_bias,
    w_up,
    up_bias,
    w_down,
    down_bias,
    grad_out,
):
    weights = (
        lax.all_gather(ln1_gain, "fsdp", axis=0, tiled=True),
        lax.all_gather(ln1_bias, "fsdp", axis=0, tiled=True),
        lax.all_gather(w_qkv, "fsdp", axis=0, tiled=True),
        lax.all_gather(w_rel, "fsdp", axis=0, tiled=True),
        lax.all_gather(bias_u, "fsdp", axis=0, tiled=True),
        lax.all_gather(bias_v, "fsdp", axis=0, tiled=True),
        lax.all_gather(w_out, "fsdp", axis=0, tiled=True),
        lax.all_gather(ln2_gain, "fsdp", axis=0, tiled=True),
        lax.all_gather(ln2_bias, "fsdp", axis=0, tiled=True),
        lax.all_gather(w_up, "fsdp", axis=0, tiled=True),
        lax.all_gather(up_bias, "fsdp", axis=0, tiled=True),
        lax.all_gather(w_down, "fsdp", axis=0, tiled=True),
        lax.all_gather(down_bias, "fsdp", axis=0, tiled=True),
    )
    (
        gain_one,
        shift_one,
        query_key_value_matrix,
        rel_weight,
        first_bias,
        second_bias,
        output_matrix,
        gain_two,
        shift_two,
        up_matrix,
        up_shift,
        down_matrix,
        down_shift,
    ) = weights
    gain_one = gain_one.astype(jnp.float32)
    shift_one = shift_one.astype(jnp.float32)
    gain_two = gain_two.astype(jnp.float32)
    shift_two = shift_two.astype(jnp.float32)
    up_shift = up_shift.astype(jnp.float32)
    down_shift = down_shift.astype(jnp.float32)
    slots, block_len, width = layer_input.shape
    seq_count = lax.axis_size("seq")
    seq_rank = lax.axis_index("seq")
    head_dim = HEAD_DIM
    group = H // seq_count
    full_len = block_len * seq_count
    score_scale = 1.0 / math.sqrt(head_dim)
    q_block = 512
    num_blocks = full_len // q_block
    win_len = full_len + q_block
    x_float = layer_input.astype(jnp.float32)
    x_hat_one, inv_std_one = norm_parts(x_float)
    first_normalized = (x_hat_one * gain_one + shift_one).astype(jnp.bfloat16)
    qkv_local = jnp.einsum(
        "mcr,rk->mck", first_normalized, query_key_value_matrix, preferred_element_type=jnp.float32
    ).astype(jnp.bfloat16)
    qkv_heads = lax.all_to_all(qkv_local, "seq", split_axis=2, concat_axis=1, tiled=True)
    qkv_heads = qkv_heads.reshape(slots, full_len, group, 3, head_dim)
    queries = qkv_heads[:, :, :, 0]
    keys = qkv_heads[:, :, :, 1]
    values = qkv_heads[:, :, :, 2]
    head_start = seq_rank * group
    head_bias_u = lax.dynamic_slice_in_dim(
        first_bias.astype(jnp.float32).reshape(H, head_dim), head_start, group, 0
    )
    head_bias_v = lax.dynamic_slice_in_dim(
        second_bias.astype(jnp.float32).reshape(H, head_dim), head_start, group, 0
    )
    query_u = (queries.astype(jnp.float32) + head_bias_u).astype(jnp.bfloat16)
    query_v = (queries.astype(jnp.float32) + head_bias_v).astype(jnp.bfloat16)
    table_rev = position_table(full_len, width).astype(jnp.bfloat16)[::-1]
    rel_cols = lax.dynamic_slice_in_dim(rel_weight, head_start * head_dim, group * head_dim, 1)
    rel_rev = jnp.dot(table_rev, rel_cols, preferred_element_type=jnp.float32).astype(jnp.bfloat16)
    rel_ext = jnp.concatenate([rel_rev, jnp.zeros_like(rel_rev)], axis=0).reshape(
        2 * full_len, group, head_dim
    )
    col_ids = lax.iota(jnp.int32, full_len)

    def scores_block(first_row):
        qu_part = lax.dynamic_slice_in_dim(query_u, first_row, q_block, 1)
        qv_part = lax.dynamic_slice_in_dim(query_v, first_row, q_block, 1)
        window_start = full_len - q_block - first_row
        rel_win = lax.dynamic_slice_in_dim(rel_ext, window_start, win_len, 0)
        content = jnp.einsum("sqhe,skhe->shqk", qu_part, keys, preferred_element_type=jnp.float32)
        rel_raw = jnp.einsum("sqhe,the->shqt", qv_part, rel_win, preferred_element_type=jnp.float32)
        rel_part = skew_rows(rel_raw)
        row_ids = first_row + lax.iota(jnp.int32, q_block)
        causal = col_ids[None, :] <= row_ids[:, None]
        inside = col_ids[None, :] < lengths[:, None]
        allowed = causal[None, None, :, :] & inside[:, None, None, :]
        scores = jnp.where(allowed, (content + rel_part) * score_scale, NEG_FILL)
        return (scores, qu_part, qv_part, rel_win, window_start)

    def forward_block(block_index):
        first_row = block_index * q_block
        scores, qu_part, qv_part, rel_win, window_start = scores_block(first_row)
        top = jnp.max(scores, axis=-1, keepdims=True)
        expo = jnp.exp(scores - top)
        total = jnp.sum(expo, axis=-1, keepdims=True)
        probs = (expo / total).astype(jnp.bfloat16)
        out_part = jnp.einsum(
            "shqk,skhe->sqhe", probs, values, preferred_element_type=jnp.float32
        ).astype(jnp.bfloat16)
        return (out_part, top[..., 0] + jnp.log(total[..., 0]))

    block_outs, block_lse = lax.map(forward_block, jnp.arange(num_blocks, dtype=jnp.int32))
    attn_heads = jnp.moveaxis(block_outs, 0, 1).reshape(slots, full_len, group * head_dim)
    attention_sequence = lax.all_to_all(attn_heads, "seq", split_axis=1, concat_axis=2, tiled=True)
    attention_projected = jnp.einsum(
        "mcr,rk->mck", attention_sequence, output_matrix, preferred_element_type=jnp.float32
    )
    resid = x_float + attention_projected
    x_hat_two, inv_std_two = norm_parts(resid)
    second_normalized = (x_hat_two * gain_two + shift_two).astype(jnp.bfloat16)
    pre_act = (
        jnp.einsum("oka,ac->okc", second_normalized, up_matrix, preferred_element_type=jnp.float32)
        + up_shift
    )
    normal_cdf = 0.5 * (1.0 + lax.erf(pre_act * (1.0 / math.sqrt(2.0))))
    hidden_state = (pre_act * normal_cdf).astype(jnp.bfloat16)
    down_proj = (
        jnp.einsum("zcp,pr->zcr", hidden_state, down_matrix, preferred_element_type=jnp.float32)
        + down_shift
    )
    output = (resid + down_proj).astype(jnp.bfloat16)
    positions = seq_rank * block_len + lax.iota(jnp.int32, block_len)
    live = (positions[None, :] < lengths[:, None]).astype(jnp.bfloat16)
    result_gradient = grad_out * live[:, :, None]
    grad_y_float = result_gradient.astype(jnp.float32)
    g_down_shift = jnp.sum(grad_y_float, axis=(0, 1))
    down_gradient = jnp.einsum(
        "hki,hku->iu", hidden_state, result_gradient, preferred_element_type=jnp.float32
    )
    hidden_gradient = jnp.einsum(
        "gvu,ju->gvj", result_gradient, down_matrix, preferred_element_type=jnp.float32
    )
    deriv = normal_cdf + pre_act * jnp.exp(-0.5 * pre_act * pre_act) * (
        1.0 / math.sqrt(2.0 * math.pi)
    )
    preactivation_gradient = (hidden_gradient * deriv).astype(jnp.bfloat16)
    g_up_shift = jnp.sum(preactivation_gradient.astype(jnp.float32), axis=(0, 1))
    up_gradient = jnp.einsum(
        "oiz,oix->zx", second_normalized, preactivation_gradient, preferred_element_type=jnp.float32
    )
    second_norm_gradient = jnp.einsum(
        "rau,ku->rak", preactivation_gradient, up_matrix, preferred_element_type=jnp.float32
    )
    g_gain_two = jnp.sum(second_norm_gradient * x_hat_two, axis=(0, 1))
    g_shift_two = jnp.sum(second_norm_gradient, axis=(0, 1))
    g_resid = grad_y_float + norm_back(second_norm_gradient * gain_two, x_hat_two, inv_std_two)
    attention_gradient = g_resid.astype(jnp.bfloat16)
    output_gradient = jnp.einsum(
        "zau,zam->um", attention_sequence, attention_gradient, preferred_element_type=jnp.float32
    )
    g_attn_seq = jnp.einsum(
        "urz,jz->urj", attention_gradient, output_matrix, preferred_element_type=jnp.float32
    ).astype(jnp.bfloat16)
    g_attn_heads = lax.all_to_all(
        g_attn_seq, "seq", split_axis=2, concat_axis=1, tiled=True
    ).reshape(slots, full_len, group, head_dim)

    def backward_block(carry, block_index):
        g_keys, g_vals, g_ext = carry
        first_row = block_index * q_block
        scores, qu_part, qv_part, rel_win, window_start = scores_block(first_row)
        probs = jnp.exp(scores - block_lse[block_index][..., None])
        d_out = lax.dynamic_slice_in_dim(g_attn_heads, first_row, q_block, 1)
        g_vals = g_vals + jnp.einsum(
            "shqk,sqhe->skhe", probs.astype(jnp.bfloat16), d_out, preferred_element_type=jnp.float32
        )
        g_probs = jnp.einsum("sqhe,skhe->shqk", d_out, values, preferred_element_type=jnp.float32)
        inner = jnp.sum(probs * g_probs, axis=-1, keepdims=True)
        g_scores = (probs * (g_probs - inner)).astype(jnp.bfloat16)
        g_qu = (
            jnp.einsum("shqk,skhe->sqhe", g_scores, keys, preferred_element_type=jnp.float32)
            * score_scale
        )
        g_keys = (
            g_keys
            + jnp.einsum("shqk,sqhe->skhe", g_scores, qu_part, preferred_element_type=jnp.float32)
            * score_scale
        )
        g_wide = unskew_rows(g_scores)
        g_qv = (
            jnp.einsum("shqt,the->sqhe", g_wide, rel_win, preferred_element_type=jnp.float32)
            * score_scale
        )
        g_win = (
            jnp.einsum("shqt,sqhe->sthe", g_wide, qv_part, preferred_element_type=jnp.float32)
            * score_scale
        )
        g_old = lax.dynamic_slice_in_dim(g_ext, window_start, win_len, 1)
        g_ext = lax.dynamic_update_slice_in_dim(g_ext, g_old + g_win, window_start, 1)
        return ((g_keys, g_vals, g_ext), (g_qu, g_qv))

    zero_heads = jnp.zeros((slots, full_len, group, head_dim), jnp.float32)
    zero_ext = jnp.zeros((slots, 2 * full_len, group, head_dim), jnp.float32)
    (g_keys, g_vals, g_ext), (g_qu_blocks, g_qv_blocks) = lax.scan(
        backward_block, (zero_heads, zero_heads, zero_ext), jnp.arange(num_blocks, dtype=jnp.int32)
    )
    g_qu = jnp.moveaxis(g_qu_blocks, 0, 1).reshape(slots, full_len, group, head_dim)
    g_qv = jnp.moveaxis(g_qv_blocks, 0, 1).reshape(slots, full_len, group, head_dim)
    g_queries = g_qu + g_qv
    g_bias_u_heads = jnp.sum(g_qu, axis=(0, 1))
    g_bias_v_heads = jnp.sum(g_qv, axis=(0, 1))
    g_qkv_heads = (
        jnp.stack([g_queries, g_keys, g_vals], axis=3)
        .astype(jnp.bfloat16)
        .reshape(slots, full_len, group * 3 * head_dim)
    )
    query_key_value_gradient = lax.all_to_all(
        g_qkv_heads, "seq", split_axis=1, concat_axis=2, tiled=True
    )
    g_rel_low = g_ext[:, :full_len].astype(jnp.bfloat16)
    g_rel_heads = jnp.einsum(
        "td,sthe->dhe", table_rev, g_rel_low, preferred_element_type=jnp.float32
    ).reshape(width, group * head_dim)
    g_rel_weight = lax.dynamic_update_slice_in_dim(
        jnp.zeros((width, width), jnp.float32), g_rel_heads, head_start * head_dim, 1
    )
    g_bias_u = lax.dynamic_update_slice_in_dim(
        jnp.zeros((H, head_dim), jnp.float32), g_bias_u_heads, head_start, 0
    ).reshape(width)
    g_bias_v = lax.dynamic_update_slice_in_dim(
        jnp.zeros((H, head_dim), jnp.float32), g_bias_v_heads, head_start, 0
    ).reshape(width)
    query_key_value_weight_gradient = jnp.einsum(
        "zau,zam->um",
        first_normalized,
        query_key_value_gradient,
        preferred_element_type=jnp.float32,
    )
    first_norm_gradient = jnp.einsum(
        "urz,jz->urj",
        query_key_value_gradient,
        query_key_value_matrix,
        preferred_element_type=jnp.float32,
    )
    g_gain_one = jnp.sum(first_norm_gradient * x_hat_one, axis=(0, 1))
    g_shift_one = jnp.sum(first_norm_gradient, axis=(0, 1))
    g_input = g_resid + norm_back(first_norm_gradient * gain_one, x_hat_one, inv_std_one)
    partial_shards = (
        lax.psum_scatter(g_gain_one, "fsdp", scatter_dimension=0, tiled=True),
        lax.psum_scatter(g_shift_one, "fsdp", scatter_dimension=0, tiled=True),
        lax.psum_scatter(query_key_value_weight_gradient, "fsdp", scatter_dimension=0, tiled=True),
        lax.psum_scatter(g_rel_weight, "fsdp", scatter_dimension=0, tiled=True),
        lax.psum_scatter(g_bias_u, "fsdp", scatter_dimension=0, tiled=True),
        lax.psum_scatter(g_bias_v, "fsdp", scatter_dimension=0, tiled=True),
        lax.psum_scatter(output_gradient, "fsdp", scatter_dimension=0, tiled=True),
        lax.psum_scatter(g_gain_two, "fsdp", scatter_dimension=0, tiled=True),
        lax.psum_scatter(g_shift_two, "fsdp", scatter_dimension=0, tiled=True),
        lax.psum_scatter(up_gradient, "fsdp", scatter_dimension=0, tiled=True),
        lax.psum_scatter(g_up_shift, "fsdp", scatter_dimension=0, tiled=True),
        lax.psum_scatter(down_gradient, "fsdp", scatter_dimension=0, tiled=True),
        lax.psum_scatter(g_down_shift, "fsdp", scatter_dimension=0, tiled=True),
    )
    shards = lax.psum(
        (
            partial_shards[0],
            partial_shards[1],
            partial_shards[2],
            partial_shards[3],
            partial_shards[4],
            partial_shards[5],
            partial_shards[6],
            partial_shards[7],
            partial_shards[8],
            partial_shards[9],
            partial_shards[10],
            partial_shards[11],
            partial_shards[12],
        ),
        "seq",
    )
    return (
        output,
        g_input,
        shards[0],
        shards[1],
        shards[2],
        shards[3],
        shards[4],
        shards[5],
        shards[6],
        shards[7],
        shards[8],
        shards[9],
        shards[10],
        shards[11],
        shards[12],
    )


def swap_core(values):
    size = lax.axis_size("fsdp")
    return lax.ppermute(values, "fsdp", [(i, i ^ 1) for i in range(size)])


def swap_chip(values, mask):
    size = lax.axis_size("fsdp")
    return lax.ppermute(values, "fsdp", [(i, i ^ (2 * mask)) for i in range(size)])


def swap_axis(values, turn):
    size = lax.axis_size("fsdp")
    return lax.ppermute(values, "fsdp", [(i, i ^ (2 << ((i & 1) ^ turn))) for i in range(size)])


def swap_seq(values, mask):
    size = lax.axis_size("seq")
    return lax.ppermute(values, "seq", [(i, i ^ mask) for i in range(size)])


def slot_pairs(turn):
    seq, pairs = lax.axis_size("seq"), []
    for f in range(lax.axis_size("fsdp")):
        for z in range(seq):
            to_f, to_z = (f & ~1) | (z & 1), 2 * (f & 1) + (turn ^ (z >> 1))
            pairs.append((f * seq + z, to_f * seq + to_z))
    return pairs


def to_slots(values, seq_rank):
    return [
        lax.ppermute(
            lax.dynamic_index_in_dim(values, turn ^ (seq_rank >> 1), 0, keepdims=False),
            ("fsdp", "seq"),
            slot_pairs(turn),
        )
        for turn in (0, 1)
    ]


def together(*values):
    return lax.optimization_barrier(values)


def whole(*shape):
    return pl.BlockSpec(shape, lambda *_: (0,) * len(shape))


def kernel_call(body, name, meta, args, outs, *, grid=(1,), in_specs=None, out_specs=None, scratch=(), flops=0, vmem=32):
    in_specs = in_specs or [whole(*a.shape) for a in args]
    out_specs = out_specs or [whole(*shape) for shape, _ in outs]
    moved = sum(a.size * a.dtype.itemsize for a in args)
    moved += sum(math.prod(shape) * jnp.dtype(kind).itemsize for shape, kind in outs)
    return pl.pallas_call(
        body,
        out_shape=[jax.ShapeDtypeStruct(shape, kind) for shape, kind in outs],
        grid_spec=pltpu.PrefetchScalarGridSpec(
            num_scalar_prefetch=1,
            grid=grid,
            in_specs=in_specs,
            out_specs=out_specs,
            scratch_shapes=scratch,
        ),
        compiler_params=pltpu.CompilerParams(vmem_limit_bytes=vmem << 20),
        cost_estimate=pl.CostEstimate(flops=0, bytes_accessed=0, transcendentals=0),
        name=name,
    )(meta, *args)


TN = (((0,), (0,)), ((), ()))
CORE, CHIP, RANK, LIVE = range(4)
DIGIT = 128


def aligned(index, size):
    return pl.multiple_of(index * size, size)


def own_place():
    device = lax.axis_index("fsdp")
    return device & 1, device >> 1, lax.axis_index("seq")


def pack_body(lengths_ref, qkv_ref, rel_ref, up_ref, out_ref, down_ref, *refs):
    small, (attn_ref, feed_ref, send_ref) = refs[:8], refs[8:]
    core, _, _ = own_place()
    shard = qkv_ref.shape[0]
    qkv, rel, up, out, down = qkv_ref[...], rel_ref[...], up_ref[...], out_ref[...], down_ref[...]
    heads, hd = rel.shape[1] // HEAD_DIM // 2, HEAD_DIM
    unit = up.shape[1] // 8
    packs, ups = [], []
    row = jnp.concatenate([ref[i : i + 1] for ref in small for i in range(ref.shape[0])], axis=1)
    lane = lax.broadcasted_iota(jnp.int32, (1, 4 * heads * hd - row.shape[1]), 1)
    digits = jnp.zeros(lane.shape, f32)
    for slot in range(lengths_ref.shape[0]):
        high = lengths_ref[slot] // DIGIT
        for at, digit in ((2 * slot, high), (2 * slot + 1, lengths_ref[slot] - high * DIGIT)):
            digits = jnp.where(lane == at, digit.astype(f32), digits)
    row = jnp.concatenate([row, digits.astype(row.dtype)], axis=1)
    rows = jnp.broadcast_to(row, (8, row.shape[1]))
    for side in (0, 1):
        parts = [
            qkv[:, ((2 * j + side) * 3 + t) * hd : ((2 * j + side) * 3 + t + 1) * hd]
            for t in range(3)
            for j in range(heads)
        ]
        parts += [rel[:, (2 * j + side) * hd : (2 * j + side + 1) * hd] for j in range(heads)]
        packs.append(jnp.concatenate(parts, axis=1))
        ups.append(
            jnp.concatenate([up[:, (2 * j + side) * unit : (2 * j + side + 1) * unit] for j in range(4)], axis=1)
        )
    first = core == 0
    folded = jnp.concatenate([out[: shard // 2], out[shard // 2 :]], axis=1)
    attn_ref[:shard] = jnp.where(first, packs[0], packs[1])
    attn_ref[shard:] = rows
    send_ref[:shard] = jnp.where(first, packs[1], packs[0])
    send_ref[shard : shard + 8] = rows
    send_ref[shard + 8 : 2 * shard + 8] = jnp.where(first, ups[1], ups[0])
    send_ref[2 * shard + 8 :] = folded
    feed_ref[:shard] = jnp.where(first, ups[0], ups[1])
    feed_ref[shard : shard + shard // 2] = folded
    feed_ref[shard + shard // 2 :] = jnp.concatenate([down[: 2 * shard], down[2 * shard :]], axis=1)


def ordered(core, own, other):
    first = core == 0
    return jnp.concatenate([jnp.where(first, own, other), jnp.where(first, other, own)], axis=0)


def slot_block(core, rank, step, own, other, store):
    turn = (step >> 1) ^ (rank & 1)
    local = (step & 1) == core
    for t in (0, 1):
        pl.when(local & (turn == t))(functools.partial(store, own[t]))
        pl.when(jnp.logical_not(local) & (turn == t))(functools.partial(store, other[t]))


def norm_rows(values):
    mean_val = jnp.mean(values, axis=1, keepdims=True)
    centered = values - mean_val
    inv_std = lax.rsqrt(jnp.mean(centered * centered, axis=1, keepdims=True) + NORM_EPS)
    return centered * inv_std, inv_std


def weights_body(_, *refs):
    packs, table_ref = refs[0:4], refs[4]
    rel_ref, w_ref, vec_ref, up_ref, *bias_refs = refs[5:11]
    step, (core, chip, _) = pl.program_id(0), own_place()
    width = w_ref.shape[0]
    shard = width // 8
    span = w_ref.shape[1] - rel_ref.shape[1]

    @pl.when(step == 0)
    def _():
        first = core == 0
        vec_ref[...] = jnp.zeros_like(vec_ref)
        own_rows = []
        for k in range(4):
            at = pl.ds(aligned(chip ^ k, 2 * shard), 2 * shard)
            own, other = packs[k][: shard + 8], packs[k][shard + 8 :]
            w_ref[at, :] = ordered(core, own[:shard], other[:shard])
            own_row, other_row = own[shard : shard + 1].astype(f32), other[shard : shard + 1].astype(f32)
            own_rows.append(own_row)
            low, high = jnp.where(first, own_row, other_row), jnp.where(first, other_row, own_row)
            for row, source in enumerate((0, 1, 4, 5, 6)):
                piece = slice(source * shard, (source + 1) * shard)
                vec_ref[row : row + 1, at] = jnp.concatenate([low[:, piece], high[:, piece]], axis=1)
            unit = up_ref.shape[1] // 4
            up_ref[:, pl.ds(aligned(chip ^ k, unit), unit)] = own_row[:, 7 * shard : 7 * shard + unit]
        even = chip & 1 == 0
        for k in (0, 2):
            at = pl.ds(aligned((chip ^ k) >> 1, 2 * shard), 2 * shard)
            low = jnp.where(even, own_rows[k], own_rows[k + 1])
            high = jnp.where(even, own_rows[k + 1], own_rows[k])
            for row, source in enumerate((2, 3)):
                piece = slice(source * shard, (source + 1) * shard)
                bias_refs[row][:, at] = jnp.concatenate([low[:, piece], high[:, piece]], axis=1)

    rel_ref[...] = dot(table_ref[...], w_ref[:, span:], NN).astype(bf)


def project_body(_, *refs):
    own_x, other_x = refs[0:2], refs[2:4]
    w_ref, vec_ref, qkv_ref, h_ref, x_ref = refs[4:9]
    step, (core, _, rank) = pl.program_id(0), own_place()

    def copy(ref):
        x_ref[...] = ref[...]

    slot_block(core, rank, step, own_x, other_x, copy)
    x_hat, _ = norm_rows(x_ref[...].astype(f32))
    h = (x_hat * vec_ref[0:1, :] + vec_ref[1:2, :]).astype(bf)
    h_ref[...] = h
    qkv_ref[...] = dot(h, w_ref[:, : qkv_ref.shape[1]], NN).astype(bf)


def feed_body(meta, *refs):
    packs, own_g, other_g = refs[0:4], refs[4:6], refs[6:8]
    x_ref, o_own, o_other, vec_ref, bias_ref = refs[8:13]
    dy_ref, x_hat_ref, rstd_ref, y_keep, dh_ref, y_send, wo_mine = refs[13:20]
    outs = refs[20:24]
    up_w, down_w, wo_theirs, up_acc, down_acc, sums = refs[24:30]
    step, chip, core = pl.program_id(0), meta[CHIP], meta[CORE]
    width = up_w.shape[0]
    shard, unit, block = width // 8, down_w.shape[0] // 4, x_ref.shape[0]
    fold = shard // 2
    unfold = lambda rows: jnp.concatenate([rows[:, :width], rows[:, width:]], axis=0)

    @pl.when(step == 0)
    def _():
        sums[...] = jnp.zeros_like(sums)
        up_acc[...] = jnp.zeros_like(up_acc)
        down_acc[...] = jnp.zeros_like(down_acc)
        masks = (0, 1 + core, 2 - core, 3)
        for pack_ref, k in zip(packs, masks):
            pack, other = pack_ref[: 3 * shard + fold], pack_ref[3 * shard + fold :]
            up_w[pl.ds(aligned(chip ^ k, 2 * shard), 2 * shard), :] = ordered(core, pack[:shard], other[:shard])
            at = pl.ds(aligned(chip ^ k, shard), shard)
            wo_mine[at, :] = unfold(pack[shard : shard + fold])
            wo_theirs[at, :] = unfold(other[shard:])
            down_w[pl.ds(aligned(chip ^ k, unit), unit), :] = unfold(pack[shard + fold :])

    at = step * block + lax.broadcasted_iota(jnp.int32, (block, 1), 0)

    def load(ref):
        dy_ref[...] = jnp.where(at < meta[LIVE], ref[...].astype(f32), 0.0).astype(bf)

    slot_block(core, meta[RANK], step, own_g, other_g, load)
    y1 = x_ref[...].astype(f32) + (dot(o_own[...], wo_mine[...], NN) + dot(o_other[...], wo_theirs[...], NN))
    x_hat, inv_std = norm_rows(y1)
    x_hat_ref[...] = x_hat.astype(bf)
    rstd_ref[...] = inv_std
    h = (x_hat * vec_ref[2:3, :] + vec_ref[3:4, :]).astype(bf)
    f = dot(h, up_w[...], NN) + bias_ref[...]
    cdf = 0.5 * (1.0 + lax.erf(f * (1.0 / math.sqrt(2.0))))
    g = (f * cdf).astype(bf)
    dy = dy_ref[...]
    dg = dot(dy, down_w[...], NT)
    df = (dg * (cdf + f * jnp.exp(-0.5 * f * f) * (1.0 / math.sqrt(2.0 * math.pi)))).astype(bf)
    z = dot(g, down_w[...], NN)
    dh = dot(df, up_w[...], NT)
    dh_ref[...] = dh.astype(bf)
    up_acc[...] += dot(h, df, TN)
    down_acc[...] += dot(g, dy, TN)
    sums[0:1, :width] += jnp.sum(dh * x_hat, axis=0, keepdims=True)
    sums[1:2, :width] += jnp.sum(dh, axis=0, keepdims=True)
    sums[3:4, :] += jnp.sum(df.astype(f32), axis=0, keepdims=True)
    local = (step & 1) == core

    @pl.when(local)
    def _():
        y_keep[...] = y1 + z + vec_ref[4:5, :]
        sums[2:3, :width] += jnp.sum(dy.astype(f32), axis=0, keepdims=True)

    @pl.when(jnp.logical_not(local))
    def _():
        y_send[...] = z.astype(bf)

    @pl.when(step == pl.num_programs(0) - 1)
    def _():
        rows = 2 * shard
        for k, out in enumerate(outs):
            at = pl.ds(aligned(chip ^ k, rows), rows)
            units = pl.ds(aligned(chip ^ k, unit), unit)
            tail = [sums[0:1, at], sums[1:2, at], sums[2:3, at], sums[3:4, units]]
            tail = jnp.concatenate(tail + [jnp.zeros((1, sums.shape[1] - 3 * rows - unit), f32)], axis=1)
            out[:rows] = up_acc[at, :].astype(out.dtype)
            out[rows : rows + 8] = jnp.broadcast_to(tail, (8, tail.shape[1])).astype(out.dtype)
            down = down_acc[units, :]
            half = unit // 2
            out[rows + 8 :] = jnp.concatenate([down[:half], down[half:]], axis=1).astype(out.dtype)


def norm_two_body(meta, x_hat_ref, rstd_ref, dh_ref, dh_came, dy_ref, vec_ref, y_keep, y_came, wo_ref, o_ref, *refs):
    out0, out1, resid_ref, do_ref, go_ref = refs
    step = pl.program_id(0)

    @pl.when(step == 0)
    def _():
        go_ref[...] = jnp.zeros_like(go_ref)

    x_hat = x_hat_ref[...].astype(f32)
    e = (dh_ref[...].astype(f32) + dh_came[...].astype(f32)) * vec_ref[2:3, :]
    first = jnp.mean(e, axis=1, keepdims=True)
    second = jnp.mean(e * x_hat, axis=1, keepdims=True)
    grad = dy_ref[...].astype(f32) + rstd_ref[...] * (e - first - x_hat * second)
    da = grad.astype(bf)
    do_ref[...] = dot(da, wo_ref[...], NT).astype(bf)
    go_ref[...] += dot(o_ref[...], da, TN)
    turn = (step >> 1) ^ (meta[RANK] & 1)
    local = (step & 1) == meta[CORE]

    @pl.when(local)
    def _():
        resid_ref[...] = grad
        y = (y_keep[...] + y_came[...].astype(f32)).astype(bf)

        @pl.when(turn == 0)
        def _():
            out0[...] = y

        @pl.when(turn == 1)
        def _():
            out1[...] = y


def qkv_back_body(meta, *refs):
    grads_a, grads_b = refs[:6], refs[6:12]
    w_ref, x_ref, h_ref, table_ref, go_ref = refs[12:17]
    keep_ref, send_ref = refs[17:19]
    outs, acc, sums = refs[19:23], refs[23], refs[24]
    step, chip = pl.program_id(0), meta[CHIP]
    width = x_ref.shape[1]
    rows = width // 4

    @pl.when(step == 0)
    def _():
        sums[...] = jnp.zeros_like(sums)
        acc[...] = jnp.zeros_like(acc)

    both = lambda i: [grads_a[i][...], grads_b[i][...]]
    dqkv = jnp.concatenate(both(0) + both(1) + both(2), axis=1)
    drel = jnp.concatenate(both(3), axis=1)
    span = dqkv.shape[1]
    acc[:, :span] += dot(h_ref[...], dqkv, TN)
    acc[:, span:] += dot(table_ref[...], drel, TN)
    dh = dot(dqkv, w_ref[:, :span], NT)
    x_hat, _ = norm_rows(x_ref[...].astype(f32))
    sums[0:1, :] += jnp.sum(dh * x_hat, axis=0, keepdims=True)
    sums[1:2, :] += jnp.sum(dh, axis=0, keepdims=True)
    local = (step & 1) == meta[CORE]

    @pl.when(local)
    def _():
        keep_ref[...] = dh

    @pl.when(jnp.logical_not(local))
    def _():
        send_ref[...] = dh.astype(bf)

    @pl.when(step == pl.num_programs(0) - 1)
    def _():
        for k, out in enumerate(outs):
            at = pl.ds(aligned(chip ^ k, rows), rows)
            low = (chip ^ k) >> 1 == 0
            tail = [sums[0:1, at], sums[1:2, at]]
            tail += [jnp.where(low, *both(i)) for i in (4, 5)]
            tail = jnp.concatenate(tail + [jnp.zeros((1, acc.shape[1] - 4 * rows), f32)], axis=1)
            out[:rows] = acc[at, :].astype(out.dtype)
            out[rows : rows + 8] = jnp.broadcast_to(tail, (8, tail.shape[1])).astype(out.dtype)
            shard = rows // 2
            lines = go_ref[pl.ds(aligned(chip ^ k, shard), shard), :]
            lines = jnp.concatenate([lines[: shard // 2], lines[shard // 2 :]], axis=1)
            out[rows + 8 :] = lines.astype(out.dtype)


def norm_one_body(meta, x_ref, dh_keep, dh_came, resid_ref, vec_ref, out0, out1):
    turn = pl.program_id(0) ^ (meta[RANK] & 1)
    x_hat, inv_std = norm_rows(x_ref[...].astype(f32))
    e = (dh_keep[...] + dh_came[...].astype(f32)) * vec_ref[0:1, :]
    first = jnp.mean(e, axis=1, keepdims=True)
    second = jnp.mean(e * x_hat, axis=1, keepdims=True)
    grad = (resid_ref[...] + inv_std * (e - first - x_hat * second)).astype(bf)

    @pl.when(turn == 0)
    def _():
        out0[...] = grad

    @pl.when(turn == 1)
    def _():
        out1[...] = grad


def rank_bit(meta, bit):
    return (meta[RANK] >> bit) & 1


def chip_sum_body(meta, own, *refs, bit):
    *came, keep, send = refs
    half = keep.shape[1]
    for out, side in ((keep, rank_bit(meta, bit)), (send, 1 - rank_bit(meta, bit))):
        at = pl.ds(aligned(side, half), half)
        total = own[:, at]
        for ref in came:
            total = total + ref[:, at].astype(f32)
        out[...] = total.astype(out.dtype)


def chip_sum(meta, parts, name, bit):
    rows, size = parts[0].shape
    return kernel_call(functools.partial(chip_sum_body, bit=bit), name, meta, parts, [((rows, size // 2), f32), ((rows, size // 2), bf)])


def own_rows_first(total, core, shard):
    theirs = lax.dynamic_slice_in_dim(total, (1 - core) * shard, shard, 0)
    mine = lax.dynamic_slice_in_dim(total, core * shard, shard, 0)
    came = swap_core(jnp.concatenate([theirs, total[2 * shard : 2 * shard + 8]], axis=0))
    return jnp.concatenate([mine, came, total[2 * shard :]], axis=0)


def halves(meta, mine, other, bit):
    low = rank_bit(meta, bit) == 0
    return jnp.concatenate([jnp.where(low, mine, other), jnp.where(low, other, mine)], axis=1)


def both_cores(meta, own, came):
    own, came = own.astype(f32), came.astype(f32)
    return own, own + came, meta[CORE] == 0


def store_half(ref, source, at, low):
    size = 2 * ref.shape[1]
    piece = source[:, at * size : (at + 1) * size]
    ref[...] = jnp.where(low, piece[:, : size // 2], piece[:, size // 2 :])


def early_out_body(meta, mine, other, came_ref, g_up, g_down, *vec_refs):
    rows = halves(meta, mine[...], other[...], 0)
    came_rows = halves(meta, came_ref[0], came_ref[1], 0)
    shard, width = g_up.shape[0], g_down.shape[1]
    first, unit = meta[CORE] == 0, rows.shape[1] // 4
    own, came = jnp.where(first, rows[:shard], rows[shard : 2 * shard]), came_rows[:shard]
    pair = (jnp.where(first, own, came), jnp.where(first, came, own))
    for j in range(4):
        for side in (0, 1):
            at = (2 * j + side) * unit
            g_up[:, at : at + unit] = pair[side][:, j * unit : (j + 1) * unit].astype(f32)
    down = rows[2 * shard + 8 :].astype(f32)
    g_down[...] = jnp.concatenate([down[:, :width], down[:, width:]], axis=0)
    own, total, low = both_cores(meta, rows[2 * shard : 2 * shard + 1], came_rows[shard : shard + 1])
    for at, ref in enumerate(vec_refs[:3]):
        store_half(ref, total, at, low)
    vec_refs[3][...] = own[:, 6 * shard : 6 * shard + unit]


def late_out_body(meta, mine, other, g_qkv, g_rel, g_out, *vec_refs):
    rows = halves(meta, mine[...], other[...], 0)
    shard, width = g_qkv.shape[0], g_out.shape[1]
    first, hd, heads = meta[CORE] == 0, HEAD_DIM, H // 2
    own, came = rows[:shard], rows[shard : 2 * shard]
    pair = (jnp.where(first, own, came), jnp.where(first, came, own))
    cols = heads * hd
    piece = lambda h, t: pair[h & 1][:, t * cols + (h >> 1) * hd : t * cols + ((h >> 1) + 1) * hd]
    g_qkv[...] = jnp.concatenate([piece(h, t) for h in range(2 * heads) for t in range(3)], axis=1).astype(f32)
    g_rel[...] = jnp.concatenate([piece(h, 3) for h in range(2 * heads)], axis=1).astype(f32)
    out = rows[2 * shard + 16 :].astype(f32)
    g_out[...] = jnp.concatenate([out[:, :width], out[:, width:]], axis=0)
    own, total, low = both_cores(meta, rows[2 * shard + 8 : 2 * shard + 9], rows[2 * shard : 2 * shard + 1])
    even = meta[CHIP] & 1 == 0
    for at, ref in enumerate(vec_refs):
        store_half(ref, total if at < 2 else own, at, low if at < 2 else even)


def place_body(meta, y0, y1, x0, x1, y_ref, x_ref):
    high = meta[RANK] >> 1 == 1
    y_ref[0] = jnp.where(high, y1[...], y0[...])
    y_ref[1] = jnp.where(high, y0[...], y1[...])
    x_ref[0] = jnp.where(high, x1[...], x0[...]).astype(f32)
    x_ref[1] = jnp.where(high, x0[...], x1[...]).astype(f32)


def slot_split_device(
    layer_input,
    lengths,
    ln1_gain,
    ln1_bias,
    w_qkv,
    w_rel,
    bias_u,
    bias_v,
    w_out,
    ln2_gain,
    ln2_bias,
    w_up,
    up_bias,
    w_down,
    down_bias,
    grad_out,
):
    slots, block, width = layer_input.shape
    rank, device = lax.axis_index("seq"), lax.axis_index("fsdp")
    core, chip = device & 1, device >> 1
    full, heads = 4 * block, H // 2
    cols, shard, unit = heads * HEAD_DIM, width // 8, up_bias.shape[0]
    mine_ff = 4 * unit

    none = jnp.zeros((4,), jnp.int32)
    x_own = to_slots(jnp.concatenate([layer_input, grad_out], axis=2), rank)
    vectors = (ln1_gain, ln1_bias, bias_u, bias_v, ln2_gain, ln2_bias, down_bias, up_bias)
    attn_rows, fold = shard + 8, shard // 2
    attn_pack, feed_pack, pack_send = kernel_call(
        pack_body,
        "pack",
        pltpu.with_memory_space_constraint(lengths, pltpu.HBM),
        [
            pltpu.with_memory_space_constraint(v, pltpu.HBM)
            for v in [w_qkv, w_rel, w_up, w_out, w_down] + [v.reshape(-1, min(128, v.size)) for v in vectors]
        ],
        [((attn_rows, 4 * cols), bf), ((3 * shard + fold, 4 * cols), bf), ((attn_rows + shard + fold, 4 * cols), bf)],
        vmem=32,
    )
    pack_came = swap_core(pack_send)
    attn_pack = jnp.concatenate([attn_pack, pack_came[:attn_rows]], axis=0)
    attn_packs = [attn_pack] + [swap_chip(attn_pack, k) for k in (1, 2, 3)]
    feed_pack = jnp.concatenate([feed_pack, pack_came[attn_rows:]], axis=0)
    digits_at = 7 * shard + unit
    digits = pack_came[shard, digits_at : digits_at + 2 * slots].astype(jnp.int32)
    lengths = jnp.where(core == rank >> 1, lengths, digits[0::2] * DIGIT + digits[1::2])
    length = jnp.where(rank & 1 == 0, lengths[0], lengths[1])
    meta = jnp.stack([core, chip, rank, length]).astype(jnp.int32)
    length_arr = length.reshape(1)
    fine = 32
    inv_freq = jnp.exp(lax.iota(f32, width // 2) * (-2.0 * math.log(10000.0) / width))
    high = (full - 1 - fine * lax.iota(jnp.int32, full // fine)).astype(f32)[:, None] * inv_freq
    low = lax.iota(f32, fine)[:, None] * inv_freq
    high_sin, high_cos, low_sin, low_cos = together(jnp.sin(high), jnp.cos(high), jnp.sin(low), jnp.cos(low))
    high_sin, high_cos = high_sin[:, None], high_cos[:, None]
    table = jnp.concatenate(
        [high_sin * low_cos - high_cos * low_sin, high_cos * low_cos + high_sin * low_sin], axis=2
    )
    table = table.astype(bf).reshape(full, width)

    feed_pack, meta, length_arr, table, *attn_packs = together(feed_pack, meta, length_arr, table, *attn_packs)
    by_step = lambda width: pl.BlockSpec((block, width), lambda i, _: (i, 0))
    rel, w_own, vecs, up_b, own_u, own_v = kernel_call(
        weights_body,
        "weights",
        none,
        [pltpu.with_memory_space_constraint(v, pltpu.HBM) for v in attn_packs] + [table],
        [((full, cols), bf), ((width, 4 * cols), bf), ((8, width), f32), ((1, mine_ff), f32)]
        + [((1, cols), f32), ((1, cols), f32)],
        grid=(4,),
        in_specs=[whole(2 * attn_rows, 4 * cols)] * 4 + [by_step(width)],
        out_specs=[by_step(cols), whole(width, 4 * cols), whole(8, width), whole(1, mine_ff)]
        + [whole(1, cols), whole(1, cols)],
    )
    w_own, vecs, *x_own = together(w_own, vecs, *x_own)
    x_other = [swap_core(x) for x in x_own]
    feed_first = swap_axis(feed_pack, 0)
    feed_second = swap_axis(feed_pack, 1)

    side = lambda at: pl.BlockSpec((block, width), lambda i, _: (0, at))
    qkv, h1, x_slot = kernel_call(
        project_body,
        "project",
        none,
        x_own + x_other + [w_own, vecs],
        [((full, 3 * cols), bf), ((full, width), bf), ((full, width), bf)],
        grid=(4,),
        in_specs=[side(0)] * 4 + [whole(width, 4 * cols), whole(8, width)],
        out_specs=[by_step(3 * cols), by_step(width), by_step(width)],
    )
    qkv, feed_first = together(qkv, feed_first)
    feed_third = swap_axis(feed_first, 1)
    attn, attn_wide, *probs = attn_fwd(length_arr, qkv, rel, own_u, own_v)
    attn, feed_second, feed_third = together(attn, feed_second, feed_third)
    feed_packs = [feed_pack, feed_first, feed_second, feed_third]

    attn_other = swap_core(attn)
    kept = lambda width: pl.BlockSpec((block, width), lambda i, _: (i >> 1, 0))
    half, rows = full // 2, 2 * shard + 8
    blocks = lambda rows: [((rows, 2 * width), f32)] + [((rows, 2 * width), bf)] * 3
    dy, x_hat, rstd, y_keep, dh, y_send, wo_mine, *early_parts = kernel_call(
        feed_body,
        "feed",
        meta,
        feed_packs + x_own + x_other + [x_slot, attn, attn_other, vecs, up_b],
        [((full, width), bf), ((full, width), bf), ((full, 1), f32), ((half, width), f32)]
        + [((full, width), bf), ((half, width), bf), ((cols, width), bf)]
        + blocks(rows + unit // 2),
        grid=(4,),
        in_specs=[whole(*feed_pack.shape)] * 4 + [side(1)] * 4
        + [by_step(width), by_step(cols), by_step(cols), whole(8, width), whole(1, mine_ff)],
        out_specs=[by_step(width), by_step(width), by_step(1), kept(width)]
        + [by_step(width), kept(width), whole(cols, width)]
        + [whole(rows + unit // 2, 2 * width)] * 4,
        scratch=[
            pltpu.VMEM((width, mine_ff), bf),
            pltpu.VMEM((mine_ff, width), bf),
            pltpu.VMEM((cols, width), bf),
            pltpu.VMEM((width, mine_ff), f32),
            pltpu.VMEM((mine_ff, width), f32),
            pltpu.VMEM((8, mine_ff), f32),
        ],
        flops=12 * full * width * mine_ff,
    )
    dh_came = swap_core(dh)
    y_came = swap_core(y_send)
    early_came = [swap_chip(early_parts[k], k) for k in (1, 2, 3)]
    out0, out1, g_resid, d_attn, g_out = kernel_call(
        norm_two_body,
        "norm_two",
        meta,
        [x_hat, rstd, dh, dh_came, dy, vecs, y_keep, y_came, wo_mine, attn],
        [((block, width), bf)] * 2 + [((half, width), f32), ((full, cols), bf), ((cols, width), f32)],
        grid=(4,),
        in_specs=[by_step(width), by_step(1)] + [by_step(width)] * 3 + [whole(8, width)] + [kept(width)] * 2
        + [whole(cols, width), by_step(cols)],
        out_specs=[whole(block, width)] * 2 + [kept(width), by_step(cols), whole(cols, width)],
        flops=4 * full * width * cols,
    )
    home = lambda outs: [
        lax.ppermute(out, ("fsdp", "seq"), [(b, a) for a, b in slot_pairs(turn)])
        for turn, out in enumerate(outs)
    ]
    y_turns = home((out0, out1))
    back = lambda pair, d_out: attn_bwd(length_arr, qkv, rel, own_u, own_v, probs, d_out, attn_wide, pair=pair)
    d_attn, *grads_a = together(d_attn, *back(0, d_attn))
    *grads_b, y0, y1, e1, e2, e3 = together(*back(1, d_attn), *y_turns, *early_came)
    early_keep, early_send = chip_sum(meta, [early_parts[0], e1, e2, e3], "early_chips", 0)
    early_send, *grads_b = together(early_send, *grads_b)
    early_came = swap_seq(early_send, 1)
    pair_step = pl.BlockSpec((block, 2 * HEAD_DIM), lambda i, _: (i, 0))
    pair_row = whole(1, 2 * HEAD_DIM)
    dh1_keep, dh1_send, *late_parts = kernel_call(
        qkv_back_body,
        "qkv_back",
        meta,
        [*grads_a, *grads_b, w_own, x_slot, h1, table, g_out],
        [((half, width), f32), ((half, width), bf)] + blocks(rows + fold),
        grid=(4,),
        in_specs=([pair_step] * 4 + [pair_row] * 2) * 2
        + [whole(width, 4 * cols)] + [by_step(width)] * 3 + [whole(cols, width)],
        out_specs=[kept(width)] * 2 + [whole(rows + fold, 2 * width)] * 4,
        scratch=[pltpu.VMEM((width, 4 * cols), f32), pltpu.VMEM((8, width), f32)],
        flops=14 * full * width * cols,
    )
    dh1_send, *late_parts = together(dh1_send, *late_parts)
    early_pair = (early_keep + early_came.astype(f32)).astype(bf)
    dh1_came = swap_core(dh1_send)
    early_came = swap_seq(early_pair, 2)
    late_came = [swap_chip(late_parts[k], k) for k in (1, 2, 3)]
    by_half = pl.BlockSpec((block, width), lambda i, _: (i, 0))
    own_rows = pl.BlockSpec((block, width), lambda i, m: (2 * i + m[CORE], 0))
    x0, x1 = kernel_call(
        norm_one_body,
        "norm_one",
        meta,
        [x_slot, dh1_keep, dh1_came, g_resid, vecs],
        [((block, width), bf)] * 2,
        grid=(2,),
        in_specs=[own_rows] + [by_half] * 3 + [whole(8, width)],
        out_specs=[whole(block, width)] * 2,
    )
    x_turns = home((x0, x1))
    late_keep, late_send = chip_sum(meta, [late_parts[0]] + late_came, "late_chips", 0)
    small = lambda size: ((1, size), f32)
    late_came, early_came, x_turns[0] = together(swap_seq(late_send, 1), early_came, x_turns[0])
    early_mine = (early_pair.astype(f32) + early_came.astype(f32)).astype(bf)
    late_pair = (late_keep + late_came.astype(f32)).astype(bf)
    late_came = swap_seq(late_pair, 2)
    early_other = swap_seq(early_mine, 1)
    late_total = (late_pair.astype(f32) + late_came.astype(f32)).astype(bf)
    late_mine = own_rows_first(late_total, core, shard)
    late_other = swap_seq(late_mine, 1)
    late_mine, g0, g1, early_other = together(late_mine, *x_turns, early_other)
    theirs = lambda rows: jnp.concatenate(
        [
            lax.dynamic_slice_in_dim(rows, (1 - core) * shard, shard, 0),
            rows[2 * shard : 2 * shard + 8],
        ],
        axis=0,
    )
    early_core = swap_core(jnp.stack([theirs(early_mine), theirs(early_other)]))
    output, grad_x = kernel_call(
        place_body,
        "place",
        meta,
        [y0, y1, g0, g1],
        [((2, block, width), bf), ((2, block, width), f32)],
    )
    g_up, g_down, g_gain_two, g_shift_two, g_down_shift, g_up_shift = kernel_call(
        early_out_body,
        "early_out",
        meta,
        [early_mine, early_other, early_core],
        [((shard, 2 * mine_ff), f32), ((unit, width), f32)] + [small(shard)] * 3 + [small(unit)],
    )
    late_other, output, grad_x, g_up = together(late_other, output, grad_x, g_up)
    g_qkv, g_rel, g_w_out, *late_vectors = kernel_call(
        late_out_body,
        "late_out",
        meta,
        [late_mine, late_other],
        [((shard, 6 * cols), f32), ((shard, 2 * cols), f32), ((shard, width), f32)] + [small(shard)] * 4,
    )
    g_gain_one, g_shift_one, g_bias_u, g_bias_v = [v.reshape(-1) for v in late_vectors]
    return (
        output,
        grad_x,
        g_gain_one,
        g_shift_one,
        g_qkv,
        g_rel,
        g_bias_u,
        g_bias_v,
        g_w_out,
        g_gain_two.reshape(-1),
        g_shift_two.reshape(-1),
        g_up,
        g_up_shift.reshape(-1),
        g_down,
        g_down_shift.reshape(-1),
    )


def per_device(*args):
    one_slot_a_chip = lax.axis_size("fsdp") == 8 and lax.axis_size("seq") == 4
    if one_slot_a_chip and args[0].shape[0] == 2:
        return slot_split_device(*args)
    return head_split_device(*args)


def solution(mesh):
    placed = (
        P("fsdp", "seq", None),
        P("fsdp"),
        P("fsdp"),
        P("fsdp"),
        P("fsdp", None),
        P("fsdp", None),
        P("fsdp"),
        P("fsdp"),
        P("fsdp", None),
        P("fsdp"),
        P("fsdp"),
        P("fsdp", None),
        P("fsdp"),
        P("fsdp", None),
        P("fsdp"),
        P("fsdp", "seq", None),
    )
    return jax.shard_map(
        per_device,
        mesh=mesh,
        in_specs=placed,
        out_specs=(
            P("fsdp", "seq", None),
            P("fsdp", "seq", None),
            P("fsdp"),
            P("fsdp"),
            P("fsdp", None),
            P("fsdp", None),
            P("fsdp"),
            P("fsdp"),
            P("fsdp", None),
            P("fsdp"),
            P("fsdp"),
            P("fsdp", None),
            P("fsdp"),
            P("fsdp", None),
            P("fsdp"),
        ),
        check_vma=False,
    )
```
